32 devices in a mesh: dp: 16 (over z, y, x), mp: 2 (over core).
Axes of the slice: x: 2, y: 2, z: 4, core: 2. Of those that a mesh axis runs over, the one named last changes fastest.
Arguments:
- series: float32 [32, 1024], P('dp'), may hold values from -10 to 10
- observed: int32 [32, 1024], P('dp'), may hold values from 0 to 1
- routes: int32 [32, 1024, 2], P('dp'), may hold values from 0 to 7, all different within a row; in each aligned block of 2048 rows (0 to 2047, 2048 to 4095, ..., all dimensions but the last counted through in order) at most 1024 rows name the same one
- step_count: int32 [1], replicated, may hold values from 2 to 20
- joint_proj: float32 [3, 384, 384], P(None, 'dp', 'mp'), may hold values from -0.3125 to 0.3125
- joint_moment: float32 [3, 384, 384], P(None, 'dp', 'mp'), may hold values from -4.172325e-07 to 4.172325e-07
- joint_square: float32 [3, 384, 384], P(None, 'dp', 'mp'), may hold values from 3.1761813e-15 to 1.2680571e-14
- mixer_proj: float32 [384, 384], P('mp', 'dp'), may hold values from -1.25 to 1.25
- mixer_moment: float32 [384, 384], P('mp', 'dp'), may hold values from -4.172325e-07 to 4.172325e-07
- mixer_square: float32 [384, 384], P('mp', 'dp'), may hold values from 3.1761813e-15 to 1.2680571e-14
- upward_proj: float32 [9, 384, 2, 1536], P(None, 'dp', None, 'mp'), may hold values from -0.3125 to 0.3125
- upward_moment: float32 [9, 384, 2, 1536], P(None, 'dp', None, 'mp'), may hold values from -4.172325e-07 to 4.172325e-07
- upward_square: float32 [9, 384, 2, 1536], P(None, 'dp', None, 'mp'), may hold values from 3.1761813e-15 to 1.2680571e-14
- downward_proj: float32 [9, 1536, 384], P(None, 'mp', 'dp'), may hold values from -0.625 to 0.625
- downward_moment: float32 [9, 1536, 384], P(None, 'mp', 'dp'), may hold values from -4.172325e-07 to 4.172325e-07
- downward_square: float32 [9, 1536, 384], P(None, 'mp', 'dp'), may hold values from 3.1761813e-15 to 1.2680571e-14
- readout: float32 [384, 114], P('dp'), may hold values from -0.3125 to 0.3125
- readout_moment: float32 [384, 114], P('dp'), may hold values from -4.172325e-07 to 4.172325e-07
- readout_square: float32 [384, 114], P('dp'), may hold values from 3.1761813e-15 to 1.2680571e-14
- vectors: float32 [5, 384], P(None, 'dp'), may hold values from -4 to 4, as said below
- vectors_moment: float32 [5, 384], P(None, 'dp'), may hold values from -3.8146973e-06 to 3.8146973e-06
- vectors_square: float32 [5, 384], P(None, 'dp'), may hold values from 3.176181e-13 to 1.2680572e-12
Outputs:
- total_loss: float32 [], replicated
- grad_norm: float32 [], replicated
- joint_updated: float32 [3, 384, 384], P(None, 'dp', 'mp')
- joint_moment_next: float32 [3, 384, 384], P(None, 'dp', 'mp')
- joint_square_next: float32 [3, 384, 384], P(None, 'dp', 'mp')
- mixer_updated: float32 [384, 384], P('mp', 'dp')
- mixer_moment_next: float32 [384, 384], P('mp', 'dp')
- mixer_square_next: float32 [384, 384], P('mp', 'dp')
- upward_updated: float32 [9, 384, 2, 1536], P(None, 'dp', None, 'mp')
- upward_moment_next: float32 [9, 384, 2, 1536], P(None, 'dp', None, 'mp')
- upward_square_next: float32 [9, 384, 2, 1536], P(None, 'dp', None, 'mp')
- downward_updated: float32 [9, 1536, 384], P(None, 'mp', 'dp')
- downward_moment_next: float32 [9, 1536, 384], P(None, 'mp', 'dp')
- downward_square_next: float32 [9, 1536, 384], P(None, 'mp', 'dp')
- readout_updated: float32 [384, 114], P('dp')
- readout_moment_next: float32 [384, 114], P('dp')
- readout_square_next: float32 [384, 114], P('dp')
- vectors_updated: float32 [5, 384], P(None, 'dp')
- vectors_moment_next: float32 [5, 384], P(None, 'dp')
- vectors_square_next: float32 [5, 384], P(None, 'dp')
The draws below stay inside these ranges and needn't reach their ends.
Inputs may be any that keep to these rules, and one draw needn't show every extreme that they name: `routes`: in the rows of one device no expert is named by more than 1024 pairs, a bound that some block reaches; a point names two different experts. `vectors`: rows 0 to 2 are positive.
All inputs are finite; a program needn't handle non-finite values.
Results may differ from the reference program's by a relative error of at most 0.00065.
The reference program's roundings to bfloat16 on the way count: a program that leaves them out, or rounds other values in their place, can miss the bound.
Values may be sent and summed in bfloat16 or wider, within the bound.
A program may use at most 320 MiB of HBM per device.

```python
import math
import jax
import jax.numpy as jnp
import numpy as np
from jax import lax

D = 384
HEADS = 12
HEAD = 32
FF = 1536
ROUTED_EXPERTS = 8
LEN = 1024
TOK_DEV = 2048
SERIES = 32
CAP = 1024
PARAMS = 16560768
N_DP = 16


def draw_vectors(key, part):
    gain_key = jax.random.fold_in(key, 11)
    embed_key = jax.random.fold_in(key, 23)
    gains = jnp.exp(jax.random.uniform(gain_key, (3, D), jnp.float32, -0.7, 0.7))
    embeds = jnp.clip(jax.random.normal(embed_key, (2, D), jnp.float32), -4.0, 4.0)
    return jnp.concatenate([gains, embeds], axis=0)


def draw_series(key, part):
    position = jnp.arange(SERIES, dtype=jnp.float32) / max(SERIES - 1, 1)
    spread = 1.0 + 1.5 * position
    base = jnp.clip(jax.random.normal(key, (SERIES, LEN), jnp.float32), -4.0, 4.0)
    return base * spread[:, None]


def draw_observed(key, part):
    rank = jnp.arange(SERIES, dtype=jnp.int32)
    threshold = 300 + 650 * rank // max(SERIES - 1, 1)
    dice = jax.random.randint(key, (SERIES, LEN), 0, 1000, dtype=jnp.int32)
    return (dice < threshold[:, None]).astype(jnp.int32)


def level_of(key, extent, cuts, smallest, largest):
    gain, own = 1.0, jax.random.fold_in(key, 6)
    for axis_at, parts in cuts:
        heights = jnp.exp(jax.random.uniform(jax.random.fold_in(own, axis_at), (parts,), jnp.float32, smallest / len(cuts), largest / len(cuts)))
        gain = gain * jnp.repeat(heights, extent[axis_at] // parts).reshape([-1 if axis == axis_at else 1 for axis in range(len(extent))])
    return gain


def deal_out(key, own, number, rows, count, top, most, slope):
    sequence = jax.random.permutation(key, count)
    heavy_load, common = load_shares(count, rows * top, most, slope, True), load_shares(count, rows * top, most, slope, False)
    places = jnp.arange(count)

    def named(lengths, offset_by):
        used = int((lengths > 0).sum())
        fixed = max(1, used // 4)
        shifted = fixed + (places - fixed + offset_by * (used - fixed)) % max(1, count - fixed)
        return jnp.zeros((count,), jnp.int32).at[sequence[jnp.where(places < fixed, places, shifted)]].set(jnp.asarray(lengths, jnp.int32))

    lengths = jnp.where(number % 4 == 0, named(heavy_load, number // 4), named(common, number - number // 4 - 1))
    mixed = jax.random.permutation(jax.random.fold_in(own, 3), count)
    giver, sink = mixed[0:count // 2 * 2:2], mixed[1:count // 2 * 2:2]
    room = jnp.minimum(lengths[giver] - 1, most - lengths[sink]) // 2
    room = jnp.where((giver == sequence[0]) | (sink == sequence[0]) | (lengths[sink] == 0), 0, jnp.maximum(room, 0))
    shifted = jax.random.randint(jax.random.fold_in(own, 4), (count // 2,), 0, 1 << 20) % (room + 1)
    lengths = lengths.at[giver].add(-shifted).at[sink].add(shifted)
    labels = jnp.searchsorted(jnp.cumsum(lengths), jnp.arange(rows * top), side="right").astype(jnp.int32)
    grid = labels.reshape(top, rows).T
    grid = grid[jax.random.permutation(jax.random.fold_in(own, 1), rows)]
    offset_by = jax.random.randint(jax.random.fold_in(own, 2), (rows, 1), 0, top)
    return jnp.take_along_axis(grid, (jnp.arange(top)[None, :] + offset_by) % top, axis=1)


def load_shares(amount, total, most, lean, full):
    weights = [(1 << 20) // math.isqrt(grade ** lean) + 1 for grade in range(1, amount + 1)]
    largest = most if full else min(most, max(-(-total // amount), total * weights[0] // sum(weights)))
    least = 1 if total - largest >= amount - 1 else 0
    counts, surplus = [largest] + [least] * (amount - 1), total - largest - least * (amount - 1)
    while surplus > 0:
        candidates = [i for i in range(1, amount) if counts[i] < largest] or [i for i in range(1, amount) if counts[i] < most]
        mass, budget = sum([weights[i] for i in candidates]), surplus
        for i in candidates:
            addition = min(most - counts[i], max(1, budget * weights[i] // mass), surplus)
            counts[i] = counts[i] + addition
            surplus = surplus - addition
    return np.array(counts)


def scatter_about(stream_key, shape, scale, bound, split=(), kind=jnp.bfloat16):
    level = level_of(stream_key, shape, split, -0.22, 0.18) if split else 1.0
    values = jax.random.normal(stream_key, shape, jnp.float32) * scale * level
    return jnp.minimum(jnp.maximum(values, -bound), bound).astype(kind)


def setup_inputs(seed: int = 0) -> dict:
    arg_keys = jax.random.split(jax.random.key(seed), 23)
    series = draw_series(jax.random.fold_in(arg_keys[22], 71), 0)
    observed = draw_observed(jax.random.fold_in(arg_keys[22], 71), 0)
    routes_keys = jax.random.split(jax.random.fold_in(arg_keys[2], 1), SERIES * LEN // TOK_DEV)
    routes_turns = jax.random.permutation(jax.random.fold_in(arg_keys[2], 3), SERIES * LEN // TOK_DEV)
    routes = jax.vmap(lambda own, number: deal_out(jax.random.fold_in(arg_keys[2], 2), own, number, TOK_DEV, ROUTED_EXPERTS, 2, CAP, 1))(routes_keys, routes_turns).reshape((SERIES, LEN, 2))
    step_count = jax.random.randint(arg_keys[3], (1,), 2, 21).astype(jnp.int32)
    joint_proj = scatter_about(arg_keys[4], (3, D, D), D ** -0.5, 0.3125, ((1, 16), (2, 2)), jnp.float32)
    joint_moment = scatter_about(arg_keys[5], (3, D, D), (0.000111 / PARAMS ** 0.5), 4.172325134277344e-07, ((1, 16), (2, 2)), jnp.float32)
    joint_square = jnp.clip(jnp.exp(math.log(1.2680571111374495e-14) - 1.3843914 * jax.random.uniform(arg_keys[6], (3, D, D), jnp.float32) ** level_of(arg_keys[6], (3, D, D), ((1, 16), (2, 2)), -0.2, 0.2)), 3.1761812757245995e-15, 1.2680571111374495e-14)
    mixer_proj = scatter_about(arg_keys[7], (D, D), (D // 16) ** -0.5, 1.25, ((0, 2), (1, 16)), jnp.float32)
    mixer_moment = scatter_about(arg_keys[8], (D, D), (0.000111 / PARAMS ** 0.5), 4.172325134277344e-07, ((0, 2), (1, 16)), jnp.float32)
    mixer_square = jnp.clip(jnp.exp(math.log(1.2680571111374495e-14) - 1.3843914 * jax.random.uniform(arg_keys[9], (D, D), jnp.float32) ** level_of(arg_keys[9], (D, D), ((0, 2), (1, 16)), -0.2, 0.2)), 3.1761812757245995e-15, 1.2680571111374495e-14)
    upward_proj = scatter_about(arg_keys[10], (ROUTED_EXPERTS + 1, D, 2, FF), D ** -0.5, 0.3125, ((1, 16), (3, 2)), jnp.float32)
    upward_moment = scatter_about(arg_keys[11], (ROUTED_EXPERTS + 1, D, 2, FF), (0.000111 / PARAMS ** 0.5), 4.172325134277344e-07, ((1, 16), (3, 2)), jnp.float32)
    upward_square = jnp.clip(jnp.exp(math.log(1.2680571111374495e-14) - 1.3843914 * jax.random.uniform(arg_keys[12], (ROUTED_EXPERTS + 1, D, 2, FF), jnp.float32) ** level_of(arg_keys[12], (ROUTED_EXPERTS + 1, D, 2, FF), ((1, 16), (3, 2)), -0.2, 0.2)), 3.1761812757245995e-15, 1.2680571111374495e-14)
    downward_proj = scatter_about(arg_keys[13], (ROUTED_EXPERTS + 1, FF, D), (FF // 16) ** -0.5, 0.625, ((1, 2), (2, 16)), jnp.float32)
    downward_moment = scatter_about(arg_keys[14], (ROUTED_EXPERTS + 1, FF, D), (0.000111 / PARAMS ** 0.5), 4.172325134277344e-07, ((1, 2), (2, 16)), jnp.float32)
    downward_square = jnp.clip(jnp.exp(math.log(1.2680571111374495e-14) - 1.3843914 * jax.random.uniform(arg_keys[15], (ROUTED_EXPERTS + 1, FF, D), jnp.float32) ** level_of(arg_keys[15], (ROUTED_EXPERTS + 1, FF, D), ((1, 2), (2, 16)), -0.2, 0.2)), 3.1761812757245995e-15, 1.2680571111374495e-14)
    readout = scatter_about(arg_keys[16], (D, ROUTED_EXPERTS + 106), D ** -0.5, 0.3125, ((0, 16),), jnp.float32)
    readout_moment = scatter_about(arg_keys[17], (D, ROUTED_EXPERTS + 106), (0.000111 / PARAMS ** 0.5), 4.172325134277344e-07, ((0, 16),), jnp.float32)
    readout_square = jnp.clip(jnp.exp(math.log(1.2680571111374495e-14) - 1.3843914 * jax.random.uniform(arg_keys[18], (D, ROUTED_EXPERTS + 106), jnp.float32) ** level_of(arg_keys[18], (D, ROUTED_EXPERTS + 106), ((0, 16),), -0.2, 0.2)), 3.1761812757245995e-15, 1.2680571111374495e-14)
    vectors = draw_vectors(jax.random.fold_in(arg_keys[22], 71), 0)
    vectors_moment = scatter_about(arg_keys[20], (5, D), (0.00111 / PARAMS ** 0.5), 3.814697265625e-06, ((1, 16),), jnp.float32)
    vectors_square = jnp.clip(jnp.exp(math.log(1.268057165347558e-12) - 1.38439147 * jax.random.uniform(arg_keys[21], (5, D), jnp.float32) ** level_of(arg_keys[21], (5, D), ((1, 16),), -0.2, 0.2)), 3.17618110631801e-13, 1.268057165347558e-12)
    return {"series": series, "observed": observed, "routes": routes, "step_count": step_count, "joint_proj": joint_proj, "joint_moment": joint_moment, "joint_square": joint_square, "mixer_proj": mixer_proj, "mixer_moment": mixer_moment, "mixer_square": mixer_square, "upward_proj": upward_proj, "upward_moment": upward_moment, "upward_square": upward_square, "downward_proj": downward_proj, "downward_moment": downward_moment, "downward_square": downward_square, "readout": readout, "readout_moment": readout_moment, "readout_square": readout_square, "vectors": vectors, "vectors_moment": vectors_moment, "vectors_square": vectors_square}


@jax.custom_vjp
def low(v):
    return lax.optimization_barrier(v.astype(jnp.bfloat16)).astype(jnp.float32)

@jax.custom_vjp
def lower_backward(v):
    return v

def low_keep(v):
    return (low(v), None)

def low_pass(kept, grad):
    return (grad,)

def back_keep(v):
    return (v, None)

def back_low(kept, grad):
    return (low(grad),)
low.defvjp(low_keep, low_pass)
lower_backward.defvjp(back_keep, back_low)
horizons = (1, 8, 32, 64)
quadratic_cutoff = 2.0
aux_factor = 0.02
clip_limit = 0.001
beta_one = 0.9
beta_two = 0.95
adam_eps = 1e-08
decay_rate = 0.1
matrix_rate = 0.05
vector_rate = 0.25
norm_eps = 1e-06
rope_base = 10000.0
highest_level = lax.Precision.HIGHEST

def rms_scale(tensor, gain_row):
    return tensor * lax.rsqrt(lax.optimization_barrier(jnp.mean(tensor * tensor, axis=-1, keepdims=True)) + norm_eps) * gain_row

def rope_tables(length, columns):
    halfway = columns // 2
    frequency = rope_base ** (-2.0 * jnp.arange(halfway, dtype=jnp.float32) / columns)
    angles = jnp.arange(length, dtype=jnp.float32)[:, None] * frequency[None, :]
    return (jnp.cos(angles), jnp.sin(angles))

def rotate(tensor, cosine_table, sine_table):
    halfway = tensor.shape[-1] // 2
    front_part = tensor[..., :halfway]
    back_part = tensor[..., halfway:]
    return jnp.concatenate([front_part * cosine_table - back_part * sine_table, back_part * cosine_table + front_part * sine_table], axis=-1)

def swiglu(tensor):
    halfway = tensor.shape[-1] // 2
    return jax.nn.silu(tensor[..., :halfway]) * tensor[..., halfway:]

def targets_of(series, observed):
    row_count, length = series.shape
    longest = max(horizons)
    padded_values = jnp.concatenate([series, jnp.zeros((row_count, longest), jnp.float32)], axis=1)
    padded_marks = jnp.concatenate([observed.astype(jnp.float32), jnp.zeros((row_count, longest), jnp.float32)], axis=1)
    value_window = jnp.stack([padded_values[:, 1 + offset:1 + offset + length] for offset in range(longest)], axis=-1)
    mark_window = jnp.stack([padded_marks[:, 1 + offset:1 + offset + length] for offset in range(longest)], axis=-1)
    observed_future_series = jnp.concatenate([value_window[..., :horizon] for horizon in horizons], axis=-1)
    valid_mask = jnp.concatenate([mark_window[..., :horizon] for horizon in horizons], axis=-1)
    return (observed_future_series.reshape(row_count * length, -1), valid_mask.reshape(row_count * length, -1))

def head_counts(valid_mask):
    beginnings = [sum(horizons[:index]) for index in range(len(horizons))]
    return jnp.stack([jnp.sum(valid_mask[:, beginning:beginning + horizon]) for beginning, horizon in zip(beginnings, horizons)])

def head_weights(head_count):
    return jnp.concatenate([jnp.zeros((horizon,), jnp.float32) + 0.25 / head_count[index] for index, horizon in enumerate(horizons)])

def dispatch_plan(route_rows, experts, capacity):
    flat_routes = route_rows.reshape(-1).astype(jnp.int32)
    entries = flat_routes.shape[0]
    onehot = (flat_routes[:, None] == jnp.arange(experts, dtype=jnp.int32)[None, :]).astype(jnp.int32)
    position = (lax.optimization_barrier(jnp.sum(jnp.cumsum(onehot, axis=0) * onehot, axis=1)) - 1).astype(jnp.int32)
    slot_index = (flat_routes * capacity + position).astype(jnp.int32)
    source = jnp.full((experts * capacity,), entries, jnp.int32).at[slot_index].set(jnp.arange(entries, dtype=jnp.int32))
    return (slot_index, source)

def adam_update(master, moment, square, gradient, factor, bias_one, bias_two, step_rate):
    clipped = gradient * factor
    new_moment = beta_one * moment + (1.0 - beta_one) * clipped
    new_square = beta_two * square + (1.0 - beta_two) * clipped * clipped
    updated = master - step_rate * (new_moment / bias_one / (jnp.sqrt(new_square / bias_two) + adam_eps) + decay_rate * master)
    return (updated, new_moment, new_square)

def attend(query_heads, key_heads, value_heads):
    length = query_heads.shape[1]
    scores = lower_backward(jnp.einsum('hqe,hke->hqk', query_heads, key_heads, precision=highest_level)) * HEAD ** (-0.5)
    allowed = jnp.arange(length)[:, None] >= jnp.arange(length)[None, :]
    scores = jnp.where(allowed[None], scores, -1e+30)
    weights = jax.nn.softmax(scores, axis=-1)
    return low(lower_backward(jnp.einsum('hqk,hke->hqe', low(weights), value_heads, precision=highest_level)))

def ffn_block(normed, route_rows, upward, downward):
    entries = normed.shape[0]
    capacity = entries // 2
    slot_index, source = dispatch_plan(route_rows, ROUTED_EXPERTS, capacity)
    padded = jnp.concatenate([normed, jnp.zeros((1, D), jnp.float32)], axis=0)
    gathered = padded[source // 2].reshape(ROUTED_EXPERTS, capacity, D)
    up_flat = upward.reshape(ROUTED_EXPERTS + 1, D, 2 * FF)
    gate_up = lower_backward(jnp.einsum('ecd,edf->ecf', gathered, up_flat[:ROUTED_EXPERTS], precision=highest_level))
    hidden = low(swiglu(gate_up))
    expert_out = lower_backward(jnp.einsum('ecf,efd->ecd', hidden, downward[:ROUTED_EXPERTS], precision=highest_level)).reshape(ROUTED_EXPERTS * capacity, D)
    picked = expert_out[slot_index].reshape(entries, 2, D)
    shared_up = lower_backward(jnp.dot(normed, up_flat[ROUTED_EXPERTS], precision=highest_level))
    shared_hidden = low(swiglu(shared_up))
    shared_out = lower_backward(jnp.dot(shared_hidden, downward[ROUTED_EXPERTS], precision=highest_level))
    return (picked, shared_out)

def forward(masters, series, observed, routes, expert_count, head_count, observed_future_series, valid_mask):
    joint, mixer, upward, downward, readout, vectors = [low(weight) for weight in masters]
    total_tokens = series.shape[0] * series.shape[1]
    inputs = (series * observed.astype(jnp.float32)).reshape(-1, 1)
    embedded = jax.nn.silu(inputs * vectors[3]) * (inputs * vectors[4])
    normed_one = low(rms_scale(embedded, vectors[0]))
    projected = lower_backward(jnp.einsum('td,cde->cte', normed_one, joint, precision=highest_level))
    heads_all = projected.reshape(3, SERIES, LEN, HEADS, HEAD).transpose(0, 1, 3, 2, 4)
    cosine_table, sine_table = rope_tables(LEN, HEAD)
    query_heads = low(rotate(heads_all[0], cosine_table, sine_table))
    key_heads = low(rotate(heads_all[1], cosine_table, sine_table))
    value_heads = low(heads_all[2])
    attended = lax.map(jax.checkpoint(lambda pieces: attend(pieces[0], pieces[1], pieces[2])), (query_heads, key_heads, value_heads))
    attended = attended.transpose(0, 2, 1, 3).reshape(total_tokens, D)
    after_attn = embedded + lower_backward(jnp.dot(attended, mixer, precision=highest_level))
    normed_two = low(rms_scale(after_attn, vectors[1]))
    logits = lower_backward(jnp.dot(normed_two, readout[:, :ROUTED_EXPERTS + 1], precision=highest_level))
    probabilities = jax.nn.softmax(logits[:, :ROUTED_EXPERTS], axis=-1)
    shared_gate = jax.nn.sigmoid(logits[:, ROUTED_EXPERTS])
    route_rows = routes.reshape(total_tokens, 2).astype(jnp.int32)
    gate_values = jnp.take_along_axis(probabilities, route_rows, axis=1)
    block_rows = total_tokens // N_DP
    picked, shared_out = lax.map(jax.checkpoint(lambda pieces: ffn_block(pieces[0], pieces[1], upward, downward)), (normed_two.reshape(N_DP, block_rows, D), route_rows.reshape(N_DP, block_rows, 2)))
    mixed = lax.optimization_barrier(jnp.sum(gate_values[:, :, None] * picked.reshape(total_tokens, 2, D), axis=1)) + shared_gate[:, None] * shared_out.reshape(total_tokens, D)
    after_mixer = after_attn + mixed
    normalized_output = low(rms_scale(after_mixer, vectors[2]))
    model_estimates = lower_backward(jnp.dot(normalized_output, readout[:, ROUTED_EXPERTS + 1:], precision=highest_level))
    prediction_misses = model_estimates - observed_future_series
    absolute_miss = jnp.abs(prediction_misses)
    robust_penalty_entries = jnp.where(absolute_miss <= quadratic_cutoff, 0.5 * prediction_misses * prediction_misses, quadratic_cutoff * (absolute_miss - 0.5 * quadratic_cutoff))
    fit_loss = jnp.sum(robust_penalty_entries * valid_mask * head_weights(head_count)[None, :])
    balance = aux_factor * ROUTED_EXPERTS * jnp.sum(expert_count / total_tokens * lax.optimization_barrier(jnp.sum(probabilities, axis=0)) / total_tokens)
    return fit_loss + balance

def reference(series, observed, routes, step_count, joint_proj, joint_moment, joint_square, mixer_proj, mixer_moment, mixer_square, upward_proj, upward_moment, upward_square, downward_proj, downward_moment, downward_square, readout, readout_moment, readout_square, vectors, vectors_moment, vectors_square):
    masters = (joint_proj, mixer_proj, upward_proj, downward_proj, readout, vectors)
    moments = (joint_moment, mixer_moment, upward_moment, downward_moment, readout_moment, vectors_moment)
    squares = (joint_square, mixer_square, upward_square, downward_square, readout_square, vectors_square)
    flat_routes = routes.reshape(-1).astype(jnp.int32)
    expert_count = lax.optimization_barrier(jnp.sum((flat_routes[:, None] == jnp.arange(ROUTED_EXPERTS, dtype=jnp.int32)[None, :]).astype(jnp.float32), axis=0))
    observed_future_series, valid_mask = targets_of(series, observed)
    head_count = head_counts(valid_mask)
    total_loss, loss_back = jax.vjp(lambda *weights: forward(weights, series, observed, routes, expert_count, head_count, observed_future_series, valid_mask), *masters)
    gradients = loss_back(jnp.ones((), jnp.float32))
    grad_norm = jnp.sqrt(sum([jnp.sum(gradient * gradient) for gradient in gradients]))
    factor = clip_limit / (grad_norm + 1e-06)
    steps_taken = step_count[0].astype(jnp.float32)
    bias_one = 1.0 - beta_one ** steps_taken
    bias_two = 1.0 - beta_two ** steps_taken
    results = [adam_update(masters[index], moments[index], squares[index], gradients[index], factor, bias_one, bias_two, vector_rate if index == 5 else matrix_rate) for index in range(6)]
    return (total_loss, grad_norm, results[0][0], results[0][1], results[0][2], results[1][0], results[1][1], results[1][2], results[2][0], results[2][1], results[2][2], results[3][0], results[3][1], results[3][2], results[4][0], results[4][1], results[4][2], results[5][0], results[5][1], results[5][2])
```

```python
import functools
import jax
import jax.numpy as jnp
from jax import lax
from jax.experimental import pallas as pl
from jax.experimental.pallas import tpu as pltpu
from jax.sharding import PartitionSpec as P

D = 384
HEAD = 32
ROUTED_EXPERTS = 8
LANES = 128
TILE = 256
SHARD = 24

horizons = (1, 8, 32, 64)
quadratic_cutoff = 2.0
aux_factor = 0.02
clip_limit = 0.001
beta_one = 0.9
beta_two = 0.95
adam_eps = 1e-08
decay_rate = 0.1
matrix_rate = 0.05
vector_rate = 0.25
norm_eps = 1e-06
rope_base = 10000.0

F32 = jnp.float32
BF16 = jnp.bfloat16
MESH = pl.DeviceIdType.MESH
VMEM = pl.BlockSpec(memory_space=pltpu.VMEM)
ANY = pl.BlockSpec(memory_space=pl.ANY)


def dot(a, b, da=1, db=0):
    return lax.dot_general(a, b, (((da,), (db,)), ((), ())), preferred_element_type=F32)


def params(megabytes=60, **more):
    return pltpu.CompilerParams(vmem_limit_bytes=megabytes * 1024 * 1024, **more)


def sigmoid(v):
    return 1.0 / (1.0 + jnp.exp(-v))


def column(row, length):
    return jnp.transpose(jnp.broadcast_to(row, (LANES, length)))


def embed_chunk(xb, gate_row, up_row):
    u = xb * gate_row
    return u * sigmoid(u) * (xb * up_row)


def rotated(t, cos, sin):
    half = HEAD // 2
    front, back = t[:half], t[half:]
    return jnp.concatenate([front * cos - back * sin, back * cos + front * sin], axis=0)


def unrotated(t, cos, sin):
    half = HEAD // 2
    front, back = t[:half], t[half:]
    return jnp.concatenate([front * cos + back * sin, back * cos - front * sin], axis=0)


def score_block(k_rows, q_cols, low, length):
    s = dot(k_rows, q_cols)
    keys = lax.broadcasted_iota(jnp.int32, s.shape, 0)
    queries = lax.broadcasted_iota(jnp.int32, s.shape, 1) + low
    return jnp.where(keys <= queries, s, -1e30)


def attend_forward_kernel(
    x_ref, rows_ref, wj_ref, wo_ref, cos_ref, sin_ref,
    x0_ref, a_ref, qkv_ref, lse_ref, o_ref, part_ref,
):
    length = x_ref.shape[-1]
    heads = wo_ref.shape[0] // HEAD
    width = heads * HEAD
    scale = HEAD ** (-0.5)

    def embed(i, carry):
        r = pl.ds(pl.multiple_of(i * TILE, TILE), TILE)
        xb = column(x_ref[0, :, r], TILE)
        cuts = []
        square = None
        for c in range(D // LANES):
            cols = slice(c * LANES, (c + 1) * LANES)
            v = embed_chunk(xb, rows_ref[1:2, cols], rows_ref[2:3, cols])
            x0_ref[r, cols] = v
            square = v * v if square is None else square + v * v
            cuts.append(v)
        scale_row = lax.rsqrt(jnp.sum(square, axis=1, keepdims=True) / D + norm_eps)
        for c in range(D // LANES):
            cols = slice(c * LANES, (c + 1) * LANES)
            a_ref[r, cols] = (cuts[c] * scale_row * rows_ref[0:1, cols]).astype(BF16)
        return carry

    lax.fori_loop(0, length // TILE, embed, 0)
    a = a_ref[...]
    cos, sin = cos_ref[...], sin_ref[...]

    def project(h, carry):
        for part in range(3):
            rows = pl.ds(pl.multiple_of(part * width + h * HEAD, HEAD), HEAD)
            t = dot(wj_ref[rows, :], a, 1, 1)
            if part < 2:
                t = rotated(t, cos, sin)
            qkv_ref[0, rows, :] = t.astype(BF16)
        return carry

    lax.fori_loop(0, heads, project, 0)

    def head(h, carry):
        q_rows = pl.ds(pl.multiple_of(h * HEAD, HEAD), HEAD)
        k_rows = pl.ds(pl.multiple_of(width + h * HEAD, HEAD), HEAD)
        v_rows = pl.ds(pl.multiple_of(2 * width + h * HEAD, HEAD), HEAD)
        k = jnp.transpose(qkv_ref[0, k_rows, :].astype(F32)).astype(BF16)
        for j in range(length // TILE):
            n = TILE * (j + 1)
            cols = slice(j * TILE, (j + 1) * TILE)
            s = score_block(k[:n], qkv_ref[0, q_rows, cols], j * TILE, n)
            peak = jnp.max(s, axis=0, keepdims=True)
            e = jnp.exp((s - peak) * scale)
            mass = jnp.sum(e, axis=0, keepdims=True)
            weights = (e * (1.0 / mass)).astype(BF16)
            o_ref[0, q_rows, cols] = dot(qkv_ref[0, v_rows, :n], weights).astype(BF16)
            lse_ref[0, pl.ds(h, 1), cols] = peak * scale + jnp.log(mass)
        return carry

    lax.fori_loop(0, heads, head, 0)
    part_ref[...] = dot(o_ref[0], wo_ref[...], 0, 0)


def attend_forward(x, rows, wj, wo, cos, sin):
    series, _, length = x.shape
    tokens = series * length
    width = wo.shape[0]
    full = lambda shape: pl.BlockSpec(shape, lambda i: (0,) * len(shape))
    tok = lambda w: pl.BlockSpec((length, w), lambda i: (i, 0))
    ser = lambda r: pl.BlockSpec((1, r, length), lambda i: (i, 0, 0))
    return pl.pallas_call(
        attend_forward_kernel,
        grid=(series,),
        in_specs=[ser(1), full(rows.shape), full(wj.shape), full(wo.shape), full(cos.shape), full(sin.shape)],
        out_specs=[tok(D), tok(D), ser(3 * width), ser(8), ser(width), tok(D)],
        out_shape=[
            jax.ShapeDtypeStruct((tokens, D), F32),
            jax.ShapeDtypeStruct((tokens, D), BF16),
            jax.ShapeDtypeStruct((series, 3 * width, length), BF16),
            jax.ShapeDtypeStruct((series, 8, length), F32),
            jax.ShapeDtypeStruct((series, width, length), BF16),
            jax.ShapeDtypeStruct((tokens, D), F32),
        ],
        compiler_params=params(),
        name="attend_forward",
    )(x, rows, wj, wo, cos, sin)


def attend_backward_kernel(
    qkv_ref, do_ref, lse_ref, a_ref, wj_ref, cos_ref, sin_ref, dw_ref, part_ref, dqkv_ref, dk_ref, dv_ref
):
    length = qkv_ref.shape[-1]
    width = do_ref.shape[1]
    heads = width // HEAD
    scale = HEAD ** (-0.5)
    cos, sin = cos_ref[...], sin_ref[...]

    def flip(t):
        return jnp.transpose(t.astype(F32)).astype(BF16)

    def head(h, carry):
        q_rows = pl.ds(pl.multiple_of(h * HEAD, HEAD), HEAD)
        k_rows = pl.ds(pl.multiple_of(width + h * HEAD, HEAD), HEAD)
        v_rows = pl.ds(pl.multiple_of(2 * width + h * HEAD, HEAD), HEAD)
        q = flip(qkv_ref[0, q_rows, :])
        k = flip(qkv_ref[0, k_rows, :])
        v = flip(qkv_ref[0, v_rows, :])
        do = flip(do_ref[0, q_rows, :])
        dk_ref[...] = jnp.zeros_like(dk_ref)
        dv_ref[...] = jnp.zeros_like(dv_ref)
        for j in range(length // TILE):
            n = TILE * (j + 1)
            cols = slice(j * TILE, (j + 1) * TILE)
            s = score_block(k[:n], qkv_ref[0, q_rows, cols], j * TILE, n)
            w = jnp.exp(s * scale - lse_ref[0, pl.ds(h, 1), cols])
            dv_ref[:n] += dot(w.astype(BF16), do[cols])
            dw = dot(v[:n], do_ref[0, q_rows, cols])
            mean = jnp.sum(w * dw, axis=0, keepdims=True)
            ds = (w * (dw - mean) * scale).astype(BF16)
            dk_ref[:n] += dot(ds, q[cols])
            dq = dot(qkv_ref[0, k_rows, :n], ds)
            dqkv_ref[q_rows, cols] = unrotated(dq, cos[:, cols], sin[:, cols]).astype(BF16)
        dqkv_ref[k_rows, :] = unrotated(jnp.transpose(dk_ref[...]), cos, sin).astype(BF16)
        dqkv_ref[v_rows, :] = jnp.transpose(dv_ref[...]).astype(BF16)
        return carry

    lax.fori_loop(0, heads, head, 0)

    @pl.when(pl.program_id(0) == 0)
    def _():
        dw_ref[...] = jnp.zeros_like(dw_ref)

    dw_ref[...] += dot(dqkv_ref[...], a_ref[...])
    part_ref[...] = dot(dqkv_ref[...], wj_ref[...], 0, 0)


def attend_backward(qkv, do, lse, a, wj, cos, sin):
    series, rows, length = qkv.shape
    tokens = series * length
    full = lambda shape: pl.BlockSpec(shape, lambda i: (0,) * len(shape))
    tok = lambda w: pl.BlockSpec((length, w), lambda i: (i, 0))
    ser = lambda r: pl.BlockSpec((1, r, length), lambda i: (i, 0, 0))
    return pl.pallas_call(
        attend_backward_kernel,
        grid=(series,),
        in_specs=[ser(rows), ser(do.shape[1]), ser(8), tok(D), full(wj.shape), full(cos.shape), full(sin.shape)],
        out_specs=[full((rows, D)), tok(D)],
        out_shape=[jax.ShapeDtypeStruct((rows, D), F32), jax.ShapeDtypeStruct((tokens, D), F32)],
        scratch_shapes=[
            pltpu.VMEM((rows, length), BF16), pltpu.VMEM((length, HEAD), F32), pltpu.VMEM((length, HEAD), F32),
        ],
        compiler_params=params(),
        name="attend_backward",
    )(qkv, do, lse, a, wj, cos, sin)


GROUP = 16


def spread_rows(dest, value, start, count):
    for c in range(value.shape[1] // LANES):
        dest[pl.ds(start * 8 + c, count, stride=8), :] = value[:, c * LANES:(c + 1) * LANES]


def pick_rows(source, tile, index_ref, base):
    def body(i, carry):
        values = []
        for k in range(GROUP):
            t = index_ref[base + i * GROUP + k]
            values.append(source[pl.ds(pl.multiple_of(t * 8, 8), 8), :])
        for k in range(GROUP):
            tile[pl.ds(pl.multiple_of((i * GROUP + k) * 8, 8), 8), :] = values[k]
        return carry

    lax.fori_loop(0, TILE // GROUP, body, 0)


def add_rows(dest, tile, index_ref, base):
    def body(i, carry):
        places, values = [], []
        for k in range(GROUP):
            t = index_ref[base + i * GROUP + k]
            place = pl.ds(pl.multiple_of(t * 8, 8), 8)
            places.append(place)
            values.append(dest[place, :] + tile[pl.ds(pl.multiple_of((i * GROUP + k) * 8, 8), 8), :])
        for k in range(GROUP):
            dest[places[k], :] = values[k]
        return carry

    lax.fori_loop(0, TILE // GROUP, body, 0)


def gathered_columns(tile, columns):
    return [tile[pl.ds(c, TILE, stride=8), :] for c in range(columns)]


def lane_of(block, lane):
    lanes = lax.broadcasted_iota(jnp.int32, block.shape, 1)
    return jnp.sum(jnp.where(lanes == lane, block, 0.0), axis=1, keepdims=True)


def expert_forward_kernel(
    counts, source, b_ref, pc_ref, w_ref, x_ref, y_ref, ys_ref, mix_ref, rows8, acc8, tile8
):
    e = pl.program_id(0)
    tokens = b_ref.shape[0]
    hidden = w_ref.shape[2] // 3

    @pl.when(e == 0)
    def _():
        def lay(i, carry):
            r = pl.ds(pl.multiple_of(i * TILE, TILE), TILE)
            spread_rows(rows8, b_ref[r, :].astype(F32), i * TILE, TILE)
            rows8[pl.ds(i * TILE * 8 + 3, TILE, stride=8), :] = pc_ref[r, :]
            acc8[pl.ds(pl.multiple_of(i * TILE * 8, 8), TILE * 8), :] = jnp.zeros((TILE * 8, LANES), F32)
            return carry
        lax.fori_loop(0, tokens // TILE, lay, 0)
        rows8[pl.ds(tokens * 8, 8), :] = jnp.zeros((8, LANES), F32)
        acc8[pl.ds(tokens * 8, 8), :] = jnp.zeros((8, LANES), F32)

    def run(x):
        g = dot(x, w_ref[0, :, : 2 * hidden])
        gate, up = g[:, :hidden], g[:, hidden:]
        h = (gate * sigmoid(gate) * up).astype(BF16)
        return dot(h, w_ref[0, :, 2 * hidden:], 1, 1)

    @pl.when(e < ROUTED_EXPERTS)
    def _():
        capacity = y_ref.shape[1]

        def step(i, carry):
            base = e * capacity + i * TILE
            r = pl.ds(pl.multiple_of(i * TILE, TILE), TILE)
            pick_rows(rows8, tile8, source, base)
            c0, c1, c2, pc = gathered_columns(tile8, 4)
            x = jnp.concatenate([c0, c1, c2], axis=1).astype(BF16)
            x_ref[0, r, :] = x
            y = run(x)
            y_ref[0, r, :] = y
            spread_rows(tile8, y * lane_of(pc, e), 0, TILE)
            add_rows(acc8, tile8, source, base)
            return carry

        lax.fori_loop(0, (counts[e] + TILE - 1) // TILE, step, 0)

    @pl.when(e == ROUTED_EXPERTS)
    def _():
        def step(i, carry):
            r = pl.ds(pl.multiple_of(i * TILE, TILE), TILE)
            y = run(b_ref[r, :])
            ys_ref[r, :] = y
            shared = y * lane_of(pc_ref[r, :], ROUTED_EXPERTS)
            for c in range(D // LANES):
                cols = slice(c * LANES, (c + 1) * LANES)
                mix_ref[r, cols] = acc8[pl.ds(i * TILE * 8 + c, TILE, stride=8), :] + shared[:, cols]
            return carry

        lax.fori_loop(0, tokens // TILE, step, 0)


def expert_forward(counts, source, b, pc, weights):
    tokens = b.shape[0]
    capacity = tokens // 2
    last = ROUTED_EXPERTS - 1
    full = lambda shape: pl.BlockSpec(shape, lambda e, *_: (0,) * len(shape))
    exp = lambda w: pl.BlockSpec((1, capacity, w), lambda e, *_: (jnp.minimum(e, last), 0, 0))
    return pl.pallas_call(
        expert_forward_kernel,
        grid_spec=pltpu.PrefetchScalarGridSpec(
            num_scalar_prefetch=2,
            grid=(ROUTED_EXPERTS + 1,),
            in_specs=[full(b.shape), full(pc.shape), pl.BlockSpec((1,) + weights.shape[1:], lambda e, *_: (e, 0, 0))],
            out_specs=[exp(D), exp(D), full((tokens, D)), full((tokens, D))],
            scratch_shapes=[
                pltpu.VMEM(((tokens + 1) * 8, LANES), F32),
                pltpu.VMEM(((tokens + 1) * 8, LANES), F32),
                pltpu.VMEM((TILE * 8, LANES), F32),
            ],
        ),
        out_shape=[
            jax.ShapeDtypeStruct((ROUTED_EXPERTS, capacity, D), BF16),
            jax.ShapeDtypeStruct((ROUTED_EXPERTS, capacity, D), F32),
            jax.ShapeDtypeStruct((tokens, D), F32),
            jax.ShapeDtypeStruct((tokens, D), F32),
        ],
        compiler_params=params(),
        name="expert_forward",
    )(counts, source, b, pc, weights)


def expert_backward_kernel(
    counts, source, b_ref, pc_ref, dx_ref, w_ref, x_ref, y_ref, ys_ref, dw_ref, acc_ref, rows8, acc8, tile8
):
    e = pl.program_id(0)
    tokens = b_ref.shape[0]
    hidden = w_ref.shape[2] // 3

    @pl.when(e == 0)
    def _():
        def lay(i, carry):
            r = pl.ds(pl.multiple_of(i * TILE, TILE), TILE)
            spread_rows(rows8, dx_ref[r, :], i * TILE, TILE)
            rows8[pl.ds(i * TILE * 8 + 3, TILE, stride=8), :] = pc_ref[r, :]
            acc8[pl.ds(pl.multiple_of(i * TILE * 8, 8), TILE * 8), :] = jnp.zeros((TILE * 8, LANES), F32)
            return carry
        lax.fori_loop(0, tokens // TILE, lay, 0)
        rows8[pl.ds(tokens * 8, 8), :] = jnp.zeros((8, LANES), F32)
        acc8[pl.ds(tokens * 8, 8), :] = jnp.zeros((8, LANES), F32)

    dw_ref[...] = jnp.zeros_like(dw_ref)

    def run(x, dy):
        u = w_ref[0, :, : 2 * hidden]
        g = dot(x, u)
        gate, up = g[:, :hidden], g[:, hidden:]
        s = sigmoid(gate)
        silu = gate * s
        h = (silu * up).astype(BF16)
        dh = dot(dy, w_ref[0, :, 2 * hidden:])
        d_up = (dh * silu).astype(BF16)
        d_gate = (dh * up * (s * (1.0 + gate * (1.0 - s)))).astype(BF16)
        dg = jnp.concatenate([d_gate, d_up], axis=1)
        dw_ref[0, :, : 2 * hidden] += dot(x, dg, 0, 0)
        dw_ref[0, :, 2 * hidden:] += dot(dy, h, 0, 0)
        return dot(dg, u, 1, 1)

    @pl.when(e < ROUTED_EXPERTS)
    def _():
        capacity = y_ref.shape[1]

        def step(i, carry):
            base = e * capacity + i * TILE
            r = pl.ds(pl.multiple_of(i * TILE, TILE), TILE)
            pick_rows(rows8, tile8, source, base)
            c0, c1, c2, pc = gathered_columns(tile8, 4)
            dx = jnp.concatenate([c0, c1, c2], axis=1)
            d_gate = jnp.sum(y_ref[0, r, :] * dx, axis=1, keepdims=True)
            dy = (dx * lane_of(pc, e)).astype(BF16)
            back = run(x_ref[0, r, :], dy)
            spread_rows(tile8, back, 0, TILE)
            lanes = lax.broadcasted_iota(jnp.int32, (TILE, LANES), 1)
            tile8[pl.ds(3, TILE, stride=8), :] = jnp.where(lanes == e, d_gate, 0.0)
            add_rows(acc8, tile8, source, base)
            return carry

        lax.fori_loop(0, (counts[e] + TILE - 1) // TILE, step, 0)

    @pl.when(e == ROUTED_EXPERTS)
    def _():
        def step(i, carry):
            r = pl.ds(pl.multiple_of(i * TILE, TILE), TILE)
            dx = dx_ref[r, :]
            d_gate = jnp.sum(ys_ref[r, :] * dx, axis=1, keepdims=True)
            dy = (dx * lane_of(pc_ref[r, :], ROUTED_EXPERTS)).astype(BF16)
            back = run(b_ref[r, :], dy)
            for c in range(D // LANES):
                cols = slice(c * LANES, (c + 1) * LANES)
                acc_ref[r, cols] = acc8[pl.ds(i * TILE * 8 + c, TILE, stride=8), :] + back[:, cols]
            lanes = lax.broadcasted_iota(jnp.int32, (TILE, LANES), 1)
            acc_ref[r, D:] = jnp.where(
                lanes == ROUTED_EXPERTS, d_gate, acc8[pl.ds(i * TILE * 8 + 3, TILE, stride=8), :])
            return carry

        lax.fori_loop(0, tokens // TILE, step, 0)


def expert_backward(counts, source, b, pc, dx, weights, x, y, ys):
    tokens = b.shape[0]
    capacity = tokens // 2
    last = ROUTED_EXPERTS - 1
    once = pl.Buffered(1)
    full = lambda shape: pl.BlockSpec(shape, lambda e, *_: (0,) * len(shape), pipeline_mode=once)
    exp = lambda w: pl.BlockSpec((1, capacity, w), lambda e, *_: (jnp.minimum(e, last), 0, 0))
    wide = pl.BlockSpec((1,) + weights.shape[1:], lambda e, *_: (e, 0, 0))
    return pl.pallas_call(
        expert_backward_kernel,
        grid_spec=pltpu.PrefetchScalarGridSpec(
            num_scalar_prefetch=2,
            grid=(ROUTED_EXPERTS + 1,),
            in_specs=[full(b.shape), full(pc.shape), full(dx.shape), wide, exp(D), exp(D), full(ys.shape)],
            out_specs=[wide, full((tokens, D + LANES))],
            scratch_shapes=[
                pltpu.VMEM(((tokens + 1) * 8, LANES), F32),
                pltpu.VMEM(((tokens + 1) * 8, LANES), F32),
                pltpu.VMEM((TILE * 8, LANES), F32),
            ],
        ),
        out_shape=[
            jax.ShapeDtypeStruct(weights.shape, F32),
            jax.ShapeDtypeStruct((tokens, D + LANES), F32),
        ],
        compiler_params=params(),
        name="expert_backward",
    )(counts, source, b, pc, dx, weights, x, y, ys)


def exchange(part, other, send_sem, recv_sem):
    dp, mp = lax.axis_index("dp"), lax.axis_index("mp")
    barrier = pltpu.get_barrier_semaphore()
    pl.semaphore_signal(barrier, inc=1, device_id=(dp, 1 - mp), device_id_type=MESH)
    pl.semaphore_wait(barrier, 1)

    def copy(i):
        r = pl.ds(pl.multiple_of(i * TILE, TILE), TILE)
        return pltpu.make_async_remote_copy(
            src_ref=part.at[r], dst_ref=other.at[r], send_sem=send_sem.at[i], recv_sem=recv_sem.at[i],
            device_id=(dp, 1 - mp), device_id_type=MESH)

    def begin(i, carry):
        copy(i).start()
        return carry

    lax.fori_loop(0, part.shape[0] // TILE, begin, 0)
    return lambda i: copy(i).wait()


def exchange_scratch(part):
    tiles = part.shape[0] // TILE
    return [pltpu.VMEM(part.shape, F32), pltpu.SemaphoreType.DMA((tiles,)), pltpu.SemaphoreType.DMA((tiles,))]


def mid_forward_kernel(part, x0, gain, router, x1, b, pc, total, other, send_sem, recv_sem):
    wait = exchange(part, other, send_sem, recv_sem)
    total[...] = jnp.zeros_like(total)

    def step(i, carry):
        r = pl.ds(pl.multiple_of(i * TILE, TILE), TILE)
        wait(i)
        x = x0[r, :] + (part[r, :] + other[r, :])
        x1[r, :] = x
        scale = lax.rsqrt(jnp.mean(x * x, axis=1, keepdims=True) + norm_eps)
        low = (x * scale * gain[...]).astype(BF16)
        b[r, :] = low
        logits = dot(low, router[...])
        lanes = lax.broadcasted_iota(jnp.int32, logits.shape, 1)
        routed = lanes < ROUTED_EXPERTS
        peak = jnp.max(jnp.where(routed, logits, -jnp.inf), axis=1, keepdims=True)
        e = jnp.where(routed, jnp.exp(jnp.where(routed, logits - peak, 0.0)), 0.0)
        probability = e / jnp.sum(e, axis=1, keepdims=True)
        pc[r, :] = jnp.where(lanes == ROUTED_EXPERTS, sigmoid(logits), probability)
        total[...] += jnp.sum(probability, axis=0, keepdims=True)
        return carry

    lax.fori_loop(0, part.shape[0] // TILE, step, 0)


def mid_forward(part, x0, gain, router, ident):
    tokens = part.shape[0]
    return pl.pallas_call(
        mid_forward_kernel,
        in_specs=[VMEM] * 4,
        out_specs=[VMEM] * 4,
        out_shape=[
            jax.ShapeDtypeStruct((tokens, D), F32), jax.ShapeDtypeStruct((tokens, D), BF16),
            jax.ShapeDtypeStruct((tokens, LANES), F32), jax.ShapeDtypeStruct((1, LANES), F32),
        ],
        scratch_shapes=exchange_scratch(part),
        compiler_params=params(collective_id=ident, has_side_effects=True),
        name="mid_forward",
    )(part, x0, gain, router)


def hankel(base, shape):
    block = jnp.broadcast_to(base, (LANES, 2 * LANES))
    m = pltpu.roll(block, 0, 1, stride=1, stride_axis=0)[:, :LANES]
    lanes = lax.broadcasted_iota(jnp.int32, (LANES, LANES), 1)
    out = pltpu.roll(m, 41, 1)
    out = jnp.where(lanes < 104, pltpu.roll(m, 40, 1), out)
    out = jnp.where(lanes < 96, pltpu.roll(m, 32, 1), out)
    return jnp.where(lanes < 64, m, out)


def loss_kernel(part, x1, gain, heads, heads_t, values, marks, weight, dx2, d_heads, d_gain, loss,
                other, send_sem, recv_sem):
    wait = exchange(part, other, send_sem, recv_sem)
    d_heads[...] = jnp.zeros_like(d_heads)
    d_gain[...] = jnp.zeros_like(d_gain)
    loss[...] = jnp.zeros_like(loss)

    def step(i, carry):
        r = pl.ds(pl.multiple_of(i * TILE, TILE), TILE)
        wait(i)
        x = x1[r, :] + (part[r, :] + other[r, :])
        scale = lax.rsqrt(jnp.mean(x * x, axis=1, keepdims=True) + norm_eps)
        unit = x * scale
        low = (unit * gain[...]).astype(BF16)
        z = dot(low, heads[...])
        target = jnp.concatenate(
            [hankel(values[pl.ds(2 * i + k, 1), :], None) for k in range(2)], axis=0)
        valid = jnp.concatenate(
            [hankel(marks[pl.ds(2 * i + k, 1), :], None) for k in range(2)], axis=0)
        factor = valid * weight[...]
        miss = z - target
        size = jnp.abs(miss)
        huber = jnp.where(
            size <= quadratic_cutoff, 0.5 * miss * miss, quadratic_cutoff * (size - 0.5 * quadratic_cutoff))
        loss[...] += jnp.sum(huber * factor, axis=0, keepdims=True)
        dz = (jnp.clip(miss, -quadratic_cutoff, quadratic_cutoff) * factor).astype(BF16)
        d_heads[...] += dot(dz, low, 0, 0)
        df = dot(dz, heads_t[...])
        d_gain[...] += jnp.sum(df * unit, axis=0, keepdims=True)
        dn = df * gain[...]
        dx2[r, :] = scale * (dn - unit * jnp.mean(dn * unit, axis=1, keepdims=True))
        return carry

    lax.fori_loop(0, part.shape[0] // TILE, step, 0)


def loss_stage(part, x1, gain, heads, heads_t, values, marks, weight, ident):
    tokens = part.shape[0]
    return pl.pallas_call(
        loss_kernel,
        in_specs=[VMEM] * 8,
        out_specs=[VMEM] * 4,
        out_shape=[
            jax.ShapeDtypeStruct((tokens, D), F32), jax.ShapeDtypeStruct((LANES, D), F32),
            jax.ShapeDtypeStruct((1, D), F32), jax.ShapeDtypeStruct((1, LANES), F32),
        ],
        scratch_shapes=exchange_scratch(part),
        compiler_params=params(collective_id=ident, has_side_effects=True),
        name="loss_stage",
    )(part, x1, gain, heads, heads_t, values, marks, weight)


def mid_backward_kernel(part, dx2, x1, b, pc, gain, router_t, balance, wo, o, dx1, do, d_router, d_wo, d_gain,
                        other, send_sem, recv_sem):
    wait = exchange(part, other, send_sem, recv_sem)
    d_router[...] = jnp.zeros_like(d_router)
    d_wo[...] = jnp.zeros_like(d_wo)
    d_gain[...] = jnp.zeros_like(d_gain)
    per = o.shape[2] // TILE

    def step(i, carry):
        r = pl.ds(pl.multiple_of(i * TILE, TILE), TILE)
        wait(i)
        dp = part[r, D:] + other[r, D:] + balance[...]
        p = pc[r, :]
        lanes = lax.broadcasted_iota(jnp.int32, p.shape, 1)
        routed = lanes < ROUTED_EXPERTS
        weighted = jnp.sum(jnp.where(routed, p * dp, 0.0), axis=1, keepdims=True)
        dl = jnp.where(routed, p * (dp - weighted), jnp.where(lanes == ROUTED_EXPERTS, dp * p * (1.0 - p), 0.0))
        dl = dl.astype(BF16)
        low = b[r, :]
        d_router[...] += dot(dl, low, 0, 0)
        db = part[r, :D] + other[r, :D] + dot(dl, router_t[...])
        x = x1[r, :]
        scale = lax.rsqrt(jnp.mean(x * x, axis=1, keepdims=True) + norm_eps)
        unit = x * scale
        d_gain[...] += jnp.sum(db * unit, axis=0, keepdims=True)
        dn = db * gain[...]
        dx = dx2[r, :] + scale * (dn - unit * jnp.mean(dn * unit, axis=1, keepdims=True))
        dx1[r, :] = dx
        d_low = dx.astype(BF16)
        n, cols = i // per, pl.ds(pl.multiple_of(lax.rem(i, per) * TILE, TILE), TILE)
        do[n, :, cols] = dot(wo[...], d_low, 1, 1).astype(BF16)
        d_wo[...] += dot(o[n, :, cols], d_low)
        return carry

    lax.fori_loop(0, part.shape[0] // TILE, step, 0)


def mid_backward(part, dx2, x1, b, pc, gain, router_t, balance, wo, o, ident):
    tokens = part.shape[0]
    return pl.pallas_call(
        mid_backward_kernel,
        in_specs=[VMEM] * 10,
        out_specs=[VMEM] * 5,
        out_shape=[
            jax.ShapeDtypeStruct((tokens, D), F32), jax.ShapeDtypeStruct(o.shape, BF16),
            jax.ShapeDtypeStruct((LANES, D), F32), jax.ShapeDtypeStruct(wo.shape, F32),
            jax.ShapeDtypeStruct((1, D), F32),
        ],
        scratch_shapes=exchange_scratch(part),
        compiler_params=params(collective_id=ident, has_side_effects=True),
        name="mid_backward",
    )(part, dx2, x1, b, pc, gain, router_t, balance, wo, o)


def embed_backward_kernel(part, dx1, x_ref, rows_ref, sums, other, send_sem, recv_sem):
    wait = exchange(part, other, send_sem, recv_sem)
    sums[...] = jnp.zeros_like(sums)
    per = x_ref.shape[2] // TILE

    def step(i, carry):
        r = pl.ds(pl.multiple_of(i * TILE, TILE), TILE)
        wait(i)
        n, cols = i // per, pl.ds(pl.multiple_of(lax.rem(i, per) * TILE, TILE), TILE)
        xb = column(x_ref[n, :, cols], TILE)
        xb = jnp.concatenate([xb] * (D // LANES), axis=1)
        u = xb * rows_ref[1:2, :]
        up = xb * rows_ref[2:3, :]
        s = sigmoid(u)
        silu = u * s
        x = silu * up
        scale = lax.rsqrt(jnp.mean(x * x, axis=1, keepdims=True) + norm_eps)
        unit = x * scale
        da = part[r, :] + other[r, :]
        sums[0:1, :] += jnp.sum(da * unit, axis=0, keepdims=True)
        dn = da * rows_ref[0:1, :]
        dx = dx1[r, :] + scale * (dn - unit * jnp.mean(dn * unit, axis=1, keepdims=True))
        du = dx * up * (s * (1.0 + u * (1.0 - s)))
        sums[1:2, :] += jnp.sum(du * xb, axis=0, keepdims=True)
        sums[2:3, :] += jnp.sum(dx * silu * xb, axis=0, keepdims=True)
        return carry

    lax.fori_loop(0, part.shape[0] // TILE, step, 0)


def embed_backward(part, dx1, x, rows, ident):
    return pl.pallas_call(
        embed_backward_kernel,
        in_specs=[VMEM] * 4,
        out_specs=VMEM,
        out_shape=jax.ShapeDtypeStruct((8, D), F32),
        scratch_shapes=exchange_scratch(part),
        compiler_params=params(collective_id=ident, has_side_effects=True),
        name="embed_backward",
    )(part, dx1, x, rows)
def place():
    dp = lax.axis_index("dp")
    return dp, lax.axis_index("mp"), lax.rem(dp, 2), lax.rem(dp // 2, 2), dp // 4


def greet(dp, mp, x, y, z):
    barrier = pltpu.get_barrier_semaphore()
    xp, yp = dp + 1 - 2 * x, dp + 2 - 4 * y
    for peer in (xp, yp):
        pl.semaphore_signal(barrier, inc=1, device_id=(peer, mp), device_id_type=MESH)

    @pl.when(z > 0)
    def _():
        pl.semaphore_signal(barrier, inc=1, device_id=(dp - 4, mp), device_id_type=MESH)

    @pl.when(z < 3)
    def _():
        pl.semaphore_signal(barrier, inc=1, device_id=(dp + 4, mp), device_id_type=MESH)

    @pl.when((z > 0) & (z < 3))
    def _():
        pl.semaphore_wait(barrier, 4)

    @pl.when((z == 0) | (z == 3))
    def _():
        pl.semaphore_wait(barrier, 3)
    return xp, yp


def gather_kernel(chunks, own, out, stage, in_sem, own_sem, send_xy, send_up, send_dn, z_sem, p2_sem, p3_sem):
    dp, mp, x, y, z = place()
    count = own.shape[0]
    load = pltpu.make_async_copy(own, stage, in_sem)
    load.start()
    xp, yp = greet(dp, mp, x, y, z)
    load.wait()

    def rows(c, slot):
        return out.at[c, pl.ds(pl.multiple_of(slot * SHARD, 8), SHARD), :]

    store = []

    def put(src, c, slot, send, recv, peer):
        pltpu.make_async_remote_copy(
            src_ref=src, dst_ref=rows(c, slot), send_sem=send, recv_sem=recv,
            device_id=(peer, mp), device_id_type=MESH).start()

    def arrived(c, slot, sem):
        pltpu.make_async_copy(rows(c, slot), rows(c, slot), sem).wait()

    def local(c):
        return pltpu.make_async_copy(stage.at[c], rows(c, dp), own_sem)

    first = (lambda k: (yp, xp) if k == 0 else (xp, yp))

    def each(fn):
        def body(i, carry):
            fn(2 * i, 0)
            fn(2 * i + 1, 1)
            return carry
        lax.fori_loop(0, count // 2, body, 0)
        if count % 2:
            fn(count - 1, 0)

    def zup(c, zs, src):
        put(src, c, zs * 4 + 2 * y + x, send_up, z_sem.at[c, zs], dp + 4)

    def zdn(c, zs, src):
        put(src, c, zs * 4 + 2 * y + x, send_dn, z_sem.at[c, zs], dp - 4)

    def spread(c, k, zs, src):
        a, b = first(k)
        slot = zs * 4 + 2 * y + x
        put(src, c, slot, send_xy, p2_sem.at[c, zs], a)
        put(src, c, slot, send_xy, p3_sem, b)

    def begin(c, k):
        @pl.when(z < 3)
        def _():
            zup(c, z, stage.at[c])

        @pl.when(z > 0)
        def _():
            zdn(c, z, stage.at[c])
        spread(c, k, z, stage.at[c])
        local(c).start()
    each(begin)

    def second(c, k, zs):
        a, b = first(k)
        slot = zs * 4 + (2 * (1 - y) + x if k == 0 else 2 * y + 1 - x)
        arrived(c, slot, p2_sem.at[c, zs])
        put(rows(c, slot), c, slot, send_xy, p3_sem, b)

    for dist in (1, 2, 3):
        def step(c, k, dist=dist):
            @pl.when(z >= dist)
            def _():
                zs = z - dist
                arrived(c, zs * 4 + 2 * y + x, z_sem.at[c, zs])
                src = rows(c, zs * 4 + 2 * y + x)

                @pl.when(z < 3)
                def _():
                    zup(c, zs, src)
                spread(c, k, zs, src)

            @pl.when(z + dist <= 3)
            def _():
                zs = z + dist
                arrived(c, zs * 4 + 2 * y + x, z_sem.at[c, zs])
                src = rows(c, zs * 4 + 2 * y + x)

                @pl.when(z > 0)
                def _():
                    zdn(c, zs, src)
                spread(c, k, zs, src)
            if dist == 1:
                second(c, k, z)
            else:
                @pl.when(z >= dist - 1)
                def _():
                    second(c, k, z - dist + 1)

                @pl.when(z + dist - 1 <= 3)
                def _():
                    second(c, k, z + dist - 1)
        each(step)

    def last(c, k):
        @pl.when(z >= 3)
        def _():
            second(c, k, z - 3)

        @pl.when(z <= 0)
        def _():
            second(c, k, z + 3)
    each(last)

    def total(n, sem):
        view = out.at[:, pl.ds(0, n * SHARD), :]
        pltpu.make_async_copy(view, view, sem).wait()
    total(8, p3_sem)
    total(12, send_xy)
    total(1, own_sem)
    for k in range(4):
        @pl.when(z == k)
        def _():
            if k < 3:
                total(k + 1, send_up)
            if k > 0:
                total(4 - k, send_dn)


def gather_rows(own, ident):
    chunks, shard, columns = own.shape
    return pl.pallas_call(
        functools.partial(gather_kernel, chunks),
        out_shape=jax.ShapeDtypeStruct((chunks, 16 * shard, columns), own.dtype),
        in_specs=[pl.BlockSpec(memory_space=pl.ANY)],
        out_specs=pl.BlockSpec(memory_space=pl.ANY),
        scratch_shapes=[
            pltpu.VMEM(own.shape, own.dtype),
            pltpu.SemaphoreType.DMA, pltpu.SemaphoreType.DMA, pltpu.SemaphoreType.DMA,
            pltpu.SemaphoreType.DMA, pltpu.SemaphoreType.DMA,
            pltpu.SemaphoreType.DMA((chunks, 4)), pltpu.SemaphoreType.DMA((chunks, 4)),
            pltpu.SemaphoreType.DMA,
        ],
        compiler_params=pltpu.CompilerParams(collective_id=ident, has_side_effects=True),
        name="gather_rows",
    )(own)


def reduce_kernel(count, halves, *refs):
    (g, out, first, mine, second, up, dn, send1, send2, send_up, send_dn, load_sem,
     sem1, sem2, up_sem, dn_sem) = refs
    dp, mp, x, y, z = place()
    width = out.shape[-1] // halves
    xp, yp = greet(dp, mp, x, y, z)

    def cut(c, k, which):
        e, h = c // halves, lax.rem(c, halves)
        cols = pl.ds(pl.multiple_of(h * width, 128), width)
        if k == 0:
            return g.at[e, :, :, which, :, cols]
        return g.at[e, :, which, :, :, cols]

    def remote(src, dst, send, recv, peer):
        return pltpu.make_async_remote_copy(
            src_ref=src, dst_ref=dst, send_sem=send, recv_sem=recv,
            device_id=(peer, mp), device_id_type=MESH)

    def arrived(view, sem):
        pltpu.make_async_copy(view, view, sem).wait()

    def each(fn):
        def body(i, carry):
            fn(2 * i, 0)
            fn(2 * i + 1, 1)
            return carry
        lax.fori_loop(0, count // 2, body, 0)
        if count % 2:
            fn(count - 1, 0)

    def keep(k):
        return x if k == 0 else y

    def load(c, k, slot):
        return pltpu.make_async_copy(cut(c, k, keep(k)), mine.at[slot], load_sem.at[slot])

    def begin(c, k):
        peer = xp if k == 0 else yp
        remote(cut(c, k, 1 - keep(k)), first.at[c], send1, sem1.at[c], peer).start()
    each(begin)
    load(0, 0, 0).start()
    if count > 1:
        load(1, 1, 1).start()

    def fold(c, k):
        load(c, k, k).wait()
        arrived(first.at[c], sem1.at[c])

        def add(i, carry):
            a, b = i // 2, lax.rem(i, 2)
            first[c, a, b] = first[c, a, b] + mine[k, a, b]
            return carry
        lax.fori_loop(0, 8, add, 0)

        @pl.when(c + 2 < count)
        def _():
            load(c + 2, k, k).start()
        peer = yp if k == 0 else xp
        other = y if k == 0 else x
        remote(first.at[c, :, 1 - other], second.at[c], send2, sem2.at[c], peer).start()
    each(fold)

    def line(c, k):
        other = y if k == 0 else x
        arrived(second.at[c], sem2.at[c])

        def add(a, carry):
            second[c, a] = second[c, a] + first[c, a, other]
            return carry
        lax.fori_loop(0, 4, add, 0)
        for t in (3, 2, 1):
            @pl.when((z < t) & (z == 0))
            def _():
                remote(second.at[c, t], up.at[c, t - 1], send_up, up_sem.at[c, t - 1], dp + 4).start()

            @pl.when((z < t) & (z > 0))
            def _():
                arrived(up.at[c, t - 1], up_sem.at[c, t - 1])
                second[c, t] = second[c, t] + up[c, t - 1]
                remote(second.at[c, t], up.at[c, t - 1], send_up, up_sem.at[c, t - 1], dp + 4).start()
        for t in (0, 1, 2):
            @pl.when((z > t) & (z == 3))
            def _():
                remote(second.at[c, t], dn.at[c, t], send_dn, dn_sem.at[c, t], dp - 4).start()

            @pl.when((z > t) & (z < 3))
            def _():
                arrived(dn.at[c, t], dn_sem.at[c, t])
                second[c, t] = second[c, t] + dn[c, t]
                remote(second.at[c, t], dn.at[c, t], send_dn, dn_sem.at[c, t], dp - 4).start()
    each(line)

    def finish(c, k):
        e, h = c // halves, lax.rem(c, halves)
        cols = pl.ds(pl.multiple_of(h * width, 128), width)
        out[e, :, cols] = second[c, z]
        for t in range(4):
            @pl.when(z == t)
            def _():
                if t > 0:
                    arrived(up.at[c, t - 1], up_sem.at[c, t - 1])
                    out[e, :, cols] = out[e, :, cols] + up[c, t - 1]
                if t < 3:
                    arrived(dn.at[c, t], dn_sem.at[c, t])
                    out[e, :, cols] = out[e, :, cols] + dn[c, t]
    each(finish)

    def total(ref, sem):
        pltpu.make_async_copy(ref, ref, sem).wait()
    total(first, send1)
    total(second, send2)
    for k in range(4):
        @pl.when(z == k)
        def _():
            if k < 3:
                total(up.at[:, pl.ds(k, 3 - k)], send_up)
            if k > 0:
                total(dn.at[:, pl.ds(0, k)], send_dn)


def reduce_rows(g, halves, ident):
    chunks, rows, columns = g.shape
    shard = rows // 16
    count, width = chunks * halves, columns // halves
    f32 = jnp.float32
    return pl.pallas_call(
        functools.partial(reduce_kernel, count, halves),
        out_shape=jax.ShapeDtypeStruct((chunks, shard, columns), f32),
        in_specs=[pl.BlockSpec(memory_space=pl.ANY)],
        out_specs=pl.BlockSpec(memory_space=pltpu.VMEM),
        scratch_shapes=[
            pltpu.VMEM((count, 4, 2, shard, width), f32),
            pltpu.VMEM((2, 4, 2, shard, width), f32),
            pltpu.VMEM((count, 4, shard, width), f32),
            pltpu.VMEM((count, 3, shard, width), f32),
            pltpu.VMEM((count, 3, shard, width), f32),
            pltpu.SemaphoreType.DMA, pltpu.SemaphoreType.DMA, pltpu.SemaphoreType.DMA, pltpu.SemaphoreType.DMA,
            pltpu.SemaphoreType.DMA((2,)),
            pltpu.SemaphoreType.DMA((count,)), pltpu.SemaphoreType.DMA((count,)),
            pltpu.SemaphoreType.DMA((count, 3)), pltpu.SemaphoreType.DMA((count, 3)),
        ],
        compiler_params=pltpu.CompilerParams(
            collective_id=ident, has_side_effects=True, vmem_limit_bytes=60 * 1024 * 1024),
        name="reduce_rows",
    )(g.reshape(chunks, 4, 2, 2, shard, columns))


def all_kernel(n_dp, value, out, send_sem, recv_sem):
    dp, mp = lax.axis_index("dp"), lax.axis_index("mp")
    me = dp * 2 + mp
    n = 2 * n_dp
    barrier = pltpu.get_barrier_semaphore()
    for k in range(1, n):
        peer = lax.rem(me + k, n)
        pl.semaphore_signal(barrier, inc=1, device_id=(peer // 2, lax.rem(peer, 2)), device_id_type=MESH)
    pl.semaphore_wait(barrier, n - 1)
    for k in range(1, n):
        peer = lax.rem(me + k, n)
        pltpu.make_async_remote_copy(src_ref=value, dst_ref=out.at[me], send_sem=send_sem, recv_sem=recv_sem,
                                     device_id=(peer // 2, lax.rem(peer, 2)), device_id_type=MESH).start()
    out[me] = value[...]
    view = out.at[pl.ds(0, n - 1)]
    pltpu.make_async_copy(view, view, recv_sem).wait()
    pltpu.make_async_copy(view, view, send_sem).wait()


def all_blocks(value, n_dp, ident):
    n = 2 * n_dp
    return pl.pallas_call(
        functools.partial(all_kernel, n_dp),
        out_shape=jax.ShapeDtypeStruct((n,) + value.shape, value.dtype),
        in_specs=[pl.BlockSpec(memory_space=pltpu.VMEM)],
        out_specs=pl.BlockSpec(memory_space=pltpu.VMEM),
        scratch_shapes=[pltpu.SemaphoreType.DMA, pltpu.SemaphoreType.DMA],
        compiler_params=pltpu.CompilerParams(collective_id=ident, has_side_effects=True),
        name="all_blocks",
    )(value)


def rope_tables(length):
    halfway = HEAD // 2
    frequency = rope_base ** (-2.0 * jnp.arange(halfway, dtype=F32) / HEAD)
    angles = frequency[:, None] * jnp.arange(length, dtype=F32)[None, :]
    return jnp.cos(angles), jnp.sin(angles)


def hankel_rows(track):
    series, length = track.shape
    padded = jnp.pad(track, ((0, 0), (63, 2 * LANES)))
    first = padded[:, :length].reshape(-1, LANES)[:, ::-1]
    second = padded[:, LANES:LANES + length].reshape(-1, LANES)[:, ::-1]
    return jnp.concatenate([first, second], axis=1)


def head_columns(matrix):
    parts, end = [], matrix.shape[1]
    for horizon in horizons[::-1]:
        parts.append(matrix[:, end - horizon:end][:, ::-1])
        end -= horizon
    return jnp.pad(jnp.concatenate(parts, axis=1), ((0, 0), (0, LANES - matrix.shape[1])))


def head_columns_back(matrix):
    parts, begin = [], 0
    for horizon in horizons[::-1]:
        parts.append(matrix[:, begin:begin + horizon][:, ::-1])
        begin += horizon
    return jnp.concatenate(parts[::-1], axis=1)


def dispatch(route_rows, capacity):
    tokens = route_rows.shape[0]
    experts = jnp.arange(ROUTED_EXPERTS, dtype=jnp.int32)
    member = jnp.any(route_rows[:, :, None] == experts[None, None, :], axis=1)
    count = jnp.cumsum(member.astype(jnp.int32), axis=0)
    total = count[-1]
    place = jnp.where(member, count - 1, -1)
    high = (place[:, :, None] // LANES == jnp.arange(capacity // LANES)[None, None, :]) & member[:, :, None]
    low = (place[:, :, None] % LANES == jnp.arange(LANES)[None, None, :]).astype(BF16)
    token = jnp.arange(tokens, dtype=jnp.int32)
    left = jnp.concatenate(
        [jnp.where(high, part[:, None, None], 0).astype(BF16) for part in (token // 16, token % 16)], axis=2)
    found = jnp.einsum("teh,tel->ehl", left, low, preferred_element_type=F32)
    half = capacity // LANES
    source = (found[:, :half] * 16.0 + found[:, half:]).reshape(ROUTED_EXPERTS, capacity).astype(jnp.int32)
    slots = jnp.arange(capacity, dtype=jnp.int32)
    source = jnp.where(slots[None, :] < total[:, None], source, tokens)
    return total, source.reshape(-1)


def adam_update(master, moment, square, gradient, factor, bias_one, bias_two, step_rate):
    clipped = gradient * factor
    new_moment = beta_one * moment + (1.0 - beta_one) * clipped
    new_square = beta_two * square + (1.0 - beta_two) * clipped * clipped
    updated = master - step_rate * (
        new_moment / bias_one / (jnp.sqrt(new_square / bias_two) + adam_eps) + decay_rate * master
    )
    return (updated, new_moment, new_square)


def on_device(
    near,
    series, observed, routes, step_count,
    joint_proj, joint_moment, joint_square,
    mixer_proj, mixer_moment, mixer_square,
    upward_proj, upward_moment, upward_square,
    downward_proj, downward_moment, downward_square,
    readout, readout_moment, readout_square,
    vectors, vectors_moment, vectors_square,
):
    dp_count = lax.axis_size("dp")
    mp_count = lax.axis_size("mp")
    shard = joint_proj.shape[1]
    width = joint_proj.shape[2]
    hidden = upward_proj.shape[3]
    experts = upward_proj.shape[0]
    series_count, length = series.shape
    tokens = series_count * length
    capacity = tokens // 2
    columns = readout.shape[1]
    small_width = -(-(4 * width + columns + 5) // LANES) * LANES

    def pack_small(joint, mixer_t, read, vec):
        flat = jnp.concatenate([joint[0], joint[1], joint[2], mixer_t, read, vec], axis=1)
        return jnp.pad(flat, ((0, 0), (0, small_width - flat.shape[1])))

    small_own = pack_small(
        joint_proj.astype(BF16), mixer_proj.T.astype(BF16), readout.astype(BF16), vectors.T.astype(BF16))
    big_own = jnp.concatenate(
        [upward_proj.astype(BF16).reshape(experts, shard, 2 * hidden), downward_proj.transpose(0, 2, 1).astype(BF16)],
        axis=2)
    marks = observed.astype(F32)
    route_rows = routes.reshape(tokens, 2)
    expert_here, source = dispatch(route_rows, capacity)
    point = jnp.arange(length, dtype=F32)
    head_here = jnp.stack(
        [jnp.sum(jnp.sum(marks, axis=0) * jnp.minimum(point, float(horizon))) for horizon in horizons])
    tally = jnp.pad(jnp.concatenate([expert_here.astype(F32), head_here]), (0, LANES - 12))
    if near:
        small = gather_rows(small_own[None], 0)[0]
        big = gather_rows(big_own, 1)
        tally = jnp.sum(all_blocks(jnp.broadcast_to(tally[None], (8, LANES)), dp_count, 2)[:, 0], axis=0) / mp_count
    else:
        small = lax.all_gather(small_own, "dp", axis=0, tiled=True)
        big = lax.all_gather(big_own, "dp", axis=1, tiled=True)
        tally = lax.psum(tally, "dp")
    expert_count, head_count = tally[:ROUTED_EXPERTS], tally[ROUTED_EXPERTS:ROUTED_EXPERTS + 4]
    total_tokens = tokens * dp_count

    wj = small[:, :3 * width].T
    wo = small[:, 3 * width:4 * width].T
    read = small[:, 4 * width:4 * width + columns]
    vec = small[:, 4 * width + columns:4 * width + columns + 5].astype(F32).T
    rows = jnp.concatenate([vec[0:1], vec[3:5], jnp.zeros((5, D), F32)], axis=0)
    router = jnp.pad(read[:, :ROUTED_EXPERTS + 1], ((0, 0), (0, LANES - ROUTED_EXPERTS - 1)))
    heads = head_columns(read[:, ROUTED_EXPERTS + 1:])
    cos, sin = rope_tables(length)
    x = (series * marks).reshape(series_count, 1, length)

    x0, a, qkv, lse, o, part = attend_forward(x, rows, wj, wo, cos, sin)
    x1, b, pc, pr_total = mid_forward(part, x0, vec[1:2], router, 3)
    xs, ys, shared, mixed = expert_forward(expert_here, source, b, pc, big)
    head_weight = jnp.concatenate(
        [jnp.zeros((horizon,), F32) + 0.25 / head_count[3 - index] for index, horizon in enumerate(horizons[::-1])])
    head_weight = jnp.pad(head_weight, (0, LANES - head_weight.shape[0]))[None]
    dx2, d_heads, d_gain3, fit = loss_stage(
        mixed, x1, vec[2:3], heads, heads.T, hankel_rows(series), hankel_rows(marks), head_weight, 4)
    d_big, back = expert_backward(expert_here, source, b, pc, dx2, big, xs, ys, shared)
    balance = aux_factor * ROUTED_EXPERTS * expert_count / total_tokens / total_tokens
    balance = jnp.pad(balance, (0, LANES - ROUTED_EXPERTS))[None]
    local_loss = jnp.sum(fit) + jnp.sum(pr_total * balance)
    dx1, do, d_router, d_wo, d_gain2 = mid_backward(
        back, dx2, x1, b, pc, vec[1:2], router.T, balance, wo, o, 5)
    d_wj, da = attend_backward(qkv, do, lse, a, wj, cos, sin)
    sums = embed_backward(da, dx1, x, rows, 6)

    d_read = jnp.concatenate([d_router[:ROUTED_EXPERTS + 1].T, head_columns_back(d_heads.T)], axis=1)
    d_vec = jnp.concatenate([sums[0:1], d_gain2, d_gain3, sums[1:3]], axis=0).T
    d_wj = d_wj.T
    d_small = pack_small(
        [d_wj[:, k * width:(k + 1) * width] for k in range(3)], d_wo.T, d_read, d_vec)
    if near:
        big_red = reduce_rows(d_big, 2, 7)
        small_red = reduce_rows(d_small[None], 1, 8)[0]
    else:
        big_red = lax.psum_scatter(d_big, "dp", scatter_dimension=1, tiled=True)
        small_red = lax.psum_scatter(d_small, "dp", scatter_dimension=0, tiled=True)
    attn_red = small_red[:, :4 * width]
    rest_red = small_red[:, 4 * width:4 * width + columns + 5]
    squares = (
        jnp.sum(big_red * big_red) + jnp.sum(attn_red * attn_red) + jnp.sum(rest_red * rest_red) / mp_count
    )
    pair = jnp.pad(jnp.stack([squares, local_loss / mp_count]), (0, LANES - 2))
    if near:
        pair = jnp.sum(all_blocks(jnp.broadcast_to(pair[None], (8, LANES)), dp_count, 9)[:, 0], axis=0)
    else:
        pair = lax.psum(pair, ("dp", "mp"))
    grad_norm, loss_total = jnp.sqrt(pair[0]), pair[1]

    factor = clip_limit / (grad_norm + 1e-06)
    steps_taken = step_count[0].astype(F32)
    bias_one = 1.0 - beta_one**steps_taken
    bias_two = 1.0 - beta_two**steps_taken

    def update(master, moment, square, gradient, rate=matrix_rate):
        return adam_update(master, moment, square, gradient, factor, bias_one, bias_two, rate)

    joint_red = jnp.stack([attn_red[:, k * width:(k + 1) * width] for k in range(3)], axis=0)
    mixer_red = attn_red[:, 3 * width:].T
    upward_red = big_red[:, :, :2 * hidden].reshape(upward_proj.shape)
    downward_red = big_red[:, :, 2 * hidden:].transpose(0, 2, 1)
    return (
        loss_total,
        grad_norm,
        *update(joint_proj, joint_moment, joint_square, joint_red),
        *update(mixer_proj, mixer_moment, mixer_square, mixer_red),
        *update(upward_proj, upward_moment, upward_square, upward_red),
        *update(downward_proj, downward_moment, downward_square, downward_red),
        *update(readout, readout_moment, readout_square, rest_red[:, :columns]),
        *update(vectors, vectors_moment, vectors_square, rest_red[:, columns:].T, vector_rate),
    )


def solution(mesh):
    token = [P("dp", None), P("dp", None), P("dp", None, None), P()]
    weights = [
        P(None, "dp", "mp"), P("mp", "dp"), P(None, "dp", None, "mp"), P(None, "mp", "dp"), P("dp", None), P(None, "dp"),
    ]
    triple = tuple(spec for spec in weights for _ in range(3))
    near = mesh.shape["dp"] == 16 and mesh.shape["mp"] == 2
    return jax.shard_map(
        functools.partial(on_device, near),
        mesh=mesh,
        in_specs=tuple(token) + triple,
        out_specs=(P(), P()) + triple,
        check_vma=False,
    )
```

```python
import functools
import jax
import jax.numpy as jnp
from jax import lax
from jax.experimental import pallas as pl
from jax.experimental.pallas import tpu as pltpu
from jax.sharding import PartitionSpec as P

D = 384
HEAD = 32
ROUTED_EXPERTS = 8
LANES = 128
TILE = 256
SHARD = 24

horizons = (1, 8, 32, 64)
quadratic_cutoff = 2.0
aux_factor = 0.02
clip_limit = 0.001
beta_one = 0.9
beta_two = 0.95
adam_eps = 1e-08
decay_rate = 0.1
matrix_rate = 0.05
vector_rate = 0.25
norm_eps = 1e-06
rope_base = 10000.0

F32 = jnp.float32
BF16 = jnp.bfloat16
MESH = pl.DeviceIdType.MESH
VMEM = pl.BlockSpec(memory_space=pltpu.VMEM)
ANY = pl.BlockSpec(memory_space=pl.ANY)


def dot(a, b, da=1, db=0):
    return lax.dot_general(a, b, (((da,), (db,)), ((), ())), preferred_element_type=F32)


def params(megabytes=60, **more):
    return pltpu.CompilerParams(vmem_limit_bytes=megabytes * 1024 * 1024, **more)


def sigmoid(v):
    return 1.0 / (1.0 + jnp.exp(-v))


def column(row, length):
    return jnp.transpose(jnp.broadcast_to(row, (LANES, length)))


def embed_chunk(xb, gate_row, up_row):
    u = xb * gate_row
    return u * sigmoid(u) * (xb * up_row)


def rotated(t, cos, sin):
    half = HEAD // 2
    front, back = t[:half], t[half:]
    return jnp.concatenate([front * cos - back * sin, back * cos + front * sin], axis=0)


def unrotated(t, cos, sin):
    half = HEAD // 2
    front, back = t[:half], t[half:]
    return jnp.concatenate([front * cos + back * sin, back * cos - front * sin], axis=0)


def score_block(k_rows, q_cols, low, length):
    s = dot(k_rows, q_cols)
    keys = lax.broadcasted_iota(jnp.int32, s.shape, 0)
    queries = lax.broadcasted_iota(jnp.int32, s.shape, 1) + low
    return jnp.where(keys <= queries, s, -1e30)


def attend_forward_kernel(
    x_ref, rows_ref, wj_ref, wo_ref, cos_ref, sin_ref,
    x0_ref, a_ref, qkv_ref, lse_ref, o_ref, part_ref,
):
    length = x_ref.shape[-1]
    heads = wo_ref.shape[0] // HEAD
    width = heads * HEAD
    scale = HEAD ** (-0.5)

    def embed(i, carry):
        r = pl.ds(pl.multiple_of(i * TILE, TILE), TILE)
        xb = column(x_ref[0, :, r], TILE)
        cuts = []
        square = None
        for c in range(D // LANES):
            cols = slice(c * LANES, (c + 1) * LANES)
            v = embed_chunk(xb, rows_ref[1:2, cols], rows_ref[2:3, cols])
            x0_ref[r, cols] = v
            square = v * v if square is None else square + v * v
            cuts.append(v)
        scale_row = lax.rsqrt(jnp.sum(square, axis=1, keepdims=True) / D + norm_eps)
        for c in range(D // LANES):
            cols = slice(c * LANES, (c + 1) * LANES)
            a_ref[r, cols] = (cuts[c] * scale_row * rows_ref[0:1, cols]).astype(BF16)
        return carry

    lax.fori_loop(0, length // TILE, embed, 0)
    a = a_ref[...]
    cos, sin = cos_ref[...], sin_ref[...]

    def project(h, carry):
        for part in range(3):
            rows = pl.ds(pl.multiple_of(part * width + h * HEAD, HEAD), HEAD)
            t = dot(wj_ref[rows, :], a, 1, 1)
            if part < 2:
                t = rotated(t, cos, sin)
            qkv_ref[0, rows, :] = t.astype(BF16)
        return carry

    lax.fori_loop(0, heads, project, 0)

    def head(h, carry):
        q_rows = pl.ds(pl.multiple_of(h * HEAD, HEAD), HEAD)
        k_rows = pl.ds(pl.multiple_of(width + h * HEAD, HEAD), HEAD)
        v_rows = pl.ds(pl.multiple_of(2 * width + h * HEAD, HEAD), HEAD)
        k = jnp.transpose(qkv_ref[0, k_rows, :].astype(F32)).astype(BF16)
        for j in range(length // TILE):
            n = TILE * (j + 1)
            cols = slice(j * TILE, (j + 1) * TILE)
            s = score_block(k[:n], qkv_ref[0, q_rows, cols], j * TILE, n)
            peak = jnp.max(s, axis=0, keepdims=True)
            e = jnp.exp((s - peak) * scale)
            mass = jnp.sum(e, axis=0, keepdims=True)
            weights = (e * (1.0 / mass)).astype(BF16)
            o_ref[0, q_rows, cols] = dot(qkv_ref[0, v_rows, :n], weights).astype(BF16)
            lse_ref[0, pl.ds(h, 1), cols] = peak * scale + jnp.log(mass)
        return carry

    lax.fori_loop(0, heads, head, 0)
    part_ref[...] = dot(o_ref[0], wo_ref[...], 0, 0)


def attend_forward(x, rows, wj, wo, cos, sin):
    series, _, length = x.shape
    tokens = series * length
    width = wo.shape[0]
    full = lambda shape: pl.BlockSpec(shape, lambda i: (0,) * len(shape))
    tok = lambda w: pl.BlockSpec((length, w), lambda i: (i, 0))
    ser = lambda r: pl.BlockSpec((1, r, length), lambda i: (i, 0, 0))
    return pl.pallas_call(
        attend_forward_kernel,
        grid=(series,),
        in_specs=[ser(1), full(rows.shape), full(wj.shape), full(wo.shape), full(cos.shape), full(sin.shape)],
        out_specs=[tok(D), tok(D), ser(3 * width), ser(8), ser(width), tok(D)],
        out_shape=[
            jax.ShapeDtypeStruct((tokens, D), F32),
            jax.ShapeDtypeStruct((tokens, D), BF16),
            jax.ShapeDtypeStruct((series, 3 * width, length), BF16),
            jax.ShapeDtypeStruct((series, 8, length), F32),
            jax.ShapeDtypeStruct((series, width, length), BF16),
            jax.ShapeDtypeStruct((tokens, D), F32),
        ],
        compiler_params=params(),
        name="attend_forward",
    )(x, rows, wj, wo, cos, sin)


def attend_backward_kernel(
    qkv_ref, do_ref, lse_ref, a_ref, wj_ref, cos_ref, sin_ref, dw_ref, part_ref, dqkv_ref, dk_ref, dv_ref
):
    length = qkv_ref.shape[-1]
    width = do_ref.shape[1]
    heads = width // HEAD
    scale = HEAD ** (-0.5)
    cos, sin = cos_ref[...], sin_ref[...]

    def flip(t):
        return jnp.transpose(t.astype(F32)).astype(BF16)

    def head(h, carry):
        q_rows = pl.ds(pl.multiple_of(h * HEAD, HEAD), HEAD)
        k_rows = pl.ds(pl.multiple_of(width + h * HEAD, HEAD), HEAD)
        v_rows = pl.ds(pl.multiple_of(2 * width + h * HEAD, HEAD), HEAD)
        q = flip(qkv_ref[0, q_rows, :])
        k = flip(qkv_ref[0, k_rows, :])
        v = flip(qkv_ref[0, v_rows, :])
        do = flip(do_ref[0, q_rows, :])
        dk_ref[...] = jnp.zeros_like(dk_ref)
        dv_ref[...] = jnp.zeros_like(dv_ref)
        for j in range(length // TILE):
            n = TILE * (j + 1)
            cols = slice(j * TILE, (j + 1) * TILE)
            s = score_block(k[:n], qkv_ref[0, q_rows, cols], j * TILE, n)
            w = jnp.exp(s * scale - lse_ref[0, pl.ds(h, 1), cols])
            dv_ref[:n] += dot(w.astype(BF16), do[cols])
            dw = dot(v[:n], do_ref[0, q_rows, cols])
            mean = jnp.sum(w * dw, axis=0, keepdims=True)
            ds = (w * (dw - mean) * scale).astype(BF16)
            dk_ref[:n] += dot(ds, q[cols])
            dq = dot(qkv_ref[0, k_rows, :n], ds)
            dqkv_ref[q_rows, cols] = unrotated(dq, cos[:, cols], sin[:, cols]).astype(BF16)
        dqkv_ref[k_rows, :] = unrotated(jnp.transpose(dk_ref[...]), cos, sin).astype(BF16)
        dqkv_ref[v_rows, :] = jnp.transpose(dv_ref[...]).astype(BF16)
        return carry

    lax.fori_loop(0, heads, head, 0)

    @pl.when(pl.program_id(0) == 0)
    def _():
        dw_ref[...] = jnp.zeros_like(dw_ref)

    dw_ref[...] += dot(dqkv_ref[...], a_ref[...])
    part_ref[...] = dot(dqkv_ref[...], wj_ref[...], 0, 0)


def attend_backward(qkv, do, lse, a, wj, cos, sin):
    series, rows, length = qkv.shape
    tokens = series * length
    full = lambda shape: pl.BlockSpec(shape, lambda i: (0,) * len(shape))
    tok = lambda w: pl.BlockSpec((length, w), lambda i: (i, 0))
    ser = lambda r: pl.BlockSpec((1, r, length), lambda i: (i, 0, 0))
    return pl.pallas_call(
        attend_backward_kernel,
        grid=(series,),
        in_specs=[ser(rows), ser(do.shape[1]), ser(8), tok(D), full(wj.shape), full(cos.shape), full(sin.shape)],
        out_specs=[full((rows, D)), tok(D)],
        out_shape=[jax.ShapeDtypeStruct((rows, D), F32), jax.ShapeDtypeStruct((tokens, D), F32)],
        scratch_shapes=[
            pltpu.VMEM((rows, length), BF16), pltpu.VMEM((length, HEAD), F32), pltpu.VMEM((length, HEAD), F32),
        ],
        compiler_params=params(),
        name="attend_backward",
    )(qkv, do, lse, a, wj, cos, sin)


GROUP = 16


def spread_rows(dest, value, start, count):
    for c in range(value.shape[1] // LANES):
        dest[pl.ds(start * 8 + c, count, stride=8), :] = value[:, c * LANES:(c + 1) * LANES]


def pick_rows(source, tile, index_ref, base):
    def body(i, carry):
        values = []
        for k in range(GROUP):
            t = index_ref[base + i * GROUP + k]
            values.append(source[pl.ds(pl.multiple_of(t * 8, 8), 8), :])
        for k in range(GROUP):
            tile[pl.ds(pl.multiple_of((i * GROUP + k) * 8, 8), 8), :] = values[k]
        return carry

    lax.fori_loop(0, TILE // GROUP, body, 0)


def add_rows(dest, tile, index_ref, base):
    def body(i, carry):
        places, values = [], []
        for k in range(GROUP):
            t = index_ref[base + i * GROUP + k]
            place = pl.ds(pl.multiple_of(t * 8, 8), 8)
            places.append(place)
            values.append(dest[place, :] + tile[pl.ds(pl.multiple_of((i * GROUP + k) * 8, 8), 8), :])
        for k in range(GROUP):
            dest[places[k], :] = values[k]
        return carry

    lax.fori_loop(0, TILE // GROUP, body, 0)


def gathered_columns(tile, columns):
    return [tile[pl.ds(c, TILE, stride=8), :] for c in range(columns)]


def lane_of(block, lane):
    lanes = lax.broadcasted_iota(jnp.int32, block.shape, 1)
    return jnp.sum(jnp.where(lanes == lane, block, 0.0), axis=1, keepdims=True)


def lay_rows(values, pc_ref, rows8, acc8):
    tokens = values.shape[0]

    def lay(i, carry):
        r = pl.ds(pl.multiple_of(i * TILE, TILE), TILE)
        spread_rows(rows8, values[r, :].astype(F32), i * TILE, TILE)
        rows8[pl.ds(i * TILE * 8 + 3, TILE, stride=8), :] = pc_ref[r, :]
        acc8[pl.ds(pl.multiple_of(i * TILE * 8, 8), TILE * 8), :] = jnp.zeros((TILE * 8, LANES), F32)
        return carry

    lax.fori_loop(0, tokens // TILE, lay, 0)
    rows8[pl.ds(tokens * 8, 8), :] = jnp.zeros((8, LANES), F32)
    acc8[pl.ds(tokens * 8, 8), :] = jnp.zeros((8, LANES), F32)


def expert_forward_kernel(counts, source, b_ref, pc_ref, w_ref, x_ref, y_ref, mix_ref, rows8, acc8, tile8):
    e = pl.program_id(0)
    hidden = w_ref.shape[2] // 3
    capacity = y_ref.shape[1]
    tiles = capacity // TILE

    @pl.when(e == 0)
    def _():
        lay_rows(b_ref, pc_ref, rows8, acc8)

    def run(x):
        g = dot(x, w_ref[0, :, : 2 * hidden])
        gate, up = g[:, :hidden], g[:, hidden:]
        h = (gate * sigmoid(gate) * up).astype(BF16)
        return dot(h, w_ref[0, :, 2 * hidden:], 1, 1)

    @pl.when(e < ROUTED_EXPERTS)
    def _():
        used = (counts[e] + TILE - 1) // TILE

        def step(i, carry):
            base = e * capacity + i * TILE
            r = pl.ds(pl.multiple_of(i * TILE, TILE), TILE)
            pick_rows(rows8, tile8, source, base)
            c0, c1, c2, pc = gathered_columns(tile8, 4)
            x = jnp.concatenate([c0, c1, c2], axis=1).astype(BF16)
            x_ref[0, r, :] = x
            y = run(x)
            y_ref[0, r, :] = y
            spread_rows(tile8, y * lane_of(pc, e), 0, TILE)
            add_rows(acc8, tile8, source, base)
            return carry

        def blank(i, carry):
            x_ref[0, pl.ds(pl.multiple_of(i * TILE, TILE), TILE), :] = jnp.zeros((TILE, D), BF16)
            return carry

        lax.fori_loop(0, used, step, 0)
        lax.fori_loop(used, tiles, blank, 0)

    @pl.when(e >= ROUTED_EXPERTS)
    def _():
        def step(i, carry):
            t = (e - ROUTED_EXPERTS) * tiles + i
            here = pl.ds(pl.multiple_of(i * TILE, TILE), TILE)
            r = pl.ds(pl.multiple_of(t * TILE, TILE), TILE)
            x = b_ref[r, :]
            x_ref[0, here, :] = x
            y = run(x)
            y_ref[0, here, :] = y
            shared = y * lane_of(pc_ref[r, :], ROUTED_EXPERTS)
            for c in range(D // LANES):
                cols = slice(c * LANES, (c + 1) * LANES)
                mix_ref[r, cols] = acc8[pl.ds(t * TILE * 8 + c, TILE, stride=8), :] + shared[:, cols]
            return carry

        lax.fori_loop(0, tiles, step, 0)


def expert_blocks(capacity, w):
    return pl.BlockSpec((1, capacity, w), lambda e, *_: (e, 0, 0))


def expert_weights(weights):
    return pl.BlockSpec((1,) + weights.shape[1:], lambda e, *_: (jnp.minimum(e, ROUTED_EXPERTS), 0, 0))


def expert_scratch(tokens):
    return [
        pltpu.VMEM(((tokens + 1) * 8, LANES), F32),
        pltpu.VMEM(((tokens + 1) * 8, LANES), F32),
        pltpu.VMEM((TILE * 8, LANES), F32),
    ]


def expert_forward(counts, source, b, pc, weights):
    tokens = b.shape[0]
    capacity = tokens // 2
    blocks = ROUTED_EXPERTS + 2
    full = lambda shape: pl.BlockSpec(shape, lambda e, *_: (0,) * len(shape), pipeline_mode=pl.Buffered(1))
    return pl.pallas_call(
        expert_forward_kernel,
        grid_spec=pltpu.PrefetchScalarGridSpec(
            num_scalar_prefetch=2,
            grid=(blocks,),
            in_specs=[full(b.shape), full(pc.shape), expert_weights(weights)],
            out_specs=[expert_blocks(capacity, D), expert_blocks(capacity, D), full((tokens, D))],
            scratch_shapes=expert_scratch(tokens),
        ),
        out_shape=[
            jax.ShapeDtypeStruct((blocks, capacity, D), BF16),
            jax.ShapeDtypeStruct((blocks, capacity, D), F32),
            jax.ShapeDtypeStruct((tokens, D), F32),
        ],
        compiler_params=params(),
        name="expert_forward",
    )(counts, source, b, pc, weights)


def expert_backward_kernel(
    counts, source, pc_ref, dx_ref, w_ref, x_ref, y_ref, dy_ref, dg_ref, h_ref, acc_ref, rows8, acc8, tile8
):
    e = pl.program_id(0)
    hidden = w_ref.shape[2] // 3
    capacity = y_ref.shape[1]
    tiles = capacity // TILE

    @pl.when(e == 0)
    def _():
        lay_rows(dx_ref, pc_ref, rows8, acc8)

    def run(r, dy):
        x = x_ref[0, r, :]
        dy_ref[0, r, :] = dy
        u = w_ref[0, :, : 2 * hidden]
        g = dot(x, u)
        gate, up = g[:, :hidden], g[:, hidden:]
        s = sigmoid(gate)
        silu = gate * s
        h_ref[0, r, :] = (silu * up).astype(BF16)
        dh = dot(dy, w_ref[0, :, 2 * hidden:])
        d_up = (dh * silu).astype(BF16)
        d_gate = (dh * up * (s * (1.0 + gate * (1.0 - s)))).astype(BF16)
        dg_ref[0, r, :hidden] = d_gate
        dg_ref[0, r, hidden:] = d_up
        return dot(d_gate, u[:, :hidden], 1, 1) + dot(d_up, u[:, hidden:], 1, 1)

    lanes = lax.broadcasted_iota(jnp.int32, (TILE, LANES), 1)

    @pl.when(e < ROUTED_EXPERTS)
    def _():
        used = (counts[e] + TILE - 1) // TILE

        def step(i, carry):
            base = e * capacity + i * TILE
            r = pl.ds(pl.multiple_of(i * TILE, TILE), TILE)
            pick_rows(rows8, tile8, source, base)
            c0, c1, c2, pc = gathered_columns(tile8, 4)
            dx = jnp.concatenate([c0, c1, c2], axis=1)
            d_gate = jnp.sum(y_ref[0, r, :] * dx, axis=1, keepdims=True)
            back = run(r, (dx * lane_of(pc, e)).astype(BF16))
            spread_rows(tile8, back, 0, TILE)
            tile8[pl.ds(3, TILE, stride=8), :] = jnp.where(lanes == e, d_gate, 0.0)
            add_rows(acc8, tile8, source, base)
            return carry

        def blank(i, carry):
            r = pl.ds(pl.multiple_of(i * TILE, TILE), TILE)
            dy_ref[0, r, :] = jnp.zeros((TILE, D), BF16)
            dg_ref[0, r, :] = jnp.zeros((TILE, 2 * hidden), BF16)
            h_ref[0, r, :] = jnp.zeros((TILE, hidden), BF16)
            return carry

        lax.fori_loop(0, used, step, 0)
        lax.fori_loop(used, tiles, blank, 0)

    @pl.when(e >= ROUTED_EXPERTS)
    def _():
        def step(i, carry):
            t = (e - ROUTED_EXPERTS) * tiles + i
            here = pl.ds(pl.multiple_of(i * TILE, TILE), TILE)
            r = pl.ds(pl.multiple_of(t * TILE, TILE), TILE)
            dx = dx_ref[r, :]
            d_gate = jnp.sum(y_ref[0, here, :] * dx, axis=1, keepdims=True)
            back = run(here, (dx * lane_of(pc_ref[r, :], ROUTED_EXPERTS)).astype(BF16))
            for c in range(D // LANES):
                cols = slice(c * LANES, (c + 1) * LANES)
                acc_ref[r, cols] = acc8[pl.ds(t * TILE * 8 + c, TILE, stride=8), :] + back[:, cols]
            acc_ref[r, D:] = jnp.where(
                lanes == ROUTED_EXPERTS, d_gate, acc8[pl.ds(t * TILE * 8 + 3, TILE, stride=8), :])
            return carry

        lax.fori_loop(0, tiles, step, 0)


def expert_backward(counts, source, pc, dx, weights, x, y):
    tokens = dx.shape[0]
    capacity = tokens // 2
    blocks = ROUTED_EXPERTS + 2
    hidden = weights.shape[2] // 3
    full = lambda shape: pl.BlockSpec(shape, lambda e, *_: (0,) * len(shape), pipeline_mode=pl.Buffered(1))
    return pl.pallas_call(
        expert_backward_kernel,
        grid_spec=pltpu.PrefetchScalarGridSpec(
            num_scalar_prefetch=2,
            grid=(blocks,),
            in_specs=[
                full(pc.shape), full(dx.shape), expert_weights(weights),
                expert_blocks(capacity, D), expert_blocks(capacity, D)],
            out_specs=[
                expert_blocks(capacity, D), expert_blocks(capacity, 2 * hidden), expert_blocks(capacity, hidden),
                full((tokens, D + LANES))],
            scratch_shapes=expert_scratch(tokens),
        ),
        out_shape=[
            jax.ShapeDtypeStruct((blocks, capacity, D), BF16),
            jax.ShapeDtypeStruct((blocks, capacity, 2 * hidden), BF16),
            jax.ShapeDtypeStruct((blocks, capacity, hidden), BF16),
            jax.ShapeDtypeStruct((tokens, D + LANES), F32),
        ],
        compiler_params=params(),
        name="expert_backward",
    )(counts, source, pc, dx, weights, x, y)


def exchange(part, other, send_sem, recv_sem):
    dp, mp = lax.axis_index("dp"), lax.axis_index("mp")
    barrier = pltpu.get_barrier_semaphore()
    pl.semaphore_signal(barrier, inc=1, device_id=(dp, 1 - mp), device_id_type=MESH)
    pl.semaphore_wait(barrier, 1)

    def copy(i):
        r = pl.ds(pl.multiple_of(i * TILE, TILE), TILE)
        return pltpu.make_async_remote_copy(
            src_ref=part.at[r], dst_ref=other.at[r], send_sem=send_sem.at[i], recv_sem=recv_sem.at[i],
            device_id=(dp, 1 - mp), device_id_type=MESH)

    def begin(i, carry):
        copy(i).start()
        return carry

    lax.fori_loop(0, part.shape[0] // TILE, begin, 0)
    return lambda i: copy(i).wait()


def exchange_scratch(part):
    tiles = part.shape[0] // TILE
    return [pltpu.VMEM(part.shape, F32), pltpu.SemaphoreType.DMA((tiles,)), pltpu.SemaphoreType.DMA((tiles,))]


def mid_forward_kernel(part, x0, gain, router, x1, b, pc, total, other, send_sem, recv_sem):
    wait = exchange(part, other, send_sem, recv_sem)
    total[...] = jnp.zeros_like(total)

    def step(i, carry):
        r = pl.ds(pl.multiple_of(i * TILE, TILE), TILE)
        wait(i)
        x = x0[r, :] + (part[r, :] + other[r, :])
        x1[r, :] = x
        scale = lax.rsqrt(jnp.mean(x * x, axis=1, keepdims=True) + norm_eps)
        low = (x * scale * gain[...]).astype(BF16)
        b[r, :] = low
        logits = dot(low, router[...])
        lanes = lax.broadcasted_iota(jnp.int32, logits.shape, 1)
        routed = lanes < ROUTED_EXPERTS
        peak = jnp.max(jnp.where(routed, logits, -jnp.inf), axis=1, keepdims=True)
        e = jnp.where(routed, jnp.exp(jnp.where(routed, logits - peak, 0.0)), 0.0)
        probability = e / jnp.sum(e, axis=1, keepdims=True)
        pc[r, :] = jnp.where(lanes == ROUTED_EXPERTS, sigmoid(logits), probability)
        total[...] += jnp.sum(probability, axis=0, keepdims=True)
        return carry

    lax.fori_loop(0, part.shape[0] // TILE, step, 0)


def mid_forward(part, x0, gain, router, ident):
    tokens = part.shape[0]
    return pl.pallas_call(
        mid_forward_kernel,
        in_specs=[VMEM] * 4,
        out_specs=[VMEM] * 4,
        out_shape=[
            jax.ShapeDtypeStruct((tokens, D), F32), jax.ShapeDtypeStruct((tokens, D), BF16),
            jax.ShapeDtypeStruct((tokens, LANES), F32), jax.ShapeDtypeStruct((1, LANES), F32),
        ],
        scratch_shapes=exchange_scratch(part),
        compiler_params=params(collective_id=ident, has_side_effects=True),
        name="mid_forward",
    )(part, x0, gain, router)


def hankel(base, shape):
    block = jnp.broadcast_to(base, (LANES, 2 * LANES))
    m = pltpu.roll(block, 0, 1, stride=1, stride_axis=0)[:, :LANES]
    lanes = lax.broadcasted_iota(jnp.int32, (LANES, LANES), 1)
    out = pltpu.roll(m, 41, 1)
    out = jnp.where(lanes < 104, pltpu.roll(m, 40, 1), out)
    out = jnp.where(lanes < 96, pltpu.roll(m, 32, 1), out)
    return jnp.where(lanes < 64, m, out)


def loss_kernel(part, x1, gain, heads, heads_t, values, marks, weight, dx2, d_heads, d_gain, loss,
                other, send_sem, recv_sem):
    wait = exchange(part, other, send_sem, recv_sem)
    d_heads[...] = jnp.zeros_like(d_heads)
    d_gain[...] = jnp.zeros_like(d_gain)
    loss[...] = jnp.zeros_like(loss)

    def step(i, carry):
        r = pl.ds(pl.multiple_of(i * TILE, TILE), TILE)
        wait(i)
        x = x1[r, :] + (part[r, :] + other[r, :])
        scale = lax.rsqrt(jnp.mean(x * x, axis=1, keepdims=True) + norm_eps)
        unit = x * scale
        low = (unit * gain[...]).astype(BF16)
        z = dot(low, heads[...])
        target = jnp.concatenate(
            [hankel(values[pl.ds(2 * i + k, 1), :], None) for k in range(2)], axis=0)
        valid = jnp.concatenate(
            [hankel(marks[pl.ds(2 * i + k, 1), :], None) for k in range(2)], axis=0)
        factor = valid * weight[...]
        miss = z - target
        size = jnp.abs(miss)
        huber = jnp.where(
            size <= quadratic_cutoff, 0.5 * miss * miss, quadratic_cutoff * (size - 0.5 * quadratic_cutoff))
        loss[...] += jnp.sum(huber * factor, axis=0, keepdims=True)
        dz = (jnp.clip(miss, -quadratic_cutoff, quadratic_cutoff) * factor).astype(BF16)
        d_heads[...] += dot(dz, low, 0, 0)
        df = dot(dz, heads_t[...])
        d_gain[...] += jnp.sum(df * unit, axis=0, keepdims=True)
        dn = df * gain[...]
        dx2[r, :] = scale * (dn - unit * jnp.mean(dn * unit, axis=1, keepdims=True))
        return carry

    lax.fori_loop(0, part.shape[0] // TILE, step, 0)


def loss_stage(part, x1, gain, heads, heads_t, values, marks, weight, ident):
    tokens = part.shape[0]
    return pl.pallas_call(
        loss_kernel,
        in_specs=[VMEM] * 8,
        out_specs=[VMEM] * 4,
        out_shape=[
            jax.ShapeDtypeStruct((tokens, D), F32), jax.ShapeDtypeStruct((LANES, D), F32),
            jax.ShapeDtypeStruct((1, D), F32), jax.ShapeDtypeStruct((1, LANES), F32),
        ],
        scratch_shapes=exchange_scratch(part),
        compiler_params=params(collective_id=ident, has_side_effects=True),
        name="loss_stage",
    )(part, x1, gain, heads, heads_t, values, marks, weight)


def mid_backward_kernel(part, dx2, x1, b, pc, gain, router_t, balance, wo, o, dx1, do, d_router, d_wo, d_gain,
                        other, send_sem, recv_sem):
    wait = exchange(part, other, send_sem, recv_sem)
    d_router[...] = jnp.zeros_like(d_router)
    d_wo[...] = jnp.zeros_like(d_wo)
    d_gain[...] = jnp.zeros_like(d_gain)
    per = o.shape[2] // TILE

    def step(i, carry):
        r = pl.ds(pl.multiple_of(i * TILE, TILE), TILE)
        wait(i)
        dp = part[r, D:] + other[r, D:] + balance[...]
        p = pc[r, :]
        lanes = lax.broadcasted_iota(jnp.int32, p.shape, 1)
        routed = lanes < ROUTED_EXPERTS
        weighted = jnp.sum(jnp.where(routed, p * dp, 0.0), axis=1, keepdims=True)
        dl = jnp.where(routed, p * (dp - weighted), jnp.where(lanes == ROUTED_EXPERTS, dp * p * (1.0 - p), 0.0))
        dl = dl.astype(BF16)
        low = b[r, :]
        d_router[...] += dot(dl, low, 0, 0)
        db = part[r, :D] + other[r, :D] + dot(dl, router_t[...])
        x = x1[r, :]
        scale = lax.rsqrt(jnp.mean(x * x, axis=1, keepdims=True) + norm_eps)
        unit = x * scale
        d_gain[...] += jnp.sum(db * unit, axis=0, keepdims=True)
        dn = db * gain[...]
        dx = dx2[r, :] + scale * (dn - unit * jnp.mean(dn * unit, axis=1, keepdims=True))
        dx1[r, :] = dx
        d_low = dx.astype(BF16)
        n, cols = i // per, pl.ds(pl.multiple_of(lax.rem(i, per) * TILE, TILE), TILE)
        do[n, :, cols] = dot(wo[...], d_low, 1, 1).astype(BF16)
        d_wo[...] += dot(o[n, :, cols], d_low)
        return carry

    lax.fori_loop(0, part.shape[0] // TILE, step, 0)


def mid_backward(part, dx2, x1, b, pc, gain, router_t, balance, wo, o, ident):
    tokens = part.shape[0]
    return pl.pallas_call(
        mid_backward_kernel,
        in_specs=[VMEM] * 10,
        out_specs=[VMEM] * 5,
        out_shape=[
            jax.ShapeDtypeStruct((tokens, D), F32), jax.ShapeDtypeStruct(o.shape, BF16),
            jax.ShapeDtypeStruct((LANES, D), F32), jax.ShapeDtypeStruct(wo.shape, F32),
            jax.ShapeDtypeStruct((1, D), F32),
        ],
        scratch_shapes=exchange_scratch(part),
        compiler_params=params(collective_id=ident, has_side_effects=True),
        name="mid_backward",
    )(part, dx2, x1, b, pc, gain, router_t, balance, wo, o)


def embed_backward_kernel(part, dx1, x_ref, rows_ref, sums, other, send_sem, recv_sem):
    wait = exchange(part, other, send_sem, recv_sem)
    sums[...] = jnp.zeros_like(sums)
    per = x_ref.shape[2] // TILE

    def step(i, carry):
        r = pl.ds(pl.multiple_of(i * TILE, TILE), TILE)
        wait(i)
        n, cols = i // per, pl.ds(pl.multiple_of(lax.rem(i, per) * TILE, TILE), TILE)
        xb = column(x_ref[n, :, cols], TILE)
        xb = jnp.concatenate([xb] * (D // LANES), axis=1)
        u = xb * rows_ref[1:2, :]
        up = xb * rows_ref[2:3, :]
        s = sigmoid(u)
        silu = u * s
        x = silu * up
        scale = lax.rsqrt(jnp.mean(x * x, axis=1, keepdims=True) + norm_eps)
        unit = x * scale
        da = part[r, :] + other[r, :]
        sums[0:1, :] += jnp.sum(da * unit, axis=0, keepdims=True)
        dn = da * rows_ref[0:1, :]
        dx = dx1[r, :] + scale * (dn - unit * jnp.mean(dn * unit, axis=1, keepdims=True))
        du = dx * up * (s * (1.0 + u * (1.0 - s)))
        sums[1:2, :] += jnp.sum(du * xb, axis=0, keepdims=True)
        sums[2:3, :] += jnp.sum(dx * silu * xb, axis=0, keepdims=True)
        return carry

    lax.fori_loop(0, part.shape[0] // TILE, step, 0)


def embed_backward(part, dx1, x, rows, ident):
    return pl.pallas_call(
        embed_backward_kernel,
        in_specs=[VMEM] * 4,
        out_specs=VMEM,
        out_shape=jax.ShapeDtypeStruct((8, D), F32),
        scratch_shapes=exchange_scratch(part),
        compiler_params=params(collective_id=ident, has_side_effects=True),
        name="embed_backward",
    )(part, dx1, x, rows)
def place():
    dp = lax.axis_index("dp")
    return dp, lax.axis_index("mp"), lax.rem(dp, 2), lax.rem(dp // 2, 2), dp // 4


def greet(dp, mp, x, y, z):
    barrier = pltpu.get_barrier_semaphore()
    xp, yp = dp + 1 - 2 * x, dp + 2 - 4 * y
    for peer in (xp, yp):
        pl.semaphore_signal(barrier, inc=1, device_id=(peer, mp), device_id_type=MESH)

    @pl.when(z > 0)
    def _():
        pl.semaphore_signal(barrier, inc=1, device_id=(dp - 4, mp), device_id_type=MESH)

    @pl.when(z < 3)
    def _():
        pl.semaphore_signal(barrier, inc=1, device_id=(dp + 4, mp), device_id_type=MESH)

    @pl.when((z > 0) & (z < 3))
    def _():
        pl.semaphore_wait(barrier, 4)

    @pl.when((z == 0) | (z == 3))
    def _():
        pl.semaphore_wait(barrier, 3)
    return xp, yp


def gather_kernel(chunks, own, out, stage, in_sem, own_sem, send_xy, send_up, send_dn, z_sem, p2_sem, p3_sem):
    dp, mp, x, y, z = place()
    count = own.shape[0]
    load = pltpu.make_async_copy(own, stage, in_sem)
    load.start()
    xp, yp = greet(dp, mp, x, y, z)
    load.wait()

    def rows(c, slot):
        return out.at[c, pl.ds(pl.multiple_of(slot * SHARD, 8), SHARD), :]

    store = []

    def put(src, c, slot, send, recv, peer):
        pltpu.make_async_remote_copy(
            src_ref=src, dst_ref=rows(c, slot), send_sem=send, recv_sem=recv,
            device_id=(peer, mp), device_id_type=MESH).start()

    def arrived(c, slot, sem):
        pltpu.make_async_copy(rows(c, slot), rows(c, slot), sem).wait()

    def local(c):
        return pltpu.make_async_copy(stage.at[c], rows(c, dp), own_sem)

    first = (lambda k: (yp, xp) if k == 0 else (xp, yp))

    def each(fn):
        def body(i, carry):
            fn(2 * i, 0)
            fn(2 * i + 1, 1)
            return carry
        lax.fori_loop(0, count // 2, body, 0)
        if count % 2:
            fn(count - 1, 0)

    def zup(c, zs, src):
        put(src, c, zs * 4 + 2 * y + x, send_up, z_sem.at[c, zs], dp + 4)

    def zdn(c, zs, src):
        put(src, c, zs * 4 + 2 * y + x, send_dn, z_sem.at[c, zs], dp - 4)

    def spread(c, k, zs, src):
        a, b = first(k)
        slot = zs * 4 + 2 * y + x
        put(src, c, slot, send_xy, p2_sem.at[c, zs], a)
        put(src, c, slot, send_xy, p3_sem, b)

    def begin(c, k):
        @pl.when(z < 3)
        def _():
            zup(c, z, stage.at[c])

        @pl.when(z > 0)
        def _():
            zdn(c, z, stage.at[c])
        spread(c, k, z, stage.at[c])
        local(c).start()
    each(begin)

    def second(c, k, zs):
        a, b = first(k)
        slot = zs * 4 + (2 * (1 - y) + x if k == 0 else 2 * y + 1 - x)
        arrived(c, slot, p2_sem.at[c, zs])
        put(rows(c, slot), c, slot, send_xy, p3_sem, b)

    for dist in (1, 2, 3):
        def step(c, k, dist=dist):
            @pl.when(z >= dist)
            def _():
                zs = z - dist
                arrived(c, zs * 4 + 2 * y + x, z_sem.at[c, zs])
                src = rows(c, zs * 4 + 2 * y + x)

                @pl.when(z < 3)
                def _():
                    zup(c, zs, src)
                spread(c, k, zs, src)

            @pl.when(z + dist <= 3)
            def _():
                zs = z + dist
                arrived(c, zs * 4 + 2 * y + x, z_sem.at[c, zs])
                src = rows(c, zs * 4 + 2 * y + x)

                @pl.when(z > 0)
                def _():
                    zdn(c, zs, src)
                spread(c, k, zs, src)
            if dist == 1:
                second(c, k, z)
            else:
                @pl.when(z >= dist - 1)
                def _():
                    second(c, k, z - dist + 1)

                @pl.when(z + dist - 1 <= 3)
                def _():
                    second(c, k, z + dist - 1)
        each(step)

    def last(c, k):
        @pl.when(z >= 3)
        def _():
            second(c, k, z - 3)

        @pl.when(z <= 0)
        def _():
            second(c, k, z + 3)
    each(last)

    def total(n, sem):
        view = out.at[:, pl.ds(0, n * SHARD), :]
        pltpu.make_async_copy(view, view, sem).wait()
    total(8, p3_sem)
    total(12, send_xy)
    total(1, own_sem)
    for k in range(4):
        @pl.when(z == k)
        def _():
            if k < 3:
                total(k + 1, send_up)
            if k > 0:
                total(4 - k, send_dn)


def gather_rows(own, ident):
    chunks, shard, columns = own.shape
    return pl.pallas_call(
        functools.partial(gather_kernel, chunks),
        out_shape=jax.ShapeDtypeStruct((chunks, 16 * shard, columns), own.dtype),
        in_specs=[pl.BlockSpec(memory_space=pl.ANY)],
        out_specs=pl.BlockSpec(memory_space=pl.ANY),
        scratch_shapes=[
            pltpu.VMEM(own.shape, own.dtype),
            pltpu.SemaphoreType.DMA, pltpu.SemaphoreType.DMA, pltpu.SemaphoreType.DMA,
            pltpu.SemaphoreType.DMA, pltpu.SemaphoreType.DMA,
            pltpu.SemaphoreType.DMA((chunks, 4)), pltpu.SemaphoreType.DMA((chunks, 4)),
            pltpu.SemaphoreType.DMA,
        ],
        compiler_params=pltpu.CompilerParams(collective_id=ident, has_side_effects=True),
        name="gather_rows",
    )(own)


def reduce_kernel(count, halves, *refs):
    (g, out, first, mine, second, up, dn, send1, send2, send_up, send_dn, load_sem,
     sem1, sem2, up_sem, dn_sem) = refs
    dp, mp, x, y, z = place()
    width = out.shape[-1] // halves
    xp, yp = greet(dp, mp, x, y, z)

    def cut(c, k, which):
        e, h = c // halves, lax.rem(c, halves)
        cols = pl.ds(pl.multiple_of(h * width, 128), width)
        if k == 0:
            return g.at[e, :, :, which, :, cols]
        return g.at[e, :, which, :, :, cols]

    def remote(src, dst, send, recv, peer):
        return pltpu.make_async_remote_copy(
            src_ref=src, dst_ref=dst, send_sem=send, recv_sem=recv,
            device_id=(peer, mp), device_id_type=MESH)

    def arrived(view, sem):
        pltpu.make_async_copy(view, view, sem).wait()

    def each(fn):
        def body(i, carry):
            fn(2 * i, 0)
            fn(2 * i + 1, 1)
            return carry
        lax.fori_loop(0, count // 2, body, 0)
        if count % 2:
            fn(count - 1, 0)

    def keep(k):
        return x if k == 0 else y

    def load(c, k, slot):
        return pltpu.make_async_copy(cut(c, k, keep(k)), mine.at[slot], load_sem.at[slot])

    def begin(c, k):
        peer = xp if k == 0 else yp
        remote(cut(c, k, 1 - keep(k)), first.at[c], send1, sem1.at[c], peer).start()
    each(begin)
    load(0, 0, 0).start()
    if count > 1:
        load(1, 1, 1).start()

    def fold(c, k):
        load(c, k, k).wait()
        arrived(first.at[c], sem1.at[c])

        def add(i, carry):
            a, b = i // 2, lax.rem(i, 2)
            first[c, a, b] = first[c, a, b] + mine[k, a, b]
            return carry
        lax.fori_loop(0, 8, add, 0)

        @pl.when(c + 2 < count)
        def _():
            load(c + 2, k, k).start()
        peer = yp if k == 0 else xp
        other = y if k == 0 else x
        remote(first.at[c, :, 1 - other], second.at[c], send2, sem2.at[c], peer).start()
    each(fold)

    def line(c, k):
        other = y if k == 0 else x
        arrived(second.at[c], sem2.at[c])

        def add(a, carry):
            second[c, a] = second[c, a] + first[c, a, other]
            return carry
        lax.fori_loop(0, 4, add, 0)
        for t in (3, 2, 1):
            @pl.when((z < t) & (z == 0))
            def _():
                remote(second.at[c, t], up.at[c, t - 1], send_up, up_sem.at[c, t - 1], dp + 4).start()

            @pl.when((z < t) & (z > 0))
            def _():
                arrived(up.at[c, t - 1], up_sem.at[c, t - 1])
                second[c, t] = second[c, t] + up[c, t - 1]
                remote(second.at[c, t], up.at[c, t - 1], send_up, up_sem.at[c, t - 1], dp + 4).start()
        for t in (0, 1, 2):
            @pl.when((z > t) & (z == 3))
            def _():
                remote(second.at[c, t], dn.at[c, t], send_dn, dn_sem.at[c, t], dp - 4).start()

            @pl.when((z > t) & (z < 3))
            def _():
                arrived(dn.at[c, t], dn_sem.at[c, t])
                second[c, t] = second[c, t] + dn[c, t]
                remote(second.at[c, t], dn.at[c, t], send_dn, dn_sem.at[c, t], dp - 4).start()
    each(line)

    def finish(c, k):
        e, h = c // halves, lax.rem(c, halves)
        cols = pl.ds(pl.multiple_of(h * width, 128), width)
        out[e, :, cols] = second[c, z]
        for t in range(4):
            @pl.when(z == t)
            def _():
                if t > 0:
                    arrived(up.at[c, t - 1], up_sem.at[c, t - 1])
                    out[e, :, cols] = out[e, :, cols] + up[c, t - 1]
                if t < 3:
                    arrived(dn.at[c, t], dn_sem.at[c, t])
                    out[e, :, cols] = out[e, :, cols] + dn[c, t]
    each(finish)

    def total(ref, sem):
        pltpu.make_async_copy(ref, ref, sem).wait()
    total(first, send1)
    total(second, send2)
    for k in range(4):
        @pl.when(z == k)
        def _():
            if k < 3:
                total(up.at[:, pl.ds(k, 3 - k)], send_up)
            if k > 0:
                total(dn.at[:, pl.ds(0, k)], send_dn)


def reduce_rows(g, halves, ident):
    chunks, rows, columns = g.shape
    shard = rows // 16
    count, width = chunks * halves, columns // halves
    f32 = jnp.float32
    return pl.pallas_call(
        functools.partial(reduce_kernel, count, halves),
        out_shape=jax.ShapeDtypeStruct((chunks, shard, columns), f32),
        in_specs=[pl.BlockSpec(memory_space=pl.ANY)],
        out_specs=pl.BlockSpec(memory_space=pltpu.VMEM),
        scratch_shapes=[
            pltpu.VMEM((count, 4, 2, shard, width), f32),
            pltpu.VMEM((2, 4, 2, shard, width), f32),
            pltpu.VMEM((count, 4, shard, width), f32),
            pltpu.VMEM((count, 3, shard, width), f32),
            pltpu.VMEM((count, 3, shard, width), f32),
            pltpu.SemaphoreType.DMA, pltpu.SemaphoreType.DMA, pltpu.SemaphoreType.DMA, pltpu.SemaphoreType.DMA,
            pltpu.SemaphoreType.DMA((2,)),
            pltpu.SemaphoreType.DMA((count,)), pltpu.SemaphoreType.DMA((count,)),
            pltpu.SemaphoreType.DMA((count, 3)), pltpu.SemaphoreType.DMA((count, 3)),
        ],
        compiler_params=pltpu.CompilerParams(
            collective_id=ident, has_side_effects=True, vmem_limit_bytes=60 * 1024 * 1024),
        name="reduce_rows",
    )(g.reshape(chunks, 4, 2, 2, shard, columns))


def all_kernel(n_dp, value, out, send_sem, recv_sem):
    dp, mp = lax.axis_index("dp"), lax.axis_index("mp")
    me = dp * 2 + mp
    n = 2 * n_dp
    barrier = pltpu.get_barrier_semaphore()
    for k in range(1, n):
        peer = lax.rem(me + k, n)
        pl.semaphore_signal(barrier, inc=1, device_id=(peer // 2, lax.rem(peer, 2)), device_id_type=MESH)
    pl.semaphore_wait(barrier, n - 1)
    for k in range(1, n):
        peer = lax.rem(me + k, n)
        pltpu.make_async_remote_copy(src_ref=value, dst_ref=out.at[me], send_sem=send_sem, recv_sem=recv_sem,
                                     device_id=(peer // 2, lax.rem(peer, 2)), device_id_type=MESH).start()
    out[me] = value[...]
    view = out.at[pl.ds(0, n - 1)]
    pltpu.make_async_copy(view, view, recv_sem).wait()
    pltpu.make_async_copy(view, view, send_sem).wait()


def all_blocks(value, n_dp, ident):
    n = 2 * n_dp
    return pl.pallas_call(
        functools.partial(all_kernel, n_dp),
        out_shape=jax.ShapeDtypeStruct((n,) + value.shape, value.dtype),
        in_specs=[pl.BlockSpec(memory_space=pltpu.VMEM)],
        out_specs=pl.BlockSpec(memory_space=pltpu.VMEM),
        scratch_shapes=[pltpu.SemaphoreType.DMA, pltpu.SemaphoreType.DMA],
        compiler_params=pltpu.CompilerParams(collective_id=ident, has_side_effects=True),
        name="all_blocks",
    )(value)


I16 = jnp.int16
SLOTS = 3


def encode(dest, v):
    width = v.shape[1]
    top = jnp.max(jnp.abs(v), axis=1, keepdims=True)
    power = jnp.ceil(jnp.log2(jnp.maximum(top, 1e-30) * (1.001 / 32767.0)))
    power = jnp.broadcast_to(power, (v.shape[0], LANES))
    inverse = jnp.exp2(-power)
    dest[:, width:] = power.astype(jnp.int32).astype(I16)
    for c in range(width // LANES):
        cols = slice(c * LANES, (c + 1) * LANES)
        dest[:, cols] = jnp.round(v[:, cols] * inverse).astype(jnp.int32).astype(I16)


def decode(source):
    width = source.shape[1] - LANES
    unit = jnp.exp2(source[:, width:].astype(jnp.int32).astype(F32))
    return jnp.concatenate(
        [source[:, c * LANES:(c + 1) * LANES].astype(jnp.int32).astype(F32) * unit for c in range(width // LANES)],
        axis=1)


def gradient_kernel(
    xs, dys, dgs, hs, out,
    x_in, dy_in, dg_in, h_in, xt, dyt, dw, acc, send1, recv1, send2, recv2, zs_up, zs_dn, up, dn,
    load_sem, sem_s1, sem_r1, sem_s2, sem_r2, sem_su, sem_sd, sem_ru, sem_rd,
):
    dp, mp, x, y, z = place()
    count = out.shape[0]
    blocks = xs.shape[0]
    hidden = hs.shape[2]

    def loads(block):
        return [
            pltpu.make_async_copy(src.at[block], dst, load_sem.at[i])
            for i, (src, dst) in enumerate(((xs, x_in), (dys, dy_in), (dgs, dg_in), (hs, h_in)))]

    for copy in loads(0):
        copy.start()
    xp, yp = greet(dp, mp, x, y, z)

    def remote(src, dst, send, recv, peer):
        return pltpu.make_async_remote_copy(
            src_ref=src, dst_ref=dst, send_sem=send, recv_sem=recv, device_id=(peer, mp), device_id_type=MESH)

    def done(view, sem):
        pltpu.make_async_copy(view, view, sem).wait()

    def shard(slot, s):
        return dw.at[slot, pl.ds(pl.multiple_of(s * SHARD, 8), SHARD), :]

    def weights(block, slot, more):
        for copy in loads(block):
            copy.wait()
        xt[...] = jnp.transpose(x_in[...])
        dyt[...] = jnp.transpose(dy_in[...])

        def wide(j, carry):
            cols = pl.ds(pl.multiple_of(j * TILE, TILE), TILE)
            v = dot(xt[...], dg_in[:, cols])
            dw[slot, :, cols] = dw[slot, :, cols] + v if more else v
            return carry

        def tall(j, carry):
            cols = pl.ds(pl.multiple_of(j * TILE, TILE), TILE)
            there = pl.ds(pl.multiple_of(2 * hidden + j * TILE, TILE), TILE)
            v = dot(dyt[...], h_in[:, cols])
            dw[slot, :, there] = dw[slot, :, there] + v if more else v
            return carry

        lax.fori_loop(0, 2 * hidden // TILE, wide, 0)
        lax.fori_loop(0, hidden // TILE, tall, 0)

        @pl.when(block + 1 < blocks)
        def _():
            for copy in loads(block + 1):
                copy.start()

    def begin(c):
        k, slot = lax.rem(c, 2), lax.rem(c, SLOTS)
        weights(c, slot, False)

        @pl.when(c == count - 1)
        def _():
            weights(c + 1, slot, True)

        @pl.when(c >= SLOTS)
        def _():
            done(send1.at[slot], sem_s1.at[slot])

        def pack(i, carry):
            a, b = i // 2, lax.rem(i, 2)
            s = a * 4 + jnp.where(k == 0, b * 2 + 1 - x, (1 - y) * 2 + b)
            encode(send1.at[slot, i], shard(slot, s)[...])
            return carry

        lax.fori_loop(0, 8, pack, 0)
        remote(send1.at[slot], recv1.at[c], sem_s1.at[slot], sem_r1.at[c], jnp.where(k == 0, xp, yp)).start()

    def fold(c):
        k, slot = lax.rem(c, 2), lax.rem(c, SLOTS)
        o = jnp.where(k == 0, y, x)
        done(recv1.at[c], sem_r1.at[c])

        @pl.when(c >= SLOTS)
        def _():
            done(send2.at[slot], sem_s2.at[slot])

        def add(a, carry):
            s = a * 4 + jnp.where(k == 0, (1 - y) * 2 + x, y * 2 + 1 - x)
            encode(send2.at[slot, a], shard(slot, s)[...] + decode(recv1.at[c, a * 2 + 1 - o]))
            acc[lax.rem(c, 5), a] = shard(slot, a * 4 + y * 2 + x)[...] + decode(recv1.at[c, a * 2 + o])
            return carry

        lax.fori_loop(0, 4, add, 0)
        remote(send2.at[slot], recv2.at[c], sem_s2.at[slot], sem_r2.at[c], jnp.where(k == 0, yp, xp)).start()

    def climb(c, t, relay):
        slot = lax.rem(c, SLOTS)
        v = acc[lax.rem(c, 5), t]
        if relay:
            done(up.at[c, t - 1], sem_ru.at[c, t - 1])
            v = v + decode(up.at[c, t - 1])

        @pl.when(c >= SLOTS)
        def _():
            done(zs_up.at[slot, t - 1], sem_su.at[slot, t - 1])
        encode(zs_up.at[slot, t - 1], v)
        remote(zs_up.at[slot, t - 1], up.at[c, t - 1], sem_su.at[slot, t - 1], sem_ru.at[c, t - 1], dp + 4).start()

    def drop(c, t, relay):
        slot = lax.rem(c, SLOTS)
        v = acc[lax.rem(c, 5), t]
        if relay:
            done(dn.at[c, t], sem_rd.at[c, t])
            v = v + decode(dn.at[c, t])

        @pl.when(c >= SLOTS)
        def _():
            done(zs_dn.at[slot, t], sem_sd.at[slot, t])
        encode(zs_dn.at[slot, t], v)
        remote(zs_dn.at[slot, t], dn.at[c, t], sem_sd.at[slot, t], sem_rd.at[c, t], dp - 4).start()

    def line_a(c):
        done(recv2.at[c], sem_r2.at[c])

        def add(a, carry):
            acc[lax.rem(c, 5), a] = acc[lax.rem(c, 5), a] + decode(recv2.at[c, a])
            return carry

        lax.fori_loop(0, 4, add, 0)
        out[c] = acc[lax.rem(c, 5), z]

        @pl.when(z == 0)
        def _():
            for t in (3, 2, 1):
                climb(c, t, False)

        @pl.when(z == 3)
        def _():
            for t in (0, 1, 2):
                drop(c, t, False)

    def line_b(c):
        @pl.when(z == 1)
        def _():
            for t in (3, 2):
                climb(c, t, True)

        @pl.when(z == 2)
        def _():
            for t in (0, 1):
                drop(c, t, True)

    def line_c(c):
        @pl.when(z == 2)
        def _():
            climb(c, 3, True)

        @pl.when(z == 1)
        def _():
            drop(c, 0, True)

    def finish(c):
        @pl.when(z > 0)
        def _():
            done(up.at[c, z - 1], sem_ru.at[c, z - 1])
            out[c] = out[c] + decode(up.at[c, z - 1])

        @pl.when(z < 3)
        def _():
            done(dn.at[c, z], sem_rd.at[c, z])
            out[c] = out[c] + decode(dn.at[c, z])

    stages = ((begin, 0), (fold, 2), (line_a, 4), (line_b, 5), (line_c, 6), (finish, 7))

    def step(i, carry):
        for stage, lag in stages:
            @pl.when((i >= lag) & (i < count + lag))
            def _(stage=stage, lag=lag):
                stage(i - lag)
        return carry

    lax.fori_loop(0, count + stages[-1][1], step, 0)

    for slot in range(SLOTS):
        done(send1.at[slot], sem_s1.at[slot])
        done(send2.at[slot], sem_s2.at[slot])
        for t in (1, 2, 3):
            @pl.when(z < t)
            def _():
                done(zs_up.at[slot, t - 1], sem_su.at[slot, t - 1])
        for t in (0, 1, 2):
            @pl.when(z > t)
            def _():
                done(zs_dn.at[slot, t], sem_sd.at[slot, t])


def gradient_sums(xs, dys, dgs, hs, ident):
    capacity, hidden = hs.shape[1], hs.shape[2]
    count = ROUTED_EXPERTS + 1
    width = 3 * hidden
    coded = width + LANES
    dma = pltpu.SemaphoreType.DMA
    return pl.pallas_call(
        gradient_kernel,
        in_specs=[ANY] * 4,
        out_specs=VMEM,
        out_shape=jax.ShapeDtypeStruct((count, SHARD, width), F32),
        scratch_shapes=[
            pltpu.VMEM((capacity, D), BF16), pltpu.VMEM((capacity, D), BF16),
            pltpu.VMEM((capacity, 2 * hidden), BF16), pltpu.VMEM((capacity, hidden), BF16),
            pltpu.VMEM((D, capacity), BF16), pltpu.VMEM((D, capacity), BF16),
            pltpu.VMEM((SLOTS, D, width), F32),
            pltpu.VMEM((5, 4, SHARD, width), F32),
            pltpu.VMEM((SLOTS, 8, SHARD, coded), I16), pltpu.VMEM((count, 8, SHARD, coded), I16),
            pltpu.VMEM((SLOTS, 4, SHARD, coded), I16), pltpu.VMEM((count, 4, SHARD, coded), I16),
            pltpu.VMEM((SLOTS, 3, SHARD, coded), I16), pltpu.VMEM((SLOTS, 3, SHARD, coded), I16),
            pltpu.VMEM((count, 3, SHARD, coded), I16), pltpu.VMEM((count, 3, SHARD, coded), I16),
            dma((4,)), dma((SLOTS,)), dma((count,)), dma((SLOTS,)), dma((count,)),
            dma((SLOTS, 3)), dma((SLOTS, 3)), dma((count, 3)), dma((count, 3)),
        ],
        compiler_params=params(63, collective_id=ident, has_side_effects=True),
        name="gradient_sums",
    )(xs, dys, dgs, hs)


def rope_tables(length):
    halfway = HEAD // 2
    frequency = rope_base ** (-2.0 * jnp.arange(halfway, dtype=F32) / HEAD)
    angles = frequency[:, None] * jnp.arange(length, dtype=F32)[None, :]
    return jnp.cos(angles), jnp.sin(angles)


def hankel_rows(track):
    series, length = track.shape
    padded = jnp.pad(track, ((0, 0), (63, 2 * LANES)))
    first = padded[:, :length].reshape(-1, LANES)[:, ::-1]
    second = padded[:, LANES:LANES + length].reshape(-1, LANES)[:, ::-1]
    return jnp.concatenate([first, second], axis=1)


def head_columns(matrix):
    parts, end = [], matrix.shape[1]
    for horizon in horizons[::-1]:
        parts.append(matrix[:, end - horizon:end][:, ::-1])
        end -= horizon
    return jnp.pad(jnp.concatenate(parts, axis=1), ((0, 0), (0, LANES - matrix.shape[1])))


def head_columns_back(matrix):
    parts, begin = [], 0
    for horizon in horizons[::-1]:
        parts.append(matrix[:, begin:begin + horizon][:, ::-1])
        begin += horizon
    return jnp.concatenate(parts[::-1], axis=1)


def dispatch(route_rows, capacity):
    tokens = route_rows.shape[0]
    experts = jnp.arange(ROUTED_EXPERTS, dtype=jnp.int32)
    member = jnp.any(route_rows[:, :, None] == experts[None, None, :], axis=1)
    count = jnp.cumsum(member.astype(jnp.int32), axis=0)
    total = count[-1]
    place = jnp.where(member, count - 1, -1)
    high = (place[:, :, None] // LANES == jnp.arange(capacity // LANES)[None, None, :]) & member[:, :, None]
    low = (place[:, :, None] % LANES == jnp.arange(LANES)[None, None, :]).astype(BF16)
    token = jnp.arange(tokens, dtype=jnp.int32)
    left = jnp.concatenate(
        [jnp.where(high, part[:, None, None], 0).astype(BF16) for part in (token // 16, token % 16)], axis=2)
    found = jnp.einsum("teh,tel->ehl", left, low, preferred_element_type=F32)
    half = capacity // LANES
    source = (found[:, :half] * 16.0 + found[:, half:]).reshape(ROUTED_EXPERTS, capacity).astype(jnp.int32)
    slots = jnp.arange(capacity, dtype=jnp.int32)
    source = jnp.where(slots[None, :] < total[:, None], source, tokens)
    return total, source.reshape(-1)


def adam_update(master, moment, square, gradient, factor, bias_one, bias_two, step_rate):
    clipped = gradient * factor
    new_moment = beta_one * moment + (1.0 - beta_one) * clipped
    new_square = beta_two * square + (1.0 - beta_two) * clipped * clipped
    updated = master - step_rate * (
        new_moment / bias_one / (jnp.sqrt(new_square / bias_two) + adam_eps) + decay_rate * master
    )
    return (updated, new_moment, new_square)


def on_device(
    near,
    series, observed, routes, step_count,
    joint_proj, joint_moment, joint_square,
    mixer_proj, mixer_moment, mixer_square,
    upward_proj, upward_moment, upward_square,
    downward_proj, downward_moment, downward_square,
    readout, readout_moment, readout_square,
    vectors, vectors_moment, vectors_square,
):
    dp_count = lax.axis_size("dp")
    mp_count = lax.axis_size("mp")
    shard = joint_proj.shape[1]
    width = joint_proj.shape[2]
    hidden = upward_proj.shape[3]
    experts = upward_proj.shape[0]
    series_count, length = series.shape
    tokens = series_count * length
    capacity = tokens // 2
    columns = readout.shape[1]
    small_width = -(-(4 * width + columns + 5) // LANES) * LANES

    def pack_small(joint, mixer_t, read, vec):
        flat = jnp.concatenate([joint[0], joint[1], joint[2], mixer_t, read, vec], axis=1)
        return jnp.pad(flat, ((0, 0), (0, small_width - flat.shape[1])))

    small_own = pack_small(
        joint_proj.astype(BF16), mixer_proj.T.astype(BF16), readout.astype(BF16), vectors.T.astype(BF16))
    big_own = jnp.concatenate(
        [upward_proj.astype(BF16).reshape(experts, shard, 2 * hidden), downward_proj.transpose(0, 2, 1).astype(BF16)],
        axis=2)
    marks = observed.astype(F32)
    route_rows = routes.reshape(tokens, 2)
    expert_here, source = dispatch(route_rows, capacity)
    point = jnp.arange(length, dtype=F32)
    head_here = jnp.stack(
        [jnp.sum(jnp.sum(marks, axis=0) * jnp.minimum(point, float(horizon))) for horizon in horizons])
    tally = jnp.pad(jnp.concatenate([expert_here.astype(F32), head_here]), (0, LANES - 12))
    if near:
        small = gather_rows(small_own[None], 0)[0]
        big = gather_rows(big_own, 1)
        tally = jnp.sum(all_blocks(jnp.broadcast_to(tally[None], (8, LANES)), dp_count, 2)[:, 0], axis=0) / mp_count
    else:
        small = lax.all_gather(small_own, "dp", axis=0, tiled=True)
        big = lax.all_gather(big_own, "dp", axis=1, tiled=True)
        tally = lax.psum(tally, "dp")
    expert_count, head_count = tally[:ROUTED_EXPERTS], tally[ROUTED_EXPERTS:ROUTED_EXPERTS + 4]
    total_tokens = tokens * dp_count

    wj = small[:, :3 * width].T
    wo = small[:, 3 * width:4 * width].T
    read = small[:, 4 * width:4 * width + columns]
    vec = small[:, 4 * width + columns:4 * width + columns + 5].astype(F32).T
    rows = jnp.concatenate([vec[0:1], vec[3:5], jnp.zeros((5, D), F32)], axis=0)
    router = jnp.pad(read[:, :ROUTED_EXPERTS + 1], ((0, 0), (0, LANES - ROUTED_EXPERTS - 1)))
    heads = head_columns(read[:, ROUTED_EXPERTS + 1:])
    cos, sin = rope_tables(length)
    x = (series * marks).reshape(series_count, 1, length)

    x0, a, qkv, lse, o, part = attend_forward(x, rows, wj, wo, cos, sin)
    x1, b, pc, pr_total = mid_forward(part, x0, vec[1:2], router, 3)
    xs, ys, mixed = expert_forward(expert_here, source, b, pc, big)
    head_weight = jnp.concatenate(
        [jnp.zeros((horizon,), F32) + 0.25 / head_count[3 - index] for index, horizon in enumerate(horizons[::-1])])
    head_weight = jnp.pad(head_weight, (0, LANES - head_weight.shape[0]))[None]
    dx2, d_heads, d_gain3, fit = loss_stage(
        mixed, x1, vec[2:3], heads, heads.T, hankel_rows(series), hankel_rows(marks), head_weight, 4)
    dys, dgs, hs, back = expert_backward(expert_here, source, pc, dx2, big, xs, ys)
    balance = aux_factor * ROUTED_EXPERTS * expert_count / total_tokens / total_tokens
    balance = jnp.pad(balance, (0, LANES - ROUTED_EXPERTS))[None]
    local_loss = jnp.sum(fit) + jnp.sum(pr_total * balance)
    dx1, do, d_router, d_wo, d_gain2 = mid_backward(
        back, dx2, x1, b, pc, vec[1:2], router.T, balance, wo, o, 5)
    d_wj, da = attend_backward(qkv, do, lse, a, wj, cos, sin)
    sums = embed_backward(da, dx1, x, rows, 6)

    d_read = jnp.concatenate([d_router[:ROUTED_EXPERTS + 1].T, head_columns_back(d_heads.T)], axis=1)
    d_vec = jnp.concatenate([sums[0:1], d_gain2, d_gain3, sums[1:3]], axis=0).T
    d_wj = d_wj.T
    d_small = pack_small(
        [d_wj[:, k * width:(k + 1) * width] for k in range(3)], d_wo.T, d_read, d_vec)
    if near:
        big_red = gradient_sums(xs, dys, dgs, hs, 7)
        small_red = reduce_rows(d_small[None], 1, 8)[0]
    else:
        d_up = jnp.einsum("ekd,ekf->edf", xs, dgs, preferred_element_type=F32)
        d_down = jnp.einsum("ekd,ekf->edf", dys, hs, preferred_element_type=F32)
        d_big = jnp.concatenate([d_up, d_down], axis=2)
        d_big = jnp.concatenate([d_big[:ROUTED_EXPERTS], jnp.sum(d_big[ROUTED_EXPERTS:], axis=0, keepdims=True)], axis=0)
        big_red = lax.psum_scatter(d_big, "dp", scatter_dimension=1, tiled=True)
        small_red = lax.psum_scatter(d_small, "dp", scatter_dimension=0, tiled=True)
    attn_red = small_red[:, :4 * width]
    rest_red = small_red[:, 4 * width:4 * width + columns + 5]
    squares = (
        jnp.sum(big_red * big_red) + jnp.sum(attn_red * attn_red) + jnp.sum(rest_red * rest_red) / mp_count
    )
    pair = jnp.pad(jnp.stack([squares, local_loss / mp_count]), (0, LANES - 2))
    if near:
        pair = jnp.sum(all_blocks(jnp.broadcast_to(pair[None], (8, LANES)), dp_count, 9)[:, 0], axis=0)
    else:
        pair = lax.psum(pair, ("dp", "mp"))
    grad_norm, loss_total = jnp.sqrt(pair[0]), pair[1]

    factor = clip_limit / (grad_norm + 1e-06)
    steps_taken = step_count[0].astype(F32)
    bias_one = 1.0 - beta_one**steps_taken
    bias_two = 1.0 - beta_two**steps_taken

    def update(master, moment, square, gradient, rate=matrix_rate):
        return adam_update(master, moment, square, gradient, factor, bias_one, bias_two, rate)

    joint_red = jnp.stack([attn_red[:, k * width:(k + 1) * width] for k in range(3)], axis=0)
    mixer_red = attn_red[:, 3 * width:].T
    upward_red = big_red[:, :, :2 * hidden].reshape(upward_proj.shape)
    downward_red = big_red[:, :, 2 * hidden:].transpose(0, 2, 1)
    return (
        loss_total,
        grad_norm,
        *update(joint_proj, joint_moment, joint_square, joint_red),
        *update(mixer_proj, mixer_moment, mixer_square, mixer_red),
        *update(upward_proj, upward_moment, upward_square, upward_red),
        *update(downward_proj, downward_moment, downward_square, downward_red),
        *update(readout, readout_moment, readout_square, rest_red[:, :columns]),
        *update(vectors, vectors_moment, vectors_square, rest_red[:, columns:].T, vector_rate),
    )


def solution(mesh):
    token = [P("dp", None), P("dp", None), P("dp", None, None), P()]
    weights = [
        P(None, "dp", "mp"), P("mp", "dp"), P(None, "dp", None, "mp"), P(None, "mp", "dp"), P("dp", None), P(None, "dp"),
    ]
    triple = tuple(spec for spec in weights for _ in range(3))
    near = mesh.shape["dp"] == 16 and mesh.shape["mp"] == 2
    return jax.shard_map(
        functools.partial(on_device, near),
        mesh=mesh,
        in_specs=tuple(token) + triple,
        out_specs=(P(), P()) + triple,
        check_vma=False,
    )
```

```python
import functools
import jax
import jax.numpy as jnp
from jax import lax
from jax.experimental import pallas as pl
from jax.experimental.pallas import tpu as pltpu
from jax.sharding import PartitionSpec as P

D = 384
HEAD = 32
ROUTED_EXPERTS = 8
LANES = 128
TILE = 256
SHARD = 24
ROUTER = 112
SHARED = ROUTER + ROUTED_EXPERTS
VECTOR = SHARED + 1

horizons = (1, 8, 32, 64)
quadratic_cutoff = 2.0
aux_factor = 0.02
clip_limit = 0.001
beta_one = 0.9
beta_two = 0.95
adam_eps = 1e-08
decay_rate = 0.1
matrix_rate = 0.05
vector_rate = 0.25
norm_eps = 1e-06
rope_base = 10000.0

F32 = jnp.float32
BF16 = jnp.bfloat16
I16 = jnp.int16
MESH = pl.DeviceIdType.MESH
VMEM = pl.BlockSpec(memory_space=pltpu.VMEM)
ANY = pl.BlockSpec(memory_space=pl.ANY)
DMA = pltpu.SemaphoreType.DMA


def dot(a, b, da=1, db=0):
    return lax.dot_general(a, b, (((da,), (db,)), ((), ())), preferred_element_type=F32)


def params(megabytes=60, **more):
    return pltpu.CompilerParams(vmem_limit_bytes=megabytes * 1024 * 1024, **more)


def sigmoid(v):
    return 1.0 / (1.0 + jnp.exp(-v))


def block(index, size, step=8):
    return pl.ds(pl.multiple_of(index * size, step), size)


def place():
    dp = lax.axis_index("dp")
    return dp, lax.axis_index("mp"), lax.rem(dp, 2), lax.rem(dp // 2, 2), dp // 4


def meet_everyone(dp, mp):
    barrier = pltpu.get_barrier_semaphore()
    me, n = dp * 2 + mp, 32

    def signal(k, carry):
        peer = lax.rem(me + k, n)
        pl.semaphore_signal(barrier, inc=1, device_id=(peer // 2, lax.rem(peer, 2)), device_id_type=MESH)
        return carry

    lax.fori_loop(1, n, signal, 0)
    pl.semaphore_wait(barrier, n - 1)


def remote(src, dst, send, recv, dp, mp):
    return pltpu.make_async_remote_copy(
        src_ref=src, dst_ref=dst, send_sem=send, recv_sem=recv, device_id=(dp, mp), device_id_type=MESH)


def done(view, sem):
    pltpu.make_async_copy(view, view, sem).wait()


def column(row, length):
    return jnp.transpose(jnp.broadcast_to(row, (LANES, length)))


def rotated(t, cos, sin):
    half = HEAD // 2
    front, back = t[:half], t[half:]
    return jnp.concatenate([front * cos - back * sin, back * cos + front * sin], axis=0)


def unrotated(t, cos, sin):
    half = HEAD // 2
    front, back = t[:half], t[half:]
    return jnp.concatenate([front * cos + back * sin, back * cos - front * sin], axis=0)


def score_block(k_rows, q_cols, low):
    s = dot(k_rows, q_cols)
    keys = lax.broadcasted_iota(jnp.int32, s.shape, 0)
    queries = lax.broadcasted_iota(jnp.int32, s.shape, 1) + low
    return jnp.where(keys <= queries, s, -1e30)


def flip(t):
    return jnp.transpose(t.astype(F32)).astype(BF16)


def embed_piece(x_row, vec, x0_ref, a_ref, r):
    xb = column(x_row, TILE)
    cuts, square = [], None
    for c in range(D // LANES):
        cols = slice(c * LANES, (c + 1) * LANES)
        u = xb * vec[3:4, cols]
        v = u * sigmoid(u) * (xb * vec[4:5, cols])
        x0_ref[r, cols] = v
        square = v * v if square is None else square + v * v
        cuts.append(v)
    scale = lax.rsqrt(jnp.sum(square, axis=1, keepdims=True) / D + norm_eps)
    for c in range(D // LANES):
        cols = slice(c * LANES, (c + 1) * LANES)
        a_ref[r, cols] = (cuts[c] * scale * vec[0:1, cols]).astype(BF16)


def project_piece(wt, a, cos, sin, qkv, width):
    for part in range(3):
        t = dot(wt[part * width:(part + 1) * width, :], a, 1, 1)
        for h in range(width // HEAD):
            u = t[h * HEAD:(h + 1) * HEAD]
            if part < 2:
                u = rotated(u, cos, sin)
            qkv[part * width + h * HEAD:part * width + (h + 1) * HEAD, :] = u.astype(BF16)


def forward_head(h, width, qkv, lse, o):
    length = qkv.shape[1]
    scale = HEAD ** (-0.5)
    q_rows = block(h, HEAD)
    k_rows = pl.ds(pl.multiple_of(width + h * HEAD, HEAD), HEAD)
    v_rows = pl.ds(pl.multiple_of(2 * width + h * HEAD, HEAD), HEAD)
    k = flip(qkv[k_rows, :])
    for j in range(length // TILE):
        n = TILE * (j + 1)
        cols = slice(j * TILE, (j + 1) * TILE)
        s = score_block(k[:n], qkv[q_rows, cols], j * TILE)
        peak = jnp.max(s, axis=0, keepdims=True)
        e = jnp.exp((s - peak) * scale)
        mass = jnp.sum(e, axis=0, keepdims=True)
        weights = (e * (1.0 / mass)).astype(BF16)
        o[q_rows, cols] = dot(qkv[v_rows, :n], weights).astype(BF16)
        lse[pl.ds(h, 1), cols] = peak * scale + jnp.log(mass)


def backward_head(h, width, qkv, do_t, lse, cos, sin, dqkv, dk_ref, dv_ref):
    length = qkv.shape[1]
    scale = HEAD ** (-0.5)
    q_rows = block(h, HEAD)
    k_rows = pl.ds(pl.multiple_of(width + h * HEAD, HEAD), HEAD)
    v_rows = pl.ds(pl.multiple_of(2 * width + h * HEAD, HEAD), HEAD)
    q, k, v, do = flip(qkv[q_rows, :]), flip(qkv[k_rows, :]), flip(qkv[v_rows, :]), flip(do_t[q_rows, :])
    dk_ref[...] = jnp.zeros_like(dk_ref)
    dv_ref[...] = jnp.zeros_like(dv_ref)
    for j in range(length // TILE):
        n = TILE * (j + 1)
        cols = slice(j * TILE, (j + 1) * TILE)
        s = score_block(k[:n], qkv[q_rows, cols], j * TILE)
        w = jnp.exp(s * scale - lse[pl.ds(h, 1), cols])
        dv_ref[:n] += dot(w.astype(BF16), do[cols])
        dw = dot(v[:n], do_t[q_rows, cols])
        mean = jnp.sum(w * dw, axis=0, keepdims=True)
        ds = (w * (dw - mean) * scale).astype(BF16)
        dk_ref[:n] += dot(ds, q[cols])
        dq = dot(qkv[k_rows, :n], ds)
        dqkv[q_rows, cols] = unrotated(dq, cos[:, cols], sin[:, cols]).astype(BF16)
    dqkv[k_rows, :] = unrotated(jnp.transpose(dk_ref[...]), cos, sin).astype(BF16)
    dqkv[v_rows, :] = jnp.transpose(dv_ref[...]).astype(BF16)


def mid_forward_piece(x, gain, table):
    scale = lax.rsqrt(jnp.mean(x * x, axis=1, keepdims=True) + norm_eps)
    low = (x * scale * gain).astype(BF16)
    logits = dot(low, table)
    lanes = lax.broadcasted_iota(jnp.int32, logits.shape, 1)
    routed = (lanes >= ROUTER) & (lanes < SHARED)
    peak = jnp.max(jnp.where(routed, logits, -jnp.inf), axis=1, keepdims=True)
    e = jnp.where(routed, jnp.exp(jnp.where(routed, logits - peak, 0.0)), 0.0)
    probability = e / jnp.sum(e, axis=1, keepdims=True)
    gates = jnp.where(lanes == SHARED, sigmoid(jnp.where(lanes == SHARED, logits, 0.0)), probability)
    return low, gates, jnp.sum(probability, axis=0, keepdims=True)


def embed_backward_piece(x_row, da, dx1, vec):
    xb = column(x_row, TILE)
    xb = jnp.concatenate([xb] * (D // LANES), axis=1)
    u = xb * vec[3:4, :]
    up = xb * vec[4:5, :]
    s = sigmoid(u)
    silu = u * s
    x = silu * up
    scale = lax.rsqrt(jnp.mean(x * x, axis=1, keepdims=True) + norm_eps)
    unit = x * scale
    dn = da * vec[0:1, :]
    dx = dx1 + scale * (dn - unit * jnp.mean(dn * unit, axis=1, keepdims=True))
    du = dx * up * (s * (1.0 + u * (1.0 - s)))
    total = lambda v: jnp.sum(v, axis=0, keepdims=True)
    return total(da * unit), total(du * xb), total(dx * silu * xb)


def forward_kernel(
    small_own, big_own, tally, x_ref, cos_ref, sin_ref,
    big, wt, vec, table, a, qkv, lse, o, x1, b, pc, total, tallies,
    stage, small, x0, part, other,
    in_sem, own_sem, send_xy, send_up, send_dn, z_sem, p2_sem, p3_sem,
    small_send, small_z, small_y, small_x, tally_send, tally_recv, pair_send, pair_recv,
):
    dp, mp, x, y, z = place()
    xp, yp = dp + 1 - 2 * x, dp + 2 - 4 * y
    count = big_own.shape[0]
    series, _, length = x_ref.shape
    width = o.shape[1]
    per = length // TILE
    load = pltpu.make_async_copy(big_own, stage, in_sem)
    load.start()
    meet_everyone(dp, mp)

    def home(zs):
        return zs * 4 + 2 * y + x

    def small_put(src, slot, recv, peer):
        remote(src, small.at[slot], small_send, recv, peer, mp).start()

    for dist in (1, 2, 3):
        @pl.when(z >= dist)
        def _():
            small_put(small_own, dp, small_z.at[z], dp - 4 * dist)

        @pl.when(z + dist <= 3)
        def _():
            small_put(small_own, dp, small_z.at[z], dp + 4 * dist)
    small_put(small_own, dp, small_y.at[z], yp)
    small_put(small_own, dp, small_x, xp)
    small[dp] = small_own[...]
    me = dp * 2 + mp

    def tell(k, carry):
        peer = lax.rem(me + k, 32)
        remote(tally, tallies.at[me], tally_send, tally_recv, peer // 2, lax.rem(peer, 2)).start()
        return carry

    lax.fori_loop(1, 32, tell, 0)
    tallies[me] = tally[...]

    load.wait()

    def rows(c, slot):
        return big.at[c, block(slot, SHARD), :]

    def put(src, c, slot, send, recv, peer):
        remote(src, rows(c, slot), send, recv, peer, mp).start()

    def climb(c, zs, src):
        put(src, c, home(zs), send_up, z_sem.at[c, zs], dp + 4)

    def drop(c, zs, src):
        put(src, c, home(zs), send_dn, z_sem.at[c, zs], dp - 4)

    def ends(c):
        k = lax.rem(c, 2)
        return jnp.where(k == 0, yp, xp), jnp.where(k == 0, xp, yp)

    def spread(c, zs, src):
        first, second = ends(c)
        put(src, c, home(zs), send_xy, p2_sem.at[c, zs], first)
        put(src, c, home(zs), send_xy, p3_sem, second)

    def own_z(c, carry):
        @pl.when(z < 3)
        def _():
            climb(c, z, stage.at[c])

        @pl.when(z > 0)
        def _():
            drop(c, z, stage.at[c])
        pltpu.make_async_copy(stage.at[c], rows(c, dp), own_sem).start()
        return carry

    lax.fori_loop(0, count, own_z, 0)

    for dist in (1, 2, 3):
        for sign in (-1, 1):
            zs = z + sign * dist

            @pl.when((zs >= 0) & (zs <= 3))
            def _():
                done(small.at[home(zs)], small_z.at[zs])
                small_put(small.at[home(zs)], home(zs), small_y.at[zs], yp)
                small_put(small.at[home(zs)], home(zs), small_x, xp)
    for turn in range(4):
        zs = lax.rem(z + turn, 4)
        slot = zs * 4 + 2 * (1 - y) + x
        done(small.at[slot], small_y.at[zs])
        small_put(small.at[slot], slot, small_x, xp)
    done(small.at[pl.ds(0, 8)], small_x)

    def own_xy(c, carry):
        spread(c, z, stage.at[c])
        return carry

    lax.fori_loop(0, count, own_xy, 0)

    whole = small[...].astype(F32).reshape(D, -1)
    table[...] = whole[:, 4 * width:].astype(BF16)
    turned = jnp.transpose(whole)
    wt[...] = turned.astype(BF16)
    vec[...] = jnp.concatenate(
        [turned[4 * width + VECTOR:4 * width + VECTOR + 5], jnp.zeros((3, D), F32)], axis=0)
    total[...] = jnp.zeros_like(total)

    def relay(c, dist):
        def second(zs):
            k = lax.rem(c, 2)
            slot = zs * 4 + jnp.where(k == 0, 2 * (1 - y) + x, 2 * y + 1 - x)
            done(rows(c, slot), p2_sem.at[c, zs])
            put(rows(c, slot), c, slot, send_xy, p3_sem, ends(c)[1])

        @pl.when(z >= dist)
        def _():
            zs = z - dist
            done(rows(c, home(zs)), z_sem.at[c, zs])

            @pl.when(z < 3)
            def _():
                climb(c, zs, rows(c, home(zs)))
            spread(c, zs, rows(c, home(zs)))

        @pl.when(z + dist <= 3)
        def _():
            zs = z + dist
            done(rows(c, home(zs)), z_sem.at[c, zs])

            @pl.when(z > 0)
            def _():
                drop(c, zs, rows(c, home(zs)))
            spread(c, zs, rows(c, home(zs)))

        @pl.when(z - (dist - 1) >= 0)
        def _():
            second(z - (dist - 1))

        @pl.when((dist > 1) & (z + dist - 1 <= 3))
        def _():
            second(z + dist - 1)

    def pair(n):
        r = block(n, length)
        return remote(part.at[r], other.at[r], pair_send.at[n], pair_recv.at[n], dp, 1 - mp)

    heads = width // HEAD
    pieces = heads + 2

    def attention(i):
        n, j = i // pieces, lax.rem(i, pieces)
        r = block(n, length)

        @pl.when(j == 0)
        def _():
            def tile(m, carry):
                t = pl.ds(pl.multiple_of(n * length + m * TILE, TILE), TILE)
                embed_piece(x_ref[n, :, block(m, TILE, TILE)], vec, x0, a, t)
                return carry
            lax.fori_loop(0, per, tile, 0)

        @pl.when(j == 1)
        def _():
            project_piece(wt, a[r, :], cos_ref[...], sin_ref[...], qkv.at[n], width)

        @pl.when(j >= 2)
        def _():
            forward_head(j - 2, width, qkv.at[n], lse.at[n], o.at[n])

        @pl.when(j == pieces - 1)
        def _():
            part[r, :] = dot(o[n], wt[3 * width:4 * width, :], 0, 0)
            pair(n).start()

    def middle(m):
        r = block(m, TILE)

        @pl.when(lax.rem(m, per) == 0)
        def _():
            pair(m // per).wait()
        v = x0[r, :] + (part[r, :] + other[r, :])
        x1[r, :] = v
        low, gates, sums = mid_forward_piece(v, vec[1:2, :], table[...])
        b[r, :] = low
        pc[r, :] = gates
        total[...] += sums

    def step(i, carry):
        relay(lax.rem(i, count), i // count + 1)

        @pl.when(i < series * pieces)
        def _():
            attention(i)

        for n in range(series):
            begin = (n + 1) * pieces + 4

            @pl.when((i >= begin) & (i < begin + per))
            def _():
                middle(n * per + i - begin)
        return carry

    lax.fori_loop(0, 4 * count, step, 0)

    def whole_wait(n, sem):
        done(big.at[:, pl.ds(0, n * SHARD), :], sem)
    whole_wait(8, p3_sem)
    whole_wait(12, send_xy)
    whole_wait(1, own_sem)
    done(small.at[pl.ds(0, 15)], small_send)
    done(tallies.at[pl.ds(0, 31)], tally_recv)
    done(tallies.at[pl.ds(0, 31)], tally_send)
    for k in range(4):
        @pl.when(z == k)
        def _():
            if k < 3:
                whole_wait(k + 1, send_up)
            if k > 0:
                whole_wait(4 - k, send_dn)


def forward_near(small_own, big_own, tally, x, cos, sin, width, ident):
    series, _, length = x.shape
    tokens = series * length
    count, shard, columns = big_own.shape
    shape = jax.ShapeDtypeStruct
    return pl.pallas_call(
        forward_kernel,
        in_specs=[VMEM, ANY, VMEM, VMEM, VMEM, VMEM],
        out_specs=[ANY] + [VMEM] * 12,
        out_shape=[
            shape((count, D, columns), BF16),
            shape((small_own.shape[1], D), BF16), shape((8, D), F32), shape((D, LANES), BF16),
            shape((tokens, D), BF16), shape((series, 3 * width, length), BF16), shape((series, 8, length), F32),
            shape((series, width, length), BF16),
            shape((tokens, D), F32), shape((tokens, D), BF16), shape((tokens, LANES), F32), shape((1, LANES), F32),
            shape((32,) + tally.shape, F32),
        ],
        scratch_shapes=[
            pltpu.VMEM(big_own.shape, BF16), pltpu.VMEM((16,) + small_own.shape, BF16),
            pltpu.VMEM((tokens, D), F32), pltpu.VMEM((tokens, D), F32), pltpu.VMEM((tokens, D), F32),
            DMA, DMA, DMA, DMA, DMA, DMA((count, 4)), DMA((count, 4)), DMA,
            DMA, DMA((4,)), DMA((4,)), DMA, DMA, DMA, DMA((series,)), DMA((series,)),
        ],
        compiler_params=params(collective_id=ident, has_side_effects=True),
        name="forward_near",
    )(small_own, big_own, tally, x, cos, sin)


GROUP = 16


def spread_rows(dest, value, start, count):
    for c in range(value.shape[1] // LANES):
        dest[pl.ds(start * 8 + c, count, stride=8), :] = value[:, c * LANES:(c + 1) * LANES]


def pick_rows(source, tile, index_ref, base):
    def body(i, carry):
        values = []
        for k in range(GROUP):
            t = index_ref[base + i * GROUP + k]
            values.append(source[pl.ds(pl.multiple_of(t * 8, 8), 8), :])
        for k in range(GROUP):
            tile[pl.ds(pl.multiple_of((i * GROUP + k) * 8, 8), 8), :] = values[k]
        return carry

    lax.fori_loop(0, TILE // GROUP, body, 0)


def add_rows(dest, tile, index_ref, base):
    def body(i, carry):
        places, values = [], []
        for k in range(GROUP):
            t = index_ref[base + i * GROUP + k]
            place = pl.ds(pl.multiple_of(t * 8, 8), 8)
            places.append(place)
            values.append(dest[place, :] + tile[pl.ds(pl.multiple_of((i * GROUP + k) * 8, 8), 8), :])
        for k in range(GROUP):
            dest[places[k], :] = values[k]
        return carry

    lax.fori_loop(0, TILE // GROUP, body, 0)


def gathered_columns(tile, columns):
    return [tile[pl.ds(c, TILE, stride=8), :] for c in range(columns)]


def lane_of(block, lane):
    lanes = lax.broadcasted_iota(jnp.int32, block.shape, 1)
    return jnp.sum(jnp.where(lanes == lane, block, 0.0), axis=1, keepdims=True)


def lay_rows(values, pc_ref, rows8, acc8):
    tokens = values.shape[0]

    def lay(i, carry):
        r = pl.ds(pl.multiple_of(i * TILE, TILE), TILE)
        spread_rows(rows8, values[r, :].astype(F32), i * TILE, TILE)
        rows8[pl.ds(i * TILE * 8 + 3, TILE, stride=8), :] = pc_ref[r, :]
        acc8[pl.ds(pl.multiple_of(i * TILE * 8, 8), TILE * 8), :] = jnp.zeros((TILE * 8, LANES), F32)
        return carry

    lax.fori_loop(0, tokens // TILE, lay, 0)
    rows8[pl.ds(tokens * 8, 8), :] = jnp.zeros((8, LANES), F32)
    acc8[pl.ds(tokens * 8, 8), :] = jnp.zeros((8, LANES), F32)


def expert_forward_kernel(counts, source, b_ref, pc_ref, w_ref, x_ref, y_ref, mix_ref, rows8, acc8, tile8):
    e = pl.program_id(0)
    hidden = w_ref.shape[2] // 3
    capacity = y_ref.shape[1]
    tiles = capacity // TILE

    @pl.when(e == 0)
    def _():
        lay_rows(b_ref, pc_ref, rows8, acc8)

    def run(x):
        g = dot(x, w_ref[0, :, : 2 * hidden])
        gate, up = g[:, :hidden], g[:, hidden:]
        h = (gate * sigmoid(gate) * up).astype(BF16)
        return dot(h, w_ref[0, :, 2 * hidden:], 1, 1)

    @pl.when(e < ROUTED_EXPERTS)
    def _():
        used = (counts[e] + TILE - 1) // TILE

        def step(i, carry):
            base = e * capacity + i * TILE
            r = pl.ds(pl.multiple_of(i * TILE, TILE), TILE)
            pick_rows(rows8, tile8, source, base)
            c0, c1, c2, pc = gathered_columns(tile8, 4)
            x = jnp.concatenate([c0, c1, c2], axis=1).astype(BF16)
            x_ref[0, r, :] = x
            y = run(x)
            y_ref[0, r, :] = y
            spread_rows(tile8, y * lane_of(pc, ROUTER + e), 0, TILE)
            add_rows(acc8, tile8, source, base)
            return carry

        def blank(i, carry):
            x_ref[0, pl.ds(pl.multiple_of(i * TILE, TILE), TILE), :] = jnp.zeros((TILE, D), BF16)
            return carry

        lax.fori_loop(0, used, step, 0)
        lax.fori_loop(used, tiles, blank, 0)

    @pl.when(e >= ROUTED_EXPERTS)
    def _():
        def step(i, carry):
            t = (e - ROUTED_EXPERTS) * tiles + i
            here = pl.ds(pl.multiple_of(i * TILE, TILE), TILE)
            r = pl.ds(pl.multiple_of(t * TILE, TILE), TILE)
            x = b_ref[r, :]
            x_ref[0, here, :] = x
            y = run(x)
            y_ref[0, here, :] = y
            shared = y * lane_of(pc_ref[r, :], SHARED)
            for c in range(D // LANES):
                cols = slice(c * LANES, (c + 1) * LANES)
                mix_ref[r, cols] = acc8[pl.ds(t * TILE * 8 + c, TILE, stride=8), :] + shared[:, cols]
            return carry

        lax.fori_loop(0, tiles, step, 0)


def expert_blocks(capacity, w):
    return pl.BlockSpec((1, capacity, w), lambda e, *_: (e, 0, 0))


def expert_weights(weights):
    return pl.BlockSpec((1,) + weights.shape[1:], lambda e, *_: (jnp.minimum(e, ROUTED_EXPERTS), 0, 0))


def expert_scratch(tokens):
    return [
        pltpu.VMEM(((tokens + 1) * 8, LANES), F32),
        pltpu.VMEM(((tokens + 1) * 8, LANES), F32),
        pltpu.VMEM((TILE * 8, LANES), F32),
    ]


def expert_forward(counts, source, b, pc, weights):
    tokens = b.shape[0]
    capacity = tokens // 2
    blocks = ROUTED_EXPERTS + 2
    full = lambda shape: pl.BlockSpec(shape, lambda e, *_: (0,) * len(shape), pipeline_mode=pl.Buffered(1))
    return pl.pallas_call(
        expert_forward_kernel,
        grid_spec=pltpu.PrefetchScalarGridSpec(
            num_scalar_prefetch=2,
            grid=(blocks,),
            in_specs=[full(b.shape), full(pc.shape), expert_weights(weights)],
            out_specs=[expert_blocks(capacity, D), expert_blocks(capacity, D), full((tokens, D))],
            scratch_shapes=expert_scratch(tokens),
        ),
        out_shape=[
            jax.ShapeDtypeStruct((blocks, capacity, D), BF16),
            jax.ShapeDtypeStruct((blocks, capacity, D), F32),
            jax.ShapeDtypeStruct((tokens, D), F32),
        ],
        compiler_params=params(),
        name="expert_forward",
    )(counts, source, b, pc, weights)


def expert_backward_kernel(
    counts, source, pc_ref, dx_ref, w_ref, x_ref, y_ref, dy_ref, dg_ref, h_ref, acc_ref, rows8, acc8, tile8
):
    e = pl.program_id(0)
    hidden = w_ref.shape[2] // 3
    capacity = y_ref.shape[1]
    tiles = capacity // TILE

    @pl.when(e == 0)
    def _():
        lay_rows(dx_ref, pc_ref, rows8, acc8)

    def run(r, dy):
        x = x_ref[0, r, :]
        dy_ref[0, r, :] = dy
        u = w_ref[0, :, : 2 * hidden]
        g = dot(x, u)
        gate, up = g[:, :hidden], g[:, hidden:]
        s = sigmoid(gate)
        silu = gate * s
        h_ref[0, r, :] = (silu * up).astype(BF16)
        dh = dot(dy, w_ref[0, :, 2 * hidden:])
        d_up = (dh * silu).astype(BF16)
        d_gate = (dh * up * (s * (1.0 + gate * (1.0 - s)))).astype(BF16)
        dg_ref[0, r, :hidden] = d_gate
        dg_ref[0, r, hidden:] = d_up
        return dot(d_gate, u[:, :hidden], 1, 1) + dot(d_up, u[:, hidden:], 1, 1)

    lanes = lax.broadcasted_iota(jnp.int32, (TILE, LANES), 1)

    @pl.when(e < ROUTED_EXPERTS)
    def _():
        used = (counts[e] + TILE - 1) // TILE

        def step(i, carry):
            base = e * capacity + i * TILE
            r = pl.ds(pl.multiple_of(i * TILE, TILE), TILE)
            pick_rows(rows8, tile8, source, base)
            c0, c1, c2, pc = gathered_columns(tile8, 4)
            dx = jnp.concatenate([c0, c1, c2], axis=1)
            d_gate = jnp.sum(y_ref[0, r, :] * dx, axis=1, keepdims=True)
            back = run(r, (dx * lane_of(pc, ROUTER + e)).astype(BF16))
            spread_rows(tile8, back, 0, TILE)
            tile8[pl.ds(3, TILE, stride=8), :] = jnp.where(lanes == ROUTER + e, d_gate, 0.0)
            add_rows(acc8, tile8, source, base)
            return carry

        def blank(i, carry):
            r = pl.ds(pl.multiple_of(i * TILE, TILE), TILE)
            dy_ref[0, r, :] = jnp.zeros((TILE, D), BF16)
            dg_ref[0, r, :] = jnp.zeros((TILE, 2 * hidden), BF16)
            h_ref[0, r, :] = jnp.zeros((TILE, hidden), BF16)
            return carry

        lax.fori_loop(0, used, step, 0)
        lax.fori_loop(used, tiles, blank, 0)

    @pl.when(e >= ROUTED_EXPERTS)
    def _():
        def step(i, carry):
            t = (e - ROUTED_EXPERTS) * tiles + i
            here = pl.ds(pl.multiple_of(i * TILE, TILE), TILE)
            r = pl.ds(pl.multiple_of(t * TILE, TILE), TILE)
            dx = dx_ref[r, :]
            d_gate = jnp.sum(y_ref[0, here, :] * dx, axis=1, keepdims=True)
            back = run(here, (dx * lane_of(pc_ref[r, :], SHARED)).astype(BF16))
            for c in range(D // LANES):
                cols = slice(c * LANES, (c + 1) * LANES)
                acc_ref[r, cols] = acc8[pl.ds(t * TILE * 8 + c, TILE, stride=8), :] + back[:, cols]
            acc_ref[r, D:] = jnp.where(
                lanes == SHARED, d_gate, acc8[pl.ds(t * TILE * 8 + 3, TILE, stride=8), :])
            return carry

        lax.fori_loop(0, tiles, step, 0)


def expert_backward(counts, source, pc, dx, weights, x, y):
    tokens = dx.shape[0]
    capacity = tokens // 2
    blocks = ROUTED_EXPERTS + 2
    hidden = weights.shape[2] // 3
    full = lambda shape: pl.BlockSpec(shape, lambda e, *_: (0,) * len(shape), pipeline_mode=pl.Buffered(1))
    return pl.pallas_call(
        expert_backward_kernel,
        grid_spec=pltpu.PrefetchScalarGridSpec(
            num_scalar_prefetch=2,
            grid=(blocks,),
            in_specs=[
                full(pc.shape), full(dx.shape), expert_weights(weights),
                expert_blocks(capacity, D), expert_blocks(capacity, D)],
            out_specs=[
                expert_blocks(capacity, D), expert_blocks(capacity, 2 * hidden), expert_blocks(capacity, hidden),
                full((tokens, D + LANES))],
            scratch_shapes=expert_scratch(tokens),
        ),
        out_shape=[
            jax.ShapeDtypeStruct((blocks, capacity, D), BF16),
            jax.ShapeDtypeStruct((blocks, capacity, 2 * hidden), BF16),
            jax.ShapeDtypeStruct((blocks, capacity, hidden), BF16),
            jax.ShapeDtypeStruct((tokens, D + LANES), F32),
        ],
        compiler_params=params(),
        name="expert_backward",
    )(counts, source, pc, dx, weights, x, y)


def exchange(part, other, send_sem, recv_sem):
    dp, mp = lax.axis_index("dp"), lax.axis_index("mp")
    barrier = pltpu.get_barrier_semaphore()
    pl.semaphore_signal(barrier, inc=1, device_id=(dp, 1 - mp), device_id_type=MESH)
    pl.semaphore_wait(barrier, 1)

    def copy(i):
        r = block(i, TILE)
        return remote(part.at[r], other.at[r], send_sem.at[i], recv_sem.at[i], dp, 1 - mp)

    def begin(i, carry):
        copy(i).start()
        return carry

    lax.fori_loop(0, part.shape[0] // TILE, begin, 0)
    return lambda i: copy(i).wait()


def exchange_scratch(part):
    tiles = part.shape[0] // TILE
    return [pltpu.VMEM(part.shape, F32), DMA((tiles,)), DMA((tiles,))]


def hankel(base):
    block_rows = jnp.broadcast_to(base, (LANES, 2 * LANES))
    m = pltpu.roll(block_rows, 0, 1, stride=1, stride_axis=0)[:, :LANES]
    lanes = lax.broadcasted_iota(jnp.int32, (LANES, LANES), 1)
    out = pltpu.roll(m, 41, 1)
    out = jnp.where(lanes < 104, pltpu.roll(m, 40, 1), out)
    out = jnp.where(lanes < 96, pltpu.roll(m, 32, 1), out)
    return jnp.where(lanes < 64, m, out)


def loss_piece(x, gain, table, table_t, value_rows, mark_rows, weight):
    scale = lax.rsqrt(jnp.mean(x * x, axis=1, keepdims=True) + norm_eps)
    unit = x * scale
    low = (unit * gain).astype(BF16)
    z = dot(low, table)
    target = jnp.concatenate([hankel(row) for row in value_rows], axis=0)
    valid = jnp.concatenate([hankel(row) for row in mark_rows], axis=0)
    factor = valid * weight
    miss = z - target
    size = jnp.abs(miss)
    huber = jnp.where(
        size <= quadratic_cutoff, 0.5 * miss * miss, quadratic_cutoff * (size - 0.5 * quadratic_cutoff))
    dz = (jnp.clip(miss, -quadratic_cutoff, quadratic_cutoff) * factor).astype(BF16)
    df = dot(dz, table_t)
    dn = df * gain
    dx = scale * (dn - unit * jnp.mean(dn * unit, axis=1, keepdims=True))
    total = lambda v: jnp.sum(v, axis=0, keepdims=True)
    return dx, dot(dz, low, 0, 0), total(df * unit), total(huber * factor)


def loss_kernel(part, x1, vec, table, table_t, values, marks, weight, dx2, d_table, d_gain, loss,
                other, send_sem, recv_sem):
    wait = exchange(part, other, send_sem, recv_sem)
    d_table[...] = jnp.zeros_like(d_table)
    d_gain[...] = jnp.zeros_like(d_gain)
    loss[...] = jnp.zeros_like(loss)
    per = TILE // LANES

    def step(i, carry):
        r = block(i, TILE)
        wait(i)
        dx, dt, dg, fit = loss_piece(
            x1[r, :] + (part[r, :] + other[r, :]), vec[2:3, :], table[...], table_t[...],
            [values[pl.ds(per * i + k, 1), :] for k in range(per)],
            [marks[pl.ds(per * i + k, 1), :] for k in range(per)], weight[...])
        dx2[r, :] = dx
        d_table[...] += dt
        d_gain[...] += dg
        loss[...] += fit
        return carry

    lax.fori_loop(0, part.shape[0] // TILE, step, 0)


def loss_stage(part, x1, vec, table, table_t, values, marks, weight, ident):
    tokens = part.shape[0]
    return pl.pallas_call(
        loss_kernel,
        in_specs=[VMEM] * 8,
        out_specs=[VMEM] * 4,
        out_shape=[
            jax.ShapeDtypeStruct((tokens, D), F32), jax.ShapeDtypeStruct((LANES, D), F32),
            jax.ShapeDtypeStruct((1, D), F32), jax.ShapeDtypeStruct((1, LANES), F32),
        ],
        scratch_shapes=exchange_scratch(part),
        compiler_params=params(collective_id=ident, has_side_effects=True),
        name="loss_stage",
    )(part, x1, vec, table, table_t, values, marks, weight)


def mid_backward_kernel(part, dx2, x1, b, pc, vec, table_t, balance, wo, o, d_table, d_gain3, dx1, do, rest,
                        other, send_sem, recv_sem):
    wait = exchange(part, other, send_sem, recv_sem)
    width = wo.shape[0]
    rest[:width, :] = jnp.zeros((width, D), F32)
    rest[width:, :] = d_table[...]
    rest[width + VECTOR + 2:width + VECTOR + 3, :] = d_gain3[...]
    per = o.shape[2] // TILE

    def step(i, carry):
        r = block(i, TILE)
        wait(i)
        dp = part[r, D:] + other[r, D:] + balance[...]
        p = pc[r, :]
        lanes = lax.broadcasted_iota(jnp.int32, p.shape, 1)
        routed = (lanes >= ROUTER) & (lanes < SHARED)
        weighted = jnp.sum(jnp.where(routed, p * dp, 0.0), axis=1, keepdims=True)
        dl = jnp.where(routed, p * (dp - weighted), jnp.where(lanes == SHARED, dp * p * (1.0 - p), 0.0))
        dl = dl.astype(BF16)
        low = b[r, :]
        rest[width:, :] += dot(dl, low, 0, 0)
        db = part[r, :D] + other[r, :D] + dot(dl, table_t[...])
        x = x1[r, :]
        scale = lax.rsqrt(jnp.mean(x * x, axis=1, keepdims=True) + norm_eps)
        unit = x * scale
        g2 = width + VECTOR + 1
        rest[g2:g2 + 1, :] += jnp.sum(db * unit, axis=0, keepdims=True)
        dn = db * vec[1:2, :]
        dx = dx2[r, :] + scale * (dn - unit * jnp.mean(dn * unit, axis=1, keepdims=True))
        dx1[r, :] = dx
        d_low = dx.astype(BF16)
        n, cols = i // per, block(lax.rem(i, per), TILE, TILE)
        do[n, :, cols] = dot(wo[...], d_low, 1, 1).astype(BF16)
        rest[:width, :] += dot(o[n, :, cols], d_low)
        return carry

    lax.fori_loop(0, part.shape[0] // TILE, step, 0)


def mid_backward(part, dx2, x1, b, pc, vec, table_t, balance, wo, o, d_table, d_gain3, ident):
    tokens = part.shape[0]
    return pl.pallas_call(
        mid_backward_kernel,
        in_specs=[VMEM] * 12,
        out_specs=[VMEM] * 3,
        out_shape=[
            jax.ShapeDtypeStruct((tokens, D), F32), jax.ShapeDtypeStruct(o.shape, BF16),
            jax.ShapeDtypeStruct((wo.shape[0] + LANES, D), F32),
        ],
        scratch_shapes=exchange_scratch(part),
        compiler_params=params(collective_id=ident, has_side_effects=True),
        name="mid_backward",
    )(part, dx2, x1, b, pc, vec, table_t, balance, wo, o, d_table, d_gain3)


SLOTS = 3
HOPS = 2
ACCS = 5


def encode(dest, v):
    width = v.shape[1]
    top = jnp.max(jnp.abs(v), axis=1, keepdims=True)
    power = jnp.ceil(jnp.log2(jnp.maximum(top, 1e-30) * (1.001 / 32767.0)))
    power = jnp.broadcast_to(power, (v.shape[0], LANES))
    inverse = jnp.exp2(-power)
    dest[:, width:] = power.astype(jnp.int32).astype(I16)
    for c in range(width // LANES):
        cols = slice(c * LANES, (c + 1) * LANES)
        dest[:, cols] = jnp.round(v[:, cols] * inverse).astype(jnp.int32).astype(I16)


def decode(source):
    width = source.shape[1] - LANES
    unit = jnp.exp2(source[:, width:].astype(jnp.int32).astype(F32))
    return jnp.concatenate(
        [source[:, c * LANES:(c + 1) * LANES].astype(jnp.int32).astype(F32) * unit for c in range(width // LANES)],
        axis=1)


def backward_kernel(
    xs, dys, dgs, hs, qkvs, dos, lses, a_all, dx1_all, rest, x_ref, wt, vec, cos_ref, sin_ref,
    out, out_small,
    x_in, dy_in, dg_in, h_in, xt, dyt, temp, dw, acc, send1, recv1, send2, recv2, zs_up, zs_dn, up, dn,
    qkv, do_t, lse, a, dx1, dqkv, dk, dv, stack, part, other,
    sm, small_a1, small_b1, small_a2, small_b2, small_up, small_dn,
    load_sem, sem_s1, sem_r1, sem_s2, sem_r2, sem_su, sem_sd, sem_ru, sem_rd,
    attn_sem, dx1_sem, rest_sem, pair_send, pair_recv,
    small_send, small_sa, small_sb, small_r, small_su, small_sd, small_ru, small_rd,
):
    dp, mp, x, y, z = place()
    xp, yp = dp + 1 - 2 * x, dp + 2 - 4 * y
    count = out.shape[0]
    blocks = xs.shape[0]
    hidden = hs.shape[2]
    series, _, length = x_ref.shape
    width = do_t.shape[0]
    heads = width // HEAD
    per = length // TILE

    def loads(n):
        return [
            pltpu.make_async_copy(src.at[n], dst, load_sem.at[i])
            for i, (src, dst) in enumerate(((xs, x_in), (dys, dy_in), (dgs, dg_in), (hs, h_in)))]

    def attn_loads(n):
        pairs = ((qkvs.at[n], qkv), (dos.at[n], do_t), (lses.at[n], lse), (a_all.at[block(n, length)], a))
        return [pltpu.make_async_copy(src, dst, attn_sem.at[i]) for i, (src, dst) in enumerate(pairs)]

    def dx1_load(n):
        return pltpu.make_async_copy(dx1_all.at[block(n, length)], dx1, dx1_sem)

    rest_load = pltpu.make_async_copy(rest, stack.at[pl.ds(3 * width, width + LANES)], rest_sem)
    for copy in loads(0) + attn_loads(0) + [dx1_load(0), rest_load]:
        copy.start()

    barrier = pltpu.get_barrier_semaphore()
    for peer, core in ((xp, mp), (yp, mp), (dp, 1 - mp)):
        pl.semaphore_signal(barrier, inc=1, device_id=(peer, core), device_id_type=MESH)

    @pl.when(z > 0)
    def _():
        pl.semaphore_signal(barrier, inc=1, device_id=(dp - 4, mp), device_id_type=MESH)

    @pl.when(z < 3)
    def _():
        pl.semaphore_signal(barrier, inc=1, device_id=(dp + 4, mp), device_id_type=MESH)

    @pl.when((z > 0) & (z < 3))
    def _():
        pl.semaphore_wait(barrier, 5)

    @pl.when((z == 0) | (z == 3))
    def _():
        pl.semaphore_wait(barrier, 4)

    stack[0:3 * width, :] = jnp.zeros((3 * width, D), F32)

    def shard(slot, i):
        return dw.at[slot, i]


    def weights(n, more):
        for copy in loads(n):
            copy.wait()
        xt[...] = jnp.transpose(x_in[...])
        dyt[...] = jnp.transpose(dy_in[...])

        def wide(j, carry):
            cols = block(j, TILE, TILE)
            v = dot(xt[...], dg_in[:, cols])
            temp[:, cols] = temp[:, cols] + v if more else v
            return carry

        def tall(j, carry):
            there = pl.ds(pl.multiple_of(2 * hidden + j * TILE, TILE), TILE)
            v = dot(dyt[...], h_in[:, block(j, TILE, TILE)])
            temp[:, there] = temp[:, there] + v if more else v
            return carry

        lax.fori_loop(0, 2 * hidden // TILE, wide, 0)
        lax.fori_loop(0, hidden // TILE, tall, 0)

        @pl.when(n + 1 < blocks)
        def _():
            for copy in loads(n + 1):
                copy.start()

    def begin(c):
        k, slot = lax.rem(c, 2), lax.rem(c, SLOTS)
        weights(c, False)

        @pl.when(c == count - 1)
        def _():
            weights(c + 1, True)

        @pl.when(c >= SLOTS)
        def _():
            done(send1.at[slot], sem_s1.at[slot])

        def pack(i, carry):
            m, n = i // 2, lax.rem(i, 2)
            gone = m * 4 + jnp.where(k == 0, n * 2 + 1 - x, (1 - y) * 2 + n)
            kept = m * 4 + jnp.where(k == 0, n * 2 + x, y * 2 + n)
            encode(send1.at[slot, i], temp[block(gone, SHARD), :])
            dw[slot, i] = temp[block(kept, SHARD), :]
            return carry

        lax.fori_loop(0, 8, pack, 0)
        remote(send1.at[slot], recv1.at[c], sem_s1.at[slot], sem_r1.at[c], jnp.where(k == 0, xp, yp), mp).start()

    def fold(c):
        k, slot, hop = lax.rem(c, 2), lax.rem(c, SLOTS), lax.rem(c, HOPS)
        o = jnp.where(k == 0, y, x)
        done(recv1.at[c], sem_r1.at[c])

        @pl.when(c >= HOPS)
        def _():
            done(send2.at[hop], sem_s2.at[hop])

        def add(m, carry):
            gone, kept = m * 2 + 1 - o, m * 2 + o
            encode(send2.at[hop, m], dw[slot, gone] + decode(recv1.at[c, gone]))
            acc[lax.rem(c, ACCS), m] = dw[slot, kept] + decode(recv1.at[c, kept])
            return carry

        lax.fori_loop(0, 4, add, 0)
        remote(send2.at[hop], recv2.at[c], sem_s2.at[hop], sem_r2.at[c], jnp.where(k == 0, yp, xp), mp).start()

    def climb(c, t, relay):
        slot = lax.rem(c, HOPS)
        v = acc[lax.rem(c, ACCS), t]
        if relay:
            done(up.at[c, t - 1], sem_ru.at[c, t - 1])
            v = v + decode(up.at[c, t - 1])

        @pl.when(c >= HOPS)
        def _():
            done(zs_up.at[slot, t - 1], sem_su.at[slot, t - 1])
        encode(zs_up.at[slot, t - 1], v)
        remote(zs_up.at[slot, t - 1], up.at[c, t - 1], sem_su.at[slot, t - 1], sem_ru.at[c, t - 1], dp + 4, mp).start()

    def drop(c, t, relay):
        slot = lax.rem(c, HOPS)
        v = acc[lax.rem(c, ACCS), t]
        if relay:
            done(dn.at[c, t], sem_rd.at[c, t])
            v = v + decode(dn.at[c, t])

        @pl.when(c >= HOPS)
        def _():
            done(zs_dn.at[slot, t], sem_sd.at[slot, t])
        encode(zs_dn.at[slot, t], v)
        remote(zs_dn.at[slot, t], dn.at[c, t], sem_sd.at[slot, t], sem_rd.at[c, t], dp - 4, mp).start()

    def line_a(c):
        done(recv2.at[c], sem_r2.at[c])
        there = lax.rem(c, ACCS)

        def add(m, carry):
            acc[there, m] = acc[there, m] + decode(recv2.at[c, m])
            return carry

        lax.fori_loop(0, 4, add, 0)
        out[c] = acc[there, z]

        @pl.when(z == 0)
        def _():
            for t in (3, 2, 1):
                climb(c, t, False)

        @pl.when(z == 3)
        def _():
            for t in (0, 1, 2):
                drop(c, t, False)

    def line_b(c):
        @pl.when(z == 1)
        def _():
            for t in (3, 2):
                climb(c, t, True)

        @pl.when(z == 2)
        def _():
            for t in (0, 1):
                drop(c, t, True)

    def line_c(c):
        @pl.when(z == 2)
        def _():
            climb(c, 3, True)

        @pl.when(z == 1)
        def _():
            drop(c, 0, True)

    def finish(c):
        @pl.when(z > 0)
        def _():
            done(up.at[c, z - 1], sem_ru.at[c, z - 1])
            out[c] = out[c] + decode(up.at[c, z - 1])

        @pl.when(z < 3)
        def _():
            done(dn.at[c, z], sem_rd.at[c, z])
            out[c] = out[c] + decode(dn.at[c, z])


    def pair(n):
        r = block(n, length)
        return remote(part, other.at[r], pair_send.at[n], pair_recv.at[n], dp, 1 - mp)

    def head(p):
        n, h = p // heads, lax.rem(p, heads)

        @pl.when(h == 0)
        def _():
            for copy in attn_loads(n):
                copy.wait()
        backward_head(h, width, qkv, do_t, lse, cos_ref[...], sin_ref[...], dqkv, dk, dv)

        @pl.when(h == heads - 1)
        def _():
            stack[0:3 * width, :] = stack[0:3 * width, :] + dot(dqkv[...], a[...])
            part[...] = dot(dqkv[...], wt[0:3 * width, :], 0, 0)
            pair(n).start()

            @pl.when(n + 1 < series)
            def _():
                for copy in attn_loads(n + 1):
                    copy.start()

    def embed(m):
        n, i = m // per, lax.rem(m, per)
        t = block(i, TILE, TILE)

        @pl.when(m == 0)
        def _():
            rest_load.wait()

        @pl.when(i == 0)
        def _():
            pair(n).wait()
            dx1_load(n).wait()
        da = part[t, :] + other[block(m, TILE), :]
        sums = embed_backward_piece(x_ref[n, :, t], da, dx1[t, :], vec)
        for row, value in zip((0, 3, 4), sums):
            there = slice(4 * width + VECTOR + row, 4 * width + VECTOR + row + 1)
            stack[there, :] = stack[there, :] + value

        @pl.when((i == per - 1) & (n + 1 < series))
        def _():
            dx1_load(n + 1).start()


    half = 512
    total_width = sm.shape[-1]
    ca, cb = pl.ds(0, half), pl.ds(half, total_width - half)

    def small_begin():
        sm[...] = jnp.transpose(stack[...]).reshape(sm.shape)
        remote(sm.at[:, :, 1 - x, :, ca], small_a1, small_sa, small_r.at[0], xp, mp).start()
        remote(sm.at[:, 1 - y, :, :, cb], small_b1, small_sb, small_r.at[1], yp, mp).start()

    def small_fold():
        done(small_a1, small_r.at[0])
        done(small_b1, small_r.at[1])
        for m in range(4):
            for n in range(2):
                sm[m, n, x, :, ca] = sm[m, n, x, :, ca] + small_a1[m, n]
                sm[m, y, n, :, cb] = sm[m, y, n, :, cb] + small_b1[m, n]
        remote(sm.at[:, 1 - y, x, :, ca], small_a2, small_send.at[0], small_r.at[2], yp, mp).start()
        remote(sm.at[:, y, 1 - x, :, cb], small_b2, small_send.at[1], small_r.at[3], xp, mp).start()

    def small_climb(t, relay):
        if relay:
            done(small_up.at[t - 1], small_ru.at[t - 1])
            sm[t, y, x] = sm[t, y, x] + small_up[t - 1]
        remote(sm.at[t, y, x], small_up.at[t - 1], small_su.at[t - 1], small_ru.at[t - 1], dp + 4, mp).start()

    def small_drop(t, relay):
        if relay:
            done(small_dn.at[t], small_rd.at[t])
            sm[t, y, x] = sm[t, y, x] + small_dn[t]
        remote(sm.at[t, y, x], small_dn.at[t], small_sd.at[t], small_rd.at[t], dp - 4, mp).start()

    def small_a():
        done(small_a2, small_r.at[2])
        done(small_b2, small_r.at[3])
        for m in range(4):
            sm[m, y, x, :, ca] = sm[m, y, x, :, ca] + small_a2[m]
            sm[m, y, x, :, cb] = sm[m, y, x, :, cb] + small_b2[m]
        out_small[...] = sm[z, y, x]

        @pl.when(z == 0)
        def _():
            for t in (3, 2, 1):
                small_climb(t, False)

        @pl.when(z == 3)
        def _():
            for t in (0, 1, 2):
                small_drop(t, False)

    def small_b():
        @pl.when(z == 1)
        def _():
            for t in (3, 2):
                small_climb(t, True)

        @pl.when(z == 2)
        def _():
            for t in (0, 1):
                small_drop(t, True)

    def small_c():
        @pl.when(z == 2)
        def _():
            small_climb(3, True)

        @pl.when(z == 1)
        def _():
            small_drop(0, True)

    def small_finish():
        @pl.when(z > 0)
        def _():
            done(small_up.at[z - 1], small_ru.at[z - 1])
            out_small[...] = out_small[...] + small_up[z - 1]

        @pl.when(z < 3)
        def _():
            done(small_dn.at[z], small_rd.at[z])
            out_small[...] = out_small[...] + small_dn[z]


    def at(i, first, number, run):
        @pl.when((i >= first) & (i < first + number))
        def _():
            run(i - first)

    small_first = count

    def step(i, carry):
        at(i, 0, count, begin)

        @pl.when(i < series * heads // 2)
        def _():
            def two(q, carry):
                head(2 * i + q)
                return carry
            lax.fori_loop(0, 2, two, 0)

        for n in range(series):
            @pl.when((i >= 3 + n * 3) & (i < 3 + n * 3 + per // 2))
            def _():
                def two(q, carry):
                    embed(n * per + 2 * (i - 3 - n * 3) + q)
                    return carry
                lax.fori_loop(0, 2, two, 0)
        at(i, small_first, 1, lambda _: small_begin())
        at(i, 2, count, fold)
        at(i, small_first + 1, 1, lambda _: small_fold())
        at(i, 4, count, line_a)
        at(i, small_first + 2, 1, lambda _: small_a())
        at(i, 5, count, line_b)
        at(i, small_first + 3, 1, lambda _: small_b())
        at(i, 6, count, line_c)
        at(i, small_first + 4, 1, lambda _: small_c())
        at(i, 7, count, finish)
        at(i, small_first + 5, 1, lambda _: small_finish())
        return carry

    lax.fori_loop(0, count + 7, step, 0)

    for slot in range(SLOTS):
        done(send1.at[slot], sem_s1.at[slot])
    for slot in range(HOPS):
        done(send2.at[slot], sem_s2.at[slot])
        for t in (1, 2, 3):
            @pl.when(z < t)
            def _():
                done(zs_up.at[slot, t - 1], sem_su.at[slot, t - 1])
        for t in (0, 1, 2):
            @pl.when(z > t)
            def _():
                done(zs_dn.at[slot, t], sem_sd.at[slot, t])
    done(small_a1, small_sa)
    done(small_b1, small_sb)
    done(small_a2, small_send.at[0])
    done(small_b2, small_send.at[1])
    for t in (1, 2, 3):
        @pl.when(z < t)
        def _():
            done(small_up.at[t - 1], small_su.at[t - 1])
    for t in (0, 1, 2):
        @pl.when(z > t)
        def _():
            done(small_dn.at[t], small_sd.at[t])


def backward_near(xs, dys, dgs, hs, qkv, do, lse, a, dx1, rest, x, wt, vec, cos, sin, ident):
    capacity, hidden = hs.shape[1], hs.shape[2]
    series, rows, length = qkv.shape
    heads_width = rows // 3
    count = ROUTED_EXPERTS + 1
    width = 3 * hidden
    coded = width + LANES
    small = 4 * heads_width + LANES
    tokens = series * length
    v = pltpu.VMEM
    return pl.pallas_call(
        backward_kernel,
        in_specs=[ANY] * 10 + [VMEM] * 5,
        out_specs=[VMEM] * 2,
        out_shape=[
            jax.ShapeDtypeStruct((count, SHARD, width), F32), jax.ShapeDtypeStruct((SHARD, small), F32)],
        scratch_shapes=[
            v((capacity, D), BF16), v((capacity, D), BF16), v((capacity, 2 * hidden), BF16), v((capacity, hidden), BF16),
            v((D, capacity), BF16), v((D, capacity), BF16),
            v((D, width), F32), v((SLOTS, 8, SHARD, width), F32), v((ACCS, 4, SHARD, width), F32),
            v((SLOTS, 8, SHARD, coded), I16), v((count, 8, SHARD, coded), I16),
            v((HOPS, 4, SHARD, coded), I16), v((count, 4, SHARD, coded), I16),
            v((HOPS, 3, SHARD, coded), I16), v((HOPS, 3, SHARD, coded), I16),
            v((count, 3, SHARD, coded), I16), v((count, 3, SHARD, coded), I16),
            v((rows, length), BF16), v((heads_width, length), BF16), v((8, length), F32), v((length, D), BF16),
            v((length, D), F32), v((rows, length), BF16), v((length, HEAD), F32), v((length, HEAD), F32),
            v((small, D), F32), v((length, D), F32), v((tokens, D), F32),
            v((4, 2, 2, SHARD, small), F32),
            v((4, 2, SHARD, 512), F32), v((4, 2, SHARD, small - 512), F32),
            v((4, SHARD, 512), F32), v((4, SHARD, small - 512), F32),
            v((3, SHARD, small), F32), v((3, SHARD, small), F32),
            DMA((4,)), DMA((SLOTS,)), DMA((count,)), DMA((HOPS,)), DMA((count,)),
            DMA((HOPS, 3)), DMA((HOPS, 3)), DMA((count, 3)), DMA((count, 3)),
            DMA((4,)), DMA, DMA, DMA((series,)), DMA((series,)),
            DMA((2,)), DMA, DMA, DMA((4,)), DMA((3,)), DMA((3,)), DMA((3,)), DMA((3,)),
        ],
        compiler_params=pltpu.CompilerParams(
            vmem_limit_bytes=67_000_000, collective_id=ident, has_side_effects=True),
        name="backward_near",
    )(xs, dys, dgs, hs, qkv, do, lse, a, dx1, rest, x, wt, vec, cos, sin)


def all_kernel(value, out, send_sem, recv_sem):
    dp, mp = lax.axis_index("dp"), lax.axis_index("mp")
    me = dp * 2 + mp
    meet_everyone(dp, mp)

    def tell(k, carry):
        peer = lax.rem(me + k, 32)
        remote(value, out.at[me], send_sem, recv_sem, peer // 2, lax.rem(peer, 2)).start()
        return carry

    lax.fori_loop(1, 32, tell, 0)
    out[me] = value[...]
    view = out.at[pl.ds(0, 31)]
    done(view, recv_sem)
    done(view, send_sem)


def all_blocks(value, ident):
    return pl.pallas_call(
        all_kernel,
        in_specs=[VMEM],
        out_specs=VMEM,
        out_shape=jax.ShapeDtypeStruct((32,) + value.shape, value.dtype),
        scratch_shapes=[DMA, DMA],
        compiler_params=pltpu.CompilerParams(collective_id=ident, has_side_effects=True),
        name="all_blocks",
    )(value)


def rope_rows(length):
    halfway = HEAD // 2
    frequency = rope_base ** (-2.0 * jnp.arange(halfway, dtype=F32) / HEAD)
    angles = frequency[:, None] * jnp.arange(length, dtype=F32)[None, :]
    return jnp.cos(angles), jnp.sin(angles)


def hankel_rows(track):
    length = track.shape[1]
    padded = jnp.pad(track, ((0, 0), (63, 2 * LANES)))
    first = padded[:, :length].reshape(-1, LANES)[:, ::-1]
    second = padded[:, LANES:LANES + length].reshape(-1, LANES)[:, ::-1]
    return jnp.concatenate([first, second], axis=1)


def table_columns(read, vec):
    parts, end = [], read.shape[1]
    for horizon in horizons[::-1]:
        parts.append(read[:, end - horizon:end][:, ::-1])
        end -= horizon
    gap = jnp.zeros((read.shape[0], ROUTER - sum(horizons)), read.dtype)
    tail = jnp.zeros((read.shape[0], LANES - VECTOR - vec.shape[1]), read.dtype)
    return jnp.concatenate(parts + [gap, read[:, :ROUTED_EXPERTS + 1], vec, tail], axis=1)


def table_columns_back(table):
    parts, begin = [], 0
    for horizon in horizons[::-1]:
        parts.append(table[:, begin:begin + horizon][:, ::-1])
        begin += horizon
    return jnp.concatenate([table[:, ROUTER:VECTOR]] + parts[::-1], axis=1)


def dispatch(route_rows, capacity):
    tokens = route_rows.shape[0]
    experts = jnp.arange(ROUTED_EXPERTS, dtype=jnp.int32)
    member = jnp.any(route_rows[:, :, None] == experts[None, None, :], axis=1)
    count = jnp.cumsum(member.astype(jnp.int32), axis=0)
    total = count[-1]
    place = jnp.where(member, count - 1, -1)
    high = (place[:, :, None] // LANES == jnp.arange(capacity // LANES)[None, None, :]) & member[:, :, None]
    low = (place[:, :, None] % LANES == jnp.arange(LANES)[None, None, :]).astype(BF16)
    token = jnp.arange(tokens, dtype=jnp.int32)
    left = jnp.concatenate(
        [jnp.where(high, part[:, None, None], 0).astype(BF16) for part in (token // 16, token % 16)], axis=2)
    found = jnp.einsum("teh,tel->ehl", left, low, preferred_element_type=F32)
    half = capacity // LANES
    source = (found[:, :half] * 16.0 + found[:, half:]).reshape(ROUTED_EXPERTS, capacity).astype(jnp.int32)
    slots = jnp.arange(capacity, dtype=jnp.int32)
    source = jnp.where(slots[None, :] < total[:, None], source, tokens)
    return total, source.reshape(-1)


def adam_update(master, moment, square, gradient, factor, bias_one, bias_two, step_rate):
    clipped = gradient * factor
    new_moment = beta_one * moment + (1.0 - beta_one) * clipped
    new_square = beta_two * square + (1.0 - beta_two) * clipped * clipped
    updated = master - step_rate * (
        new_moment / bias_one / (jnp.sqrt(new_square / bias_two) + adam_eps) + decay_rate * master
    )
    return (updated, new_moment, new_square)


def on_device(
    series, observed, routes, step_count,
    joint_proj, joint_moment, joint_square,
    mixer_proj, mixer_moment, mixer_square,
    upward_proj, upward_moment, upward_square,
    downward_proj, downward_moment, downward_square,
    readout, readout_moment, readout_square,
    vectors, vectors_moment, vectors_square,
):
    dp_count = lax.axis_size("dp")
    mp_count = lax.axis_size("mp")
    shard = joint_proj.shape[1]
    width = joint_proj.shape[2]
    hidden = upward_proj.shape[3]
    experts = upward_proj.shape[0]
    series_count, length = series.shape
    tokens = series_count * length
    capacity = tokens // 2

    small_own = jnp.concatenate(
        [joint_proj[k].astype(BF16) for k in range(3)]
        + [mixer_proj.T.astype(BF16), table_columns(readout.astype(BF16), vectors.T.astype(BF16))], axis=1)
    big_own = jnp.concatenate(
        [upward_proj.astype(BF16).reshape(experts, shard, 2 * hidden), downward_proj.transpose(0, 2, 1).astype(BF16)],
        axis=2)
    marks = observed.astype(F32)
    expert_here, source = dispatch(routes.reshape(tokens, 2), capacity)
    point = jnp.arange(length, dtype=F32)
    head_here = jnp.stack(
        [jnp.sum(jnp.sum(marks, axis=0) * jnp.minimum(point, float(horizon))) for horizon in horizons])
    tally = jnp.pad(jnp.concatenate([expert_here.astype(F32), head_here]), (0, LANES - 12))
    tally = jnp.broadcast_to(tally[None], (8, LANES))
    cos, sin = rope_rows(length)
    x = (series * marks).reshape(series_count, 1, length)

    big, wt, vec, table, a, qkv, lse, o, x1, b, pc, pr_total, tallies = forward_near(
        small_own, big_own, tally, x, cos, sin, width, 0)
    wo, table_t = wt[3 * width:4 * width], wt[4 * width:]
    tally = jnp.sum(tallies[:, 0], axis=0) / mp_count
    expert_count, head_count = tally[:ROUTED_EXPERTS], tally[ROUTED_EXPERTS:ROUTED_EXPERTS + 4]
    total_tokens = tokens * dp_count

    xs, ys, mixed = expert_forward(expert_here, source, b, pc, big)
    head_weight = jnp.concatenate(
        [jnp.zeros((horizon,), F32) + 0.25 / head_count[3 - index] for index, horizon in enumerate(horizons[::-1])])
    head_weight = jnp.pad(head_weight, (0, LANES - head_weight.shape[0]))[None]
    dx2, d_table, d_gain3, fit = loss_stage(
        mixed, x1, vec, table, table_t, hankel_rows(series), hankel_rows(marks), head_weight, 1)
    dys, dgs, hs, back = expert_backward(expert_here, source, pc, dx2, big, xs, ys)
    balance = aux_factor * ROUTED_EXPERTS * expert_count / total_tokens / total_tokens
    balance = jnp.pad(balance, (ROUTER, LANES - SHARED))[None]
    local_loss = jnp.sum(fit) + jnp.sum(pr_total * balance)
    dx1, do, rest = mid_backward(back, dx2, x1, b, pc, vec, table_t, balance, wo, o, d_table, d_gain3, 2)
    big_red, small_red = backward_near(xs, dys, dgs, hs, qkv, do, lse, a, dx1, rest, x, wt, vec, cos, sin, 3)

    attn_red, table_red = small_red[:, :4 * width], small_red[:, 4 * width:]
    squares = (
        jnp.sum(big_red * big_red) + jnp.sum(attn_red * attn_red) + jnp.sum(table_red * table_red) / mp_count
    )
    pair = jnp.pad(jnp.stack([squares, local_loss / mp_count]), (0, LANES - 2))
    pair = jnp.sum(all_blocks(jnp.broadcast_to(pair[None], (8, LANES)), 4)[:, 0], axis=0)
    grad_norm, loss_total = jnp.sqrt(pair[0]), pair[1]

    factor = clip_limit / (grad_norm + 1e-06)
    steps_taken = step_count[0].astype(F32)
    bias_one = 1.0 - beta_one**steps_taken
    bias_two = 1.0 - beta_two**steps_taken

    def update(master, moment, square, gradient, rate=matrix_rate):
        return adam_update(master, moment, square, gradient, factor, bias_one, bias_two, rate)

    joint_red = jnp.stack([attn_red[:, k * width:(k + 1) * width] for k in range(3)], axis=0)
    mixer_red = attn_red[:, 3 * width:].T
    upward_red = big_red[:, :, :2 * hidden].reshape(upward_proj.shape)
    downward_red = big_red[:, :, 2 * hidden:].transpose(0, 2, 1)
    return (
        loss_total,
        grad_norm,
        *update(joint_proj, joint_moment, joint_square, joint_red),
        *update(mixer_proj, mixer_moment, mixer_square, mixer_red),
        *update(upward_proj, upward_moment, upward_square, upward_red),
        *update(downward_proj, downward_moment, downward_square, downward_red),
        *update(readout, readout_moment, readout_square, table_columns_back(table_red)),
        *update(vectors, vectors_moment, vectors_square, table_red[:, VECTOR:VECTOR + 5].T, vector_rate),
    )


def rms_scale(tensor, gain_row):
    return (
        tensor * lax.rsqrt(jnp.mean(tensor * tensor, axis=-1, keepdims=True) + norm_eps) * gain_row
    )


def rope_tables(length, columns):
    halfway = columns // 2
    frequency = rope_base ** (-2.0 * jnp.arange(halfway, dtype=jnp.float32) / columns)
    angles = jnp.arange(length, dtype=jnp.float32)[:, None] * frequency[None, :]
    return (jnp.cos(angles), jnp.sin(angles))


def rotate(tensor, cosine_table, sine_table):
    halfway = tensor.shape[-1] // 2
    front_part = tensor[..., :halfway]
    back_part = tensor[..., halfway:]
    return jnp.concatenate(
        [
            front_part * cosine_table - back_part * sine_table,
            back_part * cosine_table + front_part * sine_table,
        ],
        axis=-1,
    )


def swiglu(tensor):
    halfway = tensor.shape[-1] // 2
    return jax.nn.silu(tensor[..., :halfway]) * tensor[..., halfway:]


def targets_of(series, observed):
    row_count, length = series.shape
    longest = max(horizons)
    padded_values = jnp.concatenate([series, jnp.zeros((row_count, longest), jnp.float32)], axis=1)
    padded_marks = jnp.concatenate(
        [observed.astype(jnp.float32), jnp.zeros((row_count, longest), jnp.float32)], axis=1
    )
    value_window = jnp.stack(
        [padded_values[:, 1 + offset : 1 + offset + length] for offset in range(longest)], axis=-1
    )
    mark_window = jnp.stack(
        [padded_marks[:, 1 + offset : 1 + offset + length] for offset in range(longest)], axis=-1
    )
    observed_future_series = jnp.concatenate(
        [value_window[..., :horizon] for horizon in horizons], axis=-1
    )
    valid_mask = jnp.concatenate([mark_window[..., :horizon] for horizon in horizons], axis=-1)
    return (
        observed_future_series.reshape(row_count * length, -1),
        valid_mask.reshape(row_count * length, -1),
    )


def head_counts(valid_mask):
    beginnings = [sum(horizons[:index]) for index in range(len(horizons))]
    return jnp.stack(
        [
            jnp.sum(valid_mask[:, beginning : beginning + horizon])
            for beginning, horizon in zip(beginnings, horizons)
        ]
    )


def head_weights(head_count):
    return jnp.concatenate(
        [
            jnp.zeros((horizon,), jnp.float32) + 0.25 / head_count[index]
            for index, horizon in enumerate(horizons)
        ]
    )


def dispatch_plan(route_rows, experts, capacity):
    flat_routes = route_rows.reshape(-1)
    entries = flat_routes.shape[0]
    onehot = (flat_routes[:, None] == jnp.arange(experts, dtype=jnp.int32)[None, :]).astype(
        jnp.int32
    )
    position = jnp.sum(jnp.cumsum(onehot, axis=0) * onehot, axis=1) - 1
    slot_index = flat_routes * capacity + position
    source = (
        jnp.full((experts * capacity,), entries, jnp.int32)
        .at[slot_index]
        .set(jnp.arange(entries, dtype=jnp.int32))
    )
    return (slot_index, source)


def split_heads(matrix, series_count, length):
    return matrix.reshape(series_count, length, matrix.shape[1] // HEAD, HEAD).transpose(0, 2, 1, 3)


def merge_heads(tensor):
    series_count, heads_here, length, head_size = tensor.shape
    return tensor.transpose(0, 2, 1, 3).reshape(series_count * length, heads_here * head_size)


def block_scores(query_block, key_heads, offset, length):
    block_rows = query_block.shape[1]
    scores = jnp.einsum(
        "hqe,hke->hqk", query_block, key_heads, preferred_element_type=jnp.float32
    ) * HEAD ** (-0.5)
    allowed = (offset + jnp.arange(block_rows))[:, None] >= jnp.arange(length)[None, :]
    return jnp.where(allowed[None], scores, -1e30)


def attend_forward(pieces):
    query_heads, key_heads, value_heads = pieces
    length = query_heads.shape[1]
    block_rows = min(length, 512)
    outputs = []
    totals = []
    for offset in range(0, length, block_rows):
        scores = block_scores(
            query_heads[:, offset : offset + block_rows], key_heads, offset, length
        )
        row_peak = jnp.max(scores, axis=-1, keepdims=True)
        exponent = jnp.exp(scores - row_peak)
        row_mass = jnp.sum(exponent, axis=-1, keepdims=True)
        outputs.append(
            jnp.einsum(
                "hqk,hke->hqe",
                (exponent / row_mass).astype(jnp.bfloat16),
                value_heads,
                preferred_element_type=jnp.float32,
            )
        )
        totals.append(row_peak + jnp.log(row_mass))
    return (jnp.concatenate(outputs, axis=1), jnp.concatenate(totals, axis=1))


def attend_backward(pieces):
    query_heads, key_heads, value_heads, grads_out, totals = pieces
    length = query_heads.shape[1]
    block_rows = min(length, 512)
    key_grad = jnp.zeros(key_heads.shape, jnp.float32)
    value_grad = jnp.zeros(value_heads.shape, jnp.float32)
    query_grads = []
    for offset in range(0, length, block_rows):
        query_block = query_heads[:, offset : offset + block_rows]
        grad_block = grads_out[:, offset : offset + block_rows]
        weights = jnp.exp(
            block_scores(query_block, key_heads, offset, length)
            - totals[:, offset : offset + block_rows]
        )
        grad_weights = jnp.einsum(
            "hqe,hke->hqk", grad_block, value_heads, preferred_element_type=jnp.float32
        )
        score_grad = (
            weights
            * (grad_weights - jnp.sum(weights * grad_weights, axis=-1, keepdims=True))
            * HEAD ** (-0.5)
        ).astype(jnp.bfloat16)
        query_grads.append(
            jnp.einsum("hqk,hke->hqe", score_grad, key_heads, preferred_element_type=jnp.float32)
        )
        key_grad = key_grad + jnp.einsum(
            "hqk,hqe->hke", score_grad, query_block, preferred_element_type=jnp.float32
        )
        value_grad = value_grad + jnp.einsum(
            "hqk,hqe->hke",
            weights.astype(jnp.bfloat16),
            grad_block,
            preferred_element_type=jnp.float32,
        )
    return (jnp.concatenate(query_grads, axis=1), key_grad, value_grad)


def branch_total(partial_sum):
    return lax.psum(partial_sum, "mp")


def input_total(partial_sum):
    return lax.psum(partial_sum, "mp")


def on_device_wide(
    series,
    observed,
    routes,
    step_count,
    joint_proj,
    joint_moment,
    joint_square,
    mixer_proj,
    mixer_moment,
    mixer_square,
    upward_proj,
    upward_moment,
    upward_square,
    downward_proj,
    downward_moment,
    downward_square,
    readout,
    readout_moment,
    readout_square,
    vectors,
    vectors_moment,
    vectors_square,
):
    dp_count = lax.axis_size("dp")
    hidden_local = upward_proj.shape[3]
    joint_full, mixer_full, upward_full, downward_full, readout_complete, vector_full = (
        lax.all_gather(joint_proj.astype(jnp.bfloat16), "dp", axis=1, tiled=True),
        lax.all_gather(mixer_proj.astype(jnp.bfloat16), "dp", axis=1, tiled=True),
        lax.all_gather(upward_proj.astype(jnp.bfloat16), "dp", axis=1, tiled=True),
        lax.all_gather(downward_proj.astype(jnp.bfloat16), "dp", axis=2, tiled=True),
        lax.all_gather(readout.astype(jnp.bfloat16), "dp", axis=0, tiled=True),
        lax.all_gather(vectors.astype(jnp.bfloat16), "dp", axis=1, tiled=True),
    )
    up_local = upward_full.reshape(upward_full.shape[0], D, -1)
    shared_up_weight = up_local[-1]
    shared_down_weight = downward_full[-1]
    expert_up = up_local[:ROUTED_EXPERTS]
    expert_down = downward_full[:ROUTED_EXPERTS]
    gain_rows = vector_full.astype(jnp.float32)
    series_count, length = series.shape
    entries = series_count * length
    route_rows = routes.reshape(entries, 2)
    onehot = route_rows[:, :, None] == jnp.arange(ROUTED_EXPERTS, dtype=jnp.int32)[None, None, :]
    observed_future_series, valid_mask = targets_of(series, observed)
    expert_count, head_count = lax.psum(
        (jnp.sum(onehot.astype(jnp.float32), axis=(0, 1)), head_counts(valid_mask)), "dp"
    )
    total_tokens = entries * dp_count
    inputs = (series * observed.astype(jnp.float32)).reshape(entries, 1)

    def embed(gate_vector, up_vector):
        return jax.nn.silu(inputs * gate_vector) * (inputs * up_vector)

    embedded, embed_back = jax.vjp(embed, gain_rows[3], gain_rows[4])
    normed_one, norm_one_back = jax.vjp(rms_scale, embedded, gain_rows[0])
    first_input = normed_one.astype(jnp.bfloat16)
    projected = jnp.einsum(
        "td,cde->cte", first_input, joint_full, preferred_element_type=jnp.float32
    )
    cosine_table, sine_table = rope_tables(length, HEAD)
    query_heads = rotate(
        split_heads(projected[0], series_count, length), cosine_table, sine_table
    ).astype(jnp.bfloat16)
    key_heads = rotate(
        split_heads(projected[1], series_count, length), cosine_table, sine_table
    ).astype(jnp.bfloat16)
    value_heads = split_heads(projected[2], series_count, length).astype(jnp.bfloat16)
    attended, totals = lax.map(attend_forward, (query_heads, key_heads, value_heads))
    attended_low = merge_heads(attended).astype(jnp.bfloat16)
    after_attn = embedded + branch_total(
        jnp.dot(attended_low, mixer_full, preferred_element_type=jnp.float32)
    )
    normed_two, norm_two_back = jax.vjp(rms_scale, after_attn, gain_rows[1])
    second_input = normed_two.astype(jnp.bfloat16)
    logits = jnp.dot(
        second_input, readout_complete[:, : ROUTED_EXPERTS + 1], preferred_element_type=jnp.float32
    )

    def gating(logit_rows):
        probabilities = jax.nn.softmax(logit_rows[:, :ROUTED_EXPERTS], axis=-1)
        chosen = jnp.sum(jnp.where(onehot, probabilities[:, None, :], 0.0), axis=-1)
        balance = (
            aux_factor
            * ROUTED_EXPERTS
            * jnp.sum(expert_count / total_tokens * jnp.sum(probabilities, axis=0) / total_tokens)
        )
        return (chosen, jax.nn.sigmoid(logit_rows[:, ROUTED_EXPERTS]), balance)

    (gate_values, shared_gate, balance), gating_back = jax.vjp(gating, logits)
    capacity = entries // 2
    slot_index, source = dispatch_plan(route_rows, ROUTED_EXPERTS, capacity)
    token_of = source // 2
    padded_input = jnp.concatenate([second_input, jnp.zeros((1, D), jnp.bfloat16)], axis=0)
    gathered = padded_input[token_of].reshape(ROUTED_EXPERTS, capacity, D)
    gate_up = jnp.einsum("ecd,edf->ecf", gathered, expert_up, preferred_element_type=jnp.float32)
    hidden_f, swiglu_back = jax.vjp(swiglu, gate_up)
    hidden = hidden_f.astype(jnp.bfloat16)
    expert_out = jnp.einsum(
        "ecf,efd->ecd", hidden, expert_down, preferred_element_type=jnp.float32
    ).reshape(ROUTED_EXPERTS * capacity, D)
    picked = expert_out[slot_index].reshape(entries, 2, D)
    shared_up = jnp.dot(second_input, shared_up_weight, preferred_element_type=jnp.float32)
    shared_f, shared_back = jax.vjp(swiglu, shared_up)
    shared_hidden = shared_f.astype(jnp.bfloat16)
    shared_out = jnp.dot(shared_hidden, shared_down_weight, preferred_element_type=jnp.float32)
    mixed_part = (
        jnp.sum(gate_values[:, :, None] * picked, axis=1) + shared_gate[:, None] * shared_out
    )
    after_mixer = after_attn + branch_total(mixed_part)
    normalized_output, norm_out_back = jax.vjp(rms_scale, after_mixer, gain_rows[2])
    output_input = normalized_output.astype(jnp.bfloat16)
    model_estimates = jnp.dot(
        output_input, readout_complete[:, ROUTED_EXPERTS + 1 :], preferred_element_type=jnp.float32
    )
    prediction_misses = model_estimates - observed_future_series
    absolute_miss = jnp.abs(prediction_misses)
    horizon_importance_factors = head_weights(head_count)[None, :] * valid_mask
    robust_penalty_entries = jnp.where(
        absolute_miss <= quadratic_cutoff,
        0.5 * prediction_misses * prediction_misses,
        quadratic_cutoff * (absolute_miss - 0.5 * quadratic_cutoff),
    )
    local_loss = jnp.sum(robust_penalty_entries * horizon_importance_factors) + balance
    mp_count = lax.axis_size("mp")
    loss_total = lax.psum(local_loss, "dp")
    predicted_gradient = (
        jnp.clip(prediction_misses, -quadratic_cutoff, quadratic_cutoff)
        * horizon_importance_factors
    ).astype(jnp.bfloat16)
    head_grad = jnp.einsum(
        "ka,ky->ay", output_input, predicted_gradient, preferred_element_type=jnp.float32
    )
    out_input_grad = jnp.einsum(
        "aw,iw->ai",
        predicted_gradient,
        readout_complete[:, ROUTED_EXPERTS + 1 :],
        preferred_element_type=jnp.float32,
    )
    mixer_grad_in, gain_three_grad = norm_out_back(out_input_grad)
    picked_dots = jnp.sum(picked * mixer_grad_in[:, None, :], axis=-1)
    shared_dots = jnp.sum(shared_out * mixer_grad_in, axis=-1)
    gate_grads, shared_gate_grad = lax.psum((picked_dots, shared_dots), "mp")
    (logit_grad,) = gating_back((gate_grads, shared_gate_grad, jnp.ones((), jnp.float32)))
    logit_low = logit_grad.astype(jnp.bfloat16)
    router_grad = jnp.einsum(
        "ka,ky->ay", second_input, logit_low, preferred_element_type=jnp.float32
    )
    router_input_grad = jnp.einsum(
        "aw,iw->ai",
        logit_low,
        readout_complete[:, : ROUTED_EXPERTS + 1],
        preferred_element_type=jnp.float32,
    )
    gates_padded = jnp.concatenate([gate_values.reshape(-1), jnp.zeros((1,), jnp.float32)], axis=0)
    residual_padded = jnp.concatenate([mixer_grad_in, jnp.zeros((1, D), jnp.float32)], axis=0)
    expert_out_grad = (
        (gates_padded[source][:, None] * residual_padded[token_of])
        .astype(jnp.bfloat16)
        .reshape(ROUTED_EXPERTS, capacity, D)
    )
    hidden_grad = jnp.einsum(
        "ecd,efd->ecf", expert_out_grad, expert_down, preferred_element_type=jnp.float32
    )
    down_grad_experts = jnp.einsum(
        "ecf,ecd->efd", hidden, expert_out_grad, preferred_element_type=jnp.float32
    )
    gate_up_grad = swiglu_back(hidden_grad)[0].astype(jnp.bfloat16)
    up_grad_experts = jnp.einsum(
        "ecd,ecf->edf", gathered, gate_up_grad, preferred_element_type=jnp.float32
    )
    rows_grad = jnp.einsum(
        "ecf,edf->ecd", gate_up_grad, expert_up, preferred_element_type=jnp.float32
    ).reshape(ROUTED_EXPERTS * capacity, D)
    routed_grad = jnp.sum(rows_grad[slot_index].reshape(entries, 2, D), axis=1)
    shared_out_grad = (shared_gate[:, None] * mixer_grad_in).astype(jnp.bfloat16)
    shared_hidden_grad = jnp.einsum(
        "td,fd->tf", shared_out_grad, shared_down_weight, preferred_element_type=jnp.float32
    )
    down_grad_shared = jnp.einsum(
        "tf,td->fd", shared_hidden, shared_out_grad, preferred_element_type=jnp.float32
    )
    shared_up_grad = shared_back(shared_hidden_grad)[0].astype(jnp.bfloat16)
    up_grad_shared = jnp.einsum(
        "td,tf->df", second_input, shared_up_grad, preferred_element_type=jnp.float32
    )
    input_part = routed_grad + jnp.einsum(
        "tf,df->td", shared_up_grad, shared_up_weight, preferred_element_type=jnp.float32
    )
    second_input_grad = input_total(input_part) + router_input_grad
    upward_grad = jnp.concatenate([up_grad_experts, up_grad_shared[None]], axis=0).reshape(
        ROUTED_EXPERTS + 1, D, 2, hidden_local
    )
    downward_grad = jnp.concatenate([down_grad_experts, down_grad_shared[None]], axis=0)
    attn_grad_in, gain_two_grad = norm_two_back(second_input_grad)
    attn_total_grad = mixer_grad_in + attn_grad_in
    attn_low = attn_total_grad.astype(jnp.bfloat16)
    mixer_grad = jnp.einsum("tf,td->fd", attended_low, attn_low, preferred_element_type=jnp.float32)
    attended_grad = jnp.einsum(
        "td,fd->tf", attn_low, mixer_full, preferred_element_type=jnp.float32
    ).astype(jnp.bfloat16)
    query_grad, key_grad, value_grad = lax.map(
        attend_backward,
        (
            query_heads,
            key_heads,
            value_heads,
            split_heads(attended_grad, series_count, length),
            totals,
        ),
    )
    projected_grad = jnp.stack(
        [
            merge_heads(rotate(query_grad, cosine_table, -sine_table)),
            merge_heads(rotate(key_grad, cosine_table, -sine_table)),
            merge_heads(value_grad),
        ],
        axis=0,
    ).astype(jnp.bfloat16)
    joint_grad = jnp.einsum(
        "td,cte->cde", first_input, projected_grad, preferred_element_type=jnp.float32
    )
    first_input_grad = input_total(
        jnp.einsum("cte,cde->td", projected_grad, joint_full, preferred_element_type=jnp.float32)
    )
    embed_grad_in, gain_one_grad = norm_one_back(first_input_grad)
    gate_vector_grad, up_vector_grad = embed_back(attn_total_grad + embed_grad_in)
    vector_grad = jnp.stack(
        [gain_one_grad, gain_two_grad, gain_three_grad, gate_vector_grad, up_vector_grad], axis=0
    )
    readout_grad = jnp.concatenate([router_grad, head_grad], axis=1)
    joint_red, mixer_red, upward_red, downward_red, readout_red, vector_red = (
        lax.psum_scatter(joint_grad, "dp", scatter_dimension=1, tiled=True),
        lax.psum_scatter(mixer_grad, "dp", scatter_dimension=1, tiled=True),
        lax.psum_scatter(upward_grad, "dp", scatter_dimension=1, tiled=True),
        lax.psum_scatter(downward_grad, "dp", scatter_dimension=2, tiled=True),
        lax.psum_scatter(readout_grad, "dp", scatter_dimension=0, tiled=True),
        lax.psum_scatter(vector_grad, "dp", scatter_dimension=1, tiled=True),
    )
    split_squares = (
        jnp.sum(joint_red * joint_red)
        + jnp.sum(mixer_red * mixer_red)
        + jnp.sum(upward_red * upward_red)
        + jnp.sum(downward_red * downward_red)
    )
    shared_squares = jnp.sum(readout_red * readout_red) + jnp.sum(vector_red * vector_red)
    partial_squares = split_squares + shared_squares / mp_count
    norm_squared = lax.psum(partial_squares, ("dp", "mp"))
    grad_norm = jnp.sqrt(norm_squared)
    factor = clip_limit / (grad_norm + 1e-06)
    steps_taken = step_count[0].astype(jnp.float32)
    bias_one = 1.0 - beta_one**steps_taken
    bias_two = 1.0 - beta_two**steps_taken
    joint_new = adam_update(
        joint_proj, joint_moment, joint_square, joint_red, factor, bias_one, bias_two, matrix_rate
    )
    mixer_new = adam_update(
        mixer_proj, mixer_moment, mixer_square, mixer_red, factor, bias_one, bias_two, matrix_rate
    )
    upward_new = adam_update(
        upward_proj,
        upward_moment,
        upward_square,
        upward_red,
        factor,
        bias_one,
        bias_two,
        matrix_rate,
    )
    downward_new = adam_update(
        downward_proj,
        downward_moment,
        downward_square,
        downward_red,
        factor,
        bias_one,
        bias_two,
        matrix_rate,
    )
    readout_new = adam_update(
        readout,
        readout_moment,
        readout_square,
        readout_red,
        factor,
        bias_one,
        bias_two,
        matrix_rate,
    )
    vector_new = adam_update(
        vectors, vectors_moment, vectors_square, vector_red, factor, bias_one, bias_two, vector_rate
    )
    return (
        loss_total,
        grad_norm,
        joint_new[0],
        joint_new[1],
        joint_new[2],
        mixer_new[0],
        mixer_new[1],
        mixer_new[2],
        upward_new[0],
        upward_new[1],
        upward_new[2],
        downward_new[0],
        downward_new[1],
        downward_new[2],
        readout_new[0],
        readout_new[1],
        readout_new[2],
        vector_new[0],
        vector_new[1],
        vector_new[2],
    )


def solution(mesh):
    token = [P("dp", None), P("dp", None), P("dp", None, None), P()]
    weights = [
        P(None, "dp", "mp"), P("mp", "dp"), P(None, "dp", None, "mp"), P(None, "mp", "dp"), P("dp", None), P(None, "dp"),
    ]
    triple = tuple(spec for spec in weights for _ in range(3))
    near = mesh.shape["dp"] == 16 and mesh.shape["mp"] == 2
    return jax.shard_map(
        on_device if near else on_device_wide,
        mesh=mesh,
        in_specs=tuple(token) + triple,
        out_specs=(P(), P()) + triple,
        check_vma=False,
    )
```

```python
import functools
import jax
import jax.numpy as jnp
from jax import lax
from jax.experimental import pallas as pl
from jax.experimental.pallas import tpu as pltpu
from jax.sharding import PartitionSpec as P

D = 384
HEAD = 32
ROUTED_EXPERTS = 8
LANES = 128
TILE = 256
SHARD = 24
ROUTER = 112
SHARED = ROUTER + ROUTED_EXPERTS
VECTOR = SHARED + 1

horizons = (1, 8, 32, 64)
quadratic_cutoff = 2.0
aux_factor = 0.02
clip_limit = 0.001
beta_one = 0.9
beta_two = 0.95
adam_eps = 1e-08
decay_rate = 0.1
matrix_rate = 0.05
vector_rate = 0.25
norm_eps = 1e-06
rope_base = 10000.0

F32 = jnp.float32
BF16 = jnp.bfloat16
I16 = jnp.int16
MESH = pl.DeviceIdType.MESH
VMEM = pl.BlockSpec(memory_space=pltpu.VMEM)
ANY = pl.BlockSpec(memory_space=pl.ANY)
DMA = pltpu.SemaphoreType.DMA


def dot(a, b, da=1, db=0):
    return lax.dot_general(a, b, (((da,), (db,)), ((), ())), preferred_element_type=F32)


def params(megabytes=60, **more):
    return pltpu.CompilerParams(vmem_limit_bytes=megabytes * 1024 * 1024, **more)


def sigmoid(v):
    return 1.0 / (1.0 + jnp.exp(-v))


def block(index, size, step=8):
    return pl.ds(pl.multiple_of(index * size, step), size)


def place():
    dp = lax.axis_index("dp")
    return dp, lax.axis_index("mp"), lax.rem(dp, 2), lax.rem(dp // 2, 2), dp // 4


def meet_everyone(dp, mp):
    barrier = pltpu.get_barrier_semaphore()
    me, n = dp * 2 + mp, 32

    def signal(k, carry):
        peer = lax.rem(me + k, n)
        pl.semaphore_signal(barrier, inc=1, device_id=(peer // 2, lax.rem(peer, 2)), device_id_type=MESH)
        return carry

    lax.fori_loop(1, n, signal, 0)
    pl.semaphore_wait(barrier, n - 1)


def remote(src, dst, send, recv, dp, mp):
    return pltpu.make_async_remote_copy(
        src_ref=src, dst_ref=dst, send_sem=send, recv_sem=recv, device_id=(dp, mp), device_id_type=MESH)


def done(view, sem):
    pltpu.make_async_copy(view, view, sem).wait()


def column(row, length):
    return jnp.transpose(jnp.broadcast_to(row, (LANES, length)))


def rotated(t, cos, sin):
    half = HEAD // 2
    front, back = t[:half], t[half:]
    return jnp.concatenate([front * cos - back * sin, back * cos + front * sin], axis=0)


def unrotated(t, cos, sin):
    half = HEAD // 2
    front, back = t[:half], t[half:]
    return jnp.concatenate([front * cos + back * sin, back * cos - front * sin], axis=0)


def score_block(k_rows, q_cols, low):
    s = dot(k_rows, q_cols)
    keys = lax.broadcasted_iota(jnp.int32, s.shape, 0)
    queries = lax.broadcasted_iota(jnp.int32, s.shape, 1) + low
    return jnp.where(keys <= queries, s, -1e30)


def flip(t):
    return jnp.transpose(t.astype(F32)).astype(BF16)


def embed_piece(x_row, vec, x0_ref, a_ref, r):
    xb = column(x_row, TILE)
    cuts, square = [], None
    for c in range(D // LANES):
        cols = slice(c * LANES, (c + 1) * LANES)
        u = xb * vec[3:4, cols]
        v = u * sigmoid(u) * (xb * vec[4:5, cols])
        x0_ref[r, cols] = v
        square = v * v if square is None else square + v * v
        cuts.append(v)
    scale = lax.rsqrt(jnp.sum(square, axis=1, keepdims=True) / D + norm_eps)
    for c in range(D // LANES):
        cols = slice(c * LANES, (c + 1) * LANES)
        a_ref[r, cols] = (cuts[c] * scale * vec[0:1, cols]).astype(BF16)


def project_piece(wt, a, cos, sin, qkv, width):
    for part in range(3):
        t = dot(wt[part * width:(part + 1) * width, :], a, 1, 1)
        for h in range(width // HEAD):
            u = t[h * HEAD:(h + 1) * HEAD]
            if part < 2:
                u = rotated(u, cos, sin)
            qkv[part * width + h * HEAD:part * width + (h + 1) * HEAD, :] = u.astype(BF16)


def forward_head(h, width, qkv, lse, o):
    length = qkv.shape[1]
    scale = HEAD ** (-0.5)
    q_rows = block(h, HEAD)
    k_rows = pl.ds(pl.multiple_of(width + h * HEAD, HEAD), HEAD)
    v_rows = pl.ds(pl.multiple_of(2 * width + h * HEAD, HEAD), HEAD)
    k = flip(qkv[k_rows, :])
    for j in range(length // TILE):
        n = TILE * (j + 1)
        cols = slice(j * TILE, (j + 1) * TILE)
        s = score_block(k[:n], qkv[q_rows, cols], j * TILE)
        peak = jnp.max(s, axis=0, keepdims=True)
        e = jnp.exp((s - peak) * scale)
        mass = jnp.sum(e, axis=0, keepdims=True)
        weights = (e * (1.0 / mass)).astype(BF16)
        o[q_rows, cols] = dot(qkv[v_rows, :n], weights).astype(BF16)
        lse[pl.ds(h, 1), cols] = peak * scale + jnp.log(mass)


def backward_head(h, width, qkv, do_t, lse, cos, sin, dqkv, dk_ref, dv_ref):
    length = qkv.shape[1]
    scale = HEAD ** (-0.5)
    q_rows = block(h, HEAD)
    k_rows = pl.ds(pl.multiple_of(width + h * HEAD, HEAD), HEAD)
    v_rows = pl.ds(pl.multiple_of(2 * width + h * HEAD, HEAD), HEAD)
    q, k, v, do = flip(qkv[q_rows, :]), flip(qkv[k_rows, :]), flip(qkv[v_rows, :]), flip(do_t[q_rows, :])
    dk_ref[...] = jnp.zeros_like(dk_ref)
    dv_ref[...] = jnp.zeros_like(dv_ref)
    for j in range(length // TILE):
        n = TILE * (j + 1)
        cols = slice(j * TILE, (j + 1) * TILE)
        s = score_block(k[:n], qkv[q_rows, cols], j * TILE)
        w = jnp.exp(s * scale - lse[pl.ds(h, 1), cols])
        dv_ref[:n] += dot(w.astype(BF16), do[cols])
        dw = dot(v[:n], do_t[q_rows, cols])
        mean = jnp.sum(w * dw, axis=0, keepdims=True)
        ds = (w * (dw - mean) * scale).astype(BF16)
        dk_ref[:n] += dot(ds, q[cols])
        dq = dot(qkv[k_rows, :n], ds)
        dqkv[q_rows, cols] = unrotated(dq, cos[:, cols], sin[:, cols]).astype(BF16)
    dqkv[k_rows, :] = unrotated(jnp.transpose(dk_ref[...]), cos, sin).astype(BF16)
    dqkv[v_rows, :] = jnp.transpose(dv_ref[...]).astype(BF16)


def mid_forward_piece(x, gain, table):
    scale = lax.rsqrt(jnp.mean(x * x, axis=1, keepdims=True) + norm_eps)
    low = (x * scale * gain).astype(BF16)
    logits = dot(low, table)
    lanes = lax.broadcasted_iota(jnp.int32, logits.shape, 1)
    routed = (lanes >= ROUTER) & (lanes < SHARED)
    peak = jnp.max(jnp.where(routed, logits, -jnp.inf), axis=1, keepdims=True)
    e = jnp.where(routed, jnp.exp(jnp.where(routed, logits - peak, 0.0)), 0.0)
    probability = e / jnp.sum(e, axis=1, keepdims=True)
    gates = jnp.where(lanes == SHARED, sigmoid(jnp.where(lanes == SHARED, logits, 0.0)), probability)
    return low, gates, jnp.sum(probability, axis=0, keepdims=True)


def embed_backward_piece(x_row, da, dx1, vec):
    xb = column(x_row, TILE)
    xb = jnp.concatenate([xb] * (D // LANES), axis=1)
    u = xb * vec[3:4, :]
    up = xb * vec[4:5, :]
    s = sigmoid(u)
    silu = u * s
    x = silu * up
    scale = lax.rsqrt(jnp.mean(x * x, axis=1, keepdims=True) + norm_eps)
    unit = x * scale
    dn = da * vec[0:1, :]
    dx = dx1 + scale * (dn - unit * jnp.mean(dn * unit, axis=1, keepdims=True))
    du = dx * up * (s * (1.0 + u * (1.0 - s)))
    total = lambda v: jnp.sum(v, axis=0, keepdims=True)
    return total(da * unit), total(du * xb), total(dx * silu * xb)


def forward_kernel(
    small_own, big_own, tally, x_ref, cos_ref, sin_ref,
    big, wt, vec, table, a, qkv, lse, o, x1, b, pc, total, tallies,
    stage, small, x0, part, other,
    in_sem, own_sem, send_xy, send_up, send_dn, z_sem, p2_sem, p3_sem,
    small_send, small_z, small_y, small_x, tally_send, tally_recv, pair_send, pair_recv,
):
    dp, mp, x, y, z = place()
    xp, yp = dp + 1 - 2 * x, dp + 2 - 4 * y
    count = big_own.shape[0]
    series, _, length = x_ref.shape
    width = o.shape[1]
    per = length // TILE
    load = pltpu.make_async_copy(big_own, stage, in_sem)
    load.start()
    meet_everyone(dp, mp)

    def home(zs):
        return zs * 4 + 2 * y + x

    def small_put(src, slot, recv, peer):
        remote(src, small.at[slot], small_send, recv, peer, mp).start()

    for dist in (1, 2, 3):
        @pl.when(z >= dist)
        def _():
            small_put(small_own, dp, small_z.at[z], dp - 4 * dist)

        @pl.when(z + dist <= 3)
        def _():
            small_put(small_own, dp, small_z.at[z], dp + 4 * dist)
    small_put(small_own, dp, small_y.at[z], yp)
    small_put(small_own, dp, small_x, xp)
    small[dp] = small_own[...]
    me = dp * 2 + mp

    def tell(k, carry):
        peer = lax.rem(me + k, 32)
        remote(tally, tallies.at[me], tally_send, tally_recv, peer // 2, lax.rem(peer, 2)).start()
        return carry

    lax.fori_loop(1, 32, tell, 0)
    tallies[me] = tally[...]

    load.wait()

    def rows(c, slot):
        return big.at[c, block(slot, SHARD), :]

    def put(src, c, slot, send, recv, peer):
        remote(src, rows(c, slot), send, recv, peer, mp).start()

    def climb(c, zs, src):
        put(src, c, home(zs), send_up, z_sem.at[c, zs], dp + 4)

    def drop(c, zs, src):
        put(src, c, home(zs), send_dn, z_sem.at[c, zs], dp - 4)

    def ends(c):
        k = lax.rem(c, 2)
        return jnp.where(k == 0, yp, xp), jnp.where(k == 0, xp, yp)

    def spread(c, zs, src):
        first, second = ends(c)
        put(src, c, home(zs), send_xy, p2_sem.at[c, zs], first)
        put(src, c, home(zs), send_xy, p3_sem, second)

    def own_z(c, carry):
        @pl.when(z < 3)
        def _():
            climb(c, z, stage.at[c])

        @pl.when(z > 0)
        def _():
            drop(c, z, stage.at[c])
        pltpu.make_async_copy(stage.at[c], rows(c, dp), own_sem).start()
        return carry

    lax.fori_loop(0, count, own_z, 0)

    for dist in (1, 2, 3):
        for sign in (-1, 1):
            zs = z + sign * dist

            @pl.when((zs >= 0) & (zs <= 3))
            def _():
                done(small.at[home(zs)], small_z.at[zs])
                small_put(small.at[home(zs)], home(zs), small_y.at[zs], yp)
                small_put(small.at[home(zs)], home(zs), small_x, xp)
    for turn in range(4):
        zs = lax.rem(z + turn, 4)
        slot = zs * 4 + 2 * (1 - y) + x
        done(small.at[slot], small_y.at[zs])
        small_put(small.at[slot], slot, small_x, xp)
    done(small.at[pl.ds(0, 8)], small_x)

    def own_xy(c, carry):
        spread(c, z, stage.at[c])
        return carry

    lax.fori_loop(0, count, own_xy, 0)

    whole = small[...].astype(F32).reshape(D, -1)
    table[...] = whole[:, 4 * width:].astype(BF16)
    turned = jnp.transpose(whole)
    wt[...] = turned.astype(BF16)
    vec[...] = jnp.concatenate(
        [turned[4 * width + VECTOR:4 * width + VECTOR + 5], jnp.zeros((3, D), F32)], axis=0)
    total[...] = jnp.zeros_like(total)

    def relay(c, dist):
        def second(zs):
            k = lax.rem(c, 2)
            slot = zs * 4 + jnp.where(k == 0, 2 * (1 - y) + x, 2 * y + 1 - x)
            done(rows(c, slot), p2_sem.at[c, zs])
            put(rows(c, slot), c, slot, send_xy, p3_sem, ends(c)[1])

        @pl.when(z >= dist)
        def _():
            zs = z - dist
            done(rows(c, home(zs)), z_sem.at[c, zs])

            @pl.when(z < 3)
            def _():
                climb(c, zs, rows(c, home(zs)))
            spread(c, zs, rows(c, home(zs)))

        @pl.when(z + dist <= 3)
        def _():
            zs = z + dist
            done(rows(c, home(zs)), z_sem.at[c, zs])

            @pl.when(z > 0)
            def _():
                drop(c, zs, rows(c, home(zs)))
            spread(c, zs, rows(c, home(zs)))

        @pl.when(z - (dist - 1) >= 0)
        def _():
            second(z - (dist - 1))

        @pl.when((dist > 1) & (z + dist - 1 <= 3))
        def _():
            second(z + dist - 1)

    def pair(n):
        r = block(n, length)
        return remote(part.at[r], other.at[r], pair_send.at[n], pair_recv.at[n], dp, 1 - mp)

    heads = width // HEAD
    pieces = heads + 2

    def attention(i):
        n, j = i // pieces, lax.rem(i, pieces)
        r = block(n, length)

        @pl.when(j == 0)
        def _():
            def tile(m, carry):
                t = pl.ds(pl.multiple_of(n * length + m * TILE, TILE), TILE)
                embed_piece(x_ref[n, :, block(m, TILE, TILE)], vec, x0, a, t)
                return carry
            lax.fori_loop(0, per, tile, 0)

        @pl.when(j == 1)
        def _():
            project_piece(wt, a[r, :], cos_ref[...], sin_ref[...], qkv.at[n], width)

        @pl.when(j >= 2)
        def _():
            forward_head(j - 2, width, qkv.at[n], lse.at[n], o.at[n])

        @pl.when(j == pieces - 1)
        def _():
            part[r, :] = dot(o[n], wt[3 * width:4 * width, :], 0, 0)
            pair(n).start()

    def middle(m):
        r = block(m, TILE)

        @pl.when(lax.rem(m, per) == 0)
        def _():
            pair(m // per).wait()
        v = x0[r, :] + (part[r, :] + other[r, :])
        x1[r, :] = v
        low, gates, sums = mid_forward_piece(v, vec[1:2, :], table[...])
        b[r, :] = low
        pc[r, :] = gates
        total[...] += sums

    def step(i, carry):
        relay(lax.rem(i, count), i // count + 1)

        @pl.when(i < series * pieces)
        def _():
            attention(i)

        for n in range(series):
            begin = (n + 1) * pieces + 4

            @pl.when((i >= begin) & (i < begin + per))
            def _():
                middle(n * per + i - begin)
        return carry

    lax.fori_loop(0, 4 * count, step, 0)

    def whole_wait(n, sem):
        done(big.at[:, pl.ds(0, n * SHARD), :], sem)
    whole_wait(8, p3_sem)
    whole_wait(12, send_xy)
    whole_wait(1, own_sem)
    done(small.at[pl.ds(0, 15)], small_send)
    done(tallies.at[pl.ds(0, 31)], tally_recv)
    done(tallies.at[pl.ds(0, 31)], tally_send)
    for k in range(4):
        @pl.when(z == k)
        def _():
            if k < 3:
                whole_wait(k + 1, send_up)
            if k > 0:
                whole_wait(4 - k, send_dn)


def forward_near(small_own, big_own, tally, x, cos, sin, width, ident):
    series, _, length = x.shape
    tokens = series * length
    count, shard, columns = big_own.shape
    shape = jax.ShapeDtypeStruct
    return pl.pallas_call(
        forward_kernel,
        in_specs=[VMEM, ANY, VMEM, VMEM, VMEM, VMEM],
        out_specs=[ANY] + [VMEM] * 12,
        out_shape=[
            shape((count, D, columns), BF16),
            shape((small_own.shape[1], D), BF16), shape((8, D), F32), shape((D, LANES), BF16),
            shape((tokens, D), BF16), shape((series, 3 * width, length), BF16), shape((series, 8, length), F32),
            shape((series, width, length), BF16),
            shape((tokens, D), F32), shape((tokens, D), BF16), shape((tokens, LANES), F32), shape((1, LANES), F32),
            shape((32,) + tally.shape, F32),
        ],
        scratch_shapes=[
            pltpu.VMEM(big_own.shape, BF16), pltpu.VMEM((16,) + small_own.shape, BF16),
            pltpu.VMEM((tokens, D), F32), pltpu.VMEM((tokens, D), F32), pltpu.VMEM((tokens, D), F32),
            DMA, DMA, DMA, DMA, DMA, DMA((count, 4)), DMA((count, 4)), DMA,
            DMA, DMA((4,)), DMA((4,)), DMA, DMA, DMA, DMA((series,)), DMA((series,)),
        ],
        compiler_params=params(collective_id=ident, has_side_effects=True),
        name="forward_near",
    )(small_own, big_own, tally, x, cos, sin)


GROUP = 16


def spread_rows(dest, value, start, count):
    for c in range(value.shape[1] // LANES):
        dest[pl.ds(start * 8 + c, count, stride=8), :] = value[:, c * LANES:(c + 1) * LANES]


def rows_at(ref, index):
    return ref[pl.ds(pl.multiple_of(index, 8), 8), :]


def pick_rows(source, tile, index_ref, base):
    for i in range(0, TILE, GROUP):
        values = [rows_at(source, index_ref[base + k]) for k in range(i, i + GROUP)]
        for k in range(i, i + GROUP):
            tile[k * 8:k * 8 + 8, :] = values[k - i]


def sum_rows(results, tile, index_ref, base, tokens):
    for i in range(0, TILE, GROUP):
        values = [
            rows_at(results, index_ref[base + k]) + rows_at(results, index_ref[tokens + base + k])
            for k in range(i, i + GROUP)]
        for k in range(i, i + GROUP):
            tile[k * 8:k * 8 + 8, :] = values[k - i]


def gathered_columns(tile, columns):
    return [tile[pl.ds(c, TILE, stride=8), :] for c in range(columns)]


def lane_of(value, lane):
    lanes = lax.broadcasted_iota(jnp.int32, value.shape, 1)
    return jnp.sum(jnp.where(lanes == lane, value, 0.0), axis=1, keepdims=True)


def lay_rows(values, pc_ref, rows8):
    tokens = values.shape[0]

    def lay(i, carry):
        r = block(i, TILE)
        spread_rows(rows8, values[r, :].astype(F32), i * TILE, TILE)
        rows8[pl.ds(i * TILE * 8 + 3, TILE, stride=8), :] = pc_ref[r, :]
        return carry

    lax.fori_loop(0, tokens // TILE, lay, 0)
    rows8[pl.ds(tokens * 8, 8), :] = jnp.zeros((8, LANES), F32)


def expert_of(s, tokens):
    return jnp.minimum(s // (tokens // 2 // TILE), ROUTED_EXPERTS)


def expert_forward_kernel(
    order, after, source, slots, b_ref, pc_ref, w_ref, x_ref, y_ref, mix_ref, rows8, done8, tile8, sum8
):
    s = pl.program_id(0)
    tokens = b_ref.shape[0]
    hidden = w_ref.shape[2] // 3
    routed = ROUTED_EXPERTS * (tokens // 2 // TILE)
    e = expert_of(s, tokens)

    @pl.when(s == 0)
    def _():
        lay_rows(b_ref, pc_ref, rows8)
        pick_rows(rows8, tile8, source, after[pl.num_programs(0)])

    def run(x):
        g = dot(x, w_ref[0, :, : 2 * hidden])
        gate, up = g[:, :hidden], g[:, hidden:]
        h = (gate * sigmoid(gate) * up).astype(BF16)
        return dot(h, w_ref[0, :, 2 * hidden:], 1, 1)

    @pl.when(order[s] >= 0)
    def _():
        c0, c1, c2, pc = gathered_columns(tile8, 4)
        x = jnp.concatenate([c0, c1, c2], axis=1).astype(BF16)
        x_ref[...] = x
        gate_column = lane_of(pc, ROUTER + e)
        pick_rows(rows8, tile8, source, after[s])
        y = run(x)
        y_ref[...] = y
        spread_rows(done8, y * gate_column, order[s] * TILE, TILE)

    @pl.when((order[s] < 0) & (s < routed))
    def _():
        x_ref[...] = jnp.zeros_like(x_ref)

    @pl.when(s >= routed)
    def _():
        r = block(s - routed, TILE)
        x = b_ref[r, :]
        x_ref[...] = x
        sum_rows(done8, sum8, slots, (s - routed) * TILE, tokens)
        y = run(x)
        y_ref[...] = y
        shared = y * lane_of(pc_ref[r, :], SHARED)
        for c, part in enumerate(gathered_columns(sum8, D // LANES)):
            cols = slice(c * LANES, (c + 1) * LANES)
            mix_ref[r, cols] = part + shared[:, cols]


def expert_specs(tokens, weights):
    tiles = 5 * tokens // TILE
    full = lambda shape: pl.BlockSpec(shape, lambda s, *_: (0,) * len(shape), pipeline_mode=pl.Buffered(1))
    tile = lambda w: pl.BlockSpec((TILE, w), lambda s, *_: (s, 0))
    weight = pl.BlockSpec((1,) + weights.shape[1:], lambda s, *_: (expert_of(s, tokens), 0, 0))
    most = 2 * tokens // TILE + ROUTED_EXPERTS - 1
    scratch = [
        pltpu.VMEM(((tokens + 1) * 8, LANES), F32), pltpu.VMEM((most * TILE * 8, LANES), F32),
        pltpu.VMEM((TILE * 8, LANES), F32), pltpu.VMEM((TILE * 8, LANES), F32)]
    return tiles, full, tile, weight, scratch


def expert_forward(plan, b, pc, weights):
    tokens = b.shape[0]
    tiles, full, tile, weight, scratch = expert_specs(tokens, weights)
    return pl.pallas_call(
        expert_forward_kernel,
        grid_spec=pltpu.PrefetchScalarGridSpec(
            num_scalar_prefetch=4,
            grid=(tiles,),
            in_specs=[full(b.shape), full(pc.shape), weight],
            out_specs=[tile(D), tile(D), full((tokens, D))],
            scratch_shapes=scratch,
        ),
        out_shape=[
            jax.ShapeDtypeStruct((tiles * TILE, D), BF16),
            jax.ShapeDtypeStruct((tiles * TILE, D), F32),
            jax.ShapeDtypeStruct((tokens, D), F32),
        ],
        compiler_params=params(),
        name="expert_forward",
    )(*plan, b, pc, weights)


def expert_backward_kernel(
    order, after, source, slots, pc_ref, dx_ref, w_ref, x_ref, y_ref, dy_ref, dg_ref, h_ref, acc_ref,
    rows8, done8, tile8, sum8,
):
    s = pl.program_id(0)
    tokens = dx_ref.shape[0]
    hidden = w_ref.shape[2] // 3
    routed = ROUTED_EXPERTS * (tokens // 2 // TILE)
    e = expert_of(s, tokens)
    lanes = lax.broadcasted_iota(jnp.int32, (TILE, LANES), 1)

    @pl.when(s == 0)
    def _():
        lay_rows(dx_ref, pc_ref, rows8)
        pick_rows(rows8, tile8, source, after[pl.num_programs(0)])

    def run(dy):
        dy_ref[...] = dy
        u = w_ref[0, :, : 2 * hidden]
        g = dot(x_ref[...], u)
        gate, up = g[:, :hidden], g[:, hidden:]
        sig = sigmoid(gate)
        silu = gate * sig
        h_ref[...] = (silu * up).astype(BF16)
        dh = dot(dy, w_ref[0, :, 2 * hidden:])
        d_up = (dh * silu).astype(BF16)
        d_gate = (dh * up * (sig * (1.0 + gate * (1.0 - sig)))).astype(BF16)
        dg_ref[:, :hidden] = d_gate
        dg_ref[:, hidden:] = d_up
        return dot(d_gate, u[:, :hidden], 1, 1) + dot(d_up, u[:, hidden:], 1, 1)

    @pl.when(order[s] >= 0)
    def _():
        c0, c1, c2, pc = gathered_columns(tile8, 4)
        dx = jnp.concatenate([c0, c1, c2], axis=1)
        d_value = jnp.sum(y_ref[...] * dx, axis=1, keepdims=True)
        dy = (dx * lane_of(pc, ROUTER + e)).astype(BF16)
        pick_rows(rows8, tile8, source, after[s])
        back = run(dy)
        spread_rows(done8, back, order[s] * TILE, TILE)
        done8[pl.ds(order[s] * TILE * 8 + 3, TILE, stride=8), :] = jnp.where(lanes == ROUTER + e, d_value, 0.0)

    @pl.when((order[s] < 0) & (s < routed))
    def _():
        dy_ref[...] = jnp.zeros_like(dy_ref)
        dg_ref[...] = jnp.zeros_like(dg_ref)
        h_ref[...] = jnp.zeros_like(h_ref)

    @pl.when(s >= routed)
    def _():
        r = block(s - routed, TILE)
        dx = dx_ref[r, :]
        d_value = jnp.sum(y_ref[...] * dx, axis=1, keepdims=True)
        sum_rows(done8, sum8, slots, (s - routed) * TILE, tokens)
        back = run((dx * lane_of(pc_ref[r, :], SHARED)).astype(BF16))
        sums = gathered_columns(sum8, D // LANES + 1)
        for c in range(D // LANES):
            cols = slice(c * LANES, (c + 1) * LANES)
            acc_ref[r, cols] = sums[c] + back[:, cols]
        acc_ref[r, D:] = jnp.where(lanes == SHARED, d_value, sums[-1])


def expert_backward(plan, pc, dx, weights, x, y):
    tokens = dx.shape[0]
    hidden = weights.shape[2] // 3
    tiles, full, tile, weight, scratch = expert_specs(tokens, weights)
    return pl.pallas_call(
        expert_backward_kernel,
        grid_spec=pltpu.PrefetchScalarGridSpec(
            num_scalar_prefetch=4,
            grid=(tiles,),
            in_specs=[full(pc.shape), full(dx.shape), weight, tile(D), tile(D)],
            out_specs=[tile(D), tile(2 * hidden), tile(hidden), full((tokens, D + LANES))],
            scratch_shapes=scratch,
        ),
        out_shape=[
            jax.ShapeDtypeStruct((tiles * TILE, D), BF16),
            jax.ShapeDtypeStruct((tiles * TILE, 2 * hidden), BF16),
            jax.ShapeDtypeStruct((tiles * TILE, hidden), BF16),
            jax.ShapeDtypeStruct((tokens, D + LANES), F32),
        ],
        compiler_params=params(),
        name="expert_backward",
    )(*plan, pc, dx, weights, x, y)


def exchange(part, other, send_sem, recv_sem):
    dp, mp = lax.axis_index("dp"), lax.axis_index("mp")
    barrier = pltpu.get_barrier_semaphore()
    pl.semaphore_signal(barrier, inc=1, device_id=(dp, 1 - mp), device_id_type=MESH)
    pl.semaphore_wait(barrier, 1)

    def copy(i):
        r = block(i, TILE)
        return remote(part.at[r], other.at[r], send_sem.at[i], recv_sem.at[i], dp, 1 - mp)

    def begin(i, carry):
        copy(i).start()
        return carry

    lax.fori_loop(0, part.shape[0] // TILE, begin, 0)
    return lambda i: copy(i).wait()


def exchange_scratch(part):
    tiles = part.shape[0] // TILE
    return [pltpu.VMEM(part.shape, F32), DMA((tiles,)), DMA((tiles,))]


def hankel(base):
    block_rows = jnp.broadcast_to(base, (LANES, 2 * LANES))
    m = pltpu.roll(block_rows, 0, 1, stride=1, stride_axis=0)[:, :LANES]
    lanes = lax.broadcasted_iota(jnp.int32, (LANES, LANES), 1)
    out = pltpu.roll(m, 41, 1)
    out = jnp.where(lanes < 104, pltpu.roll(m, 40, 1), out)
    out = jnp.where(lanes < 96, pltpu.roll(m, 32, 1), out)
    return jnp.where(lanes < 64, m, out)


def loss_piece(x, gain, table, table_t, value_rows, mark_rows, weight):
    scale = lax.rsqrt(jnp.mean(x * x, axis=1, keepdims=True) + norm_eps)
    unit = x * scale
    low = (unit * gain).astype(BF16)
    z = dot(low, table)
    target = jnp.concatenate([hankel(row) for row in value_rows], axis=0)
    valid = jnp.concatenate([hankel(row) for row in mark_rows], axis=0)
    factor = valid * weight
    miss = z - target
    size = jnp.abs(miss)
    huber = jnp.where(
        size <= quadratic_cutoff, 0.5 * miss * miss, quadratic_cutoff * (size - 0.5 * quadratic_cutoff))
    dz = (jnp.clip(miss, -quadratic_cutoff, quadratic_cutoff) * factor).astype(BF16)
    df = dot(dz, table_t)
    dn = df * gain
    dx = scale * (dn - unit * jnp.mean(dn * unit, axis=1, keepdims=True))
    total = lambda v: jnp.sum(v, axis=0, keepdims=True)
    return dx, dot(dz, low, 0, 0), total(df * unit), total(huber * factor)


def loss_kernel(part, x1, vec, table, table_t, values, marks, weight, dx2, d_table, d_gain, loss,
                other, send_sem, recv_sem):
    wait = exchange(part, other, send_sem, recv_sem)
    d_table[...] = jnp.zeros_like(d_table)
    d_gain[...] = jnp.zeros_like(d_gain)
    loss[...] = jnp.zeros_like(loss)
    per = TILE // LANES

    def step(i, carry):
        r = block(i, TILE)
        wait(i)
        dx, dt, dg, fit = loss_piece(
            x1[r, :] + (part[r, :] + other[r, :]), vec[2:3, :], table[...], table_t[...],
            [values[pl.ds(per * i + k, 1), :] for k in range(per)],
            [marks[pl.ds(per * i + k, 1), :] for k in range(per)], weight[...])
        dx2[r, :] = dx
        d_table[...] += dt
        d_gain[...] += dg
        loss[...] += fit
        return carry

    lax.fori_loop(0, part.shape[0] // TILE, step, 0)


def loss_stage(part, x1, vec, table, table_t, values, marks, weight, ident):
    tokens = part.shape[0]
    return pl.pallas_call(
        loss_kernel,
        in_specs=[VMEM] * 8,
        out_specs=[VMEM] * 4,
        out_shape=[
            jax.ShapeDtypeStruct((tokens, D), F32), jax.ShapeDtypeStruct((LANES, D), F32),
            jax.ShapeDtypeStruct((1, D), F32), jax.ShapeDtypeStruct((1, LANES), F32),
        ],
        scratch_shapes=exchange_scratch(part),
        compiler_params=params(collective_id=ident, has_side_effects=True),
        name="loss_stage",
    )(part, x1, vec, table, table_t, values, marks, weight)


def mid_backward_kernel(part, dx2, x1, b, pc, vec, table_t, balance, wo, o, d_table, d_gain3, dx1, do, rest,
                        other, send_sem, recv_sem):
    wait = exchange(part, other, send_sem, recv_sem)
    width = wo.shape[0]
    rest[:width, :] = jnp.zeros((width, D), F32)
    rest[width:, :] = d_table[...]
    rest[width + VECTOR + 2:width + VECTOR + 3, :] = d_gain3[...]
    per = o.shape[2] // TILE

    def step(i, carry):
        r = block(i, TILE)
        wait(i)
        dp = part[r, D:] + other[r, D:] + balance[...]
        p = pc[r, :]
        lanes = lax.broadcasted_iota(jnp.int32, p.shape, 1)
        routed = (lanes >= ROUTER) & (lanes < SHARED)
        weighted = jnp.sum(jnp.where(routed, p * dp, 0.0), axis=1, keepdims=True)
        dl = jnp.where(routed, p * (dp - weighted), jnp.where(lanes == SHARED, dp * p * (1.0 - p), 0.0))
        dl = dl.astype(BF16)
        low = b[r, :]
        rest[width:, :] += dot(dl, low, 0, 0)
        db = part[r, :D] + other[r, :D] + dot(dl, table_t[...])
        x = x1[r, :]
        scale = lax.rsqrt(jnp.mean(x * x, axis=1, keepdims=True) + norm_eps)
        unit = x * scale
        g2 = width + VECTOR + 1
        rest[g2:g2 + 1, :] += jnp.sum(db * unit, axis=0, keepdims=True)
        dn = db * vec[1:2, :]
        dx = dx2[r, :] + scale * (dn - unit * jnp.mean(dn * unit, axis=1, keepdims=True))
        dx1[r, :] = dx
        d_low = dx.astype(BF16)
        n, cols = i // per, block(lax.rem(i, per), TILE, TILE)
        do[n, :, cols] = dot(wo[...], d_low, 1, 1).astype(BF16)
        rest[:width, :] += dot(o[n, :, cols], d_low)
        return carry

    lax.fori_loop(0, part.shape[0] // TILE, step, 0)


def mid_backward(part, dx2, x1, b, pc, vec, table_t, balance, wo, o, d_table, d_gain3, ident):
    tokens = part.shape[0]
    return pl.pallas_call(
        mid_backward_kernel,
        in_specs=[VMEM] * 12,
        out_specs=[VMEM] * 3,
        out_shape=[
            jax.ShapeDtypeStruct((tokens, D), F32), jax.ShapeDtypeStruct(o.shape, BF16),
            jax.ShapeDtypeStruct((wo.shape[0] + LANES, D), F32),
        ],
        scratch_shapes=exchange_scratch(part),
        compiler_params=params(collective_id=ident, has_side_effects=True),
        name="mid_backward",
    )(part, dx2, x1, b, pc, vec, table_t, balance, wo, o, d_table, d_gain3)


SLOTS = 3
HOPS = 2
ACCS = 5


def encode(dest, v):
    width = v.shape[1]
    top = jnp.max(jnp.abs(v), axis=1, keepdims=True)
    power = jnp.ceil(jnp.log2(jnp.maximum(top, 1e-30) * (1.001 / 32767.0)))
    power = jnp.broadcast_to(power, (v.shape[0], LANES))
    inverse = jnp.exp2(-power)
    dest[:, width:] = power.astype(jnp.int32).astype(I16)
    for c in range(width // LANES):
        cols = slice(c * LANES, (c + 1) * LANES)
        dest[:, cols] = jnp.round(v[:, cols] * inverse).astype(jnp.int32).astype(I16)


def decode(source):
    width = source.shape[1] - LANES
    unit = jnp.exp2(source[:, width:].astype(jnp.int32).astype(F32))
    return jnp.concatenate(
        [source[:, c * LANES:(c + 1) * LANES].astype(jnp.int32).astype(F32) * unit for c in range(width // LANES)],
        axis=1)


def backward_kernel(
    xs, dys, dgs, hs, qkvs, dos, lses, a_all, dx1_all, rest, x_ref, wt, vec, cos_ref, sin_ref,
    out, out_small,
    x_in, dy_in, dg_in, h_in, xt, dyt, temp, dw, acc, send1, recv1, send2, recv2, zs_up, zs_dn, up, dn,
    qkv, do_t, lse, a, dx1, dqkv, dk, dv, stack, part, other,
    sm, small_a1, small_b1, small_a2, small_b2, small_up, small_dn,
    load_sem, sem_s1, sem_r1, sem_s2, sem_r2, sem_su, sem_sd, sem_ru, sem_rd,
    attn_sem, dx1_sem, rest_sem, pair_send, pair_recv,
    small_send, small_sa, small_sb, small_r, small_su, small_sd, small_ru, small_rd,
):
    dp, mp, x, y, z = place()
    xp, yp = dp + 1 - 2 * x, dp + 2 - 4 * y
    count = out.shape[0]
    blocks = xs.shape[0]
    hidden = hs.shape[2]
    series, _, length = x_ref.shape
    width = do_t.shape[0]
    heads = width // HEAD
    per = length // TILE

    def loads(n):
        return [
            pltpu.make_async_copy(src.at[n], dst, load_sem.at[i])
            for i, (src, dst) in enumerate(((xs, x_in), (dys, dy_in), (dgs, dg_in), (hs, h_in)))]

    def attn_loads(n):
        pairs = ((qkvs.at[n], qkv), (dos.at[n], do_t), (lses.at[n], lse), (a_all.at[block(n, length)], a))
        return [pltpu.make_async_copy(src, dst, attn_sem.at[i]) for i, (src, dst) in enumerate(pairs)]

    def dx1_load(n):
        return pltpu.make_async_copy(dx1_all.at[block(n, length)], dx1, dx1_sem)

    rest_load = pltpu.make_async_copy(rest, stack.at[pl.ds(3 * width, width + LANES)], rest_sem)
    for copy in loads(0) + attn_loads(0) + [dx1_load(0), rest_load]:
        copy.start()

    barrier = pltpu.get_barrier_semaphore()
    for peer, core in ((xp, mp), (yp, mp), (dp, 1 - mp)):
        pl.semaphore_signal(barrier, inc=1, device_id=(peer, core), device_id_type=MESH)

    @pl.when(z > 0)
    def _():
        pl.semaphore_signal(barrier, inc=1, device_id=(dp - 4, mp), device_id_type=MESH)

    @pl.when(z < 3)
    def _():
        pl.semaphore_signal(barrier, inc=1, device_id=(dp + 4, mp), device_id_type=MESH)

    @pl.when((z > 0) & (z < 3))
    def _():
        pl.semaphore_wait(barrier, 5)

    @pl.when((z == 0) | (z == 3))
    def _():
        pl.semaphore_wait(barrier, 4)

    stack[0:3 * width, :] = jnp.zeros((3 * width, D), F32)

    def shard(slot, i):
        return dw.at[slot, i]


    def weights(n, more):
        for copy in loads(n):
            copy.wait()
        xt[...] = jnp.transpose(x_in[...])
        dyt[...] = jnp.transpose(dy_in[...])

        def wide(j, carry):
            cols = block(j, TILE, TILE)
            v = dot(xt[...], dg_in[:, cols])
            temp[:, cols] = temp[:, cols] + v if more else v
            return carry

        def tall(j, carry):
            there = pl.ds(pl.multiple_of(2 * hidden + j * TILE, TILE), TILE)
            v = dot(dyt[...], h_in[:, block(j, TILE, TILE)])
            temp[:, there] = temp[:, there] + v if more else v
            return carry

        lax.fori_loop(0, 2 * hidden // TILE, wide, 0)
        lax.fori_loop(0, hidden // TILE, tall, 0)

        @pl.when(n + 1 < blocks)
        def _():
            for copy in loads(n + 1):
                copy.start()

    def begin(c):
        k, slot = lax.rem(c, 2), lax.rem(c, SLOTS)
        weights(c, False)

        @pl.when(c == count - 1)
        def _():
            weights(c + 1, True)

        @pl.when(c >= SLOTS)
        def _():
            done(send1.at[slot], sem_s1.at[slot])

        def pack(i, carry):
            m, n = i // 2, lax.rem(i, 2)
            gone = m * 4 + jnp.where(k == 0, n * 2 + 1 - x, (1 - y) * 2 + n)
            kept = m * 4 + jnp.where(k == 0, n * 2 + x, y * 2 + n)
            encode(send1.at[slot, i], temp[block(gone, SHARD), :])
            dw[slot, i] = temp[block(kept, SHARD), :]
            return carry

        lax.fori_loop(0, 8, pack, 0)
        remote(send1.at[slot], recv1.at[c], sem_s1.at[slot], sem_r1.at[c], jnp.where(k == 0, xp, yp), mp).start()

    def fold(c):
        k, slot, hop = lax.rem(c, 2), lax.rem(c, SLOTS), lax.rem(c, HOPS)
        o = jnp.where(k == 0, y, x)
        done(recv1.at[c], sem_r1.at[c])

        @pl.when(c >= HOPS)
        def _():
            done(send2.at[hop], sem_s2.at[hop])

        def add(m, carry):
            gone, kept = m * 2 + 1 - o, m * 2 + o
            encode(send2.at[hop, m], dw[slot, gone] + decode(recv1.at[c, gone]))
            acc[lax.rem(c, ACCS), m] = dw[slot, kept] + decode(recv1.at[c, kept])
            return carry

        lax.fori_loop(0, 4, add, 0)
        remote(send2.at[hop], recv2.at[c], sem_s2.at[hop], sem_r2.at[c], jnp.where(k == 0, yp, xp), mp).start()

    def climb(c, t, relay):
        slot = lax.rem(c, HOPS)
        v = acc[lax.rem(c, ACCS), t]
        if relay:
            done(up.at[c, t - 1], sem_ru.at[c, t - 1])
            v = v + decode(up.at[c, t - 1])

        @pl.when(c >= HOPS)
        def _():
            done(zs_up.at[slot, t - 1], sem_su.at[slot, t - 1])
        encode(zs_up.at[slot, t - 1], v)
        remote(zs_up.at[slot, t - 1], up.at[c, t - 1], sem_su.at[slot, t - 1], sem_ru.at[c, t - 1], dp + 4, mp).start()

    def drop(c, t, relay):
        slot = lax.rem(c, HOPS)
        v = acc[lax.rem(c, ACCS), t]
        if relay:
            done(dn.at[c, t], sem_rd.at[c, t])
            v = v + decode(dn.at[c, t])

        @pl.when(c >= HOPS)
        def _():
            done(zs_dn.at[slot, t], sem_sd.at[slot, t])
        encode(zs_dn.at[slot, t], v)
        remote(zs_dn.at[slot, t], dn.at[c, t], sem_sd.at[slot, t], sem_rd.at[c, t], dp - 4, mp).start()

    def line_a(c):
        done(recv2.at[c], sem_r2.at[c])
        there = lax.rem(c, ACCS)

        def add(m, carry):
            acc[there, m] = acc[there, m] + decode(recv2.at[c, m])
            return carry

        lax.fori_loop(0, 4, add, 0)
        out[c] = acc[there, z]

        @pl.when(z == 0)
        def _():
            for t in (3, 2, 1):
                climb(c, t, False)

        @pl.when(z == 3)
        def _():
            for t in (0, 1, 2):
                drop(c, t, False)

    def line_b(c):
        @pl.when(z == 1)
        def _():
            for t in (3, 2):
                climb(c, t, True)

        @pl.when(z == 2)
        def _():
            for t in (0, 1):
                drop(c, t, True)

    def line_c(c):
        @pl.when(z == 2)
        def _():
            climb(c, 3, True)

        @pl.when(z == 1)
        def _():
            drop(c, 0, True)

    def finish(c):
        @pl.when(z > 0)
        def _():
            done(up.at[c, z - 1], sem_ru.at[c, z - 1])
            out[c] = out[c] + decode(up.at[c, z - 1])

        @pl.when(z < 3)
        def _():
            done(dn.at[c, z], sem_rd.at[c, z])
            out[c] = out[c] + decode(dn.at[c, z])


    def pair(n):
        r = block(n, length)
        return remote(part, other.at[r], pair_send.at[n], pair_recv.at[n], dp, 1 - mp)

    def head(p):
        n, h = p // heads, lax.rem(p, heads)

        @pl.when(h == 0)
        def _():
            for copy in attn_loads(n):
                copy.wait()
        backward_head(h, width, qkv, do_t, lse, cos_ref[...], sin_ref[...], dqkv, dk, dv)

        @pl.when(h == heads - 1)
        def _():
            stack[0:3 * width, :] = stack[0:3 * width, :] + dot(dqkv[...], a[...])
            part[...] = dot(dqkv[...], wt[0:3 * width, :], 0, 0)
            pair(n).start()

            @pl.when(n + 1 < series)
            def _():
                for copy in attn_loads(n + 1):
                    copy.start()

    def embed(m):
        n, i = m // per, lax.rem(m, per)
        t = block(i, TILE, TILE)

        @pl.when(m == 0)
        def _():
            rest_load.wait()

        @pl.when(i == 0)
        def _():
            pair(n).wait()
            dx1_load(n).wait()
        da = part[t, :] + other[block(m, TILE), :]
        sums = embed_backward_piece(x_ref[n, :, t], da, dx1[t, :], vec)
        for row, value in zip((0, 3, 4), sums):
            there = slice(4 * width + VECTOR + row, 4 * width + VECTOR + row + 1)
            stack[there, :] = stack[there, :] + value

        @pl.when((i == per - 1) & (n + 1 < series))
        def _():
            dx1_load(n + 1).start()


    half = 512
    total_width = sm.shape[-1]
    ca, cb = pl.ds(0, half), pl.ds(half, total_width - half)

    def small_begin():
        sm[...] = jnp.transpose(stack[...]).reshape(sm.shape)
        remote(sm.at[:, :, 1 - x, :, ca], small_a1, small_sa, small_r.at[0], xp, mp).start()
        remote(sm.at[:, 1 - y, :, :, cb], small_b1, small_sb, small_r.at[1], yp, mp).start()

    def small_fold():
        done(small_a1, small_r.at[0])
        done(small_b1, small_r.at[1])
        for m in range(4):
            for n in range(2):
                sm[m, n, x, :, ca] = sm[m, n, x, :, ca] + small_a1[m, n]
                sm[m, y, n, :, cb] = sm[m, y, n, :, cb] + small_b1[m, n]
        remote(sm.at[:, 1 - y, x, :, ca], small_a2, small_send.at[0], small_r.at[2], yp, mp).start()
        remote(sm.at[:, y, 1 - x, :, cb], small_b2, small_send.at[1], small_r.at[3], xp, mp).start()

    def small_climb(t, relay):
        if relay:
            done(small_up.at[t - 1], small_ru.at[t - 1])
            sm[t, y, x] = sm[t, y, x] + small_up[t - 1]
        remote(sm.at[t, y, x], small_up.at[t - 1], small_su.at[t - 1], small_ru.at[t - 1], dp + 4, mp).start()

    def small_drop(t, relay):
        if relay:
            done(small_dn.at[t], small_rd.at[t])
            sm[t, y, x] = sm[t, y, x] + small_dn[t]
        remote(sm.at[t, y, x], small_dn.at[t], small_sd.at[t], small_rd.at[t], dp - 4, mp).start()

    def small_a():
        done(small_a2, small_r.at[2])
        done(small_b2, small_r.at[3])
        for m in range(4):
            sm[m, y, x, :, ca] = sm[m, y, x, :, ca] + small_a2[m]
            sm[m, y, x, :, cb] = sm[m, y, x, :, cb] + small_b2[m]
        out_small[...] = sm[z, y, x]

        @pl.when(z == 0)
        def _():
            for t in (3, 2, 1):
                small_climb(t, False)

        @pl.when(z == 3)
        def _():
            for t in (0, 1, 2):
                small_drop(t, False)

    def small_b():
        @pl.when(z == 1)
        def _():
            for t in (3, 2):
                small_climb(t, True)

        @pl.when(z == 2)
        def _():
            for t in (0, 1):
                small_drop(t, True)

    def small_c():
        @pl.when(z == 2)
        def _():
            small_climb(3, True)

        @pl.when(z == 1)
        def _():
            small_drop(0, True)

    def small_finish():
        @pl.when(z > 0)
        def _():
            done(small_up.at[z - 1], small_ru.at[z - 1])
            out_small[...] = out_small[...] + small_up[z - 1]

        @pl.when(z < 3)
        def _():
            done(small_dn.at[z], small_rd.at[z])
            out_small[...] = out_small[...] + small_dn[z]


    def at(i, first, number, run):
        @pl.when((i >= first) & (i < first + number))
        def _():
            run(i - first)

    small_first = count

    def step(i, carry):
        at(i, 0, count, begin)

        @pl.when(i < series * heads // 2)
        def _():
            def two(q, carry):
                head(2 * i + q)
                return carry
            lax.fori_loop(0, 2, two, 0)

        for n in range(series):
            @pl.when((i >= 3 + n * 3) & (i < 3 + n * 3 + per // 2))
            def _():
                def two(q, carry):
                    embed(n * per + 2 * (i - 3 - n * 3) + q)
                    return carry
                lax.fori_loop(0, 2, two, 0)
        at(i, small_first, 1, lambda _: small_begin())
        at(i, 2, count, fold)
        at(i, small_first + 1, 1, lambda _: small_fold())
        at(i, 4, count, line_a)
        at(i, small_first + 2, 1, lambda _: small_a())
        at(i, 5, count, line_b)
        at(i, small_first + 3, 1, lambda _: small_b())
        at(i, 6, count, line_c)
        at(i, small_first + 4, 1, lambda _: small_c())
        at(i, 7, count, finish)
        at(i, small_first + 5, 1, lambda _: small_finish())
        return carry

    lax.fori_loop(0, count + 7, step, 0)

    for slot in range(SLOTS):
        done(send1.at[slot], sem_s1.at[slot])
    for slot in range(HOPS):
        done(send2.at[slot], sem_s2.at[slot])
        for t in (1, 2, 3):
            @pl.when(z < t)
            def _():
                done(zs_up.at[slot, t - 1], sem_su.at[slot, t - 1])
        for t in (0, 1, 2):
            @pl.when(z > t)
            def _():
                done(zs_dn.at[slot, t], sem_sd.at[slot, t])
    done(small_a1, small_sa)
    done(small_b1, small_sb)
    done(small_a2, small_send.at[0])
    done(small_b2, small_send.at[1])
    for t in (1, 2, 3):
        @pl.when(z < t)
        def _():
            done(small_up.at[t - 1], small_su.at[t - 1])
    for t in (0, 1, 2):
        @pl.when(z > t)
        def _():
            done(small_dn.at[t], small_sd.at[t])


def backward_near(xs, dys, dgs, hs, qkv, do, lse, a, dx1, rest, x, wt, vec, cos, sin, ident):
    capacity, hidden = hs.shape[1], hs.shape[2]
    series, rows, length = qkv.shape
    heads_width = rows // 3
    count = ROUTED_EXPERTS + 1
    width = 3 * hidden
    coded = width + LANES
    small = 4 * heads_width + LANES
    tokens = series * length
    v = pltpu.VMEM
    return pl.pallas_call(
        backward_kernel,
        in_specs=[ANY] * 10 + [VMEM] * 5,
        out_specs=[VMEM] * 2,
        out_shape=[
            jax.ShapeDtypeStruct((count, SHARD, width), F32), jax.ShapeDtypeStruct((SHARD, small), F32)],
        scratch_shapes=[
            v((capacity, D), BF16), v((capacity, D), BF16), v((capacity, 2 * hidden), BF16), v((capacity, hidden), BF16),
            v((D, capacity), BF16), v((D, capacity), BF16),
            v((D, width), F32), v((SLOTS, 8, SHARD, width), F32), v((ACCS, 4, SHARD, width), F32),
            v((SLOTS, 8, SHARD, coded), I16), v((count, 8, SHARD, coded), I16),
            v((HOPS, 4, SHARD, coded), I16), v((count, 4, SHARD, coded), I16),
            v((HOPS, 3, SHARD, coded), I16), v((HOPS, 3, SHARD, coded), I16),
            v((count, 3, SHARD, coded), I16), v((count, 3, SHARD, coded), I16),
            v((rows, length), BF16), v((heads_width, length), BF16), v((8, length), F32), v((length, D), BF16),
            v((length, D), F32), v((rows, length), BF16), v((length, HEAD), F32), v((length, HEAD), F32),
            v((small, D), F32), v((length, D), F32), v((tokens, D), F32),
            v((4, 2, 2, SHARD, small), F32),
            v((4, 2, SHARD, 512), F32), v((4, 2, SHARD, small - 512), F32),
            v((4, SHARD, 512), F32), v((4, SHARD, small - 512), F32),
            v((3, SHARD, small), F32), v((3, SHARD, small), F32),
            DMA((4,)), DMA((SLOTS,)), DMA((count,)), DMA((HOPS,)), DMA((count,)),
            DMA((HOPS, 3)), DMA((HOPS, 3)), DMA((count, 3)), DMA((count, 3)),
            DMA((4,)), DMA, DMA, DMA((series,)), DMA((series,)),
            DMA((2,)), DMA, DMA, DMA((4,)), DMA((3,)), DMA((3,)), DMA((3,)), DMA((3,)),
        ],
        compiler_params=pltpu.CompilerParams(
            vmem_limit_bytes=67_000_000, collective_id=ident, has_side_effects=True),
        name="backward_near",
    )(xs, dys, dgs, hs, qkv, do, lse, a, dx1, rest, x, wt, vec, cos, sin)


def all_kernel(value, out, send_sem, recv_sem):
    dp, mp = lax.axis_index("dp"), lax.axis_index("mp")
    me = dp * 2 + mp
    meet_everyone(dp, mp)

    def tell(k, carry):
        peer = lax.rem(me + k, 32)
        remote(value, out.at[me], send_sem, recv_sem, peer // 2, lax.rem(peer, 2)).start()
        return carry

    lax.fori_loop(1, 32, tell, 0)
    out[me] = value[...]
    view = out.at[pl.ds(0, 31)]
    done(view, recv_sem)
    done(view, send_sem)


def all_blocks(value, ident):
    return pl.pallas_call(
        all_kernel,
        in_specs=[VMEM],
        out_specs=VMEM,
        out_shape=jax.ShapeDtypeStruct((32,) + value.shape, value.dtype),
        scratch_shapes=[DMA, DMA],
        compiler_params=pltpu.CompilerParams(collective_id=ident, has_side_effects=True),
        name="all_blocks",
    )(value)


def rope_rows(length):
    halfway = HEAD // 2
    frequency = rope_base ** (-2.0 * jnp.arange(halfway, dtype=F32) / HEAD)
    angles = frequency[:, None] * jnp.arange(length, dtype=F32)[None, :]
    return jnp.cos(angles), jnp.sin(angles)


def hankel_rows(track):
    length = track.shape[1]
    padded = jnp.pad(track, ((0, 0), (63, 2 * LANES)))
    first = padded[:, :length].reshape(-1, LANES)[:, ::-1]
    second = padded[:, LANES:LANES + length].reshape(-1, LANES)[:, ::-1]
    return jnp.concatenate([first, second], axis=1)


def table_columns(read, vec):
    parts, end = [], read.shape[1]
    for horizon in horizons[::-1]:
        parts.append(read[:, end - horizon:end][:, ::-1])
        end -= horizon
    gap = jnp.zeros((read.shape[0], ROUTER - sum(horizons)), read.dtype)
    tail = jnp.zeros((read.shape[0], LANES - VECTOR - vec.shape[1]), read.dtype)
    return jnp.concatenate(parts + [gap, read[:, :ROUTED_EXPERTS + 1], vec, tail], axis=1)


def table_columns_back(table):
    parts, begin = [], 0
    for horizon in horizons[::-1]:
        parts.append(table[:, begin:begin + horizon][:, ::-1])
        begin += horizon
    return jnp.concatenate([table[:, ROUTER:VECTOR]] + parts[::-1], axis=1)


def dispatch(route_rows, capacity):
    tokens = route_rows.shape[0]
    experts = jnp.arange(ROUTED_EXPERTS, dtype=jnp.int32)
    member = jnp.any(route_rows[:, :, None] == experts[None, None, :], axis=1)
    count = jnp.cumsum(member.astype(jnp.int32), axis=0)
    total = count[-1]
    place = jnp.where(member, count - 1, -1)
    high = (place[:, :, None] // LANES == jnp.arange(capacity // LANES)[None, None, :]) & member[:, :, None]
    low = (place[:, :, None] % LANES == jnp.arange(LANES)[None, None, :]).astype(BF16)
    token = jnp.arange(tokens, dtype=jnp.int32)
    left = jnp.concatenate(
        [jnp.where(high, part[:, None, None], 0).astype(BF16) for part in (token // 16, token % 16)], axis=2)
    found = jnp.einsum("teh,tel->ehl", left, low, preferred_element_type=F32)
    half = capacity // LANES
    source = (found[:, :half] * 16.0 + found[:, half:]).reshape(ROUTED_EXPERTS, capacity).astype(jnp.int32)
    source = jnp.where(jnp.arange(capacity, dtype=jnp.int32)[None, :] < total[:, None], source, tokens)
    source = jnp.concatenate([source.reshape(-1), jnp.full((TILE,), tokens, jnp.int32)]) * 8
    per = capacity // TILE
    routed = ROUTED_EXPERTS * per
    tile = jnp.arange(routed + tokens // TILE, dtype=jnp.int32)
    need = (total + TILE - 1) // TILE
    begin = jnp.sum(jnp.where(experts[None, :] < experts[:, None], need[None, :], 0), axis=1)
    mine = jnp.minimum(tile // per, ROUTED_EXPERTS - 1)[:, None] == experts[None, :]
    used = (tile < routed) & (tile % per < jnp.sum(jnp.where(mine, need[None, :], 0), axis=1))
    order = jnp.where(used, jnp.sum(jnp.where(mine, begin[None, :], 0), axis=1) + tile % per, -1)
    next_tile = jnp.concatenate([tile, jnp.full((1,), -1, jnp.int32)])
    later = used[None, :] & (tile[None, :] > next_tile[:, None])
    after = jnp.min(jnp.where(later, tile[None, :], routed), axis=1) * TILE
    slot = (begin[None, :] * TILE + count - 1) * 8
    slots = jnp.sum(jnp.where(route_rows[:, :, None] == experts[None, None, :], slot[:, None, :], 0), axis=2)
    return total, (order, after, source, slots.T.reshape(-1))


def adam_update(master, moment, square, gradient, factor, bias_one, bias_two, step_rate):
    clipped = gradient * factor
    new_moment = beta_one * moment + (1.0 - beta_one) * clipped
    new_square = beta_two * square + (1.0 - beta_two) * clipped * clipped
    updated = master - step_rate * (
        new_moment / bias_one / (jnp.sqrt(new_square / bias_two) + adam_eps) + decay_rate * master
    )
    return (updated, new_moment, new_square)


def on_device(
    series, observed, routes, step_count,
    joint_proj, joint_moment, joint_square,
    mixer_proj, mixer_moment, mixer_square,
    upward_proj, upward_moment, upward_square,
    downward_proj, downward_moment, downward_square,
    readout, readout_moment, readout_square,
    vectors, vectors_moment, vectors_square,
):
    dp_count = lax.axis_size("dp")
    mp_count = lax.axis_size("mp")
    shard = joint_proj.shape[1]
    width = joint_proj.shape[2]
    hidden = upward_proj.shape[3]
    experts = upward_proj.shape[0]
    series_count, length = series.shape
    tokens = series_count * length
    capacity = tokens // 2

    small_own = jnp.concatenate(
        [joint_proj[k].astype(BF16) for k in range(3)]
        + [mixer_proj.T.astype(BF16), table_columns(readout.astype(BF16), vectors.T.astype(BF16))], axis=1)
    big_own = jnp.concatenate(
        [upward_proj.astype(BF16).reshape(experts, shard, 2 * hidden), downward_proj.transpose(0, 2, 1).astype(BF16)],
        axis=2)
    marks = observed.astype(F32)
    expert_here, plan = dispatch(routes.reshape(tokens, 2), capacity)
    point = jnp.arange(length, dtype=F32)
    head_here = jnp.stack(
        [jnp.sum(jnp.sum(marks, axis=0) * jnp.minimum(point, float(horizon))) for horizon in horizons])
    tally = jnp.pad(jnp.concatenate([expert_here.astype(F32), head_here]), (0, LANES - 12))
    tally = jnp.broadcast_to(tally[None], (8, LANES))
    cos, sin = rope_rows(length)
    x = (series * marks).reshape(series_count, 1, length)

    big, wt, vec, table, a, qkv, lse, o, x1, b, pc, pr_total, tallies = forward_near(
        small_own, big_own, tally, x, cos, sin, width, 0)
    wo, table_t = wt[3 * width:4 * width], wt[4 * width:]
    tally = jnp.sum(tallies[:, 0], axis=0) / mp_count
    expert_count, head_count = tally[:ROUTED_EXPERTS], tally[ROUTED_EXPERTS:ROUTED_EXPERTS + 4]
    total_tokens = tokens * dp_count

    xs, ys, mixed = expert_forward(plan, b, pc, big)
    head_weight = jnp.concatenate(
        [jnp.zeros((horizon,), F32) + 0.25 / head_count[3 - index] for index, horizon in enumerate(horizons[::-1])])
    head_weight = jnp.pad(head_weight, (0, LANES - head_weight.shape[0]))[None]
    dx2, d_table, d_gain3, fit = loss_stage(
        mixed, x1, vec, table, table_t, hankel_rows(series), hankel_rows(marks), head_weight, 1)
    dys, dgs, hs, back = expert_backward(plan, pc, dx2, big, xs, ys)
    balance = aux_factor * ROUTED_EXPERTS * expert_count / total_tokens / total_tokens
    balance = jnp.pad(balance, (ROUTER, LANES - SHARED))[None]
    local_loss = jnp.sum(fit) + jnp.sum(pr_total * balance)
    dx1, do, rest = mid_backward(back, dx2, x1, b, pc, vec, table_t, balance, wo, o, d_table, d_gain3, 2)
    xs, dys, dgs, hs = [v.reshape(-1, capacity, v.shape[1]) for v in (xs, dys, dgs, hs)]
    big_red, small_red = backward_near(xs, dys, dgs, hs, qkv, do, lse, a, dx1, rest, x, wt, vec, cos, sin, 3)

    attn_red, table_red = small_red[:, :4 * width], small_red[:, 4 * width:]
    squares = (
        jnp.sum(big_red * big_red) + jnp.sum(attn_red * attn_red) + jnp.sum(table_red * table_red) / mp_count
    )
    pair = jnp.pad(jnp.stack([squares, local_loss / mp_count]), (0, LANES - 2))
    pair = jnp.sum(all_blocks(jnp.broadcast_to(pair[None], (8, LANES)), 4)[:, 0], axis=0)
    grad_norm, loss_total = jnp.sqrt(pair[0]), pair[1]

    factor = clip_limit / (grad_norm + 1e-06)
    steps_taken = step_count[0].astype(F32)
    bias_one = 1.0 - beta_one**steps_taken
    bias_two = 1.0 - beta_two**steps_taken

    def update(master, moment, square, gradient, rate=matrix_rate):
        return adam_update(master, moment, square, gradient, factor, bias_one, bias_two, rate)

    joint_red = jnp.stack([attn_red[:, k * width:(k + 1) * width] for k in range(3)], axis=0)
    mixer_red = attn_red[:, 3 * width:].T
    upward_red = big_red[:, :, :2 * hidden].reshape(upward_proj.shape)
    downward_red = big_red[:, :, 2 * hidden:].transpose(0, 2, 1)
    return (
        loss_total,
        grad_norm,
        *update(joint_proj, joint_moment, joint_square, joint_red),
        *update(mixer_proj, mixer_moment, mixer_square, mixer_red),
        *update(upward_proj, upward_moment, upward_square, upward_red),
        *update(downward_proj, downward_moment, downward_square, downward_red),
        *update(readout, readout_moment, readout_square, table_columns_back(table_red)),
        *update(vectors, vectors_moment, vectors_square, table_red[:, VECTOR:VECTOR + 5].T, vector_rate),
    )


def rms_scale(tensor, gain_row):
    return (
        tensor * lax.rsqrt(jnp.mean(tensor * tensor, axis=-1, keepdims=True) + norm_eps) * gain_row
    )


def rope_tables(length, columns):
    halfway = columns // 2
    frequency = rope_base ** (-2.0 * jnp.arange(halfway, dtype=jnp.float32) / columns)
    angles = jnp.arange(length, dtype=jnp.float32)[:, None] * frequency[None, :]
    return (jnp.cos(angles), jnp.sin(angles))


def rotate(tensor, cosine_table, sine_table):
    halfway = tensor.shape[-1] // 2
    front_part = tensor[..., :halfway]
    back_part = tensor[..., halfway:]
    return jnp.concatenate(
        [
            front_part * cosine_table - back_part * sine_table,
            back_part * cosine_table + front_part * sine_table,
        ],
        axis=-1,
    )


def swiglu(tensor):
    halfway = tensor.shape[-1] // 2
    return jax.nn.silu(tensor[..., :halfway]) * tensor[..., halfway:]


def targets_of(series, observed):
    row_count, length = series.shape
    longest = max(horizons)
    padded_values = jnp.concatenate([series, jnp.zeros((row_count, longest), jnp.float32)], axis=1)
    padded_marks = jnp.concatenate(
        [observed.astype(jnp.float32), jnp.zeros((row_count, longest), jnp.float32)], axis=1
    )
    value_window = jnp.stack(
        [padded_values[:, 1 + offset : 1 + offset + length] for offset in range(longest)], axis=-1
    )
    mark_window = jnp.stack(
        [padded_marks[:, 1 + offset : 1 + offset + length] for offset in range(longest)], axis=-1
    )
    observed_future_series = jnp.concatenate(
        [value_window[..., :horizon] for horizon in horizons], axis=-1
    )
    valid_mask = jnp.concatenate([mark_window[..., :horizon] for horizon in horizons], axis=-1)
    return (
        observed_future_series.reshape(row_count * length, -1),
        valid_mask.reshape(row_count * length, -1),
    )


def head_counts(valid_mask):
    beginnings = [sum(horizons[:index]) for index in range(len(horizons))]
    return jnp.stack(
        [
            jnp.sum(valid_mask[:, beginning : beginning + horizon])
            for beginning, horizon in zip(beginnings, horizons)
        ]
    )


def head_weights(head_count):
    return jnp.concatenate(
        [
            jnp.zeros((horizon,), jnp.float32) + 0.25 / head_count[index]
            for index, horizon in enumerate(horizons)
        ]
    )


def dispatch_plan(route_rows, experts, capacity):
    flat_routes = route_rows.reshape(-1)
    entries = flat_routes.shape[0]
    onehot = (flat_routes[:, None] == jnp.arange(experts, dtype=jnp.int32)[None, :]).astype(
        jnp.int32
    )
    position = jnp.sum(jnp.cumsum(onehot, axis=0) * onehot, axis=1) - 1
    slot_index = flat_routes * capacity + position
    source = (
        jnp.full((experts * capacity,), entries, jnp.int32)
        .at[slot_index]
        .set(jnp.arange(entries, dtype=jnp.int32))
    )
    return (slot_index, source)


def split_heads(matrix, series_count, length):
    return matrix.reshape(series_count, length, matrix.shape[1] // HEAD, HEAD).transpose(0, 2, 1, 3)


def merge_heads(tensor):
    series_count, heads_here, length, head_size = tensor.shape
    return tensor.transpose(0, 2, 1, 3).reshape(series_count * length, heads_here * head_size)


def block_scores(query_block, key_heads, offset, length):
    block_rows = query_block.shape[1]
    scores = jnp.einsum(
        "hqe,hke->hqk", query_block, key_heads, preferred_element_type=jnp.float32
    ) * HEAD ** (-0.5)
    allowed = (offset + jnp.arange(block_rows))[:, None] >= jnp.arange(length)[None, :]
    return jnp.where(allowed[None], scores, -1e30)


def attend_forward(pieces):
    query_heads, key_heads, value_heads = pieces
    length = query_heads.shape[1]
    block_rows = min(length, 512)
    outputs = []
    totals = []
    for offset in range(0, length, block_rows):
        scores = block_scores(
            query_heads[:, offset : offset + block_rows], key_heads, offset, length
        )
        row_peak = jnp.max(scores, axis=-1, keepdims=True)
        exponent = jnp.exp(scores - row_peak)
        row_mass = jnp.sum(exponent, axis=-1, keepdims=True)
        outputs.append(
            jnp.einsum(
                "hqk,hke->hqe",
                (exponent / row_mass).astype(jnp.bfloat16),
                value_heads,
                preferred_element_type=jnp.float32,
            )
        )
        totals.append(row_peak + jnp.log(row_mass))
    return (jnp.concatenate(outputs, axis=1), jnp.concatenate(totals, axis=1))


def attend_backward(pieces):
    query_heads, key_heads, value_heads, grads_out, totals = pieces
    length = query_heads.shape[1]
    block_rows = min(length, 512)
    key_grad = jnp.zeros(key_heads.shape, jnp.float32)
    value_grad = jnp.zeros(value_heads.shape, jnp.float32)
    query_grads = []
    for offset in range(0, length, block_rows):
        query_block = query_heads[:, offset : offset + block_rows]
        grad_block = grads_out[:, offset : offset + block_rows]
        weights = jnp.exp(
            block_scores(query_block, key_heads, offset, length)
            - totals[:, offset : offset + block_rows]
        )
        grad_weights = jnp.einsum(
            "hqe,hke->hqk", grad_block, value_heads, preferred_element_type=jnp.float32
        )
        score_grad = (
            weights
            * (grad_weights - jnp.sum(weights * grad_weights, axis=-1, keepdims=True))
            * HEAD ** (-0.5)
        ).astype(jnp.bfloat16)
        query_grads.append(
            jnp.einsum("hqk,hke->hqe", score_grad, key_heads, preferred_element_type=jnp.float32)
        )
        key_grad = key_grad + jnp.einsum(
            "hqk,hqe->hke", score_grad, query_block, preferred_element_type=jnp.float32
        )
        value_grad = value_grad + jnp.einsum(
            "hqk,hqe->hke",
            weights.astype(jnp.bfloat16),
            grad_block,
            preferred_element_type=jnp.float32,
        )
    return (jnp.concatenate(query_grads, axis=1), key_grad, value_grad)


def branch_total(partial_sum):
    return lax.psum(partial_sum, "mp")


def input_total(partial_sum):
    return lax.psum(partial_sum, "mp")


def on_device_wide(
    series,
    observed,
    routes,
    step_count,
    joint_proj,
    joint_moment,
    joint_square,
    mixer_proj,
    mixer_moment,
    mixer_square,
    upward_proj,
    upward_moment,
    upward_square,
    downward_proj,
    downward_moment,
    downward_square,
    readout,
    readout_moment,
    readout_square,
    vectors,
    vectors_moment,
    vectors_square,
):
    dp_count = lax.axis_size("dp")
    hidden_local = upward_proj.shape[3]
    joint_full, mixer_full, upward_full, downward_full, readout_complete, vector_full = (
        lax.all_gather(joint_proj.astype(jnp.bfloat16), "dp", axis=1, tiled=True),
        lax.all_gather(mixer_proj.astype(jnp.bfloat16), "dp", axis=1, tiled=True),
        lax.all_gather(upward_proj.astype(jnp.bfloat16), "dp", axis=1, tiled=True),
        lax.all_gather(downward_proj.astype(jnp.bfloat16), "dp", axis=2, tiled=True),
        lax.all_gather(readout.astype(jnp.bfloat16), "dp", axis=0, tiled=True),
        lax.all_gather(vectors.astype(jnp.bfloat16), "dp", axis=1, tiled=True),
    )
    up_local = upward_full.reshape(upward_full.shape[0], D, -1)
    shared_up_weight = up_local[-1]
    shared_down_weight = downward_full[-1]
    expert_up = up_local[:ROUTED_EXPERTS]
    expert_down = downward_full[:ROUTED_EXPERTS]
    gain_rows = vector_full.astype(jnp.float32)
    series_count, length = series.shape
    entries = series_count * length
    route_rows = routes.reshape(entries, 2)
    onehot = route_rows[:, :, None] == jnp.arange(ROUTED_EXPERTS, dtype=jnp.int32)[None, None, :]
    observed_future_series, valid_mask = targets_of(series, observed)
    expert_count, head_count = lax.psum(
        (jnp.sum(onehot.astype(jnp.float32), axis=(0, 1)), head_counts(valid_mask)), "dp"
    )
    total_tokens = entries * dp_count
    inputs = (series * observed.astype(jnp.float32)).reshape(entries, 1)

    def embed(gate_vector, up_vector):
        return jax.nn.silu(inputs * gate_vector) * (inputs * up_vector)

    embedded, embed_back = jax.vjp(embed, gain_rows[3], gain_rows[4])
    normed_one, norm_one_back = jax.vjp(rms_scale, embedded, gain_rows[0])
    first_input = normed_one.astype(jnp.bfloat16)
    projected = jnp.einsum(
        "td,cde->cte", first_input, joint_full, preferred_element_type=jnp.float32
    )
    cosine_table, sine_table = rope_tables(length, HEAD)
    query_heads = rotate(
        split_heads(projected[0], series_count, length), cosine_table, sine_table
    ).astype(jnp.bfloat16)
    key_heads = rotate(
        split_heads(projected[1], series_count, length), cosine_table, sine_table
    ).astype(jnp.bfloat16)
    value_heads = split_heads(projected[2], series_count, length).astype(jnp.bfloat16)
    attended, totals = lax.map(attend_forward, (query_heads, key_heads, value_heads))
    attended_low = merge_heads(attended).astype(jnp.bfloat16)
    after_attn = embedded + branch_total(
        jnp.dot(attended_low, mixer_full, preferred_element_type=jnp.float32)
    )
    normed_two, norm_two_back = jax.vjp(rms_scale, after_attn, gain_rows[1])
    second_input = normed_two.astype(jnp.bfloat16)
    logits = jnp.dot(
        second_input, readout_complete[:, : ROUTED_EXPERTS + 1], preferred_element_type=jnp.float32
    )

    def gating(logit_rows):
        probabilities = jax.nn.softmax(logit_rows[:, :ROUTED_EXPERTS], axis=-1)
        chosen = jnp.sum(jnp.where(onehot, probabilities[:, None, :], 0.0), axis=-1)
        balance = (
            aux_factor
            * ROUTED_EXPERTS
            * jnp.sum(expert_count / total_tokens * jnp.sum(probabilities, axis=0) / total_tokens)
        )
        return (chosen, jax.nn.sigmoid(logit_rows[:, ROUTED_EXPERTS]), balance)

    (gate_values, shared_gate, balance), gating_back = jax.vjp(gating, logits)
    capacity = entries // 2
    slot_index, source = dispatch_plan(route_rows, ROUTED_EXPERTS, capacity)
    token_of = source // 2
    padded_input = jnp.concatenate([second_input, jnp.zeros((1, D), jnp.bfloat16)], axis=0)
    gathered = padded_input[token_of].reshape(ROUTED_EXPERTS, capacity, D)
    gate_up = jnp.einsum("ecd,edf->ecf", gathered, expert_up, preferred_element_type=jnp.float32)
    hidden_f, swiglu_back = jax.vjp(swiglu, gate_up)
    hidden = hidden_f.astype(jnp.bfloat16)
    expert_out = jnp.einsum(
        "ecf,efd->ecd", hidden, expert_down, preferred_element_type=jnp.float32
    ).reshape(ROUTED_EXPERTS * capacity, D)
    picked = expert_out[slot_index].reshape(entries, 2, D)
    shared_up = jnp.dot(second_input, shared_up_weight, preferred_element_type=jnp.float32)
    shared_f, shared_back = jax.vjp(swiglu, shared_up)
    shared_hidden = shared_f.astype(jnp.bfloat16)
    shared_out = jnp.dot(shared_hidden, shared_down_weight, preferred_element_type=jnp.float32)
    mixed_part = (
        jnp.sum(gate_values[:, :, None] * picked, axis=1) + shared_gate[:, None] * shared_out
    )
    after_mixer = after_attn + branch_total(mixed_part)
    normalized_output, norm_out_back = jax.vjp(rms_scale, after_mixer, gain_rows[2])
    output_input = normalized_output.astype(jnp.bfloat16)
    model_estimates = jnp.dot(
        output_input, readout_complete[:, ROUTED_EXPERTS + 1 :], preferred_element_type=jnp.float32
    )
    prediction_misses = model_estimates - observed_future_series
    absolute_miss = jnp.abs(prediction_misses)
    horizon_importance_factors = head_weights(head_count)[None, :] * valid_mask
    robust_penalty_entries = jnp.where(
        absolute_miss <= quadratic_cutoff,
        0.5 * prediction_misses * prediction_misses,
        quadratic_cutoff * (absolute_miss - 0.5 * quadratic_cutoff),
    )
    local_loss = jnp.sum(robust_penalty_entries * horizon_importance_factors) + balance
    mp_count = lax.axis_size("mp")
    loss_total = lax.psum(local_loss, "dp")
    predicted_gradient = (
        jnp.clip(prediction_misses, -quadratic_cutoff, quadratic_cutoff)
        * horizon_importance_factors
    ).astype(jnp.bfloat16)
    head_grad = jnp.einsum(
        "ka,ky->ay", output_input, predicted_gradient, preferred_element_type=jnp.float32
    )
    out_input_grad = jnp.einsum(
        "aw,iw->ai",
        predicted_gradient,
        readout_complete[:, ROUTED_EXPERTS + 1 :],
        preferred_element_type=jnp.float32,
    )
    mixer_grad_in, gain_three_grad = norm_out_back(out_input_grad)
    picked_dots = jnp.sum(picked * mixer_grad_in[:, None, :], axis=-1)
    shared_dots = jnp.sum(shared_out * mixer_grad_in, axis=-1)
    gate_grads, shared_gate_grad = lax.psum((picked_dots, shared_dots), "mp")
    (logit_grad,) = gating_back((gate_grads, shared_gate_grad, jnp.ones((), jnp.float32)))
    logit_low = logit_grad.astype(jnp.bfloat16)
    router_grad = jnp.einsum(
        "ka,ky->ay", second_input, logit_low, preferred_element_type=jnp.float32
    )
    router_input_grad = jnp.einsum(
        "aw,iw->ai",
        logit_low,
        readout_complete[:, : ROUTED_EXPERTS + 1],
        preferred_element_type=jnp.float32,
    )
    gates_padded = jnp.concatenate([gate_values.reshape(-1), jnp.zeros((1,), jnp.float32)], axis=0)
    residual_padded = jnp.concatenate([mixer_grad_in, jnp.zeros((1, D), jnp.float32)], axis=0)
    expert_out_grad = (
        (gates_padded[source][:, None] * residual_padded[token_of])
        .astype(jnp.bfloat16)
        .reshape(ROUTED_EXPERTS, capacity, D)
    )
    hidden_grad = jnp.einsum(
        "ecd,efd->ecf", expert_out_grad, expert_down, preferred_element_type=jnp.float32
    )
    down_grad_experts = jnp.einsum(
        "ecf,ecd->efd", hidden, expert_out_grad, preferred_element_type=jnp.float32
    )
    gate_up_grad = swiglu_back(hidden_grad)[0].astype(jnp.bfloat16)
    up_grad_experts = jnp.einsum(
        "ecd,ecf->edf", gathered, gate_up_grad, preferred_element_type=jnp.float32
    )
    rows_grad = jnp.einsum(
        "ecf,edf->ecd", gate_up_grad, expert_up, preferred_element_type=jnp.float32
    ).reshape(ROUTED_EXPERTS * capacity, D)
    routed_grad = jnp.sum(rows_grad[slot_index].reshape(entries, 2, D), axis=1)
    shared_out_grad = (shared_gate[:, None] * mixer_grad_in).astype(jnp.bfloat16)
    shared_hidden_grad = jnp.einsum(
        "td,fd->tf", shared_out_grad, shared_down_weight, preferred_element_type=jnp.float32
    )
    down_grad_shared = jnp.einsum(
        "tf,td->fd", shared_hidden, shared_out_grad, preferred_element_type=jnp.float32
    )
    shared_up_grad = shared_back(shared_hidden_grad)[0].astype(jnp.bfloat16)
    up_grad_shared = jnp.einsum(
        "td,tf->df", second_input, shared_up_grad, preferred_element_type=jnp.float32
    )
    input_part = routed_grad + jnp.einsum(
        "tf,df->td", shared_up_grad, shared_up_weight, preferred_element_type=jnp.float32
    )
    second_input_grad = input_total(input_part) + router_input_grad
    upward_grad = jnp.concatenate([up_grad_experts, up_grad_shared[None]], axis=0).reshape(
        ROUTED_EXPERTS + 1, D, 2, hidden_local
    )
    downward_grad = jnp.concatenate([down_grad_experts, down_grad_shared[None]], axis=0)
    attn_grad_in, gain_two_grad = norm_two_back(second_input_grad)
    attn_total_grad = mixer_grad_in + attn_grad_in
    attn_low = attn_total_grad.astype(jnp.bfloat16)
    mixer_grad = jnp.einsum("tf,td->fd", attended_low, attn_low, preferred_element_type=jnp.float32)
    attended_grad = jnp.einsum(
        "td,fd->tf", attn_low, mixer_full, preferred_element_type=jnp.float32
    ).astype(jnp.bfloat16)
    query_grad, key_grad, value_grad = lax.map(
        attend_backward,
        (
            query_heads,
            key_heads,
            value_heads,
            split_heads(attended_grad, series_count, length),
            totals,
        ),
    )
    projected_grad = jnp.stack(
        [
            merge_heads(rotate(query_grad, cosine_table, -sine_table)),
            merge_heads(rotate(key_grad, cosine_table, -sine_table)),
            merge_heads(value_grad),
        ],
        axis=0,
    ).astype(jnp.bfloat16)
    joint_grad = jnp.einsum(
        "td,cte->cde", first_input, projected_grad, preferred_element_type=jnp.float32
    )
    first_input_grad = input_total(
        jnp.einsum("cte,cde->td", projected_grad, joint_full, preferred_element_type=jnp.float32)
    )
    embed_grad_in, gain_one_grad = norm_one_back(first_input_grad)
    gate_vector_grad, up_vector_grad = embed_back(attn_total_grad + embed_grad_in)
    vector_grad = jnp.stack(
        [gain_one_grad, gain_two_grad, gain_three_grad, gate_vector_grad, up_vector_grad], axis=0
    )
    readout_grad = jnp.concatenate([router_grad, head_grad], axis=1)
    joint_red, mixer_red, upward_red, downward_red, readout_red, vector_red = (
        lax.psum_scatter(joint_grad, "dp", scatter_dimension=1, tiled=True),
        lax.psum_scatter(mixer_grad, "dp", scatter_dimension=1, tiled=True),
        lax.psum_scatter(upward_grad, "dp", scatter_dimension=1, tiled=True),
        lax.psum_scatter(downward_grad, "dp", scatter_dimension=2, tiled=True),
        lax.psum_scatter(readout_grad, "dp", scatter_dimension=0, tiled=True),
        lax.psum_scatter(vector_grad, "dp", scatter_dimension=1, tiled=True),
    )
    split_squares = (
        jnp.sum(joint_red * joint_red)
        + jnp.sum(mixer_red * mixer_red)
        + jnp.sum(upward_red * upward_red)
        + jnp.sum(downward_red * downward_red)
    )
    shared_squares = jnp.sum(readout_red * readout_red) + jnp.sum(vector_red * vector_red)
    partial_squares = split_squares + shared_squares / mp_count
    norm_squared = lax.psum(partial_squares, ("dp", "mp"))
    grad_norm = jnp.sqrt(norm_squared)
    factor = clip_limit / (grad_norm + 1e-06)
    steps_taken = step_count[0].astype(jnp.float32)
    bias_one = 1.0 - beta_one**steps_taken
    bias_two = 1.0 - beta_two**steps_taken
    joint_new = adam_update(
        joint_proj, joint_moment, joint_square, joint_red, factor, bias_one, bias_two, matrix_rate
    )
    mixer_new = adam_update(
        mixer_proj, mixer_moment, mixer_square, mixer_red, factor, bias_one, bias_two, matrix_rate
    )
    upward_new = adam_update(
        upward_proj,
        upward_moment,
        upward_square,
        upward_red,
        factor,
        bias_one,
        bias_two,
        matrix_rate,
    )
    downward_new = adam_update(
        downward_proj,
        downward_moment,
        downward_square,
        downward_red,
        factor,
        bias_one,
        bias_two,
        matrix_rate,
    )
    readout_new = adam_update(
        readout,
        readout_moment,
        readout_square,
        readout_red,
        factor,
        bias_one,
        bias_two,
        matrix_rate,
    )
    vector_new = adam_update(
        vectors, vectors_moment, vectors_square, vector_red, factor, bias_one, bias_two, vector_rate
    )
    return (
        loss_total,
        grad_norm,
        joint_new[0],
        joint_new[1],
        joint_new[2],
        mixer_new[0],
        mixer_new[1],
        mixer_new[2],
        upward_new[0],
        upward_new[1],
        upward_new[2],
        downward_new[0],
        downward_new[1],
        downward_new[2],
        readout_new[0],
        readout_new[1],
        readout_new[2],
        vector_new[0],
        vector_new[1],
        vector_new[2],
    )


def solution(mesh):
    token = [P("dp", None), P("dp", None), P("dp", None, None), P()]
    weights = [
        P(None, "dp", "mp"), P("mp", "dp"), P(None, "dp", None, "mp"), P(None, "mp", "dp"), P("dp", None), P(None, "dp"),
    ]
    triple = tuple(spec for spec in weights for _ in range(3))
    near = mesh.shape["dp"] == 16 and mesh.shape["mp"] == 2
    return jax.shard_map(
        on_device if near else on_device_wide,
        mesh=mesh,
        in_specs=tuple(token) + triple,
        out_specs=(P(), P()) + triple,
        check_vma=False,
    )
```

```python
import functools
import jax
import jax.numpy as jnp
from jax import lax
from jax.experimental import pallas as pl
from jax.experimental.pallas import tpu as pltpu
from jax.sharding import PartitionSpec as P

D = 384
HEAD = 32
ROUTED_EXPERTS = 8
LANES = 128
TILE = 256
SHARD = 24
ROUTER = 112
SHARED = ROUTER + ROUTED_EXPERTS
VECTOR = SHARED + 1

horizons = (1, 8, 32, 64)
quadratic_cutoff = 2.0
aux_factor = 0.02
clip_limit = 0.001
beta_one = 0.9
beta_two = 0.95
adam_eps = 1e-08
decay_rate = 0.1
matrix_rate = 0.05
vector_rate = 0.25
norm_eps = 1e-06
rope_base = 10000.0

F32 = jnp.float32
BF16 = jnp.bfloat16
I16 = jnp.int16
MESH = pl.DeviceIdType.MESH
VMEM = pl.BlockSpec(memory_space=pltpu.VMEM)
ANY = pl.BlockSpec(memory_space=pl.ANY)
DMA = pltpu.SemaphoreType.DMA


def dot(a, b, da=1, db=0):
    return lax.dot_general(a, b, (((da,), (db,)), ((), ())), preferred_element_type=F32)


def params(megabytes=60, **more):
    return pltpu.CompilerParams(vmem_limit_bytes=megabytes * 1024 * 1024, **more)


def sigmoid(v):
    return 1.0 / (1.0 + jnp.exp(-v))


def block(index, size, step=8):
    return pl.ds(pl.multiple_of(index * size, step), size)


def place():
    dp = lax.axis_index("dp")
    return dp, lax.axis_index("mp"), lax.rem(dp, 2), lax.rem(dp // 2, 2), dp // 4


def meet_everyone(dp, mp):
    barrier = pltpu.get_barrier_semaphore()
    me, n = dp * 2 + mp, 32

    def signal(k, carry):
        peer = lax.rem(me + k, n)
        pl.semaphore_signal(barrier, inc=1, device_id=(peer // 2, lax.rem(peer, 2)), device_id_type=MESH)
        return carry

    lax.fori_loop(1, n, signal, 0)
    pl.semaphore_wait(barrier, n - 1)


def remote(src, dst, send, recv, dp, mp):
    return pltpu.make_async_remote_copy(
        src_ref=src, dst_ref=dst, send_sem=send, recv_sem=recv, device_id=(dp, mp), device_id_type=MESH)


def done(view, sem):
    pltpu.make_async_copy(view, view, sem).wait()


def column(row, length):
    return jnp.transpose(jnp.broadcast_to(row, (LANES, length)))


def rotated(t, cos, sin):
    half = HEAD // 2
    front, back = t[:half], t[half:]
    return jnp.concatenate([front * cos - back * sin, back * cos + front * sin], axis=0)


def unrotated(t, cos, sin):
    half = HEAD // 2
    front, back = t[:half], t[half:]
    return jnp.concatenate([front * cos + back * sin, back * cos - front * sin], axis=0)


def score_block(k_rows, q_cols, low):
    s = dot(k_rows, q_cols)
    keys = lax.broadcasted_iota(jnp.int32, s.shape, 0)
    queries = lax.broadcasted_iota(jnp.int32, s.shape, 1) + low
    return jnp.where(keys <= queries, s, -1e30)


def flip(t):
    return jnp.transpose(t.astype(F32)).astype(BF16)


def embed_piece(x_row, vec, x0_ref, a_ref, r):
    xb = column(x_row, TILE)
    cuts, square = [], None
    for c in range(D // LANES):
        cols = slice(c * LANES, (c + 1) * LANES)
        u = xb * vec[3:4, cols]
        v = u * sigmoid(u) * (xb * vec[4:5, cols])
        x0_ref[r, cols] = v
        square = v * v if square is None else square + v * v
        cuts.append(v)
    scale = lax.rsqrt(jnp.sum(square, axis=1, keepdims=True) / D + norm_eps)
    for c in range(D // LANES):
        cols = slice(c * LANES, (c + 1) * LANES)
        a_ref[r, cols] = (cuts[c] * scale * vec[0:1, cols]).astype(BF16)


def project_piece(wt, a, cos, sin, qkv, width):
    for part in range(3):
        t = dot(wt[part * width:(part + 1) * width, :], a, 1, 1)
        for h in range(width // HEAD):
            u = t[h * HEAD:(h + 1) * HEAD]
            if part < 2:
                u = rotated(u, cos, sin)
            qkv[part * width + h * HEAD:part * width + (h + 1) * HEAD, :] = u.astype(BF16)


def forward_head(h, width, qkv, lse, o):
    length = qkv.shape[1]
    scale = HEAD ** (-0.5)
    q_rows = block(h, HEAD)
    k_rows = pl.ds(pl.multiple_of(width + h * HEAD, HEAD), HEAD)
    v_rows = pl.ds(pl.multiple_of(2 * width + h * HEAD, HEAD), HEAD)
    k = flip(qkv[k_rows, :])
    for j in range(length // TILE):
        n = TILE * (j + 1)
        cols = slice(j * TILE, (j + 1) * TILE)
        s = score_block(k[:n], qkv[q_rows, cols], j * TILE)
        peak = jnp.max(s, axis=0, keepdims=True)
        e = jnp.exp((s - peak) * scale)
        mass = jnp.sum(e, axis=0, keepdims=True)
        weights = (e * (1.0 / mass)).astype(BF16)
        o[q_rows, cols] = dot(qkv[v_rows, :n], weights).astype(BF16)
        lse[pl.ds(h, 1), cols] = peak * scale + jnp.log(mass)


def backward_head(h, width, qkv, do_t, lse, cos, sin, dqkv, dk_ref, dv_ref):
    length = qkv.shape[1]
    scale = HEAD ** (-0.5)
    q_rows = block(h, HEAD)
    k_rows = pl.ds(pl.multiple_of(width + h * HEAD, HEAD), HEAD)
    v_rows = pl.ds(pl.multiple_of(2 * width + h * HEAD, HEAD), HEAD)
    q, k, v, do = flip(qkv[q_rows, :]), flip(qkv[k_rows, :]), flip(qkv[v_rows, :]), flip(do_t[q_rows, :])
    dk_ref[...] = jnp.zeros_like(dk_ref)
    dv_ref[...] = jnp.zeros_like(dv_ref)
    for j in range(length // TILE):
        n = TILE * (j + 1)
        cols = slice(j * TILE, (j + 1) * TILE)
        s = score_block(k[:n], qkv[q_rows, cols], j * TILE)
        w = jnp.exp(s * scale - lse[pl.ds(h, 1), cols])
        dv_ref[:n] += dot(w.astype(BF16), do[cols])
        dw = dot(v[:n], do_t[q_rows, cols])
        mean = jnp.sum(w * dw, axis=0, keepdims=True)
        ds = (w * (dw - mean) * scale).astype(BF16)
        dk_ref[:n] += dot(ds, q[cols])
        dq = dot(qkv[k_rows, :n], ds)
        dqkv[q_rows, cols] = unrotated(dq, cos[:, cols], sin[:, cols]).astype(BF16)
    dqkv[k_rows, :] = unrotated(jnp.transpose(dk_ref[...]), cos, sin).astype(BF16)
    dqkv[v_rows, :] = jnp.transpose(dv_ref[...]).astype(BF16)


def mid_forward_piece(x, gain, table):
    scale = lax.rsqrt(jnp.mean(x * x, axis=1, keepdims=True) + norm_eps)
    low = (x * scale * gain).astype(BF16)
    logits = dot(low, table)
    lanes = lax.broadcasted_iota(jnp.int32, logits.shape, 1)
    routed = (lanes >= ROUTER) & (lanes < SHARED)
    peak = jnp.max(jnp.where(routed, logits, -jnp.inf), axis=1, keepdims=True)
    e = jnp.where(routed, jnp.exp(jnp.where(routed, logits - peak, 0.0)), 0.0)
    probability = e / jnp.sum(e, axis=1, keepdims=True)
    gates = jnp.where(lanes == SHARED, sigmoid(jnp.where(lanes == SHARED, logits, 0.0)), probability)
    return low, gates, jnp.sum(probability, axis=0, keepdims=True)


def embed_backward_piece(x_row, da, dx1, vec):
    xb = column(x_row, TILE)
    xb = jnp.concatenate([xb] * (D // LANES), axis=1)
    u = xb * vec[3:4, :]
    up = xb * vec[4:5, :]
    s = sigmoid(u)
    silu = u * s
    x = silu * up
    scale = lax.rsqrt(jnp.mean(x * x, axis=1, keepdims=True) + norm_eps)
    unit = x * scale
    dn = da * vec[0:1, :]
    dx = dx1 + scale * (dn - unit * jnp.mean(dn * unit, axis=1, keepdims=True))
    du = dx * up * (s * (1.0 + u * (1.0 - s)))
    total = lambda v: jnp.sum(v, axis=0, keepdims=True)
    return total(da * unit), total(du * xb), total(dx * silu * xb)


def forward_kernel(
    small_own, big_own, tally, x_ref, cos_ref, sin_ref,
    big, wt, vec, table, a, qkv, lse, o, x1, b, pc, total, tallies,
    stage, small, x0, part, other,
    in_sem, own_sem, send_xy, send_up, send_dn, z_sem, p2_sem, p3_sem,
    small_send, small_z, small_y, small_x, tally_send, tally_recv, pair_send, pair_recv,
):
    dp, mp, x, y, z = place()
    xp, yp = dp + 1 - 2 * x, dp + 2 - 4 * y
    count = big_own.shape[0]
    series, _, length = x_ref.shape
    width = o.shape[1]
    per = length // TILE
    load = pltpu.make_async_copy(big_own, stage, in_sem)
    load.start()
    meet_everyone(dp, mp)

    def home(zs):
        return zs * 4 + 2 * y + x

    def small_put(src, slot, recv, peer):
        remote(src, small.at[slot], small_send, recv, peer, mp).start()

    for dist in (1, 2, 3):
        @pl.when(z >= dist)
        def _():
            small_put(small_own, dp, small_z.at[z], dp - 4 * dist)

        @pl.when(z + dist <= 3)
        def _():
            small_put(small_own, dp, small_z.at[z], dp + 4 * dist)
    small_put(small_own, dp, small_y.at[z], yp)
    small_put(small_own, dp, small_x, xp)
    small[dp] = small_own[...]
    me = dp * 2 + mp

    def tell(k, carry):
        peer = lax.rem(me + k, 32)
        remote(tally, tallies.at[me], tally_send, tally_recv, peer // 2, lax.rem(peer, 2)).start()
        return carry

    lax.fori_loop(1, 32, tell, 0)
    tallies[me] = tally[...]

    load.wait()

    def rows(c, slot):
        return big.at[c, block(slot, SHARD), :]

    def put(src, c, slot, send, recv, peer):
        remote(src, rows(c, slot), send, recv, peer, mp).start()

    def climb(c, zs, src):
        put(src, c, home(zs), send_up, z_sem.at[c, zs], dp + 4)

    def drop(c, zs, src):
        put(src, c, home(zs), send_dn, z_sem.at[c, zs], dp - 4)

    def ends(c):
        k = lax.rem(c, 2)
        return jnp.where(k == 0, yp, xp), jnp.where(k == 0, xp, yp)

    def spread(c, zs, src):
        first, second = ends(c)
        put(src, c, home(zs), send_xy, p2_sem.at[c, zs], first)
        put(src, c, home(zs), send_xy, p3_sem, second)

    def own_z(c, carry):
        @pl.when(z < 3)
        def _():
            climb(c, z, stage.at[c])

        @pl.when(z > 0)
        def _():
            drop(c, z, stage.at[c])
        pltpu.make_async_copy(stage.at[c], rows(c, dp), own_sem).start()
        return carry

    lax.fori_loop(0, count, own_z, 0)

    for dist in (1, 2, 3):
        for sign in (-1, 1):
            zs = z + sign * dist

            @pl.when((zs >= 0) & (zs <= 3))
            def _():
                done(small.at[home(zs)], small_z.at[zs])
                small_put(small.at[home(zs)], home(zs), small_y.at[zs], yp)
                small_put(small.at[home(zs)], home(zs), small_x, xp)
    for turn in range(4):
        zs = lax.rem(z + turn, 4)
        slot = zs * 4 + 2 * (1 - y) + x
        done(small.at[slot], small_y.at[zs])
        small_put(small.at[slot], slot, small_x, xp)
    done(small.at[pl.ds(0, 8)], small_x)

    def own_xy(c, carry):
        spread(c, z, stage.at[c])
        return carry

    lax.fori_loop(0, count, own_xy, 0)

    whole = small[...].astype(F32).reshape(D, -1)
    table[...] = whole[:, 4 * width:].astype(BF16)
    turned = jnp.transpose(whole)
    wt[...] = turned.astype(BF16)
    vec[...] = jnp.concatenate(
        [turned[4 * width + VECTOR:4 * width + VECTOR + 5], jnp.zeros((3, D), F32)], axis=0)
    total[...] = jnp.zeros_like(total)

    def relay(c, dist):
        def second(zs):
            k = lax.rem(c, 2)
            slot = zs * 4 + jnp.where(k == 0, 2 * (1 - y) + x, 2 * y + 1 - x)
            done(rows(c, slot), p2_sem.at[c, zs])
            put(rows(c, slot), c, slot, send_xy, p3_sem, ends(c)[1])

        @pl.when(z >= dist)
        def _():
            zs = z - dist
            done(rows(c, home(zs)), z_sem.at[c, zs])

            @pl.when(z < 3)
            def _():
                climb(c, zs, rows(c, home(zs)))
            spread(c, zs, rows(c, home(zs)))

        @pl.when(z + dist <= 3)
        def _():
            zs = z + dist
            done(rows(c, home(zs)), z_sem.at[c, zs])

            @pl.when(z > 0)
            def _():
                drop(c, zs, rows(c, home(zs)))
            spread(c, zs, rows(c, home(zs)))

        @pl.when(z - (dist - 1) >= 0)
        def _():
            second(z - (dist - 1))

        @pl.when((dist > 1) & (z + dist - 1 <= 3))
        def _():
            second(z + dist - 1)

    def pair(n):
        r = block(n, length)
        return remote(part.at[r], other.at[r], pair_send.at[n], pair_recv.at[n], dp, 1 - mp)

    heads = width // HEAD
    pieces = heads + 2

    def attention(i):
        n, j = i // pieces, lax.rem(i, pieces)
        r = block(n, length)

        @pl.when(j == 0)
        def _():
            def tile(m, carry):
                t = pl.ds(pl.multiple_of(n * length + m * TILE, TILE), TILE)
                embed_piece(x_ref[n, :, block(m, TILE, TILE)], vec, x0, a, t)
                return carry
            lax.fori_loop(0, per, tile, 0)

        @pl.when(j == 1)
        def _():
            project_piece(wt, a[r, :], cos_ref[...], sin_ref[...], qkv.at[n], width)

        @pl.when(j >= 2)
        def _():
            forward_head(j - 2, width, qkv.at[n], lse.at[n], o.at[n])

        @pl.when(j == pieces - 1)
        def _():
            part[r, :] = dot(o[n], wt[3 * width:4 * width, :], 0, 0)
            pair(n).start()

    def middle(m):
        r = block(m, TILE)

        @pl.when(lax.rem(m, per) == 0)
        def _():
            pair(m // per).wait()
        v = x0[r, :] + (part[r, :] + other[r, :])
        x1[r, :] = v
        low, gates, sums = mid_forward_piece(v, vec[1:2, :], table[...])
        b[r, :] = low
        pc[r, :] = gates
        total[...] += sums

    def step(i, carry):
        relay(lax.rem(i, count), i // count + 1)

        @pl.when(i < series * pieces)
        def _():
            attention(i)

        for n in range(series):
            begin = (n + 1) * pieces + 4

            @pl.when((i >= begin) & (i < begin + per))
            def _():
                middle(n * per + i - begin)
        return carry

    lax.fori_loop(0, 4 * count, step, 0)

    def whole_wait(n, sem):
        done(big.at[:, pl.ds(0, n * SHARD), :], sem)
    whole_wait(8, p3_sem)
    whole_wait(12, send_xy)
    whole_wait(1, own_sem)
    done(small.at[pl.ds(0, 15)], small_send)
    done(tallies.at[pl.ds(0, 31)], tally_recv)
    done(tallies.at[pl.ds(0, 31)], tally_send)
    for k in range(4):
        @pl.when(z == k)
        def _():
            if k < 3:
                whole_wait(k + 1, send_up)
            if k > 0:
                whole_wait(4 - k, send_dn)


def forward_near(small_own, big_own, tally, x, cos, sin, width, ident):
    series, _, length = x.shape
    tokens = series * length
    count, shard, columns = big_own.shape
    shape = jax.ShapeDtypeStruct
    return pl.pallas_call(
        forward_kernel,
        in_specs=[VMEM, ANY, VMEM, VMEM, VMEM, VMEM],
        out_specs=[ANY] + [VMEM] * 12,
        out_shape=[
            shape((count, D, columns), BF16),
            shape((small_own.shape[1], D), BF16), shape((8, D), F32), shape((D, LANES), BF16),
            shape((tokens, D), BF16), shape((series, 3 * width, length), BF16), shape((series, 8, length), F32),
            shape((series, width, length), BF16),
            shape((tokens, D), F32), shape((tokens, D), BF16), shape((tokens, LANES), F32), shape((1, LANES), F32),
            shape((32,) + tally.shape, F32),
        ],
        scratch_shapes=[
            pltpu.VMEM(big_own.shape, BF16), pltpu.VMEM((16,) + small_own.shape, BF16),
            pltpu.VMEM((tokens, D), F32), pltpu.VMEM((tokens, D), F32), pltpu.VMEM((tokens, D), F32),
            DMA, DMA, DMA, DMA, DMA, DMA((count, 4)), DMA((count, 4)), DMA,
            DMA, DMA((4,)), DMA((4,)), DMA, DMA, DMA, DMA((series,)), DMA((series,)),
        ],
        compiler_params=params(collective_id=ident, has_side_effects=True),
        name="forward_near",
    )(small_own, big_own, tally, x, cos, sin)


GROUP = 16


def spread_rows(dest, value, start, count):
    for c in range(value.shape[1] // LANES):
        dest[pl.ds(start * 8 + c, count, stride=8), :] = value[:, c * LANES:(c + 1) * LANES]


def rows_at(ref, index):
    return ref[pl.ds(pl.multiple_of(index, 8), 8), :]


def pick_rows(source, tile, index_ref, base):
    for i in range(0, TILE, GROUP):
        values = [rows_at(source, index_ref[base + k]) for k in range(i, i + GROUP)]
        for k in range(i, i + GROUP):
            tile[k * 8:k * 8 + 8, :] = values[k - i]


def sum_rows(results, tile, index_ref, base, tokens):
    for i in range(0, TILE, GROUP):
        values = [
            rows_at(results, index_ref[base + k]) + rows_at(results, index_ref[tokens + base + k])
            for k in range(i, i + GROUP)]
        for k in range(i, i + GROUP):
            tile[k * 8:k * 8 + 8, :] = values[k - i]


def gathered_columns(tile, columns):
    return [tile[pl.ds(c, TILE, stride=8), :] for c in range(columns)]


def lane_of(value, lane):
    lanes = lax.broadcasted_iota(jnp.int32, value.shape, 1)
    return jnp.sum(jnp.where(lanes == lane, value, 0.0), axis=1, keepdims=True)


def lay_rows(values, pc_ref, rows8):
    tokens = values.shape[0]

    def lay(i, carry):
        r = block(i, TILE)
        spread_rows(rows8, values[r, :].astype(F32), i * TILE, TILE)
        rows8[pl.ds(i * TILE * 8 + 3, TILE, stride=8), :] = pc_ref[r, :]
        return carry

    lax.fori_loop(0, tokens // TILE, lay, 0)
    rows8[pl.ds(tokens * 8, 8), :] = jnp.zeros((8, LANES), F32)


def expert_tiles(e, used, capacity, tile, blank, shared):
    tiles = capacity // TILE

    @pl.when(e < ROUTED_EXPERTS)
    def _():
        def one(i, carry):
            tile(e * tiles + i, block(i, TILE))
            return carry

        def none(i, carry):
            blank(block(i, TILE))
            return carry

        lax.fori_loop(0, used[e], one, 0)
        lax.fori_loop(used[e], tiles, none, 0)

    @pl.when(e >= ROUTED_EXPERTS)
    def _():
        def one(i, carry):
            shared((e - ROUTED_EXPERTS) * tiles + i, block(i, TILE))
            return carry

        lax.fori_loop(0, tiles, one, 0)


def expert_forward_kernel(
    used, order, after, source, slots, b_ref, pc_ref, w_ref, x_ref, y_ref, mix_ref, rows8, done8, tile8, sum8
):
    e = pl.program_id(0)
    tokens = b_ref.shape[0]
    hidden = w_ref.shape[2] // 3

    @pl.when(e == 0)
    def _():
        lay_rows(b_ref, pc_ref, rows8)
        pick_rows(rows8, tile8, source, after[after.shape[0] - 1])

    def run(x):
        g = dot(x, w_ref[0, :, : 2 * hidden])
        gate, up = g[:, :hidden], g[:, hidden:]
        h = (gate * sigmoid(gate) * up).astype(BF16)
        return dot(h, w_ref[0, :, 2 * hidden:], 1, 1)

    def tile(s, here):
        c0, c1, c2, pc = gathered_columns(tile8, 4)
        x = jnp.concatenate([c0, c1, c2], axis=1).astype(BF16)
        x_ref[0, here, :] = x
        gate_column = lane_of(pc, ROUTER + e)
        pick_rows(rows8, tile8, source, after[s])
        y = run(x)
        y_ref[0, here, :] = y
        spread_rows(done8, y * gate_column, order[s], TILE)

    def blank(here):
        x_ref[0, here, :] = jnp.zeros((TILE, D), BF16)

    def shared(j, here):
        r = block(j, TILE)
        x = b_ref[r, :]
        x_ref[0, here, :] = x
        sum_rows(done8, sum8, slots, j * TILE, tokens)
        y = run(x)
        y_ref[0, here, :] = y
        scaled = y * lane_of(pc_ref[r, :], SHARED)
        for c, part in enumerate(gathered_columns(sum8, D // LANES)):
            cols = slice(c * LANES, (c + 1) * LANES)
            mix_ref[r, cols] = part + scaled[:, cols]

    expert_tiles(e, used, y_ref.shape[1], tile, blank, shared)


def expert_specs(tokens, weights):
    full = lambda shape: pl.BlockSpec(shape, lambda e, *_: (0,) * len(shape), pipeline_mode=pl.Buffered(1))
    tile = lambda w: pl.BlockSpec((1, tokens // 2, w), lambda e, *_: (e, 0, 0))
    weight = pl.BlockSpec((1,) + weights.shape[1:], lambda e, *_: (jnp.minimum(e, ROUTED_EXPERTS), 0, 0))
    scratch = [
        pltpu.VMEM(((tokens + 1) * 8, LANES), F32), pltpu.VMEM(((2 * tokens + TILE) * 8, LANES), F32),
        pltpu.VMEM((TILE * 8, LANES), F32), pltpu.VMEM((TILE * 8, LANES), F32)]
    return full, tile, weight, scratch


def expert_forward(plan, b, pc, weights):
    tokens = b.shape[0]
    full, tile, weight, scratch = expert_specs(tokens, weights)
    return pl.pallas_call(
        expert_forward_kernel,
        grid_spec=pltpu.PrefetchScalarGridSpec(
            num_scalar_prefetch=5,
            grid=(ROUTED_EXPERTS + 2,),
            in_specs=[full(b.shape), full(pc.shape), weight],
            out_specs=[tile(D), tile(D), full((tokens, D))],
            scratch_shapes=scratch,
        ),
        out_shape=[
            jax.ShapeDtypeStruct((ROUTED_EXPERTS + 2, tokens // 2, D), BF16),
            jax.ShapeDtypeStruct((ROUTED_EXPERTS + 2, tokens // 2, D), F32),
            jax.ShapeDtypeStruct((tokens, D), F32),
        ],
        compiler_params=params(),
        name="expert_forward",
    )(*plan, b, pc, weights)


def expert_backward_kernel(
    used, order, after, source, slots, pc_ref, dx_ref, w_ref, x_ref, y_ref, dy_ref, dg_ref, h_ref, acc_ref,
    rows8, done8, tile8, sum8,
):
    e = pl.program_id(0)
    tokens = dx_ref.shape[0]
    hidden = w_ref.shape[2] // 3
    lanes = lax.broadcasted_iota(jnp.int32, (TILE, LANES), 1)

    @pl.when(e == 0)
    def _():
        lay_rows(dx_ref, pc_ref, rows8)
        pick_rows(rows8, tile8, source, after[after.shape[0] - 1])

    def run(here, dy):
        dy_ref[0, here, :] = dy
        u = w_ref[0, :, : 2 * hidden]
        g = dot(x_ref[0, here, :], u)
        gate, up = g[:, :hidden], g[:, hidden:]
        sig = sigmoid(gate)
        silu = gate * sig
        h_ref[0, here, :] = (silu * up).astype(BF16)
        dh = dot(dy, w_ref[0, :, 2 * hidden:])
        d_up = (dh * silu).astype(BF16)
        d_gate = (dh * up * (sig * (1.0 + gate * (1.0 - sig)))).astype(BF16)
        dg_ref[0, here, :hidden] = d_gate
        dg_ref[0, here, hidden:] = d_up
        return dot(d_gate, u[:, :hidden], 1, 1) + dot(d_up, u[:, hidden:], 1, 1)

    def tile(s, here):
        c0, c1, c2, pc = gathered_columns(tile8, 4)
        dx = jnp.concatenate([c0, c1, c2], axis=1)
        d_value = jnp.sum(y_ref[0, here, :] * dx, axis=1, keepdims=True)
        dy = (dx * lane_of(pc, ROUTER + e)).astype(BF16)
        pick_rows(rows8, tile8, source, after[s])
        back = run(here, dy)
        spread_rows(done8, back, order[s], TILE)
        done8[pl.ds(order[s] * 8 + 3, TILE, stride=8), :] = jnp.where(lanes == ROUTER + e, d_value, 0.0)

    def blank(here):
        dy_ref[0, here, :] = jnp.zeros((TILE, D), BF16)
        dg_ref[0, here, :] = jnp.zeros((TILE, 2 * hidden), BF16)
        h_ref[0, here, :] = jnp.zeros((TILE, hidden), BF16)

    def shared(j, here):
        r = block(j, TILE)
        dx = dx_ref[r, :]
        d_value = jnp.sum(y_ref[0, here, :] * dx, axis=1, keepdims=True)
        sum_rows(done8, sum8, slots, j * TILE, tokens)
        back = run(here, (dx * lane_of(pc_ref[r, :], SHARED)).astype(BF16))
        sums = gathered_columns(sum8, D // LANES + 1)
        for c in range(D // LANES):
            cols = slice(c * LANES, (c + 1) * LANES)
            acc_ref[r, cols] = sums[c] + back[:, cols]
        acc_ref[r, D:] = jnp.where(lanes == SHARED, d_value, sums[-1])

    expert_tiles(e, used, y_ref.shape[1], tile, blank, shared)


def expert_backward(plan, pc, dx, weights, x, y):
    tokens = dx.shape[0]
    hidden = weights.shape[2] // 3
    full, tile, weight, scratch = expert_specs(tokens, weights)
    return pl.pallas_call(
        expert_backward_kernel,
        grid_spec=pltpu.PrefetchScalarGridSpec(
            num_scalar_prefetch=5,
            grid=(ROUTED_EXPERTS + 2,),
            in_specs=[full(pc.shape), full(dx.shape), weight, tile(D), tile(D)],
            out_specs=[tile(D), tile(2 * hidden), tile(hidden), full((tokens, D + LANES))],
            scratch_shapes=scratch,
        ),
        out_shape=[
            jax.ShapeDtypeStruct((ROUTED_EXPERTS + 2, tokens // 2, D), BF16),
            jax.ShapeDtypeStruct((ROUTED_EXPERTS + 2, tokens // 2, 2 * hidden), BF16),
            jax.ShapeDtypeStruct((ROUTED_EXPERTS + 2, tokens // 2, hidden), BF16),
            jax.ShapeDtypeStruct((tokens, D + LANES), F32),
        ],
        compiler_params=params(),
        name="expert_backward",
    )(*plan, pc, dx, weights, x, y)


def exchange(part, other, send_sem, recv_sem):
    dp, mp = lax.axis_index("dp"), lax.axis_index("mp")
    barrier = pltpu.get_barrier_semaphore()
    pl.semaphore_signal(barrier, inc=1, device_id=(dp, 1 - mp), device_id_type=MESH)
    pl.semaphore_wait(barrier, 1)

    def copy(i):
        r = block(i, TILE)
        return remote(part.at[r], other.at[r], send_sem.at[i], recv_sem.at[i], dp, 1 - mp)

    def begin(i, carry):
        copy(i).start()
        return carry

    lax.fori_loop(0, part.shape[0] // TILE, begin, 0)
    return lambda i: copy(i).wait()


def exchange_scratch(part):
    tiles = part.shape[0] // TILE
    return [pltpu.VMEM(part.shape, F32), DMA((tiles,)), DMA((tiles,))]


def hankel(base):
    block_rows = jnp.broadcast_to(base, (LANES, 2 * LANES))
    m = pltpu.roll(block_rows, 0, 1, stride=1, stride_axis=0)[:, :LANES]
    lanes = lax.broadcasted_iota(jnp.int32, (LANES, LANES), 1)
    out = pltpu.roll(m, 41, 1)
    out = jnp.where(lanes < 104, pltpu.roll(m, 40, 1), out)
    out = jnp.where(lanes < 96, pltpu.roll(m, 32, 1), out)
    return jnp.where(lanes < 64, m, out)


def loss_piece(x, gain, table, table_t, value_rows, mark_rows, weight):
    scale = lax.rsqrt(jnp.mean(x * x, axis=1, keepdims=True) + norm_eps)
    unit = x * scale
    low = (unit * gain).astype(BF16)
    z = dot(low, table)
    target = jnp.concatenate([hankel(row) for row in value_rows], axis=0)
    valid = jnp.concatenate([hankel(row) for row in mark_rows], axis=0)
    factor = valid * weight
    miss = z - target
    size = jnp.abs(miss)
    huber = jnp.where(
        size <= quadratic_cutoff, 0.5 * miss * miss, quadratic_cutoff * (size - 0.5 * quadratic_cutoff))
    dz = (jnp.clip(miss, -quadratic_cutoff, quadratic_cutoff) * factor).astype(BF16)
    df = dot(dz, table_t)
    dn = df * gain
    dx = scale * (dn - unit * jnp.mean(dn * unit, axis=1, keepdims=True))
    total = lambda v: jnp.sum(v, axis=0, keepdims=True)
    return dx, dot(dz, low, 0, 0), total(df * unit), total(huber * factor)


def loss_kernel(part, x1, vec, table, table_t, values, marks, weight, dx2, d_table, d_gain, loss,
                other, send_sem, recv_sem):
    wait = exchange(part, other, send_sem, recv_sem)
    d_table[...] = jnp.zeros_like(d_table)
    d_gain[...] = jnp.zeros_like(d_gain)
    loss[...] = jnp.zeros_like(loss)
    per = TILE // LANES

    def step(i, carry):
        r = block(i, TILE)
        wait(i)
        dx, dt, dg, fit = loss_piece(
            x1[r, :] + (part[r, :] + other[r, :]), vec[2:3, :], table[...], table_t[...],
            [values[pl.ds(per * i + k, 1), :] for k in range(per)],
            [marks[pl.ds(per * i + k, 1), :] for k in range(per)], weight[...])
        dx2[r, :] = dx
        d_table[...] += dt
        d_gain[...] += dg
        loss[...] += fit
        return carry

    lax.fori_loop(0, part.shape[0] // TILE, step, 0)


def loss_stage(part, x1, vec, table, table_t, values, marks, weight, ident):
    tokens = part.shape[0]
    return pl.pallas_call(
        loss_kernel,
        in_specs=[VMEM] * 8,
        out_specs=[VMEM] * 4,
        out_shape=[
            jax.ShapeDtypeStruct((tokens, D), F32), jax.ShapeDtypeStruct((LANES, D), F32),
            jax.ShapeDtypeStruct((1, D), F32), jax.ShapeDtypeStruct((1, LANES), F32),
        ],
        scratch_shapes=exchange_scratch(part),
        compiler_params=params(collective_id=ident, has_side_effects=True),
        name="loss_stage",
    )(part, x1, vec, table, table_t, values, marks, weight)


def mid_backward_kernel(part, dx2, x1, b, pc, vec, table_t, balance, wo, o, d_table, d_gain3, dx1, do, rest,
                        other, send_sem, recv_sem):
    wait = exchange(part, other, send_sem, recv_sem)
    width = wo.shape[0]
    rest[:width, :] = jnp.zeros((width, D), F32)
    rest[width:, :] = d_table[...]
    rest[width + VECTOR + 2:width + VECTOR + 3, :] = d_gain3[...]
    per = o.shape[2] // TILE

    def step(i, carry):
        r = block(i, TILE)
        wait(i)
        dp = part[r, D:] + other[r, D:] + balance[...]
        p = pc[r, :]
        lanes = lax.broadcasted_iota(jnp.int32, p.shape, 1)
        routed = (lanes >= ROUTER) & (lanes < SHARED)
        weighted = jnp.sum(jnp.where(routed, p * dp, 0.0), axis=1, keepdims=True)
        dl = jnp.where(routed, p * (dp - weighted), jnp.where(lanes == SHARED, dp * p * (1.0 - p), 0.0))
        dl = dl.astype(BF16)
        low = b[r, :]
        rest[width:, :] += dot(dl, low, 0, 0)
        db = part[r, :D] + other[r, :D] + dot(dl, table_t[...])
        x = x1[r, :]
        scale = lax.rsqrt(jnp.mean(x * x, axis=1, keepdims=True) + norm_eps)
        unit = x * scale
        g2 = width + VECTOR + 1
        rest[g2:g2 + 1, :] += jnp.sum(db * unit, axis=0, keepdims=True)
        dn = db * vec[1:2, :]
        dx = dx2[r, :] + scale * (dn - unit * jnp.mean(dn * unit, axis=1, keepdims=True))
        dx1[r, :] = dx
        d_low = dx.astype(BF16)
        n, cols = i // per, block(lax.rem(i, per), TILE, TILE)
        do[n, :, cols] = dot(wo[...], d_low, 1, 1).astype(BF16)
        rest[:width, :] += dot(o[n, :, cols], d_low)
        return carry

    lax.fori_loop(0, part.shape[0] // TILE, step, 0)


def mid_backward(part, dx2, x1, b, pc, vec, table_t, balance, wo, o, d_table, d_gain3, ident):
    tokens = part.shape[0]
    return pl.pallas_call(
        mid_backward_kernel,
        in_specs=[VMEM] * 12,
        out_specs=[VMEM] * 3,
        out_shape=[
            jax.ShapeDtypeStruct((tokens, D), F32), jax.ShapeDtypeStruct(o.shape, BF16),
            jax.ShapeDtypeStruct((wo.shape[0] + LANES, D), F32),
        ],
        scratch_shapes=exchange_scratch(part),
        compiler_params=params(collective_id=ident, has_side_effects=True),
        name="mid_backward",
    )(part, dx2, x1, b, pc, vec, table_t, balance, wo, o, d_table, d_gain3)


SLOTS = 3
HOPS = 2
ACCS = 5


def encode(dest, v):
    width = v.shape[1]
    top = jnp.max(jnp.abs(v), axis=1, keepdims=True)
    power = jnp.ceil(jnp.log2(jnp.maximum(top, 1e-30) * (1.001 / 32767.0)))
    power = jnp.broadcast_to(power, (v.shape[0], LANES))
    inverse = jnp.exp2(-power)
    dest[:, width:] = power.astype(jnp.int32).astype(I16)
    for c in range(width // LANES):
        cols = slice(c * LANES, (c + 1) * LANES)
        dest[:, cols] = jnp.round(v[:, cols] * inverse).astype(jnp.int32).astype(I16)


def decode(source):
    width = source.shape[1] - LANES
    unit = jnp.exp2(source[:, width:].astype(jnp.int32).astype(F32))
    return jnp.concatenate(
        [source[:, c * LANES:(c + 1) * LANES].astype(jnp.int32).astype(F32) * unit for c in range(width // LANES)],
        axis=1)


def backward_kernel(
    xs, dys, dgs, hs, qkvs, dos, lses, a_all, dx1_all, rest, x_ref, wt, vec, cos_ref, sin_ref,
    out, out_small,
    x_in, dy_in, dg_in, h_in, xt, dyt, temp, dw, acc, send1, recv1, send2, recv2, zs_up, zs_dn, up, dn,
    qkv, do_t, lse, a, dx1, dqkv, dk, dv, stack, part, other,
    sm, small_a1, small_b1, small_a2, small_b2, small_up, small_dn,
    load_sem, sem_s1, sem_r1, sem_s2, sem_r2, sem_su, sem_sd, sem_ru, sem_rd,
    attn_sem, dx1_sem, rest_sem, pair_send, pair_recv,
    small_send, small_sa, small_sb, small_r, small_su, small_sd, small_ru, small_rd,
):
    dp, mp, x, y, z = place()
    xp, yp = dp + 1 - 2 * x, dp + 2 - 4 * y
    count = out.shape[0]
    blocks = xs.shape[0]
    hidden = hs.shape[2]
    series, _, length = x_ref.shape
    width = do_t.shape[0]
    heads = width // HEAD
    per = length // TILE

    def loads(n):
        return [
            pltpu.make_async_copy(src.at[n], dst, load_sem.at[i])
            for i, (src, dst) in enumerate(((xs, x_in), (dys, dy_in), (dgs, dg_in), (hs, h_in)))]

    def attn_loads(n):
        pairs = ((qkvs.at[n], qkv), (dos.at[n], do_t), (lses.at[n], lse), (a_all.at[block(n, length)], a))
        return [pltpu.make_async_copy(src, dst, attn_sem.at[i]) for i, (src, dst) in enumerate(pairs)]

    def dx1_load(n):
        return pltpu.make_async_copy(dx1_all.at[block(n, length)], dx1, dx1_sem)

    rest_load = pltpu.make_async_copy(rest, stack.at[pl.ds(3 * width, width + LANES)], rest_sem)
    for copy in loads(0) + attn_loads(0) + [dx1_load(0), rest_load]:
        copy.start()

    barrier = pltpu.get_barrier_semaphore()
    for peer, core in ((xp, mp), (yp, mp), (dp, 1 - mp)):
        pl.semaphore_signal(barrier, inc=1, device_id=(peer, core), device_id_type=MESH)

    @pl.when(z > 0)
    def _():
        pl.semaphore_signal(barrier, inc=1, device_id=(dp - 4, mp), device_id_type=MESH)

    @pl.when(z < 3)
    def _():
        pl.semaphore_signal(barrier, inc=1, device_id=(dp + 4, mp), device_id_type=MESH)

    @pl.when((z > 0) & (z < 3))
    def _():
        pl.semaphore_wait(barrier, 5)

    @pl.when((z == 0) | (z == 3))
    def _():
        pl.semaphore_wait(barrier, 4)

    stack[0:3 * width, :] = jnp.zeros((3 * width, D), F32)

    def shard(slot, i):
        return dw.at[slot, i]


    def weights(n, more):
        for copy in loads(n):
            copy.wait()
        xt[...] = jnp.transpose(x_in[...])
        dyt[...] = jnp.transpose(dy_in[...])

        def wide(j, carry):
            cols = block(j, TILE, TILE)
            v = dot(xt[...], dg_in[:, cols])
            temp[:, cols] = temp[:, cols] + v if more else v
            return carry

        def tall(j, carry):
            there = pl.ds(pl.multiple_of(2 * hidden + j * TILE, TILE), TILE)
            v = dot(dyt[...], h_in[:, block(j, TILE, TILE)])
            temp[:, there] = temp[:, there] + v if more else v
            return carry

        lax.fori_loop(0, 2 * hidden // TILE, wide, 0)
        lax.fori_loop(0, hidden // TILE, tall, 0)

        @pl.when(n + 1 < blocks)
        def _():
            for copy in loads(n + 1):
                copy.start()

    def begin(c):
        k, slot = lax.rem(c, 2), lax.rem(c, SLOTS)
        weights(c, False)

        @pl.when(c == count - 1)
        def _():
            weights(c + 1, True)

        @pl.when(c >= SLOTS)
        def _():
            done(send1.at[slot], sem_s1.at[slot])

        def pack(i, carry):
            m, n = i // 2, lax.rem(i, 2)
            gone = m * 4 + jnp.where(k == 0, n * 2 + 1 - x, (1 - y) * 2 + n)
            kept = m * 4 + jnp.where(k == 0, n * 2 + x, y * 2 + n)
            encode(send1.at[slot, i], temp[block(gone, SHARD), :])
            dw[slot, i] = temp[block(kept, SHARD), :]
            return carry

        lax.fori_loop(0, 8, pack, 0)
        remote(send1.at[slot], recv1.at[c], sem_s1.at[slot], sem_r1.at[c], jnp.where(k == 0, xp, yp), mp).start()

    def fold(c):
        k, slot, hop = lax.rem(c, 2), lax.rem(c, SLOTS), lax.rem(c, HOPS)
        o = jnp.where(k == 0, y, x)
        done(recv1.at[c], sem_r1.at[c])

        @pl.when(c >= HOPS)
        def _():
            done(send2.at[hop], sem_s2.at[hop])

        def add(m, carry):
            gone, kept = m * 2 + 1 - o, m * 2 + o
            encode(send2.at[hop, m], dw[slot, gone] + decode(recv1.at[c, gone]))
            acc[lax.rem(c, ACCS), m] = dw[slot, kept] + decode(recv1.at[c, kept])
            return carry

        lax.fori_loop(0, 4, add, 0)
        remote(send2.at[hop], recv2.at[c], sem_s2.at[hop], sem_r2.at[c], jnp.where(k == 0, yp, xp), mp).start()

    def climb(c, t, relay):
        slot = lax.rem(c, HOPS)
        v = acc[lax.rem(c, ACCS), t]
        if relay:
            done(up.at[c, t - 1], sem_ru.at[c, t - 1])
            v = v + decode(up.at[c, t - 1])

        @pl.when(c >= HOPS)
        def _():
            done(zs_up.at[slot, t - 1], sem_su.at[slot, t - 1])
        encode(zs_up.at[slot, t - 1], v)
        remote(zs_up.at[slot, t - 1], up.at[c, t - 1], sem_su.at[slot, t - 1], sem_ru.at[c, t - 1], dp + 4, mp).start()

    def drop(c, t, relay):
        slot = lax.rem(c, HOPS)
        v = acc[lax.rem(c, ACCS), t]
        if relay:
            done(dn.at[c, t], sem_rd.at[c, t])
            v = v + decode(dn.at[c, t])

        @pl.when(c >= HOPS)
        def _():
            done(zs_dn.at[slot, t], sem_sd.at[slot, t])
        encode(zs_dn.at[slot, t], v)
        remote(zs_dn.at[slot, t], dn.at[c, t], sem_sd.at[slot, t], sem_rd.at[c, t], dp - 4, mp).start()

    def line_a(c):
        done(recv2.at[c], sem_r2.at[c])
        there = lax.rem(c, ACCS)

        def add(m, carry):
            acc[there, m] = acc[there, m] + decode(recv2.at[c, m])
            return carry

        lax.fori_loop(0, 4, add, 0)
        out[c] = acc[there, z]

        @pl.when(z == 0)
        def _():
            for t in (3, 2, 1):
                climb(c, t, False)

        @pl.when(z == 3)
        def _():
            for t in (0, 1, 2):
                drop(c, t, False)

    def line_b(c):
        @pl.when(z == 1)
        def _():
            for t in (3, 2):
                climb(c, t, True)

        @pl.when(z == 2)
        def _():
            for t in (0, 1):
                drop(c, t, True)

    def line_c(c):
        @pl.when(z == 2)
        def _():
            climb(c, 3, True)

        @pl.when(z == 1)
        def _():
            drop(c, 0, True)

    def finish(c):
        @pl.when(z > 0)
        def _():
            done(up.at[c, z - 1], sem_ru.at[c, z - 1])
            out[c] = out[c] + decode(up.at[c, z - 1])

        @pl.when(z < 3)
        def _():
            done(dn.at[c, z], sem_rd.at[c, z])
            out[c] = out[c] + decode(dn.at[c, z])


    def pair(n):
        r = block(n, length)
        return remote(part, other.at[r], pair_send.at[n], pair_recv.at[n], dp, 1 - mp)

    def head(p):
        n, h = p // heads, lax.rem(p, heads)

        @pl.when(h == 0)
        def _():
            for copy in attn_loads(n):
                copy.wait()
        backward_head(h, width, qkv, do_t, lse, cos_ref[...], sin_ref[...], dqkv, dk, dv)

        @pl.when(h == heads - 1)
        def _():
            stack[0:3 * width, :] = stack[0:3 * width, :] + dot(dqkv[...], a[...])
            part[...] = dot(dqkv[...], wt[0:3 * width, :], 0, 0)
            pair(n).start()

            @pl.when(n + 1 < series)
            def _():
                for copy in attn_loads(n + 1):
                    copy.start()

    def embed(m):
        n, i = m // per, lax.rem(m, per)
        t = block(i, TILE, TILE)

        @pl.when(m == 0)
        def _():
            rest_load.wait()

        @pl.when(i == 0)
        def _():
            pair(n).wait()
            dx1_load(n).wait()
        da = part[t, :] + other[block(m, TILE), :]
        sums = embed_backward_piece(x_ref[n, :, t], da, dx1[t, :], vec)
        for row, value in zip((0, 3, 4), sums):
            there = slice(4 * width + VECTOR + row, 4 * width + VECTOR + row + 1)
            stack[there, :] = stack[there, :] + value

        @pl.when((i == per - 1) & (n + 1 < series))
        def _():
            dx1_load(n + 1).start()


    half = 512
    total_width = sm.shape[-1]
    ca, cb = pl.ds(0, half), pl.ds(half, total_width - half)

    def small_begin():
        sm[...] = jnp.transpose(stack[...]).reshape(sm.shape)
        remote(sm.at[:, :, 1 - x, :, ca], small_a1, small_sa, small_r.at[0], xp, mp).start()
        remote(sm.at[:, 1 - y, :, :, cb], small_b1, small_sb, small_r.at[1], yp, mp).start()

    def small_fold():
        done(small_a1, small_r.at[0])
        done(small_b1, small_r.at[1])
        for m in range(4):
            for n in range(2):
                sm[m, n, x, :, ca] = sm[m, n, x, :, ca] + small_a1[m, n]
                sm[m, y, n, :, cb] = sm[m, y, n, :, cb] + small_b1[m, n]
        remote(sm.at[:, 1 - y, x, :, ca], small_a2, small_send.at[0], small_r.at[2], yp, mp).start()
        remote(sm.at[:, y, 1 - x, :, cb], small_b2, small_send.at[1], small_r.at[3], xp, mp).start()

    def small_climb(t, relay):
        if relay:
            done(small_up.at[t - 1], small_ru.at[t - 1])
            sm[t, y, x] = sm[t, y, x] + small_up[t - 1]
        remote(sm.at[t, y, x], small_up.at[t - 1], small_su.at[t - 1], small_ru.at[t - 1], dp + 4, mp).start()

    def small_drop(t, relay):
        if relay:
            done(small_dn.at[t], small_rd.at[t])
            sm[t, y, x] = sm[t, y, x] + small_dn[t]
        remote(sm.at[t, y, x], small_dn.at[t], small_sd.at[t], small_rd.at[t], dp - 4, mp).start()

    def small_a():
        done(small_a2, small_r.at[2])
        done(small_b2, small_r.at[3])
        for m in range(4):
            sm[m, y, x, :, ca] = sm[m, y, x, :, ca] + small_a2[m]
            sm[m, y, x, :, cb] = sm[m, y, x, :, cb] + small_b2[m]
        out_small[...] = sm[z, y, x]

        @pl.when(z == 0)
        def _():
            for t in (3, 2, 1):
                small_climb(t, False)

        @pl.when(z == 3)
        def _():
            for t in (0, 1, 2):
                small_drop(t, False)

    def small_b():
        @pl.when(z == 1)
        def _():
            for t in (3, 2):
                small_climb(t, True)

        @pl.when(z == 2)
        def _():
            for t in (0, 1):
                small_drop(t, True)

    def small_c():
        @pl.when(z == 2)
        def _():
            small_climb(3, True)

        @pl.when(z == 1)
        def _():
            small_drop(0, True)

    def small_finish():
        @pl.when(z > 0)
        def _():
            done(small_up.at[z - 1], small_ru.at[z - 1])
            out_small[...] = out_small[...] + small_up[z - 1]

        @pl.when(z < 3)
        def _():
            done(small_dn.at[z], small_rd.at[z])
            out_small[...] = out_small[...] + small_dn[z]


    def at(i, first, number, run):
        @pl.when((i >= first) & (i < first + number))
        def _():
            run(i - first)

    small_first = count

    def step(i, carry):
        at(i, 0, count, begin)

        @pl.when(i < series * heads // 2)
        def _():
            def two(q, carry):
                head(2 * i + q)
                return carry
            lax.fori_loop(0, 2, two, 0)

        for n in range(series):
            @pl.when((i >= 3 + n * 3) & (i < 3 + n * 3 + per // 2))
            def _():
                def two(q, carry):
                    embed(n * per + 2 * (i - 3 - n * 3) + q)
                    return carry
                lax.fori_loop(0, 2, two, 0)
        at(i, small_first, 1, lambda _: small_begin())
        at(i, 2, count, fold)
        at(i, small_first + 1, 1, lambda _: small_fold())
        at(i, 4, count, line_a)
        at(i, small_first + 2, 1, lambda _: small_a())
        at(i, 5, count, line_b)
        at(i, small_first + 3, 1, lambda _: small_b())
        at(i, 6, count, line_c)
        at(i, small_first + 4, 1, lambda _: small_c())
        at(i, 7, count, finish)
        at(i, small_first + 5, 1, lambda _: small_finish())
        return carry

    lax.fori_loop(0, count + 7, step, 0)

    for slot in range(SLOTS):
        done(send1.at[slot], sem_s1.at[slot])
    for slot in range(HOPS):
        done(send2.at[slot], sem_s2.at[slot])
        for t in (1, 2, 3):
            @pl.when(z < t)
            def _():
                done(zs_up.at[slot, t - 1], sem_su.at[slot, t - 1])
        for t in (0, 1, 2):
            @pl.when(z > t)
            def _():
                done(zs_dn.at[slot, t], sem_sd.at[slot, t])
    done(small_a1, small_sa)
    done(small_b1, small_sb)
    done(small_a2, small_send.at[0])
    done(small_b2, small_send.at[1])
    for t in (1, 2, 3):
        @pl.when(z < t)
        def _():
            done(small_up.at[t - 1], small_su.at[t - 1])
    for t in (0, 1, 2):
        @pl.when(z > t)
        def _():
            done(small_dn.at[t], small_sd.at[t])


def backward_near(xs, dys, dgs, hs, qkv, do, lse, a, dx1, rest, x, wt, vec, cos, sin, ident):
    capacity, hidden = hs.shape[1], hs.shape[2]
    series, rows, length = qkv.shape
    heads_width = rows // 3
    count = ROUTED_EXPERTS + 1
    width = 3 * hidden
    coded = width + LANES
    small = 4 * heads_width + LANES
    tokens = series * length
    v = pltpu.VMEM
    return pl.pallas_call(
        backward_kernel,
        in_specs=[ANY] * 10 + [VMEM] * 5,
        out_specs=[VMEM] * 2,
        out_shape=[
            jax.ShapeDtypeStruct((count, SHARD, width), F32), jax.ShapeDtypeStruct((SHARD, small), F32)],
        scratch_shapes=[
            v((capacity, D), BF16), v((capacity, D), BF16), v((capacity, 2 * hidden), BF16), v((capacity, hidden), BF16),
            v((D, capacity), BF16), v((D, capacity), BF16),
            v((D, width), F32), v((SLOTS, 8, SHARD, width), F32), v((ACCS, 4, SHARD, width), F32),
            v((SLOTS, 8, SHARD, coded), I16), v((count, 8, SHARD, coded), I16),
            v((HOPS, 4, SHARD, coded), I16), v((count, 4, SHARD, coded), I16),
            v((HOPS, 3, SHARD, coded), I16), v((HOPS, 3, SHARD, coded), I16),
            v((count, 3, SHARD, coded), I16), v((count, 3, SHARD, coded), I16),
            v((rows, length), BF16), v((heads_width, length), BF16), v((8, length), F32), v((length, D), BF16),
            v((length, D), F32), v((rows, length), BF16), v((length, HEAD), F32), v((length, HEAD), F32),
            v((small, D), F32), v((length, D), F32), v((tokens, D), F32),
            v((4, 2, 2, SHARD, small), F32),
            v((4, 2, SHARD, 512), F32), v((4, 2, SHARD, small - 512), F32),
            v((4, SHARD, 512), F32), v((4, SHARD, small - 512), F32),
            v((3, SHARD, small), F32), v((3, SHARD, small), F32),
            DMA((4,)), DMA((SLOTS,)), DMA((count,)), DMA((HOPS,)), DMA((count,)),
            DMA((HOPS, 3)), DMA((HOPS, 3)), DMA((count, 3)), DMA((count, 3)),
            DMA((4,)), DMA, DMA, DMA((series,)), DMA((series,)),
            DMA((2,)), DMA, DMA, DMA((4,)), DMA((3,)), DMA((3,)), DMA((3,)), DMA((3,)),
        ],
        compiler_params=pltpu.CompilerParams(
            vmem_limit_bytes=67_000_000, collective_id=ident, has_side_effects=True),
        name="backward_near",
    )(xs, dys, dgs, hs, qkv, do, lse, a, dx1, rest, x, wt, vec, cos, sin)


def all_kernel(value, out, send_sem, recv_sem):
    dp, mp = lax.axis_index("dp"), lax.axis_index("mp")
    me = dp * 2 + mp
    meet_everyone(dp, mp)

    def tell(k, carry):
        peer = lax.rem(me + k, 32)
        remote(value, out.at[me], send_sem, recv_sem, peer // 2, lax.rem(peer, 2)).start()
        return carry

    lax.fori_loop(1, 32, tell, 0)
    out[me] = value[...]
    view = out.at[pl.ds(0, 31)]
    done(view, recv_sem)
    done(view, send_sem)


def all_blocks(value, ident):
    return pl.pallas_call(
        all_kernel,
        in_specs=[VMEM],
        out_specs=VMEM,
        out_shape=jax.ShapeDtypeStruct((32,) + value.shape, value.dtype),
        scratch_shapes=[DMA, DMA],
        compiler_params=pltpu.CompilerParams(collective_id=ident, has_side_effects=True),
        name="all_blocks",
    )(value)


def rope_rows(length):
    halfway = HEAD // 2
    frequency = rope_base ** (-2.0 * jnp.arange(halfway, dtype=F32) / HEAD)
    angles = frequency[:, None] * jnp.arange(length, dtype=F32)[None, :]
    return jnp.cos(angles), jnp.sin(angles)


def hankel_rows(track):
    length = track.shape[1]
    padded = jnp.pad(track, ((0, 0), (63, 2 * LANES)))
    first = padded[:, :length].reshape(-1, LANES)[:, ::-1]
    second = padded[:, LANES:LANES + length].reshape(-1, LANES)[:, ::-1]
    return jnp.concatenate([first, second], axis=1)


def table_columns(read, vec):
    parts, end = [], read.shape[1]
    for horizon in horizons[::-1]:
        parts.append(read[:, end - horizon:end][:, ::-1])
        end -= horizon
    gap = jnp.zeros((read.shape[0], ROUTER - sum(horizons)), read.dtype)
    tail = jnp.zeros((read.shape[0], LANES - VECTOR - vec.shape[1]), read.dtype)
    return jnp.concatenate(parts + [gap, read[:, :ROUTED_EXPERTS + 1], vec, tail], axis=1)


def table_columns_back(table):
    parts, begin = [], 0
    for horizon in horizons[::-1]:
        parts.append(table[:, begin:begin + horizon][:, ::-1])
        begin += horizon
    return jnp.concatenate([table[:, ROUTER:VECTOR]] + parts[::-1], axis=1)


def dispatch(route_rows, capacity):
    tokens = route_rows.shape[0]
    experts = jnp.arange(ROUTED_EXPERTS, dtype=jnp.int32)
    member = jnp.any(route_rows[:, :, None] == experts[None, None, :], axis=1)
    count = jnp.cumsum(member.astype(jnp.int32), axis=0)
    total = count[-1]
    place = jnp.where(member, count - 1, -1)
    high = (place[:, :, None] // LANES == jnp.arange(capacity // LANES)[None, None, :]) & member[:, :, None]
    low = (place[:, :, None] % LANES == jnp.arange(LANES)[None, None, :]).astype(BF16)
    token = jnp.arange(tokens, dtype=jnp.int32)
    left = jnp.concatenate(
        [jnp.where(high, part[:, None, None], 0).astype(BF16) for part in (token // 16, token % 16)], axis=2)
    found = jnp.einsum("teh,tel->ehl", left, low, preferred_element_type=F32)
    half = capacity // LANES
    source = (found[:, :half] * 16.0 + found[:, half:]).reshape(ROUTED_EXPERTS, capacity).astype(jnp.int32)
    source = jnp.where(jnp.arange(capacity, dtype=jnp.int32)[None, :] < total[:, None], source, tokens)
    source = jnp.concatenate([source.reshape(-1), jnp.full((TILE,), tokens, jnp.int32)]) * 8
    per = capacity // TILE
    routed = ROUTED_EXPERTS * per
    tile = jnp.arange(routed + tokens // TILE, dtype=jnp.int32)
    need = (total + TILE - 1) // TILE
    begin = jnp.sum(jnp.where(experts[None, :] < experts[:, None], total[None, :], 0), axis=1)
    mine = jnp.minimum(tile // per, ROUTED_EXPERTS - 1)[:, None] == experts[None, :]
    used = (tile < routed) & (tile % per < jnp.sum(jnp.where(mine, need[None, :], 0), axis=1))
    order = jnp.where(used, jnp.sum(jnp.where(mine, begin[None, :], 0), axis=1) + tile % per * TILE, -1)
    next_tile = jnp.concatenate([tile, jnp.full((1,), -1, jnp.int32)])
    later = used[None, :] & (tile[None, :] > next_tile[:, None])
    after = jnp.min(jnp.where(later, tile[None, :], routed), axis=1) * TILE
    slot = (begin[None, :] + count - 1) * 8
    slots = jnp.sum(jnp.where(route_rows[:, :, None] == experts[None, None, :], slot[:, None, :], 0), axis=2)
    return total, (need, order, after, source, slots.T.reshape(-1))


def adam_update(master, moment, square, gradient, factor, bias_one, bias_two, step_rate):
    clipped = gradient * factor
    new_moment = beta_one * moment + (1.0 - beta_one) * clipped
    new_square = beta_two * square + (1.0 - beta_two) * clipped * clipped
    updated = master - step_rate * (
        new_moment / bias_one / (jnp.sqrt(new_square / bias_two) + adam_eps) + decay_rate * master
    )
    return (updated, new_moment, new_square)


def on_device(
    series, observed, routes, step_count,
    joint_proj, joint_moment, joint_square,
    mixer_proj, mixer_moment, mixer_square,
    upward_proj, upward_moment, upward_square,
    downward_proj, downward_moment, downward_square,
    readout, readout_moment, readout_square,
    vectors, vectors_moment, vectors_square,
):
    dp_count = lax.axis_size("dp")
    mp_count = lax.axis_size("mp")
    shard = joint_proj.shape[1]
    width = joint_proj.shape[2]
    hidden = upward_proj.shape[3]
    experts = upward_proj.shape[0]
    series_count, length = series.shape
    tokens = series_count * length
    capacity = tokens // 2

    small_own = jnp.concatenate(
        [joint_proj[k].astype(BF16) for k in range(3)]
        + [mixer_proj.T.astype(BF16), table_columns(readout.astype(BF16), vectors.T.astype(BF16))], axis=1)
    big_own = jnp.concatenate(
        [upward_proj.astype(BF16).reshape(experts, shard, 2 * hidden), downward_proj.transpose(0, 2, 1).astype(BF16)],
        axis=2)
    marks = observed.astype(F32)
    expert_here, plan = dispatch(routes.reshape(tokens, 2), capacity)
    point = jnp.arange(length, dtype=F32)
    head_here = jnp.stack(
        [jnp.sum(jnp.sum(marks, axis=0) * jnp.minimum(point, float(horizon))) for horizon in horizons])
    tally = jnp.pad(jnp.concatenate([expert_here.astype(F32), head_here]), (0, LANES - 12))
    tally = jnp.broadcast_to(tally[None], (8, LANES))
    cos, sin = rope_rows(length)
    x = (series * marks).reshape(series_count, 1, length)

    big, wt, vec, table, a, qkv, lse, o, x1, b, pc, pr_total, tallies = forward_near(
        small_own, big_own, tally, x, cos, sin, width, 0)
    wo, table_t = wt[3 * width:4 * width], wt[4 * width:]
    tally = jnp.sum(tallies[:, 0], axis=0) / mp_count
    expert_count, head_count = tally[:ROUTED_EXPERTS], tally[ROUTED_EXPERTS:ROUTED_EXPERTS + 4]
    total_tokens = tokens * dp_count

    xs, ys, mixed = expert_forward(plan, b, pc, big)
    head_weight = jnp.concatenate(
        [jnp.zeros((horizon,), F32) + 0.25 / head_count[3 - index] for index, horizon in enumerate(horizons[::-1])])
    head_weight = jnp.pad(head_weight, (0, LANES - head_weight.shape[0]))[None]
    dx2, d_table, d_gain3, fit = loss_stage(
        mixed, x1, vec, table, table_t, hankel_rows(series), hankel_rows(marks), head_weight, 1)
    dys, dgs, hs, back = expert_backward(plan, pc, dx2, big, xs, ys)
    balance = aux_factor * ROUTED_EXPERTS * expert_count / total_tokens / total_tokens
    balance = jnp.pad(balance, (ROUTER, LANES - SHARED))[None]
    local_loss = jnp.sum(fit) + jnp.sum(pr_total * balance)
    dx1, do, rest = mid_backward(back, dx2, x1, b, pc, vec, table_t, balance, wo, o, d_table, d_gain3, 2)
    big_red, small_red = backward_near(xs, dys, dgs, hs, qkv, do, lse, a, dx1, rest, x, wt, vec, cos, sin, 3)

    attn_red, table_red = small_red[:, :4 * width], small_red[:, 4 * width:]
    squares = (
        jnp.sum(big_red * big_red) + jnp.sum(attn_red * attn_red) + jnp.sum(table_red * table_red) / mp_count
    )
    pair = jnp.pad(jnp.stack([squares, local_loss / mp_count]), (0, LANES - 2))
    pair = jnp.sum(all_blocks(jnp.broadcast_to(pair[None], (8, LANES)), 4)[:, 0], axis=0)
    grad_norm, loss_total = jnp.sqrt(pair[0]), pair[1]

    factor = clip_limit / (grad_norm + 1e-06)
    steps_taken = step_count[0].astype(F32)
    bias_one = 1.0 - beta_one**steps_taken
    bias_two = 1.0 - beta_two**steps_taken

    def update(master, moment, square, gradient, rate=matrix_rate):
        return adam_update(master, moment, square, gradient, factor, bias_one, bias_two, rate)

    joint_red = jnp.stack([attn_red[:, k * width:(k + 1) * width] for k in range(3)], axis=0)
    mixer_red = attn_red[:, 3 * width:].T
    upward_red = big_red[:, :, :2 * hidden].reshape(upward_proj.shape)
    downward_red = big_red[:, :, 2 * hidden:].transpose(0, 2, 1)
    return (
        loss_total,
        grad_norm,
        *update(joint_proj, joint_moment, joint_square, joint_red),
        *update(mixer_proj, mixer_moment, mixer_square, mixer_red),
        *update(upward_proj, upward_moment, upward_square, upward_red),
        *update(downward_proj, downward_moment, downward_square, downward_red),
        *update(readout, readout_moment, readout_square, table_columns_back(table_red)),
        *update(vectors, vectors_moment, vectors_square, table_red[:, VECTOR:VECTOR + 5].T, vector_rate),
    )


def rms_scale(tensor, gain_row):
    return (
        tensor * lax.rsqrt(jnp.mean(tensor * tensor, axis=-1, keepdims=True) + norm_eps) * gain_row
    )


def rope_tables(length, columns):
    halfway = columns // 2
    frequency = rope_base ** (-2.0 * jnp.arange(halfway, dtype=jnp.float32) / columns)
    angles = jnp.arange(length, dtype=jnp.float32)[:, None] * frequency[None, :]
    return (jnp.cos(angles), jnp.sin(angles))


def rotate(tensor, cosine_table, sine_table):
    halfway = tensor.shape[-1] // 2
    front_part = tensor[..., :halfway]
    back_part = tensor[..., halfway:]
    return jnp.concatenate(
        [
            front_part * cosine_table - back_part * sine_table,
            back_part * cosine_table + front_part * sine_table,
        ],
        axis=-1,
    )


def swiglu(tensor):
    halfway = tensor.shape[-1] // 2
    return jax.nn.silu(tensor[..., :halfway]) * tensor[..., halfway:]


def targets_of(series, observed):
    row_count, length = series.shape
    longest = max(horizons)
    padded_values = jnp.concatenate([series, jnp.zeros((row_count, longest), jnp.float32)], axis=1)
    padded_marks = jnp.concatenate(
        [observed.astype(jnp.float32), jnp.zeros((row_count, longest), jnp.float32)], axis=1
    )
    value_window = jnp.stack(
        [padded_values[:, 1 + offset : 1 + offset + length] for offset in range(longest)], axis=-1
    )
    mark_window = jnp.stack(
        [padded_marks[:, 1 + offset : 1 + offset + length] for offset in range(longest)], axis=-1
    )
    observed_future_series = jnp.concatenate(
        [value_window[..., :horizon] for horizon in horizons], axis=-1
    )
    valid_mask = jnp.concatenate([mark_window[..., :horizon] for horizon in horizons], axis=-1)
    return (
        observed_future_series.reshape(row_count * length, -1),
        valid_mask.reshape(row_count * length, -1),
    )


def head_counts(valid_mask):
    beginnings = [sum(horizons[:index]) for index in range(len(horizons))]
    return jnp.stack(
        [
            jnp.sum(valid_mask[:, beginning : beginning + horizon])
            for beginning, horizon in zip(beginnings, horizons)
        ]
    )


def head_weights(head_count):
    return jnp.concatenate(
        [
            jnp.zeros((horizon,), jnp.float32) + 0.25 / head_count[index]
            for index, horizon in enumerate(horizons)
        ]
    )


def dispatch_plan(route_rows, experts, capacity):
    flat_routes = route_rows.reshape(-1)
    entries = flat_routes.shape[0]
    onehot = (flat_routes[:, None] == jnp.arange(experts, dtype=jnp.int32)[None, :]).astype(
        jnp.int32
    )
    position = jnp.sum(jnp.cumsum(onehot, axis=0) * onehot, axis=1) - 1
    slot_index = flat_routes * capacity + position
    source = (
        jnp.full((experts * capacity,), entries, jnp.int32)
        .at[slot_index]
        .set(jnp.arange(entries, dtype=jnp.int32))
    )
    return (slot_index, source)


def split_heads(matrix, series_count, length):
    return matrix.reshape(series_count, length, matrix.shape[1] // HEAD, HEAD).transpose(0, 2, 1, 3)


def merge_heads(tensor):
    series_count, heads_here, length, head_size = tensor.shape
    return tensor.transpose(0, 2, 1, 3).reshape(series_count * length, heads_here * head_size)


def block_scores(query_block, key_heads, offset, length):
    block_rows = query_block.shape[1]
    scores = jnp.einsum(
        "hqe,hke->hqk", query_block, key_heads, preferred_element_type=jnp.float32
    ) * HEAD ** (-0.5)
    allowed = (offset + jnp.arange(block_rows))[:, None] >= jnp.arange(length)[None, :]
    return jnp.where(allowed[None], scores, -1e30)


def attend_forward(pieces):
    query_heads, key_heads, value_heads = pieces
    length = query_heads.shape[1]
    block_rows = min(length, 512)
    outputs = []
    totals = []
    for offset in range(0, length, block_rows):
        scores = block_scores(
            query_heads[:, offset : offset + block_rows], key_heads, offset, length
        )
        row_peak = jnp.max(scores, axis=-1, keepdims=True)
        exponent = jnp.exp(scores - row_peak)
        row_mass = jnp.sum(exponent, axis=-1, keepdims=True)
        outputs.append(
            jnp.einsum(
                "hqk,hke->hqe",
                (exponent / row_mass).astype(jnp.bfloat16),
                value_heads,
                preferred_element_type=jnp.float32,
            )
        )
        totals.append(row_peak + jnp.log(row_mass))
    return (jnp.concatenate(outputs, axis=1), jnp.concatenate(totals, axis=1))


def attend_backward(pieces):
    query_heads, key_heads, value_heads, grads_out, totals = pieces
    length = query_heads.shape[1]
    block_rows = min(length, 512)
    key_grad = jnp.zeros(key_heads.shape, jnp.float32)
    value_grad = jnp.zeros(value_heads.shape, jnp.float32)
    query_grads = []
    for offset in range(0, length, block_rows):
        query_block = query_heads[:, offset : offset + block_rows]
        grad_block = grads_out[:, offset : offset + block_rows]
        weights = jnp.exp(
            block_scores(query_block, key_heads, offset, length)
            - totals[:, offset : offset + block_rows]
        )
        grad_weights = jnp.einsum(
            "hqe,hke->hqk", grad_block, value_heads, preferred_element_type=jnp.float32
        )
        score_grad = (
            weights
            * (grad_weights - jnp.sum(weights * grad_weights, axis=-1, keepdims=True))
            * HEAD ** (-0.5)
        ).astype(jnp.bfloat16)
        query_grads.append(
            jnp.einsum("hqk,hke->hqe", score_grad, key_heads, preferred_element_type=jnp.float32)
        )
        key_grad = key_grad + jnp.einsum(
            "hqk,hqe->hke", score_grad, query_block, preferred_element_type=jnp.float32
        )
        value_grad = value_grad + jnp.einsum(
            "hqk,hqe->hke",
            weights.astype(jnp.bfloat16),
            grad_block,
            preferred_element_type=jnp.float32,
        )
    return (jnp.concatenate(query_grads, axis=1), key_grad, value_grad)


def branch_total(partial_sum):
    return lax.psum(partial_sum, "mp")


def input_total(partial_sum):
    return lax.psum(partial_sum, "mp")


def on_device_wide(
    series,
    observed,
    routes,
    step_count,
    joint_proj,
    joint_moment,
    joint_square,
    mixer_proj,
    mixer_moment,
    mixer_square,
    upward_proj,
    upward_moment,
    upward_square,
    downward_proj,
    downward_moment,
    downward_square,
    readout,
    readout_moment,
    readout_square,
    vectors,
    vectors_moment,
    vectors_square,
):
    dp_count = lax.axis_size("dp")
    hidden_local = upward_proj.shape[3]
    joint_full, mixer_full, upward_full, downward_full, readout_complete, vector_full = (
        lax.all_gather(joint_proj.astype(jnp.bfloat16), "dp", axis=1, tiled=True),
        lax.all_gather(mixer_proj.astype(jnp.bfloat16), "dp", axis=1, tiled=True),
        lax.all_gather(upward_proj.astype(jnp.bfloat16), "dp", axis=1, tiled=True),
        lax.all_gather(downward_proj.astype(jnp.bfloat16), "dp", axis=2, tiled=True),
        lax.all_gather(readout.astype(jnp.bfloat16), "dp", axis=0, tiled=True),
        lax.all_gather(vectors.astype(jnp.bfloat16), "dp", axis=1, tiled=True),
    )
    up_local = upward_full.reshape(upward_full.shape[0], D, -1)
    shared_up_weight = up_local[-1]
    shared_down_weight = downward_full[-1]
    expert_up = up_local[:ROUTED_EXPERTS]
    expert_down = downward_full[:ROUTED_EXPERTS]
    gain_rows = vector_full.astype(jnp.float32)
    series_count, length = series.shape
    entries = series_count * length
    route_rows = routes.reshape(entries, 2)
    onehot = route_rows[:, :, None] == jnp.arange(ROUTED_EXPERTS, dtype=jnp.int32)[None, None, :]
    observed_future_series, valid_mask = targets_of(series, observed)
    expert_count, head_count = lax.psum(
        (jnp.sum(onehot.astype(jnp.float32), axis=(0, 1)), head_counts(valid_mask)), "dp"
    )
    total_tokens = entries * dp_count
    inputs = (series * observed.astype(jnp.float32)).reshape(entries, 1)

    def embed(gate_vector, up_vector):
        return jax.nn.silu(inputs * gate_vector) * (inputs * up_vector)

    embedded, embed_back = jax.vjp(embed, gain_rows[3], gain_rows[4])
    normed_one, norm_one_back = jax.vjp(rms_scale, embedded, gain_rows[0])
    first_input = normed_one.astype(jnp.bfloat16)
    projected = jnp.einsum(
        "td,cde->cte", first_input, joint_full, preferred_element_type=jnp.float32
    )
    cosine_table, sine_table = rope_tables(length, HEAD)
    query_heads = rotate(
        split_heads(projected[0], series_count, length), cosine_table, sine_table
    ).astype(jnp.bfloat16)
    key_heads = rotate(
        split_heads(projected[1], series_count, length), cosine_table, sine_table
    ).astype(jnp.bfloat16)
    value_heads = split_heads(projected[2], series_count, length).astype(jnp.bfloat16)
    attended, totals = lax.map(attend_forward, (query_heads, key_heads, value_heads))
    attended_low = merge_heads(attended).astype(jnp.bfloat16)
    after_attn = embedded + branch_total(
        jnp.dot(attended_low, mixer_full, preferred_element_type=jnp.float32)
    )
    normed_two, norm_two_back = jax.vjp(rms_scale, after_attn, gain_rows[1])
    second_input = normed_two.astype(jnp.bfloat16)
    logits = jnp.dot(
        second_input, readout_complete[:, : ROUTED_EXPERTS + 1], preferred_element_type=jnp.float32
    )

    def gating(logit_rows):
        probabilities = jax.nn.softmax(logit_rows[:, :ROUTED_EXPERTS], axis=-1)
        chosen = jnp.sum(jnp.where(onehot, probabilities[:, None, :], 0.0), axis=-1)
        balance = (
            aux_factor
            * ROUTED_EXPERTS
            * jnp.sum(expert_count / total_tokens * jnp.sum(probabilities, axis=0) / total_tokens)
        )
        return (chosen, jax.nn.sigmoid(logit_rows[:, ROUTED_EXPERTS]), balance)

    (gate_values, shared_gate, balance), gating_back = jax.vjp(gating, logits)
    capacity = entries // 2
    slot_index, source = dispatch_plan(route_rows, ROUTED_EXPERTS, capacity)
    token_of = source // 2
    padded_input = jnp.concatenate([second_input, jnp.zeros((1, D), jnp.bfloat16)], axis=0)
    gathered = padded_input[token_of].reshape(ROUTED_EXPERTS, capacity, D)
    gate_up = jnp.einsum("ecd,edf->ecf", gathered, expert_up, preferred_element_type=jnp.float32)
    hidden_f, swiglu_back = jax.vjp(swiglu, gate_up)
    hidden = hidden_f.astype(jnp.bfloat16)
    expert_out = jnp.einsum(
        "ecf,efd->ecd", hidden, expert_down, preferred_element_type=jnp.float32
    ).reshape(ROUTED_EXPERTS * capacity, D)
    picked = expert_out[slot_index].reshape(entries, 2, D)
    shared_up = jnp.dot(second_input, shared_up_weight, preferred_element_type=jnp.float32)
    shared_f, shared_back = jax.vjp(swiglu, shared_up)
    shared_hidden = shared_f.astype(jnp.bfloat16)
    shared_out = jnp.dot(shared_hidden, shared_down_weight, preferred_element_type=jnp.float32)
    mixed_part = (
        jnp.sum(gate_values[:, :, None] * picked, axis=1) + shared_gate[:, None] * shared_out
    )
    after_mixer = after_attn + branch_total(mixed_part)
    normalized_output, norm_out_back = jax.vjp(rms_scale, after_mixer, gain_rows[2])
    output_input = normalized_output.astype(jnp.bfloat16)
    model_estimates = jnp.dot(
        output_input, readout_complete[:, ROUTED_EXPERTS + 1 :], preferred_element_type=jnp.float32
    )
    prediction_misses = model_estimates - observed_future_series
    absolute_miss = jnp.abs(prediction_misses)
    horizon_importance_factors = head_weights(head_count)[None, :] * valid_mask
    robust_penalty_entries = jnp.where(
        absolute_miss <= quadratic_cutoff,
        0.5 * prediction_misses * prediction_misses,
        quadratic_cutoff * (absolute_miss - 0.5 * quadratic_cutoff),
    )
    local_loss = jnp.sum(robust_penalty_entries * horizon_importance_factors) + balance
    mp_count = lax.axis_size("mp")
    loss_total = lax.psum(local_loss, "dp")
    predicted_gradient = (
        jnp.clip(prediction_misses, -quadratic_cutoff, quadratic_cutoff)
        * horizon_importance_factors
    ).astype(jnp.bfloat16)
    head_grad = jnp.einsum(
        "ka,ky->ay", output_input, predicted_gradient, preferred_element_type=jnp.float32
    )
    out_input_grad = jnp.einsum(
        "aw,iw->ai",
        predicted_gradient,
        readout_complete[:, ROUTED_EXPERTS + 1 :],
        preferred_element_type=jnp.float32,
    )
    mixer_grad_in, gain_three_grad = norm_out_back(out_input_grad)
    picked_dots = jnp.sum(picked * mixer_grad_in[:, None, :], axis=-1)
    shared_dots = jnp.sum(shared_out * mixer_grad_in, axis=-1)
    gate_grads, shared_gate_grad = lax.psum((picked_dots, shared_dots), "mp")
    (logit_grad,) = gating_back((gate_grads, shared_gate_grad, jnp.ones((), jnp.float32)))
    logit_low = logit_grad.astype(jnp.bfloat16)
    router_grad = jnp.einsum(
        "ka,ky->ay", second_input, logit_low, preferred_element_type=jnp.float32
    )
    router_input_grad = jnp.einsum(
        "aw,iw->ai",
        logit_low,
        readout_complete[:, : ROUTED_EXPERTS + 1],
        preferred_element_type=jnp.float32,
    )
    gates_padded = jnp.concatenate([gate_values.reshape(-1), jnp.zeros((1,), jnp.float32)], axis=0)
    residual_padded = jnp.concatenate([mixer_grad_in, jnp.zeros((1, D), jnp.float32)], axis=0)
    expert_out_grad = (
        (gates_padded[source][:, None] * residual_padded[token_of])
        .astype(jnp.bfloat16)
        .reshape(ROUTED_EXPERTS, capacity, D)
    )
    hidden_grad = jnp.einsum(
        "ecd,efd->ecf", expert_out_grad, expert_down, preferred_element_type=jnp.float32
    )
    down_grad_experts = jnp.einsum(
        "ecf,ecd->efd", hidden, expert_out_grad, preferred_element_type=jnp.float32
    )
    gate_up_grad = swiglu_back(hidden_grad)[0].astype(jnp.bfloat16)
    up_grad_experts = jnp.einsum(
        "ecd,ecf->edf", gathered, gate_up_grad, preferred_element_type=jnp.float32
    )
    rows_grad = jnp.einsum(
        "ecf,edf->ecd", gate_up_grad, expert_up, preferred_element_type=jnp.float32
    ).reshape(ROUTED_EXPERTS * capacity, D)
    routed_grad = jnp.sum(rows_grad[slot_index].reshape(entries, 2, D), axis=1)
    shared_out_grad = (shared_gate[:, None] * mixer_grad_in).astype(jnp.bfloat16)
    shared_hidden_grad = jnp.einsum(
        "td,fd->tf", shared_out_grad, shared_down_weight, preferred_element_type=jnp.float32
    )
    down_grad_shared = jnp.einsum(
        "tf,td->fd", shared_hidden, shared_out_grad, preferred_element_type=jnp.float32
    )
    shared_up_grad = shared_back(shared_hidden_grad)[0].astype(jnp.bfloat16)
    up_grad_shared = jnp.einsum(
        "td,tf->df", second_input, shared_up_grad, preferred_element_type=jnp.float32
    )
    input_part = routed_grad + jnp.einsum(
        "tf,df->td", shared_up_grad, shared_up_weight, preferred_element_type=jnp.float32
    )
    second_input_grad = input_total(input_part) + router_input_grad
    upward_grad = jnp.concatenate([up_grad_experts, up_grad_shared[None]], axis=0).reshape(
        ROUTED_EXPERTS + 1, D, 2, hidden_local
    )
    downward_grad = jnp.concatenate([down_grad_experts, down_grad_shared[None]], axis=0)
    attn_grad_in, gain_two_grad = norm_two_back(second_input_grad)
    attn_total_grad = mixer_grad_in + attn_grad_in
    attn_low = attn_total_grad.astype(jnp.bfloat16)
    mixer_grad = jnp.einsum("tf,td->fd", attended_low, attn_low, preferred_element_type=jnp.float32)
    attended_grad = jnp.einsum(
        "td,fd->tf", attn_low, mixer_full, preferred_element_type=jnp.float32
    ).astype(jnp.bfloat16)
    query_grad, key_grad, value_grad = lax.map(
        attend_backward,
        (
            query_heads,
            key_heads,
            value_heads,
            split_heads(attended_grad, series_count, length),
            totals,
        ),
    )
    projected_grad = jnp.stack(
        [
            merge_heads(rotate(query_grad, cosine_table, -sine_table)),
            merge_heads(rotate(key_grad, cosine_table, -sine_table)),
            merge_heads(value_grad),
        ],
        axis=0,
    ).astype(jnp.bfloat16)
    joint_grad = jnp.einsum(
        "td,cte->cde", first_input, projected_grad, preferred_element_type=jnp.float32
    )
    first_input_grad = input_total(
        jnp.einsum("cte,cde->td", projected_grad, joint_full, preferred_element_type=jnp.float32)
    )
    embed_grad_in, gain_one_grad = norm_one_back(first_input_grad)
    gate_vector_grad, up_vector_grad = embed_back(attn_total_grad + embed_grad_in)
    vector_grad = jnp.stack(
        [gain_one_grad, gain_two_grad, gain_three_grad, gate_vector_grad, up_vector_grad], axis=0
    )
    readout_grad = jnp.concatenate([router_grad, head_grad], axis=1)
    joint_red, mixer_red, upward_red, downward_red, readout_red, vector_red = (
        lax.psum_scatter(joint_grad, "dp", scatter_dimension=1, tiled=True),
        lax.psum_scatter(mixer_grad, "dp", scatter_dimension=1, tiled=True),
        lax.psum_scatter(upward_grad, "dp", scatter_dimension=1, tiled=True),
        lax.psum_scatter(downward_grad, "dp", scatter_dimension=2, tiled=True),
        lax.psum_scatter(readout_grad, "dp", scatter_dimension=0, tiled=True),
        lax.psum_scatter(vector_grad, "dp", scatter_dimension=1, tiled=True),
    )
    split_squares = (
        jnp.sum(joint_red * joint_red)
        + jnp.sum(mixer_red * mixer_red)
        + jnp.sum(upward_red * upward_red)
        + jnp.sum(downward_red * downward_red)
    )
    shared_squares = jnp.sum(readout_red * readout_red) + jnp.sum(vector_red * vector_red)
    partial_squares = split_squares + shared_squares / mp_count
    norm_squared = lax.psum(partial_squares, ("dp", "mp"))
    grad_norm = jnp.sqrt(norm_squared)
    factor = clip_limit / (grad_norm + 1e-06)
    steps_taken = step_count[0].astype(jnp.float32)
    bias_one = 1.0 - beta_one**steps_taken
    bias_two = 1.0 - beta_two**steps_taken
    joint_new = adam_update(
        joint_proj, joint_moment, joint_square, joint_red, factor, bias_one, bias_two, matrix_rate
    )
    mixer_new = adam_update(
        mixer_proj, mixer_moment, mixer_square, mixer_red, factor, bias_one, bias_two, matrix_rate
    )
    upward_new = adam_update(
        upward_proj,
        upward_moment,
        upward_square,
        upward_red,
        factor,
        bias_one,
        bias_two,
        matrix_rate,
    )
    downward_new = adam_update(
        downward_proj,
        downward_moment,
        downward_square,
        downward_red,
        factor,
        bias_one,
        bias_two,
        matrix_rate,
    )
    readout_new = adam_update(
        readout,
        readout_moment,
        readout_square,
        readout_red,
        factor,
        bias_one,
        bias_two,
        matrix_rate,
    )
    vector_new = adam_update(
        vectors, vectors_moment, vectors_square, vector_red, factor, bias_one, bias_two, vector_rate
    )
    return (
        loss_total,
        grad_norm,
        joint_new[0],
        joint_new[1],
        joint_new[2],
        mixer_new[0],
        mixer_new[1],
        mixer_new[2],
        upward_new[0],
        upward_new[1],
        upward_new[2],
        downward_new[0],
        downward_new[1],
        downward_new[2],
        readout_new[0],
        readout_new[1],
        readout_new[2],
        vector_new[0],
        vector_new[1],
        vector_new[2],
    )


def solution(mesh):
    token = [P("dp", None), P("dp", None), P("dp", None, None), P()]
    weights = [
        P(None, "dp", "mp"), P("mp", "dp"), P(None, "dp", None, "mp"), P(None, "mp", "dp"), P("dp", None), P(None, "dp"),
    ]
    triple = tuple(spec for spec in weights for _ in range(3))
    near = mesh.shape["dp"] == 16 and mesh.shape["mp"] == 2
    return jax.shard_map(
        on_device if near else on_device_wide,
        mesh=mesh,
        in_specs=tuple(token) + triple,
        out_specs=(P(), P()) + triple,
        check_vma=False,
    )
```

```python
import functools
import jax
import jax.numpy as jnp
from jax import lax
from jax.experimental import pallas as pl
from jax.experimental.pallas import tpu as pltpu
from jax.sharding import PartitionSpec as P

D = 384
HEAD = 32
ROUTED_EXPERTS = 8
LANES = 128
TILE = 256
SHARD = 24
ROUTER = 112
SHARED = ROUTER + ROUTED_EXPERTS
VECTOR = SHARED + 1

horizons = (1, 8, 32, 64)
quadratic_cutoff = 2.0
aux_factor = 0.02
clip_limit = 0.001
beta_one = 0.9
beta_two = 0.95
adam_eps = 1e-08
decay_rate = 0.1
matrix_rate = 0.05
vector_rate = 0.25
norm_eps = 1e-06
rope_base = 10000.0

F32 = jnp.float32
BF16 = jnp.bfloat16
I16 = jnp.int16
MESH = pl.DeviceIdType.MESH
VMEM = pl.BlockSpec(memory_space=pltpu.VMEM)
ANY = pl.BlockSpec(memory_space=pl.ANY)
DMA = pltpu.SemaphoreType.DMA


def dot(a, b, da=1, db=0):
    return lax.dot_general(a, b, (((da,), (db,)), ((), ())), preferred_element_type=F32)


def params(megabytes=60, **more):
    return pltpu.CompilerParams(vmem_limit_bytes=megabytes * 1024 * 1024, **more)


def sigmoid(v):
    return 1.0 / (1.0 + jnp.exp(-v))


def block(index, size, step=8):
    return pl.ds(pl.multiple_of(index * size, step), size)


def place():
    dp = lax.axis_index("dp")
    return dp, lax.axis_index("mp"), lax.rem(dp, 2), lax.rem(dp // 2, 2), dp // 4


def meet_everyone(dp, mp):
    barrier = pltpu.get_barrier_semaphore()
    me, n = dp * 2 + mp, 32

    def signal(k, carry):
        peer = lax.rem(me + k, n)
        pl.semaphore_signal(barrier, inc=1, device_id=(peer // 2, lax.rem(peer, 2)), device_id_type=MESH)
        return carry

    lax.fori_loop(1, n, signal, 0)
    pl.semaphore_wait(barrier, n - 1)


def remote(src, dst, send, recv, dp, mp):
    return pltpu.make_async_remote_copy(
        src_ref=src, dst_ref=dst, send_sem=send, recv_sem=recv, device_id=(dp, mp), device_id_type=MESH)


def done(view, sem):
    pltpu.make_async_copy(view, view, sem).wait()


def column(row, length):
    return jnp.transpose(jnp.broadcast_to(row, (LANES, length)))


def rotated(t, cos, sin):
    half = HEAD // 2
    front, back = t[:half], t[half:]
    return jnp.concatenate([front * cos - back * sin, back * cos + front * sin], axis=0)


def unrotated(t, cos, sin):
    half = HEAD // 2
    front, back = t[:half], t[half:]
    return jnp.concatenate([front * cos + back * sin, back * cos - front * sin], axis=0)


def score_block(k_rows, q_cols, low):
    s = dot(k_rows, q_cols)
    keys = lax.broadcasted_iota(jnp.int32, s.shape, 0)
    queries = lax.broadcasted_iota(jnp.int32, s.shape, 1) + low
    return jnp.where(keys <= queries, s, -1e30)


def flip(t):
    return jnp.transpose(t.astype(F32)).astype(BF16)


def embed_piece(x_row, vec, x0_ref, a_ref, r):
    xb = column(x_row, TILE)
    cuts, square = [], None
    for c in range(D // LANES):
        cols = slice(c * LANES, (c + 1) * LANES)
        u = xb * vec[3:4, cols]
        v = u * sigmoid(u) * (xb * vec[4:5, cols])
        x0_ref[r, cols] = v
        square = v * v if square is None else square + v * v
        cuts.append(v)
    scale = lax.rsqrt(jnp.sum(square, axis=1, keepdims=True) / D + norm_eps)
    for c in range(D // LANES):
        cols = slice(c * LANES, (c + 1) * LANES)
        a_ref[r, cols] = (cuts[c] * scale * vec[0:1, cols]).astype(BF16)


def project_piece(wt, a, cos, sin, qkv, width):
    for part in range(3):
        t = dot(wt[part * width:(part + 1) * width, :], a, 1, 1)
        for h in range(width // HEAD):
            u = t[h * HEAD:(h + 1) * HEAD]
            if part < 2:
                u = rotated(u, cos, sin)
            qkv[part * width + h * HEAD:part * width + (h + 1) * HEAD, :] = u.astype(BF16)


def forward_head(h, width, qkv, lse, o):
    length = qkv.shape[1]
    scale = HEAD ** (-0.5)
    q_rows = block(h, HEAD)
    k_rows = pl.ds(pl.multiple_of(width + h * HEAD, HEAD), HEAD)
    v_rows = pl.ds(pl.multiple_of(2 * width + h * HEAD, HEAD), HEAD)
    k = flip(qkv[k_rows, :])
    for j in range(length // TILE):
        n = TILE * (j + 1)
        cols = slice(j * TILE, (j + 1) * TILE)
        s = score_block(k[:n], qkv[q_rows, cols], j * TILE)
        peak = jnp.max(s, axis=0, keepdims=True)
        e = jnp.exp((s - peak) * scale)
        mass = jnp.sum(e, axis=0, keepdims=True)
        weights = (e * (1.0 / mass)).astype(BF16)
        o[q_rows, cols] = dot(qkv[v_rows, :n], weights).astype(BF16)
        lse[pl.ds(h, 1), cols] = peak * scale + jnp.log(mass)


def backward_head(h, width, qkv, do_t, lse, cos, sin, dqkv, dk_ref, dv_ref):
    length = qkv.shape[1]
    scale = HEAD ** (-0.5)
    q_rows = block(h, HEAD)
    k_rows = pl.ds(pl.multiple_of(width + h * HEAD, HEAD), HEAD)
    v_rows = pl.ds(pl.multiple_of(2 * width + h * HEAD, HEAD), HEAD)
    q, k, v, do = flip(qkv[q_rows, :]), flip(qkv[k_rows, :]), flip(qkv[v_rows, :]), flip(do_t[q_rows, :])
    dk_ref[...] = jnp.zeros_like(dk_ref)
    dv_ref[...] = jnp.zeros_like(dv_ref)
    for j in range(length // TILE):
        n = TILE * (j + 1)
        cols = slice(j * TILE, (j + 1) * TILE)
        s = score_block(k[:n], qkv[q_rows, cols], j * TILE)
        w = jnp.exp(s * scale - lse[pl.ds(h, 1), cols])
        dv_ref[:n] += dot(w.astype(BF16), do[cols])
        dw = dot(v[:n], do_t[q_rows, cols])
        mean = jnp.sum(w * dw, axis=0, keepdims=True)
        ds = (w * (dw - mean) * scale).astype(BF16)
        dk_ref[:n] += dot(ds, q[cols])
        dq = dot(qkv[k_rows, :n], ds)
        dqkv[q_rows, cols] = unrotated(dq, cos[:, cols], sin[:, cols]).astype(BF16)
    dqkv[k_rows, :] = unrotated(jnp.transpose(dk_ref[...]), cos, sin).astype(BF16)
    dqkv[v_rows, :] = jnp.transpose(dv_ref[...]).astype(BF16)


def mid_forward_piece(x, gain, table):
    scale = lax.rsqrt(jnp.mean(x * x, axis=1, keepdims=True) + norm_eps)
    low = (x * scale * gain).astype(BF16)
    logits = dot(low, table)
    lanes = lax.broadcasted_iota(jnp.int32, logits.shape, 1)
    routed = (lanes >= ROUTER) & (lanes < SHARED)
    peak = jnp.max(jnp.where(routed, logits, -jnp.inf), axis=1, keepdims=True)
    e = jnp.where(routed, jnp.exp(jnp.where(routed, logits - peak, 0.0)), 0.0)
    probability = e / jnp.sum(e, axis=1, keepdims=True)
    gates = jnp.where(lanes == SHARED, sigmoid(jnp.where(lanes == SHARED, logits, 0.0)), probability)
    return low, gates, jnp.sum(probability, axis=0, keepdims=True)


def embed_backward_piece(x_row, da, dx1, vec):
    xb = column(x_row, TILE)
    xb = jnp.concatenate([xb] * (D // LANES), axis=1)
    u = xb * vec[3:4, :]
    up = xb * vec[4:5, :]
    s = sigmoid(u)
    silu = u * s
    x = silu * up
    scale = lax.rsqrt(jnp.mean(x * x, axis=1, keepdims=True) + norm_eps)
    unit = x * scale
    dn = da * vec[0:1, :]
    dx = dx1 + scale * (dn - unit * jnp.mean(dn * unit, axis=1, keepdims=True))
    du = dx * up * (s * (1.0 + u * (1.0 - s)))
    total = lambda v: jnp.sum(v, axis=0, keepdims=True)
    return total(da * unit), total(du * xb), total(dx * silu * xb)


def forward_kernel(
    small_own, big_own, tally, x_ref, cos_ref, sin_ref,
    big, wt, vec, table, a, qkv, lse, o, x1, b, pc, total, tallies,
    stage, small, x0, part, other,
    in_sem, own_sem, send_xy, send_up, send_dn, z_sem, p2_sem, p3_sem,
    small_send, small_z, small_y, small_x, tally_send, tally_recv, pair_send, pair_recv,
):
    dp, mp, x, y, z = place()
    xp, yp = dp + 1 - 2 * x, dp + 2 - 4 * y
    count = big_own.shape[0]
    series, _, length = x_ref.shape
    width = o.shape[1]
    per = length // TILE
    load = pltpu.make_async_copy(big_own, stage, in_sem)
    load.start()
    meet_everyone(dp, mp)

    def home(zs):
        return zs * 4 + 2 * y + x

    def small_put(src, slot, recv, peer):
        remote(src, small.at[slot], small_send, recv, peer, mp).start()

    for dist in (1, 2, 3):
        @pl.when(z >= dist)
        def _():
            small_put(small_own, dp, small_z.at[z], dp - 4 * dist)

        @pl.when(z + dist <= 3)
        def _():
            small_put(small_own, dp, small_z.at[z], dp + 4 * dist)
    small_put(small_own, dp, small_y.at[z], yp)
    small_put(small_own, dp, small_x, xp)
    small[dp] = small_own[...]
    me = dp * 2 + mp

    def tell(k, carry):
        peer = lax.rem(me + k, 32)
        remote(tally, tallies.at[me], tally_send, tally_recv, peer // 2, lax.rem(peer, 2)).start()
        return carry

    lax.fori_loop(1, 32, tell, 0)
    tallies[me] = tally[...]

    load.wait()

    def rows(c, slot):
        return big.at[c, block(slot, SHARD), :]

    def put(src, c, slot, send, recv, peer):
        remote(src, rows(c, slot), send, recv, peer, mp).start()

    def climb(c, zs, src):
        put(src, c, home(zs), send_up, z_sem.at[c, zs], dp + 4)

    def drop(c, zs, src):
        put(src, c, home(zs), send_dn, z_sem.at[c, zs], dp - 4)

    def ends(c):
        k = lax.rem(c, 2)
        return jnp.where(k == 0, yp, xp), jnp.where(k == 0, xp, yp)

    def spread(c, zs, src):
        first, second = ends(c)
        put(src, c, home(zs), send_xy, p2_sem.at[c, zs], first)
        put(src, c, home(zs), send_xy, p3_sem, second)

    def own_z(c, carry):
        @pl.when(z < 3)
        def _():
            climb(c, z, stage.at[c])

        @pl.when(z > 0)
        def _():
            drop(c, z, stage.at[c])
        pltpu.make_async_copy(stage.at[c], rows(c, dp), own_sem).start()
        return carry

    lax.fori_loop(0, count, own_z, 0)

    for dist in (1, 2, 3):
        for sign in (-1, 1):
            zs = z + sign * dist

            @pl.when((zs >= 0) & (zs <= 3))
            def _():
                done(small.at[home(zs)], small_z.at[zs])
                small_put(small.at[home(zs)], home(zs), small_y.at[zs], yp)
                small_put(small.at[home(zs)], home(zs), small_x, xp)
    for turn in range(4):
        zs = lax.rem(z + turn, 4)
        slot = zs * 4 + 2 * (1 - y) + x
        done(small.at[slot], small_y.at[zs])
        small_put(small.at[slot], slot, small_x, xp)
    done(small.at[pl.ds(0, 8)], small_x)

    def own_xy(c, carry):
        spread(c, z, stage.at[c])
        return carry

    lax.fori_loop(0, count, own_xy, 0)

    whole = small[...].astype(F32).reshape(D, -1)
    table[...] = whole[:, 4 * width:].astype(BF16)
    turned = jnp.transpose(whole)
    wt[...] = turned.astype(BF16)
    vec[...] = jnp.concatenate(
        [turned[4 * width + VECTOR:4 * width + VECTOR + 5], jnp.zeros((3, D), F32)], axis=0)
    total[...] = jnp.zeros_like(total)

    def relay(c, dist):
        def second(zs):
            k = lax.rem(c, 2)
            slot = zs * 4 + jnp.where(k == 0, 2 * (1 - y) + x, 2 * y + 1 - x)
            done(rows(c, slot), p2_sem.at[c, zs])
            put(rows(c, slot), c, slot, send_xy, p3_sem, ends(c)[1])

        @pl.when(z >= dist)
        def _():
            zs = z - dist
            done(rows(c, home(zs)), z_sem.at[c, zs])

            @pl.when(z < 3)
            def _():
                climb(c, zs, rows(c, home(zs)))
            spread(c, zs, rows(c, home(zs)))

        @pl.when(z + dist <= 3)
        def _():
            zs = z + dist
            done(rows(c, home(zs)), z_sem.at[c, zs])

            @pl.when(z > 0)
            def _():
                drop(c, zs, rows(c, home(zs)))
            spread(c, zs, rows(c, home(zs)))

        @pl.when(z - (dist - 1) >= 0)
        def _():
            second(z - (dist - 1))

        @pl.when((dist > 1) & (z + dist - 1 <= 3))
        def _():
            second(z + dist - 1)

    def pair(n):
        r = block(n, length)
        return remote(part.at[r], other.at[r], pair_send.at[n], pair_recv.at[n], dp, 1 - mp)

    heads = width // HEAD
    pieces = heads + 2

    def attention(i):
        n, j = i // pieces, lax.rem(i, pieces)
        r = block(n, length)

        @pl.when(j == 0)
        def _():
            def tile(m, carry):
                t = pl.ds(pl.multiple_of(n * length + m * TILE, TILE), TILE)
                embed_piece(x_ref[n, :, block(m, TILE, TILE)], vec, x0, a, t)
                return carry
            lax.fori_loop(0, per, tile, 0)

        @pl.when(j == 1)
        def _():
            project_piece(wt, a[r, :], cos_ref[...], sin_ref[...], qkv.at[n], width)

        @pl.when(j >= 2)
        def _():
            forward_head(j - 2, width, qkv.at[n], lse.at[n], o.at[n])

        @pl.when(j == pieces - 1)
        def _():
            part[r, :] = dot(o[n], wt[3 * width:4 * width, :], 0, 0)
            pair(n).start()

    def middle(m):
        r = block(m, TILE)

        @pl.when(lax.rem(m, per) == 0)
        def _():
            pair(m // per).wait()
        v = x0[r, :] + (part[r, :] + other[r, :])
        x1[r, :] = v
        low, gates, sums = mid_forward_piece(v, vec[1:2, :], table[...])
        b[r, :] = low
        pc[r, :] = gates
        total[...] += sums

    def step(i, carry):
        relay(lax.rem(i, count), i // count + 1)

        @pl.when(i < series * pieces)
        def _():
            attention(i)

        for n in range(series):
            begin = (n + 1) * pieces + 4

            @pl.when((i >= begin) & (i < begin + per))
            def _():
                middle(n * per + i - begin)
        return carry

    lax.fori_loop(0, 4 * count, step, 0)

    def whole_wait(n, sem):
        done(big.at[:, pl.ds(0, n * SHARD), :], sem)
    whole_wait(8, p3_sem)
    whole_wait(12, send_xy)
    whole_wait(1, own_sem)
    done(small.at[pl.ds(0, 15)], small_send)
    done(tallies.at[pl.ds(0, 31)], tally_recv)
    done(tallies.at[pl.ds(0, 31)], tally_send)
    for k in range(4):
        @pl.when(z == k)
        def _():
            if k < 3:
                whole_wait(k + 1, send_up)
            if k > 0:
                whole_wait(4 - k, send_dn)


def forward_near(small_own, big_own, tally, x, cos, sin, width, ident):
    series, _, length = x.shape
    tokens = series * length
    count, shard, columns = big_own.shape
    shape = jax.ShapeDtypeStruct
    return pl.pallas_call(
        forward_kernel,
        in_specs=[VMEM, ANY, VMEM, VMEM, VMEM, VMEM],
        out_specs=[ANY] + [VMEM] * 12,
        out_shape=[
            shape((count, D, columns), BF16),
            shape((small_own.shape[1], D), BF16), shape((8, D), F32), shape((D, LANES), BF16),
            shape((tokens, D), BF16), shape((series, 3 * width, length), BF16), shape((series, 8, length), F32),
            shape((series, width, length), BF16),
            shape((tokens, D), F32), shape((tokens, D), BF16), shape((tokens, LANES), F32), shape((1, LANES), F32),
            shape((32,) + tally.shape, F32),
        ],
        scratch_shapes=[
            pltpu.VMEM(big_own.shape, BF16), pltpu.VMEM((16,) + small_own.shape, BF16),
            pltpu.VMEM((tokens, D), F32), pltpu.VMEM((tokens, D), F32), pltpu.VMEM((tokens, D), F32),
            DMA, DMA, DMA, DMA, DMA, DMA((count, 4)), DMA((count, 4)), DMA,
            DMA, DMA((4,)), DMA((4,)), DMA, DMA, DMA, DMA((series,)), DMA((series,)),
        ],
        compiler_params=params(collective_id=ident, has_side_effects=True),
        name="forward_near",
    )(small_own, big_own, tally, x, cos, sin)


GROUP = 16


def spread_rows(dest, value, start, count):
    for c in range(value.shape[1] // LANES):
        dest[pl.ds(start * 8 + c, count, stride=8), :] = value[:, c * LANES:(c + 1) * LANES]


def rows_at(ref, index):
    return ref[pl.ds(pl.multiple_of(index, 8), 8), :]


def pick_rows(source, tile, index_ref, base):
    for i in range(0, TILE, GROUP):
        values = [rows_at(source, index_ref[base + k]) for k in range(i, i + GROUP)]
        for k in range(i, i + GROUP):
            tile[k * 8:k * 8 + 8, :] = values[k - i]


def sum_rows(results, tile, index_ref, base, tokens):
    for i in range(0, TILE, GROUP):
        values = [
            rows_at(results, index_ref[base + k]) + rows_at(results, index_ref[tokens + base + k])
            for k in range(i, i + GROUP)]
        for k in range(i, i + GROUP):
            tile[k * 8:k * 8 + 8, :] = values[k - i]


def gathered_columns(tile, columns):
    return [tile[pl.ds(c, TILE, stride=8), :] for c in range(columns)]


def lane_of(value, lane):
    lanes = lax.broadcasted_iota(jnp.int32, value.shape, 1)
    return jnp.sum(jnp.where(lanes == lane, value, 0.0), axis=1, keepdims=True)


def lay_rows(values, pc_ref, rows8):
    tokens = values.shape[0]

    def lay(i, carry):
        r = block(i, TILE)
        spread_rows(rows8, values[r, :].astype(F32), i * TILE, TILE)
        rows8[pl.ds(i * TILE * 8 + 3, TILE, stride=8), :] = pc_ref[r, :]
        return carry

    lax.fori_loop(0, tokens // TILE, lay, 0)
    rows8[pl.ds(tokens * 8, 8), :] = jnp.zeros((8, LANES), F32)


def expert_tiles(e, used, capacity, tile, blank, shared):
    tiles = capacity // TILE

    @pl.when(e < ROUTED_EXPERTS)
    def _():
        def one(i, carry):
            tile(e * tiles + i, block(i, TILE))
            return carry

        def none(i, carry):
            blank(block(i, TILE))
            return carry

        lax.fori_loop(0, used[e], one, 0)
        lax.fori_loop(used[e], tiles, none, 0)

    @pl.when(e >= ROUTED_EXPERTS)
    def _():
        def one(i, carry):
            shared((e - ROUTED_EXPERTS) * tiles + i, block(i, TILE))
            return carry

        lax.fori_loop(0, tiles, one, 0)


def expert_forward_kernel(
    used, order, after, source, slots, b_ref, pc_ref, w_ref, x_ref, y_ref, mix_ref, rows8, done8, tile8, sum8
):
    e = pl.program_id(0)
    tokens = b_ref.shape[0]
    hidden = w_ref.shape[2] // 3

    @pl.when(e == 0)
    def _():
        lay_rows(b_ref, pc_ref, rows8)
        pick_rows(rows8, tile8, source, after[after.shape[0] - 1])

    def run(x):
        g = dot(x, w_ref[0, :, : 2 * hidden])
        gate, up = g[:, :hidden], g[:, hidden:]
        h = (gate * sigmoid(gate) * up).astype(BF16)
        return dot(h, w_ref[0, :, 2 * hidden:], 1, 1)

    def tile(s, here):
        c0, c1, c2, pc = gathered_columns(tile8, 4)
        x = jnp.concatenate([c0, c1, c2], axis=1).astype(BF16)
        x_ref[0, here, :] = x
        gate_column = lane_of(pc, ROUTER + e)
        pick_rows(rows8, tile8, source, after[s])
        y = run(x)
        y_ref[0, here, :] = y
        spread_rows(done8, y * gate_column, order[s], TILE)

    def blank(here):
        x_ref[0, here, :] = jnp.zeros((TILE, D), BF16)

    def shared(j, here):
        r = block(j, TILE)
        x = b_ref[r, :]
        x_ref[0, here, :] = x
        sum_rows(done8, sum8, slots, j * TILE, tokens)
        y = run(x)
        y_ref[0, here, :] = y
        scaled = y * lane_of(pc_ref[r, :], SHARED)
        for c, part in enumerate(gathered_columns(sum8, D // LANES)):
            cols = slice(c * LANES, (c + 1) * LANES)
            mix_ref[r, cols] = part + scaled[:, cols]

    expert_tiles(e, used, y_ref.shape[1], tile, blank, shared)


def expert_specs(tokens, weights):
    full = lambda shape: pl.BlockSpec(shape, lambda e, *_: (0,) * len(shape), pipeline_mode=pl.Buffered(1))
    tile = lambda w: pl.BlockSpec((1, tokens // 2, w), lambda e, *_: (e, 0, 0))
    weight = pl.BlockSpec((1,) + weights.shape[1:], lambda e, *_: (jnp.minimum(e, ROUTED_EXPERTS), 0, 0))
    scratch = [
        pltpu.VMEM(((tokens + 1) * 8, LANES), F32), pltpu.VMEM(((2 * tokens + TILE) * 8, LANES), F32),
        pltpu.VMEM((TILE * 8, LANES), F32), pltpu.VMEM((TILE * 8, LANES), F32)]
    return full, tile, weight, scratch


def expert_forward(plan, b, pc, weights):
    tokens = b.shape[0]
    full, tile, weight, scratch = expert_specs(tokens, weights)
    return pl.pallas_call(
        expert_forward_kernel,
        grid_spec=pltpu.PrefetchScalarGridSpec(
            num_scalar_prefetch=5,
            grid=(ROUTED_EXPERTS + 2,),
            in_specs=[full(b.shape), full(pc.shape), weight],
            out_specs=[tile(D), tile(D), full((tokens, D))],
            scratch_shapes=scratch,
        ),
        out_shape=[
            jax.ShapeDtypeStruct((ROUTED_EXPERTS + 2, tokens // 2, D), BF16),
            jax.ShapeDtypeStruct((ROUTED_EXPERTS + 2, tokens // 2, D), F32),
            jax.ShapeDtypeStruct((tokens, D), F32),
        ],
        compiler_params=params(),
        name="expert_forward",
    )(*plan, b, pc, weights)


def expert_backward_kernel(
    used, order, after, source, slots, pc_ref, dx_ref, w_ref, x_ref, y_ref, dy_ref, dg_ref, h_ref, acc_ref,
    rows8, done8, tile8, sum8,
):
    e = pl.program_id(0)
    tokens = dx_ref.shape[0]
    hidden = w_ref.shape[2] // 3
    lanes = lax.broadcasted_iota(jnp.int32, (TILE, LANES), 1)

    @pl.when(e == 0)
    def _():
        lay_rows(dx_ref, pc_ref, rows8)
        pick_rows(rows8, tile8, source, after[after.shape[0] - 1])

    def run(here, dy):
        dy_ref[0, here, :] = dy
        u = w_ref[0, :, : 2 * hidden]
        g = dot(x_ref[0, here, :], u)
        gate, up = g[:, :hidden], g[:, hidden:]
        sig = sigmoid(gate)
        silu = gate * sig
        h_ref[0, here, :] = (silu * up).astype(BF16)
        dh = dot(dy, w_ref[0, :, 2 * hidden:])
        d_up = (dh * silu).astype(BF16)
        d_gate = (dh * up * (sig * (1.0 + gate * (1.0 - sig)))).astype(BF16)
        dg_ref[0, here, :hidden] = d_gate
        dg_ref[0, here, hidden:] = d_up
        return dot(d_gate, u[:, :hidden], 1, 1) + dot(d_up, u[:, hidden:], 1, 1)

    def tile(s, here):
        c0, c1, c2, pc = gathered_columns(tile8, 4)
        dx = jnp.concatenate([c0, c1, c2], axis=1)
        d_value = jnp.sum(y_ref[0, here, :] * dx, axis=1, keepdims=True)
        dy = (dx * lane_of(pc, ROUTER + e)).astype(BF16)
        pick_rows(rows8, tile8, source, after[s])
        back = run(here, dy)
        spread_rows(done8, back, order[s], TILE)
        done8[pl.ds(order[s] * 8 + 3, TILE, stride=8), :] = jnp.where(lanes == ROUTER + e, d_value, 0.0)

    def blank(here):
        dy_ref[0, here, :] = jnp.zeros((TILE, D), BF16)
        dg_ref[0, here, :] = jnp.zeros((TILE, 2 * hidden), BF16)
        h_ref[0, here, :] = jnp.zeros((TILE, hidden), BF16)

    def shared(j, here):
        r = block(j, TILE)
        dx = dx_ref[r, :]
        d_value = jnp.sum(y_ref[0, here, :] * dx, axis=1, keepdims=True)
        sum_rows(done8, sum8, slots, j * TILE, tokens)
        back = run(here, (dx * lane_of(pc_ref[r, :], SHARED)).astype(BF16))
        sums = gathered_columns(sum8, D // LANES + 1)
        for c in range(D // LANES):
            cols = slice(c * LANES, (c + 1) * LANES)
            acc_ref[r, cols] = sums[c] + back[:, cols]
        acc_ref[r, D:] = jnp.where(lanes == SHARED, d_value, sums[-1])

    expert_tiles(e, used, y_ref.shape[1], tile, blank, shared)


def expert_backward(plan, pc, dx, weights, x, y):
    tokens = dx.shape[0]
    hidden = weights.shape[2] // 3
    full, tile, weight, scratch = expert_specs(tokens, weights)
    return pl.pallas_call(
        expert_backward_kernel,
        grid_spec=pltpu.PrefetchScalarGridSpec(
            num_scalar_prefetch=5,
            grid=(ROUTED_EXPERTS + 2,),
            in_specs=[full(pc.shape), full(dx.shape), weight, tile(D), tile(D)],
            out_specs=[tile(D), tile(2 * hidden), tile(hidden), full((tokens, D + LANES))],
            scratch_shapes=scratch,
        ),
        out_shape=[
            jax.ShapeDtypeStruct((ROUTED_EXPERTS + 2, tokens // 2, D), BF16),
            jax.ShapeDtypeStruct((ROUTED_EXPERTS + 2, tokens // 2, 2 * hidden), BF16),
            jax.ShapeDtypeStruct((ROUTED_EXPERTS + 2, tokens // 2, hidden), BF16),
            jax.ShapeDtypeStruct((tokens, D + LANES), F32),
        ],
        compiler_params=params(),
        name="expert_backward",
    )(*plan, pc, dx, weights, x, y)


def exchange(part, other, send_sem, recv_sem):
    dp, mp = lax.axis_index("dp"), lax.axis_index("mp")
    barrier = pltpu.get_barrier_semaphore()
    pl.semaphore_signal(barrier, inc=1, device_id=(dp, 1 - mp), device_id_type=MESH)
    pl.semaphore_wait(barrier, 1)

    def copy(i):
        r = block(i, TILE)
        return remote(part.at[r], other.at[r], send_sem.at[i], recv_sem.at[i], dp, 1 - mp)

    def begin(i, carry):
        copy(i).start()
        return carry

    lax.fori_loop(0, part.shape[0] // TILE, begin, 0)
    return lambda i: copy(i).wait()


def exchange_scratch(part):
    tiles = part.shape[0] // TILE
    return [pltpu.VMEM(part.shape, F32), DMA((tiles,)), DMA((tiles,))]


def hankel(base):
    block_rows = jnp.broadcast_to(base, (LANES, 2 * LANES))
    m = pltpu.roll(block_rows, 0, 1, stride=1, stride_axis=0)[:, :LANES]
    lanes = lax.broadcasted_iota(jnp.int32, (LANES, LANES), 1)
    out = pltpu.roll(m, 41, 1)
    out = jnp.where(lanes < 104, pltpu.roll(m, 40, 1), out)
    out = jnp.where(lanes < 96, pltpu.roll(m, 32, 1), out)
    return jnp.where(lanes < 64, m, out)


def loss_piece(x, gain, table, table_t, value_rows, mark_rows, weight):
    scale = lax.rsqrt(jnp.mean(x * x, axis=1, keepdims=True) + norm_eps)
    unit = x * scale
    low = (unit * gain).astype(BF16)
    z = dot(low, table)
    target = jnp.concatenate([hankel(row) for row in value_rows], axis=0)
    valid = jnp.concatenate([hankel(row) for row in mark_rows], axis=0)
    factor = valid * weight
    miss = z - target
    size = jnp.abs(miss)
    huber = jnp.where(
        size <= quadratic_cutoff, 0.5 * miss * miss, quadratic_cutoff * (size - 0.5 * quadratic_cutoff))
    dz = (jnp.clip(miss, -quadratic_cutoff, quadratic_cutoff) * factor).astype(BF16)
    df = dot(dz, table_t)
    dn = df * gain
    dx = scale * (dn - unit * jnp.mean(dn * unit, axis=1, keepdims=True))
    total = lambda v: jnp.sum(v, axis=0, keepdims=True)
    return dx, dot(dz, low, 0, 0), total(df * unit), total(huber * factor)


def loss_kernel(part, x1, vec, table, table_t, values, marks, weight, dx2, d_table, d_gain, loss,
                other, send_sem, recv_sem):
    wait = exchange(part, other, send_sem, recv_sem)
    d_table[...] = jnp.zeros_like(d_table)
    d_gain[...] = jnp.zeros_like(d_gain)
    loss[...] = jnp.zeros_like(loss)
    per = TILE // LANES

    def step(i, carry):
        r = block(i, TILE)
        wait(i)
        dx, dt, dg, fit = loss_piece(
            x1[r, :] + (part[r, :] + other[r, :]), vec[2:3, :], table[...], table_t[...],
            [values[pl.ds(per * i + k, 1), :] for k in range(per)],
            [marks[pl.ds(per * i + k, 1), :] for k in range(per)], weight[...])
        dx2[r, :] = dx
        d_table[...] += dt
        d_gain[...] += dg
        loss[...] += fit
        return carry

    lax.fori_loop(0, part.shape[0] // TILE, step, 0)


def loss_stage(part, x1, vec, table, table_t, values, marks, weight, ident):
    tokens = part.shape[0]
    return pl.pallas_call(
        loss_kernel,
        in_specs=[VMEM] * 8,
        out_specs=[VMEM] * 4,
        out_shape=[
            jax.ShapeDtypeStruct((tokens, D), F32), jax.ShapeDtypeStruct((LANES, D), F32),
            jax.ShapeDtypeStruct((1, D), F32), jax.ShapeDtypeStruct((1, LANES), F32),
        ],
        scratch_shapes=exchange_scratch(part),
        compiler_params=params(collective_id=ident, has_side_effects=True),
        name="loss_stage",
    )(part, x1, vec, table, table_t, values, marks, weight)


def mid_backward_kernel(part, dx2, x1, b, pc, vec, table_t, balance, wo, o, d_table, d_gain3, dx1, do, rest,
                        other, send_sem, recv_sem):
    wait = exchange(part, other, send_sem, recv_sem)
    width = wo.shape[0]
    rest[:width, :] = jnp.zeros((width, D), F32)
    rest[width:, :] = d_table[...]
    rest[width + VECTOR + 2:width + VECTOR + 3, :] = d_gain3[...]
    per = o.shape[2] // TILE

    def step(i, carry):
        r = block(i, TILE)
        wait(i)
        dp = part[r, D:] + other[r, D:] + balance[...]
        p = pc[r, :]
        lanes = lax.broadcasted_iota(jnp.int32, p.shape, 1)
        routed = (lanes >= ROUTER) & (lanes < SHARED)
        weighted = jnp.sum(jnp.where(routed, p * dp, 0.0), axis=1, keepdims=True)
        dl = jnp.where(routed, p * (dp - weighted), jnp.where(lanes == SHARED, dp * p * (1.0 - p), 0.0))
        dl = dl.astype(BF16)
        low = b[r, :]
        rest[width:, :] += dot(dl, low, 0, 0)
        db = part[r, :D] + other[r, :D] + dot(dl, table_t[...])
        x = x1[r, :]
        scale = lax.rsqrt(jnp.mean(x * x, axis=1, keepdims=True) + norm_eps)
        unit = x * scale
        g2 = width + VECTOR + 1
        rest[g2:g2 + 1, :] += jnp.sum(db * unit, axis=0, keepdims=True)
        dn = db * vec[1:2, :]
        dx = dx2[r, :] + scale * (dn - unit * jnp.mean(dn * unit, axis=1, keepdims=True))
        dx1[r, :] = dx
        d_low = dx.astype(BF16)
        n, cols = i // per, block(lax.rem(i, per), TILE, TILE)
        do[n, :, cols] = dot(wo[...], d_low, 1, 1).astype(BF16)
        rest[:width, :] += dot(o[n, :, cols], d_low)
        return carry

    lax.fori_loop(0, part.shape[0] // TILE, step, 0)


def mid_backward(part, dx2, x1, b, pc, vec, table_t, balance, wo, o, d_table, d_gain3, ident):
    tokens = part.shape[0]
    return pl.pallas_call(
        mid_backward_kernel,
        in_specs=[VMEM] * 12,
        out_specs=[VMEM] * 3,
        out_shape=[
            jax.ShapeDtypeStruct((tokens, D), F32), jax.ShapeDtypeStruct(o.shape, BF16),
            jax.ShapeDtypeStruct((wo.shape[0] + LANES, D), F32),
        ],
        scratch_shapes=exchange_scratch(part),
        compiler_params=params(collective_id=ident, has_side_effects=True),
        name="mid_backward",
    )(part, dx2, x1, b, pc, vec, table_t, balance, wo, o, d_table, d_gain3)


SLOTS = 3
HOPS = 2
ACCS = 5


def encode(dest, v):
    width = v.shape[1]
    top = jnp.max(jnp.abs(v), axis=1, keepdims=True)
    power = jnp.ceil(jnp.log2(jnp.maximum(top, 1e-30) * (1.001 / 32767.0)))
    power = jnp.broadcast_to(power, (v.shape[0], LANES))
    inverse = jnp.exp2(-power)
    dest[:, width:] = power.astype(jnp.int32).astype(I16)
    for c in range(width // LANES):
        cols = slice(c * LANES, (c + 1) * LANES)
        dest[:, cols] = jnp.round(v[:, cols] * inverse).astype(jnp.int32).astype(I16)


def decode(source):
    width = source.shape[1] - LANES
    unit = jnp.exp2(source[:, width:].astype(jnp.int32).astype(F32))
    return jnp.concatenate(
        [source[:, c * LANES:(c + 1) * LANES].astype(jnp.int32).astype(F32) * unit for c in range(width // LANES)],
        axis=1)


def squared(v):
    v = jnp.sum(v * v, axis=0, keepdims=True)
    total = v[:, :LANES]
    for c in range(1, v.shape[1] // LANES):
        total = total + v[:, c * LANES:(c + 1) * LANES]
    return total


def backward_kernel(
    xs, dys, dgs, hs, qkvs, dos, lses, a_all, dx1_all, rest, x_ref, wt, vec, cos_ref, sin_ref, losses,
    out_up, out_down, out_small, sums,
    x_in, dy_in, dg_in, h_in, xt, dyt, temp, dw, acc, send1, recv1, send2, recv2, zs_up, zs_dn, up, dn,
    qkv, do_t, lse, a, dx1, dqkv, dk, dv, stack, part, other,
    sm, small_a1, small_b1, small_a2, small_b2, small_up, small_dn,
    load_sem, sem_s1, sem_r1, sem_s2, sem_r2, sem_su, sem_sd, sem_ru, sem_rd,
    attn_sem, dx1_sem, rest_sem, pair_send, pair_recv,
    small_send, small_sa, small_sb, small_r, small_su, small_sd, small_ru, small_rd,
    mine, everyone, sum_send, sum_recv,
):
    dp, mp, x, y, z = place()
    xp, yp = dp + 1 - 2 * x, dp + 2 - 4 * y
    count = out_up.shape[0]
    blocks = xs.shape[0]
    hidden = hs.shape[2]
    series, _, length = x_ref.shape
    width = do_t.shape[0]
    heads = width // HEAD
    per = length // TILE

    def loads(n):
        return [
            pltpu.make_async_copy(src.at[n], dst, load_sem.at[i])
            for i, (src, dst) in enumerate(((xs, x_in), (dys, dy_in), (dgs, dg_in), (hs, h_in)))]

    def attn_loads(n):
        pairs = ((qkvs.at[n], qkv), (dos.at[n], do_t), (lses.at[n], lse), (a_all.at[block(n, length)], a))
        return [pltpu.make_async_copy(src, dst, attn_sem.at[i]) for i, (src, dst) in enumerate(pairs)]

    def dx1_load(n):
        return pltpu.make_async_copy(dx1_all.at[block(n, length)], dx1, dx1_sem)

    rest_load = pltpu.make_async_copy(rest, stack.at[pl.ds(3 * width, width + LANES)], rest_sem)
    for copy in loads(0) + attn_loads(0) + [dx1_load(0), rest_load]:
        copy.start()

    meet_everyone(dp, mp)
    mine[...] = losses[...]
    stack[0:3 * width, :] = jnp.zeros((3 * width, D), F32)

    def shard(slot, i):
        return dw.at[slot, i]


    def weights(n, more):
        for copy in loads(n):
            copy.wait()
        xt[...] = jnp.transpose(x_in[...])
        dyt[...] = jnp.transpose(dy_in[...])

        def wide(j, carry):
            cols = block(j, TILE, TILE)
            v = dot(xt[...], dg_in[:, cols])
            temp[:, cols] = temp[:, cols] + v if more else v
            return carry

        def tall(j, carry):
            there = pl.ds(pl.multiple_of(2 * hidden + j * TILE, TILE), TILE)
            v = dot(dyt[...], h_in[:, block(j, TILE, TILE)])
            temp[:, there] = temp[:, there] + v if more else v
            return carry

        lax.fori_loop(0, 2 * hidden // TILE, wide, 0)
        lax.fori_loop(0, hidden // TILE, tall, 0)

        @pl.when(n + 1 < blocks)
        def _():
            for copy in loads(n + 1):
                copy.start()

    def begin(c):
        k, slot = lax.rem(c, 2), lax.rem(c, SLOTS)
        weights(c, False)

        @pl.when(c == count - 1)
        def _():
            weights(c + 1, True)

        @pl.when(c >= SLOTS)
        def _():
            done(send1.at[slot], sem_s1.at[slot])

        def pack(i, carry):
            m, n = i // 2, lax.rem(i, 2)
            gone = m * 4 + jnp.where(k == 0, n * 2 + 1 - x, (1 - y) * 2 + n)
            kept = m * 4 + jnp.where(k == 0, n * 2 + x, y * 2 + n)
            encode(send1.at[slot, i], temp[block(gone, SHARD), :])
            dw[slot, i] = temp[block(kept, SHARD), :]
            return carry

        lax.fori_loop(0, 8, pack, 0)
        remote(send1.at[slot], recv1.at[c], sem_s1.at[slot], sem_r1.at[c], jnp.where(k == 0, xp, yp), mp).start()

    def fold(c):
        k, slot, hop = lax.rem(c, 2), lax.rem(c, SLOTS), lax.rem(c, HOPS)
        o = jnp.where(k == 0, y, x)
        done(recv1.at[c], sem_r1.at[c])

        @pl.when(c >= HOPS)
        def _():
            done(send2.at[hop], sem_s2.at[hop])

        def add(m, carry):
            gone, kept = m * 2 + 1 - o, m * 2 + o
            encode(send2.at[hop, m], dw[slot, gone] + decode(recv1.at[c, gone]))
            acc[lax.rem(c, ACCS), m] = dw[slot, kept] + decode(recv1.at[c, kept])
            return carry

        lax.fori_loop(0, 4, add, 0)
        remote(send2.at[hop], recv2.at[c], sem_s2.at[hop], sem_r2.at[c], jnp.where(k == 0, yp, xp), mp).start()

    def climb(c, t, relay):
        slot = lax.rem(c, HOPS)
        v = acc[lax.rem(c, ACCS), t]
        if relay:
            done(up.at[c, t - 1], sem_ru.at[c, t - 1])
            v = v + decode(up.at[c, t - 1])

        @pl.when(c >= HOPS)
        def _():
            done(zs_up.at[slot, t - 1], sem_su.at[slot, t - 1])
        encode(zs_up.at[slot, t - 1], v)
        remote(zs_up.at[slot, t - 1], up.at[c, t - 1], sem_su.at[slot, t - 1], sem_ru.at[c, t - 1], dp + 4, mp).start()

    def drop(c, t, relay):
        slot = lax.rem(c, HOPS)
        v = acc[lax.rem(c, ACCS), t]
        if relay:
            done(dn.at[c, t], sem_rd.at[c, t])
            v = v + decode(dn.at[c, t])

        @pl.when(c >= HOPS)
        def _():
            done(zs_dn.at[slot, t], sem_sd.at[slot, t])
        encode(zs_dn.at[slot, t], v)
        remote(zs_dn.at[slot, t], dn.at[c, t], sem_sd.at[slot, t], sem_rd.at[c, t], dp - 4, mp).start()

    def line_a(c):
        done(recv2.at[c], sem_r2.at[c])
        there = lax.rem(c, ACCS)

        def add(m, carry):
            acc[there, m] = acc[there, m] + decode(recv2.at[c, m])
            return carry

        lax.fori_loop(0, 4, add, 0)

        @pl.when(z == 0)
        def _():
            for t in (3, 2, 1):
                climb(c, t, False)

        @pl.when(z == 3)
        def _():
            for t in (0, 1, 2):
                drop(c, t, False)

    def line_b(c):
        @pl.when(z == 1)
        def _():
            for t in (3, 2):
                climb(c, t, True)

        @pl.when(z == 2)
        def _():
            for t in (0, 1):
                drop(c, t, True)

    def line_c(c):
        @pl.when(z == 2)
        def _():
            climb(c, 3, True)

        @pl.when(z == 1)
        def _():
            drop(c, 0, True)

    def finish(c):
        there = lax.rem(c, ACCS)

        @pl.when(z > 0)
        def _():
            done(up.at[c, z - 1], sem_ru.at[c, z - 1])
            acc[there, z] = acc[there, z] + decode(up.at[c, z - 1])

        @pl.when(z < 3)
        def _():
            done(dn.at[c, z], sem_rd.at[c, z])
            acc[there, z] = acc[there, z] + decode(dn.at[c, z])
        v = acc[there, z]
        mine[0:1, :] = mine[0:1, :] + squared(v)
        for r in range(SHARD):
            for part in range(2):
                out_up[c, r, part:part + 1, :] = v[r:r + 1, part * hidden:(part + 1) * hidden]
        out_down[c] = v[:, 2 * hidden:]


    def pair(n):
        r = block(n, length)
        return remote(part, other.at[r], pair_send.at[n], pair_recv.at[n], dp, 1 - mp)

    def head(p):
        n, h = p // heads, lax.rem(p, heads)

        @pl.when(h == 0)
        def _():
            for copy in attn_loads(n):
                copy.wait()
        backward_head(h, width, qkv, do_t, lse, cos_ref[...], sin_ref[...], dqkv, dk, dv)

        @pl.when(h == heads - 1)
        def _():
            stack[0:3 * width, :] = stack[0:3 * width, :] + dot(dqkv[...], a[...])
            part[...] = dot(dqkv[...], wt[0:3 * width, :], 0, 0)
            pair(n).start()

            @pl.when(n + 1 < series)
            def _():
                for copy in attn_loads(n + 1):
                    copy.start()

    def embed(m):
        n, i = m // per, lax.rem(m, per)
        t = block(i, TILE, TILE)

        @pl.when(m == 0)
        def _():
            rest_load.wait()

        @pl.when(i == 0)
        def _():
            pair(n).wait()
            dx1_load(n).wait()
        da = part[t, :] + other[block(m, TILE), :]
        sums = embed_backward_piece(x_ref[n, :, t], da, dx1[t, :], vec)
        for row, value in zip((0, 3, 4), sums):
            there = slice(4 * width + VECTOR + row, 4 * width + VECTOR + row + 1)
            stack[there, :] = stack[there, :] + value

        @pl.when((i == per - 1) & (n + 1 < series))
        def _():
            dx1_load(n + 1).start()


    half = 512
    total_width = sm.shape[-1]
    ca, cb = pl.ds(0, half), pl.ds(half, total_width - half)

    def small_begin():
        sm[...] = jnp.transpose(stack[...]).reshape(sm.shape)
        remote(sm.at[:, :, 1 - x, :, ca], small_a1, small_sa, small_r.at[0], xp, mp).start()
        remote(sm.at[:, 1 - y, :, :, cb], small_b1, small_sb, small_r.at[1], yp, mp).start()

    def small_fold():
        done(small_a1, small_r.at[0])
        done(small_b1, small_r.at[1])
        for m in range(4):
            for n in range(2):
                sm[m, n, x, :, ca] = sm[m, n, x, :, ca] + small_a1[m, n]
                sm[m, y, n, :, cb] = sm[m, y, n, :, cb] + small_b1[m, n]
        remote(sm.at[:, 1 - y, x, :, ca], small_a2, small_send.at[0], small_r.at[2], yp, mp).start()
        remote(sm.at[:, y, 1 - x, :, cb], small_b2, small_send.at[1], small_r.at[3], xp, mp).start()

    def small_climb(t, relay):
        if relay:
            done(small_up.at[t - 1], small_ru.at[t - 1])
            sm[t, y, x] = sm[t, y, x] + small_up[t - 1]
        remote(sm.at[t, y, x], small_up.at[t - 1], small_su.at[t - 1], small_ru.at[t - 1], dp + 4, mp).start()

    def small_drop(t, relay):
        if relay:
            done(small_dn.at[t], small_rd.at[t])
            sm[t, y, x] = sm[t, y, x] + small_dn[t]
        remote(sm.at[t, y, x], small_dn.at[t], small_sd.at[t], small_rd.at[t], dp - 4, mp).start()

    def small_a():
        done(small_a2, small_r.at[2])
        done(small_b2, small_r.at[3])
        for m in range(4):
            sm[m, y, x, :, ca] = sm[m, y, x, :, ca] + small_a2[m]
            sm[m, y, x, :, cb] = sm[m, y, x, :, cb] + small_b2[m]
        out_small[...] = sm[z, y, x]

        @pl.when(z == 0)
        def _():
            for t in (3, 2, 1):
                small_climb(t, False)

        @pl.when(z == 3)
        def _():
            for t in (0, 1, 2):
                small_drop(t, False)

    def small_b():
        @pl.when(z == 1)
        def _():
            for t in (3, 2):
                small_climb(t, True)

        @pl.when(z == 2)
        def _():
            for t in (0, 1):
                small_drop(t, True)

    def small_c():
        @pl.when(z == 2)
        def _():
            small_climb(3, True)

        @pl.when(z == 1)
        def _():
            small_drop(0, True)

    def small_finish():
        @pl.when(z > 0)
        def _():
            done(small_up.at[z - 1], small_ru.at[z - 1])
            out_small[...] = out_small[...] + small_up[z - 1]

        @pl.when(z < 3)
        def _():
            done(small_dn.at[z], small_rd.at[z])
            out_small[...] = out_small[...] + small_dn[z]
        mine[0:1, :] = mine[0:1, :] + squared(out_small[:, :4 * width]) + 0.5 * squared(out_small[:, 4 * width:])


    def at(i, first, number, run):
        @pl.when((i >= first) & (i < first + number))
        def _():
            run(i - first)

    small_first = count + 1

    def step(i, carry):
        at(i, 0, count, begin)

        def run(p, carry):
            head(p)
            return carry

        @pl.when(i <= count)
        def _():
            lax.fori_loop(i, jnp.where(i == count, series * heads, i + 1), run, 0)

        def piece(m, carry):
            embed(m)
            return carry

        at(i, heads + 1, 1, lambda _: lax.fori_loop(0, per, piece, 0))
        at(i, count + 1, 1, lambda _: lax.fori_loop(per, series * per, piece, 0))
        at(i, small_first, 1, lambda _: small_begin())
        at(i, 7, count, finish)
        at(i, 2, count, fold)
        at(i, small_first + 1, 1, lambda _: small_fold())
        at(i, 4, count, line_a)
        at(i, small_first + 2, 1, lambda _: small_a())
        at(i, 5, count, line_b)
        at(i, small_first + 3, 1, lambda _: small_b())
        at(i, 6, count, line_c)
        at(i, small_first + 4, 1, lambda _: small_c())
        at(i, small_first + 5, 1, lambda _: small_finish())
        return carry

    lax.fori_loop(0, count + 7, step, 0)

    me = dp * 2 + mp

    def tell(k, carry):
        peer = lax.rem(me + k, 32)
        remote(mine, everyone.at[me], sum_send, sum_recv, peer // 2, lax.rem(peer, 2)).start()
        return carry

    lax.fori_loop(1, 32, tell, 0)
    everyone[me] = mine[...]

    for slot in range(SLOTS):
        done(send1.at[slot], sem_s1.at[slot])
    for slot in range(HOPS):
        done(send2.at[slot], sem_s2.at[slot])
        for t in (1, 2, 3):
            @pl.when(z < t)
            def _():
                done(zs_up.at[slot, t - 1], sem_su.at[slot, t - 1])
        for t in (0, 1, 2):
            @pl.when(z > t)
            def _():
                done(zs_dn.at[slot, t], sem_sd.at[slot, t])
    done(small_a1, small_sa)
    done(small_b1, small_sb)
    done(small_a2, small_send.at[0])
    done(small_b2, small_send.at[1])
    for t in (1, 2, 3):
        @pl.when(z < t)
        def _():
            done(small_up.at[t - 1], small_su.at[t - 1])
    for t in (0, 1, 2):
        @pl.when(z > t)
        def _():
            done(small_dn.at[t], small_sd.at[t])
    done(everyone.at[pl.ds(0, 31)], sum_recv)
    done(everyone.at[pl.ds(0, 31)], sum_send)
    sums[...] = jnp.sum(everyone[...], axis=0)


def backward_near(xs, dys, dgs, hs, qkv, do, lse, a, dx1, rest, x, wt, vec, cos, sin, losses, ident):
    capacity, hidden = hs.shape[1], hs.shape[2]
    series, rows, length = qkv.shape
    heads_width = rows // 3
    count = ROUTED_EXPERTS + 1
    width = 3 * hidden
    coded = width + LANES
    small = 4 * heads_width + LANES
    tokens = series * length
    v = pltpu.VMEM
    return pl.pallas_call(
        backward_kernel,
        in_specs=[ANY] * 10 + [VMEM] * 6,
        out_specs=[VMEM] * 4,
        out_shape=[
            jax.ShapeDtypeStruct((count, SHARD, 2, hidden), F32),
            jax.ShapeDtypeStruct((count, SHARD, hidden), F32), jax.ShapeDtypeStruct((SHARD, small), F32),
            jax.ShapeDtypeStruct((8, LANES), F32)],
        scratch_shapes=[
            v((capacity, D), BF16), v((capacity, D), BF16), v((capacity, 2 * hidden), BF16), v((capacity, hidden), BF16),
            v((D, capacity), BF16), v((D, capacity), BF16),
            v((D, width), F32), v((SLOTS, 8, SHARD, width), F32), v((ACCS, 4, SHARD, width), F32),
            v((SLOTS, 8, SHARD, coded), I16), v((count, 8, SHARD, coded), I16),
            v((HOPS, 4, SHARD, coded), I16), v((count, 4, SHARD, coded), I16),
            v((HOPS, 3, SHARD, coded), I16), v((HOPS, 3, SHARD, coded), I16),
            v((count, 3, SHARD, coded), I16), v((count, 3, SHARD, coded), I16),
            v((rows, length), BF16), v((heads_width, length), BF16), v((8, length), F32), v((length, D), BF16),
            v((length, D), F32), v((rows, length), BF16), v((length, HEAD), F32), v((length, HEAD), F32),
            v((small, D), F32), v((length, D), F32), v((tokens, D), F32),
            v((4, 2, 2, SHARD, small), F32),
            v((4, 2, SHARD, 512), F32), v((4, 2, SHARD, small - 512), F32),
            v((4, SHARD, 512), F32), v((4, SHARD, small - 512), F32),
            v((3, SHARD, small), F32), v((3, SHARD, small), F32),
            DMA((4,)), DMA((SLOTS,)), DMA((count,)), DMA((HOPS,)), DMA((count,)),
            DMA((HOPS, 3)), DMA((HOPS, 3)), DMA((count, 3)), DMA((count, 3)),
            DMA((4,)), DMA, DMA, DMA((series,)), DMA((series,)),
            DMA((2,)), DMA, DMA, DMA((4,)), DMA((3,)), DMA((3,)), DMA((3,)), DMA((3,)),
            v((8, LANES), F32), v((32, 8, LANES), F32), DMA, DMA,
        ],
        compiler_params=pltpu.CompilerParams(
            vmem_limit_bytes=67_000_000, collective_id=ident, has_side_effects=True),
        name="backward_near",
    )(xs, dys, dgs, hs, qkv, do, lse, a, dx1, rest, x, wt, vec, cos, sin, losses)


def rope_rows(length):
    halfway = HEAD // 2
    frequency = rope_base ** (-2.0 * jnp.arange(halfway, dtype=F32) / HEAD)
    angles = frequency[:, None] * jnp.arange(length, dtype=F32)[None, :]
    return jnp.cos(angles), jnp.sin(angles)


def hankel_rows(track):
    length = track.shape[1]
    padded = jnp.pad(track, ((0, 0), (63, 2 * LANES)))
    first = padded[:, :length].reshape(-1, LANES)[:, ::-1]
    second = padded[:, LANES:LANES + length].reshape(-1, LANES)[:, ::-1]
    return jnp.concatenate([first, second], axis=1)


def table_columns(read, vec):
    parts, end = [], read.shape[1]
    for horizon in horizons[::-1]:
        parts.append(read[:, end - horizon:end][:, ::-1])
        end -= horizon
    gap = jnp.zeros((read.shape[0], ROUTER - sum(horizons)), read.dtype)
    tail = jnp.zeros((read.shape[0], LANES - VECTOR - vec.shape[1]), read.dtype)
    return jnp.concatenate(parts + [gap, read[:, :ROUTED_EXPERTS + 1], vec, tail], axis=1)


def table_columns_back(table):
    parts, begin = [], 0
    for horizon in horizons[::-1]:
        parts.append(table[:, begin:begin + horizon][:, ::-1])
        begin += horizon
    return jnp.concatenate([table[:, ROUTER:VECTOR]] + parts[::-1], axis=1)


def dispatch(route_rows, capacity):
    tokens = route_rows.shape[0]
    experts = jnp.arange(ROUTED_EXPERTS, dtype=jnp.int32)
    member = jnp.any(route_rows[:, :, None] == experts[None, None, :], axis=1)
    count = jnp.cumsum(member.astype(jnp.int32), axis=0)
    total = count[-1]
    place = jnp.where(member, count - 1, -1)
    high = (place[:, :, None] // LANES == jnp.arange(capacity // LANES)[None, None, :]) & member[:, :, None]
    low = (place[:, :, None] % LANES == jnp.arange(LANES)[None, None, :]).astype(BF16)
    token = jnp.arange(tokens, dtype=jnp.int32)
    left = jnp.concatenate(
        [jnp.where(high, part[:, None, None], 0).astype(BF16) for part in (token // 16, token % 16)], axis=2)
    found = jnp.einsum("teh,tel->ehl", left, low, preferred_element_type=F32)
    half = capacity // LANES
    source = (found[:, :half] * 16.0 + found[:, half:]).reshape(ROUTED_EXPERTS, capacity).astype(jnp.int32)
    source = jnp.where(jnp.arange(capacity, dtype=jnp.int32)[None, :] < total[:, None], source, tokens)
    source = jnp.concatenate([source.reshape(-1), jnp.full((TILE,), tokens, jnp.int32)]) * 8
    per = capacity // TILE
    routed = ROUTED_EXPERTS * per
    tile = jnp.arange(routed + tokens // TILE, dtype=jnp.int32)
    need = (total + TILE - 1) // TILE
    begin = jnp.sum(jnp.where(experts[None, :] < experts[:, None], total[None, :], 0), axis=1)
    mine = jnp.minimum(tile // per, ROUTED_EXPERTS - 1)[:, None] == experts[None, :]
    used = (tile < routed) & (tile % per < jnp.sum(jnp.where(mine, need[None, :], 0), axis=1))
    order = jnp.where(used, jnp.sum(jnp.where(mine, begin[None, :], 0), axis=1) + tile % per * TILE, -1)
    next_tile = jnp.concatenate([tile, jnp.full((1,), -1, jnp.int32)])
    later = used[None, :] & (tile[None, :] > next_tile[:, None])
    after = jnp.min(jnp.where(later, tile[None, :], routed), axis=1) * TILE
    slot = (begin[None, :] + count - 1) * 8
    slots = jnp.sum(jnp.where(route_rows[:, :, None] == experts[None, None, :], slot[:, None, :], 0), axis=2)
    return total, (need, order, after, source, slots.T.reshape(-1))


def adam_update(master, moment, square, gradient, factor, bias_one, bias_two, step_rate):
    clipped = gradient * factor
    new_moment = beta_one * moment + (1.0 - beta_one) * clipped
    new_square = beta_two * square + (1.0 - beta_two) * clipped * clipped
    updated = master - step_rate * (
        new_moment / bias_one / (jnp.sqrt(new_square / bias_two) + adam_eps) + decay_rate * master
    )
    return (updated, new_moment, new_square)


def on_device(
    series, observed, routes, step_count,
    joint_proj, joint_moment, joint_square,
    mixer_proj, mixer_moment, mixer_square,
    upward_proj, upward_moment, upward_square,
    downward_proj, downward_moment, downward_square,
    readout, readout_moment, readout_square,
    vectors, vectors_moment, vectors_square,
):
    dp_count = lax.axis_size("dp")
    mp_count = lax.axis_size("mp")
    shard = joint_proj.shape[1]
    width = joint_proj.shape[2]
    hidden = upward_proj.shape[3]
    experts = upward_proj.shape[0]
    series_count, length = series.shape
    tokens = series_count * length
    capacity = tokens // 2

    small_own = jnp.concatenate(
        [joint_proj[k].astype(BF16) for k in range(3)]
        + [mixer_proj.T.astype(BF16), table_columns(readout.astype(BF16), vectors.T.astype(BF16))], axis=1)
    big_own = jnp.concatenate(
        [upward_proj.astype(BF16).reshape(experts, shard, 2 * hidden), downward_proj.transpose(0, 2, 1).astype(BF16)],
        axis=2)
    marks = observed.astype(F32)
    expert_here, plan = dispatch(routes.reshape(tokens, 2), capacity)
    point = jnp.arange(length, dtype=F32)
    head_here = jnp.stack(
        [jnp.sum(jnp.sum(marks, axis=0) * jnp.minimum(point, float(horizon))) for horizon in horizons])
    tally = jnp.pad(jnp.concatenate([expert_here.astype(F32), head_here]), (0, LANES - 12))
    tally = jnp.broadcast_to(tally[None], (8, LANES))
    cos, sin = rope_rows(length)
    x = (series * marks).reshape(series_count, 1, length)

    big, wt, vec, table, a, qkv, lse, o, x1, b, pc, pr_total, tallies = forward_near(
        small_own, big_own, tally, x, cos, sin, width, 0)
    wo, table_t = wt[3 * width:4 * width], wt[4 * width:]
    tally = jnp.sum(tallies[:, 0], axis=0) / mp_count
    expert_count, head_count = tally[:ROUTED_EXPERTS], tally[ROUTED_EXPERTS:ROUTED_EXPERTS + 4]
    total_tokens = tokens * dp_count

    xs, ys, mixed = expert_forward(plan, b, pc, big)
    head_weight = jnp.concatenate(
        [jnp.zeros((horizon,), F32) + 0.25 / head_count[3 - index] for index, horizon in enumerate(horizons[::-1])])
    head_weight = jnp.pad(head_weight, (0, LANES - head_weight.shape[0]))[None]
    dx2, d_table, d_gain3, fit = loss_stage(
        mixed, x1, vec, table, table_t, hankel_rows(series), hankel_rows(marks), head_weight, 1)
    dys, dgs, hs, back = expert_backward(plan, pc, dx2, big, xs, ys)
    balance = aux_factor * ROUTED_EXPERTS * expert_count / total_tokens / total_tokens
    balance = jnp.pad(balance, (ROUTER, LANES - SHARED))[None]
    dx1, do, rest = mid_backward(back, dx2, x1, b, pc, vec, table_t, balance, wo, o, d_table, d_gain3, 2)
    losses = jnp.pad((fit + pr_total * balance) / mp_count, ((1, 6), (0, 0)))
    upward_red, down_red, small_red, sums = backward_near(
        xs, dys, dgs, hs, qkv, do, lse, a, dx1, rest, x, wt, vec, cos, sin, losses, 3)

    attn_red, table_red = small_red[:, :4 * width], small_red[:, 4 * width:]
    grad_norm, loss_total = jnp.sqrt(jnp.sum(sums[0])), jnp.sum(sums[1])

    factor = clip_limit / (grad_norm + 1e-06)
    steps_taken = step_count[0].astype(F32)
    bias_one = 1.0 - beta_one**steps_taken
    bias_two = 1.0 - beta_two**steps_taken

    def update(master, moment, square, gradient, rate=matrix_rate):
        return adam_update(master, moment, square, gradient, factor, bias_one, bias_two, rate)

    joint_red = jnp.stack([attn_red[:, k * width:(k + 1) * width] for k in range(3)], axis=0)
    mixer_red = attn_red[:, 3 * width:].T
    downward_red = down_red.transpose(0, 2, 1)
    return (
        loss_total,
        grad_norm,
        *update(joint_proj, joint_moment, joint_square, joint_red),
        *update(mixer_proj, mixer_moment, mixer_square, mixer_red),
        *update(upward_proj, upward_moment, upward_square, upward_red),
        *update(downward_proj, downward_moment, downward_square, downward_red),
        *update(readout, readout_moment, readout_square, table_columns_back(table_red)),
        *update(vectors, vectors_moment, vectors_square, table_red[:, VECTOR:VECTOR + 5].T, vector_rate),
    )


def rms_scale(tensor, gain_row):
    return (
        tensor * lax.rsqrt(jnp.mean(tensor * tensor, axis=-1, keepdims=True) + norm_eps) * gain_row
    )


def rope_tables(length, columns):
    halfway = columns // 2
    frequency = rope_base ** (-2.0 * jnp.arange(halfway, dtype=jnp.float32) / columns)
    angles = jnp.arange(length, dtype=jnp.float32)[:, None] * frequency[None, :]
    return (jnp.cos(angles), jnp.sin(angles))


def rotate(tensor, cosine_table, sine_table):
    halfway = tensor.shape[-1] // 2
    front_part = tensor[..., :halfway]
    back_part = tensor[..., halfway:]
    return jnp.concatenate(
        [
            front_part * cosine_table - back_part * sine_table,
            back_part * cosine_table + front_part * sine_table,
        ],
        axis=-1,
    )


def swiglu(tensor):
    halfway = tensor.shape[-1] // 2
    return jax.nn.silu(tensor[..., :halfway]) * tensor[..., halfway:]


def targets_of(series, observed):
    row_count, length = series.shape
    longest = max(horizons)
    padded_values = jnp.concatenate([series, jnp.zeros((row_count, longest), jnp.float32)], axis=1)
    padded_marks = jnp.concatenate(
        [observed.astype(jnp.float32), jnp.zeros((row_count, longest), jnp.float32)], axis=1
    )
    value_window = jnp.stack(
        [padded_values[:, 1 + offset : 1 + offset + length] for offset in range(longest)], axis=-1
    )
    mark_window = jnp.stack(
        [padded_marks[:, 1 + offset : 1 + offset + length] for offset in range(longest)], axis=-1
    )
    observed_future_series = jnp.concatenate(
        [value_window[..., :horizon] for horizon in horizons], axis=-1
    )
    valid_mask = jnp.concatenate([mark_window[..., :horizon] for horizon in horizons], axis=-1)
    return (
        observed_future_series.reshape(row_count * length, -1),
        valid_mask.reshape(row_count * length, -1),
    )


def head_counts(valid_mask):
    beginnings = [sum(horizons[:index]) for index in range(len(horizons))]
    return jnp.stack(
        [
            jnp.sum(valid_mask[:, beginning : beginning + horizon])
            for beginning, horizon in zip(beginnings, horizons)
        ]
    )


def head_weights(head_count):
    return jnp.concatenate(
        [
            jnp.zeros((horizon,), jnp.float32) + 0.25 / head_count[index]
            for index, horizon in enumerate(horizons)
        ]
    )


def dispatch_plan(route_rows, experts, capacity):
    flat_routes = route_rows.reshape(-1)
    entries = flat_routes.shape[0]
    onehot = (flat_routes[:, None] == jnp.arange(experts, dtype=jnp.int32)[None, :]).astype(
        jnp.int32
    )
    position = jnp.sum(jnp.cumsum(onehot, axis=0) * onehot, axis=1) - 1
    slot_index = flat_routes * capacity + position
    source = (
        jnp.full((experts * capacity,), entries, jnp.int32)
        .at[slot_index]
        .set(jnp.arange(entries, dtype=jnp.int32))
    )
    return (slot_index, source)


def split_heads(matrix, series_count, length):
    return matrix.reshape(series_count, length, matrix.shape[1] // HEAD, HEAD).transpose(0, 2, 1, 3)


def merge_heads(tensor):
    series_count, heads_here, length, head_size = tensor.shape
    return tensor.transpose(0, 2, 1, 3).reshape(series_count * length, heads_here * head_size)


def block_scores(query_block, key_heads, offset, length):
    block_rows = query_block.shape[1]
    scores = jnp.einsum(
        "hqe,hke->hqk", query_block, key_heads, preferred_element_type=jnp.float32
    ) * HEAD ** (-0.5)
    allowed = (offset + jnp.arange(block_rows))[:, None] >= jnp.arange(length)[None, :]
    return jnp.where(allowed[None], scores, -1e30)


def attend_forward(pieces):
    query_heads, key_heads, value_heads = pieces
    length = query_heads.shape[1]
    block_rows = min(length, 512)
    outputs = []
    totals = []
    for offset in range(0, length, block_rows):
        scores = block_scores(
            query_heads[:, offset : offset + block_rows], key_heads, offset, length
        )
        row_peak = jnp.max(scores, axis=-1, keepdims=True)
        exponent = jnp.exp(scores - row_peak)
        row_mass = jnp.sum(exponent, axis=-1, keepdims=True)
        outputs.append(
            jnp.einsum(
                "hqk,hke->hqe",
                (exponent / row_mass).astype(jnp.bfloat16),
                value_heads,
                preferred_element_type=jnp.float32,
            )
        )
        totals.append(row_peak + jnp.log(row_mass))
    return (jnp.concatenate(outputs, axis=1), jnp.concatenate(totals, axis=1))


def attend_backward(pieces):
    query_heads, key_heads, value_heads, grads_out, totals = pieces
    length = query_heads.shape[1]
    block_rows = min(length, 512)
    key_grad = jnp.zeros(key_heads.shape, jnp.float32)
    value_grad = jnp.zeros(value_heads.shape, jnp.float32)
    query_grads = []
    for offset in range(0, length, block_rows):
        query_block = query_heads[:, offset : offset + block_rows]
        grad_block = grads_out[:, offset : offset + block_rows]
        weights = jnp.exp(
            block_scores(query_block, key_heads, offset, length)
            - totals[:, offset : offset + block_rows]
        )
        grad_weights = jnp.einsum(
            "hqe,hke->hqk", grad_block, value_heads, preferred_element_type=jnp.float32
        )
        score_grad = (
            weights
            * (grad_weights - jnp.sum(weights * grad_weights, axis=-1, keepdims=True))
            * HEAD ** (-0.5)
        ).astype(jnp.bfloat16)
        query_grads.append(
            jnp.einsum("hqk,hke->hqe", score_grad, key_heads, preferred_element_type=jnp.float32)
        )
        key_grad = key_grad + jnp.einsum(
            "hqk,hqe->hke", score_grad, query_block, preferred_element_type=jnp.float32
        )
        value_grad = value_grad + jnp.einsum(
            "hqk,hqe->hke",
            weights.astype(jnp.bfloat16),
            grad_block,
            preferred_element_type=jnp.float32,
        )
    return (jnp.concatenate(query_grads, axis=1), key_grad, value_grad)


def branch_total(partial_sum):
    return lax.psum(partial_sum, "mp")


def input_total(partial_sum):
    return lax.psum(partial_sum, "mp")


def on_device_wide(
    series,
    observed,
    routes,
    step_count,
    joint_proj,
    joint_moment,
    joint_square,
    mixer_proj,
    mixer_moment,
    mixer_square,
    upward_proj,
    upward_moment,
    upward_square,
    downward_proj,
    downward_moment,
    downward_square,
    readout,
    readout_moment,
    readout_square,
    vectors,
    vectors_moment,
    vectors_square,
):
    dp_count = lax.axis_size("dp")
    hidden_local = upward_proj.shape[3]
    joint_full, mixer_full, upward_full, downward_full, readout_complete, vector_full = (
        lax.all_gather(joint_proj.astype(jnp.bfloat16), "dp", axis=1, tiled=True),
        lax.all_gather(mixer_proj.astype(jnp.bfloat16), "dp", axis=1, tiled=True),
        lax.all_gather(upward_proj.astype(jnp.bfloat16), "dp", axis=1, tiled=True),
        lax.all_gather(downward_proj.astype(jnp.bfloat16), "dp", axis=2, tiled=True),
        lax.all_gather(readout.astype(jnp.bfloat16), "dp", axis=0, tiled=True),
        lax.all_gather(vectors.astype(jnp.bfloat16), "dp", axis=1, tiled=True),
    )
    up_local = upward_full.reshape(upward_full.shape[0], D, -1)
    shared_up_weight = up_local[-1]
    shared_down_weight = downward_full[-1]
    expert_up = up_local[:ROUTED_EXPERTS]
    expert_down = downward_full[:ROUTED_EXPERTS]
    gain_rows = vector_full.astype(jnp.float32)
    series_count, length = series.shape
    entries = series_count * length
    route_rows = routes.reshape(entries, 2)
    onehot = route_rows[:, :, None] == jnp.arange(ROUTED_EXPERTS, dtype=jnp.int32)[None, None, :]
    observed_future_series, valid_mask = targets_of(series, observed)
    expert_count, head_count = lax.psum(
        (jnp.sum(onehot.astype(jnp.float32), axis=(0, 1)), head_counts(valid_mask)), "dp"
    )
    total_tokens = entries * dp_count
    inputs = (series * observed.astype(jnp.float32)).reshape(entries, 1)

    def embed(gate_vector, up_vector):
        return jax.nn.silu(inputs * gate_vector) * (inputs * up_vector)

    embedded, embed_back = jax.vjp(embed, gain_rows[3], gain_rows[4])
    normed_one, norm_one_back = jax.vjp(rms_scale, embedded, gain_rows[0])
    first_input = normed_one.astype(jnp.bfloat16)
    projected = jnp.einsum(
        "td,cde->cte", first_input, joint_full, preferred_element_type=jnp.float32
    )
    cosine_table, sine_table = rope_tables(length, HEAD)
    query_heads = rotate(
        split_heads(projected[0], series_count, length), cosine_table, sine_table
    ).astype(jnp.bfloat16)
    key_heads = rotate(
        split_heads(projected[1], series_count, length), cosine_table, sine_table
    ).astype(jnp.bfloat16)
    value_heads = split_heads(projected[2], series_count, length).astype(jnp.bfloat16)
    attended, totals = lax.map(attend_forward, (query_heads, key_heads, value_heads))
    attended_low = merge_heads(attended).astype(jnp.bfloat16)
    after_attn = embedded + branch_total(
        jnp.dot(attended_low, mixer_full, preferred_element_type=jnp.float32)
    )
    normed_two, norm_two_back = jax.vjp(rms_scale, after_attn, gain_rows[1])
    second_input = normed_two.astype(jnp.bfloat16)
    logits = jnp.dot(
        second_input, readout_complete[:, : ROUTED_EXPERTS + 1], preferred_element_type=jnp.float32
    )

    def gating(logit_rows):
        probabilities = jax.nn.softmax(logit_rows[:, :ROUTED_EXPERTS], axis=-1)
        chosen = jnp.sum(jnp.where(onehot, probabilities[:, None, :], 0.0), axis=-1)
        balance = (
            aux_factor
            * ROUTED_EXPERTS
            * jnp.sum(expert_count / total_tokens * jnp.sum(probabilities, axis=0) / total_tokens)
        )
        return (chosen, jax.nn.sigmoid(logit_rows[:, ROUTED_EXPERTS]), balance)

    (gate_values, shared_gate, balance), gating_back = jax.vjp(gating, logits)
    capacity = entries // 2
    slot_index, source = dispatch_plan(route_rows, ROUTED_EXPERTS, capacity)
    token_of = source // 2
    padded_input = jnp.concatenate([second_input, jnp.zeros((1, D), jnp.bfloat16)], axis=0)
    gathered = padded_input[token_of].reshape(ROUTED_EXPERTS, capacity, D)
    gate_up = jnp.einsum("ecd,edf->ecf", gathered, expert_up, preferred_element_type=jnp.float32)
    hidden_f, swiglu_back = jax.vjp(swiglu, gate_up)
    hidden = hidden_f.astype(jnp.bfloat16)
    expert_out = jnp.einsum(
        "ecf,efd->ecd", hidden, expert_down, preferred_element_type=jnp.float32
    ).reshape(ROUTED_EXPERTS * capacity, D)
    picked = expert_out[slot_index].reshape(entries, 2, D)
    shared_up = jnp.dot(second_input, shared_up_weight, preferred_element_type=jnp.float32)
    shared_f, shared_back = jax.vjp(swiglu, shared_up)
    shared_hidden = shared_f.astype(jnp.bfloat16)
    shared_out = jnp.dot(shared_hidden, shared_down_weight, preferred_element_type=jnp.float32)
    mixed_part = (
        jnp.sum(gate_values[:, :, None] * picked, axis=1) + shared_gate[:, None] * shared_out
    )
    after_mixer = after_attn + branch_total(mixed_part)
    normalized_output, norm_out_back = jax.vjp(rms_scale, after_mixer, gain_rows[2])
    output_input = normalized_output.astype(jnp.bfloat16)
    model_estimates = jnp.dot(
        output_input, readout_complete[:, ROUTED_EXPERTS + 1 :], preferred_element_type=jnp.float32
    )
    prediction_misses = model_estimates - observed_future_series
    absolute_miss = jnp.abs(prediction_misses)
    horizon_importance_factors = head_weights(head_count)[None, :] * valid_mask
    robust_penalty_entries = jnp.where(
        absolute_miss <= quadratic_cutoff,
        0.5 * prediction_misses * prediction_misses,
        quadratic_cutoff * (absolute_miss - 0.5 * quadratic_cutoff),
    )
    local_loss = jnp.sum(robust_penalty_entries * horizon_importance_factors) + balance
    mp_count = lax.axis_size("mp")
    loss_total = lax.psum(local_loss, "dp")
    predicted_gradient = (
        jnp.clip(prediction_misses, -quadratic_cutoff, quadratic_cutoff)
        * horizon_importance_factors
    ).astype(jnp.bfloat16)
    head_grad = jnp.einsum(
        "ka,ky->ay", output_input, predicted_gradient, preferred_element_type=jnp.float32
    )
    out_input_grad = jnp.einsum(
        "aw,iw->ai",
        predicted_gradient,
        readout_complete[:, ROUTED_EXPERTS + 1 :],
        preferred_element_type=jnp.float32,
    )
    mixer_grad_in, gain_three_grad = norm_out_back(out_input_grad)
    picked_dots = jnp.sum(picked * mixer_grad_in[:, None, :], axis=-1)
    shared_dots = jnp.sum(shared_out * mixer_grad_in, axis=-1)
    gate_grads, shared_gate_grad = lax.psum((picked_dots, shared_dots), "mp")
    (logit_grad,) = gating_back((gate_grads, shared_gate_grad, jnp.ones((), jnp.float32)))
    logit_low = logit_grad.astype(jnp.bfloat16)
    router_grad = jnp.einsum(
        "ka,ky->ay", second_input, logit_low, preferred_element_type=jnp.float32
    )
    router_input_grad = jnp.einsum(
        "aw,iw->ai",
        logit_low,
        readout_complete[:, : ROUTED_EXPERTS + 1],
        preferred_element_type=jnp.float32,
    )
    gates_padded = jnp.concatenate([gate_values.reshape(-1), jnp.zeros((1,), jnp.float32)], axis=0)
    residual_padded = jnp.concatenate([mixer_grad_in, jnp.zeros((1, D), jnp.float32)], axis=0)
    expert_out_grad = (
        (gates_padded[source][:, None] * residual_padded[token_of])
        .astype(jnp.bfloat16)
        .reshape(ROUTED_EXPERTS, capacity, D)
    )
    hidden_grad = jnp.einsum(
        "ecd,efd->ecf", expert_out_grad, expert_down, preferred_element_type=jnp.float32
    )
    down_grad_experts = jnp.einsum(
        "ecf,ecd->efd", hidden, expert_out_grad, preferred_element_type=jnp.float32
    )
    gate_up_grad = swiglu_back(hidden_grad)[0].astype(jnp.bfloat16)
    up_grad_experts = jnp.einsum(
        "ecd,ecf->edf", gathered, gate_up_grad, preferred_element_type=jnp.float32
    )
    rows_grad = jnp.einsum(
        "ecf,edf->ecd", gate_up_grad, expert_up, preferred_element_type=jnp.float32
    ).reshape(ROUTED_EXPERTS * capacity, D)
    routed_grad = jnp.sum(rows_grad[slot_index].reshape(entries, 2, D), axis=1)
    shared_out_grad = (shared_gate[:, None] * mixer_grad_in).astype(jnp.bfloat16)
    shared_hidden_grad = jnp.einsum(
        "td,fd->tf", shared_out_grad, shared_down_weight, preferred_element_type=jnp.float32
    )
    down_grad_shared = jnp.einsum(
        "tf,td->fd", shared_hidden, shared_out_grad, preferred_element_type=jnp.float32
    )
    shared_up_grad = shared_back(shared_hidden_grad)[0].astype(jnp.bfloat16)
    up_grad_shared = jnp.einsum(
        "td,tf->df", second_input, shared_up_grad, preferred_element_type=jnp.float32
    )
    input_part = routed_grad + jnp.einsum(
        "tf,df->td", shared_up_grad, shared_up_weight, preferred_element_type=jnp.float32
    )
    second_input_grad = input_total(input_part) + router_input_grad
    upward_grad = jnp.concatenate([up_grad_experts, up_grad_shared[None]], axis=0).reshape(
        ROUTED_EXPERTS + 1, D, 2, hidden_local
    )
    downward_grad = jnp.concatenate([down_grad_experts, down_grad_shared[None]], axis=0)
    attn_grad_in, gain_two_grad = norm_two_back(second_input_grad)
    attn_total_grad = mixer_grad_in + attn_grad_in
    attn_low = attn_total_grad.astype(jnp.bfloat16)
    mixer_grad = jnp.einsum("tf,td->fd", attended_low, attn_low, preferred_element_type=jnp.float32)
    attended_grad = jnp.einsum(
        "td,fd->tf", attn_low, mixer_full, preferred_element_type=jnp.float32
    ).astype(jnp.bfloat16)
    query_grad, key_grad, value_grad = lax.map(
        attend_backward,
        (
            query_heads,
            key_heads,
            value_heads,
            split_heads(attended_grad, series_count, length),
            totals,
        ),
    )
    projected_grad = jnp.stack(
        [
            merge_heads(rotate(query_grad, cosine_table, -sine_table)),
            merge_heads(rotate(key_grad, cosine_table, -sine_table)),
            merge_heads(value_grad),
        ],
        axis=0,
    ).astype(jnp.bfloat16)
    joint_grad = jnp.einsum(
        "td,cte->cde", first_input, projected_grad, preferred_element_type=jnp.float32
    )
    first_input_grad = input_total(
        jnp.einsum("cte,cde->td", projected_grad, joint_full, preferred_element_type=jnp.float32)
    )
    embed_grad_in, gain_one_grad = norm_one_back(first_input_grad)
    gate_vector_grad, up_vector_grad = embed_back(attn_total_grad + embed_grad_in)
    vector_grad = jnp.stack(
        [gain_one_grad, gain_two_grad, gain_three_grad, gate_vector_grad, up_vector_grad], axis=0
    )
    readout_grad = jnp.concatenate([router_grad, head_grad], axis=1)
    joint_red, mixer_red, upward_red, downward_red, readout_red, vector_red = (
        lax.psum_scatter(joint_grad, "dp", scatter_dimension=1, tiled=True),
        lax.psum_scatter(mixer_grad, "dp", scatter_dimension=1, tiled=True),
        lax.psum_scatter(upward_grad, "dp", scatter_dimension=1, tiled=True),
        lax.psum_scatter(downward_grad, "dp", scatter_dimension=2, tiled=True),
        lax.psum_scatter(readout_grad, "dp", scatter_dimension=0, tiled=True),
        lax.psum_scatter(vector_grad, "dp", scatter_dimension=1, tiled=True),
    )
    split_squares = (
        jnp.sum(joint_red * joint_red)
        + jnp.sum(mixer_red * mixer_red)
        + jnp.sum(upward_red * upward_red)
        + jnp.sum(downward_red * downward_red)
    )
    shared_squares = jnp.sum(readout_red * readout_red) + jnp.sum(vector_red * vector_red)
    partial_squares = split_squares + shared_squares / mp_count
    norm_squared = lax.psum(partial_squares, ("dp", "mp"))
    grad_norm = jnp.sqrt(norm_squared)
    factor = clip_limit / (grad_norm + 1e-06)
    steps_taken = step_count[0].astype(jnp.float32)
    bias_one = 1.0 - beta_one**steps_taken
    bias_two = 1.0 - beta_two**steps_taken
    joint_new = adam_update(
        joint_proj, joint_moment, joint_square, joint_red, factor, bias_one, bias_two, matrix_rate
    )
    mixer_new = adam_update(
        mixer_proj, mixer_moment, mixer_square, mixer_red, factor, bias_one, bias_two, matrix_rate
    )
    upward_new = adam_update(
        upward_proj,
        upward_moment,
        upward_square,
        upward_red,
        factor,
        bias_one,
        bias_two,
        matrix_rate,
    )
    downward_new = adam_update(
        downward_proj,
        downward_moment,
        downward_square,
        downward_red,
        factor,
        bias_one,
        bias_two,
        matrix_rate,
    )
    readout_new = adam_update(
        readout,
        readout_moment,
        readout_square,
        readout_red,
        factor,
        bias_one,
        bias_two,
        matrix_rate,
    )
    vector_new = adam_update(
        vectors, vectors_moment, vectors_square, vector_red, factor, bias_one, bias_two, vector_rate
    )
    return (
        loss_total,
        grad_norm,
        joint_new[0],
        joint_new[1],
        joint_new[2],
        mixer_new[0],
        mixer_new[1],
        mixer_new[2],
        upward_new[0],
        upward_new[1],
        upward_new[2],
        downward_new[0],
        downward_new[1],
        downward_new[2],
        readout_new[0],
        readout_new[1],
        readout_new[2],
        vector_new[0],
        vector_new[1],
        vector_new[2],
    )


def solution(mesh):
    token = [P("dp", None), P("dp", None), P("dp", None, None), P()]
    weights = [
        P(None, "dp", "mp"), P("mp", "dp"), P(None, "dp", None, "mp"), P(None, "mp", "dp"), P("dp", None), P(None, "dp"),
    ]
    triple = tuple(spec for spec in weights for _ in range(3))
    near = mesh.shape["dp"] == 16 and mesh.shape["mp"] == 2
    return jax.shard_map(
        on_device if near else on_device_wide,
        mesh=mesh,
        in_specs=tuple(token) + triple,
        out_specs=(P(), P()) + triple,
        check_vma=False,
    )
```

```python
import functools
import jax
import jax.numpy as jnp
from jax import lax
from jax.experimental import pallas as pl
from jax.experimental.pallas import tpu as pltpu
from jax.sharding import PartitionSpec as P

D = 384
HEAD = 32
ROUTED_EXPERTS = 8
LANES = 128
TILE = 256
SHARD = 24
ROUTER = 112
SHARED = ROUTER + ROUTED_EXPERTS
VECTOR = SHARED + 1

horizons = (1, 8, 32, 64)
quadratic_cutoff = 2.0
aux_factor = 0.02
clip_limit = 0.001
beta_one = 0.9
beta_two = 0.95
adam_eps = 1e-08
decay_rate = 0.1
matrix_rate = 0.05
vector_rate = 0.25
norm_eps = 1e-06
rope_base = 10000.0

F32 = jnp.float32
BF16 = jnp.bfloat16
I16 = jnp.int16
MESH = pl.DeviceIdType.MESH
VMEM = pl.BlockSpec(memory_space=pltpu.VMEM)
ANY = pl.BlockSpec(memory_space=pl.ANY)
DMA = pltpu.SemaphoreType.DMA


def dot(a, b, da=1, db=0):
    return lax.dot_general(a, b, (((da,), (db,)), ((), ())), preferred_element_type=F32)


def params(megabytes=60, **more):
    return pltpu.CompilerParams(vmem_limit_bytes=megabytes * 1024 * 1024, **more)


def sigmoid(v):
    return 1.0 / (1.0 + jnp.exp(-v))


def block(index, size, step=8):
    return pl.ds(pl.multiple_of(index * size, step), size)


def place():
    dp = lax.axis_index("dp")
    return dp, lax.axis_index("mp"), lax.rem(dp, 2), lax.rem(dp // 2, 2), dp // 4


def meet_everyone(dp, mp):
    barrier = pltpu.get_barrier_semaphore()
    me, n = dp * 2 + mp, 32

    def signal(k, carry):
        peer = lax.rem(me + k, n)
        pl.semaphore_signal(barrier, inc=1, device_id=(peer // 2, lax.rem(peer, 2)), device_id_type=MESH)
        return carry

    lax.fori_loop(1, n, signal, 0)
    pl.semaphore_wait(barrier, n - 1)


def remote(src, dst, send, recv, dp, mp):
    return pltpu.make_async_remote_copy(
        src_ref=src, dst_ref=dst, send_sem=send, recv_sem=recv, device_id=(dp, mp), device_id_type=MESH)


def done(view, sem):
    pltpu.make_async_copy(view, view, sem).wait()


def column(row, length):
    return jnp.transpose(jnp.broadcast_to(row, (LANES, length)))


def rotated(t, cos, sin):
    half = HEAD // 2
    front, back = t[:half], t[half:]
    return jnp.concatenate([front * cos - back * sin, back * cos + front * sin], axis=0)


def unrotated(t, cos, sin):
    half = HEAD // 2
    front, back = t[:half], t[half:]
    return jnp.concatenate([front * cos + back * sin, back * cos - front * sin], axis=0)


def score_block(k_rows, q_cols, low):
    s = dot(k_rows, q_cols)
    keys = lax.broadcasted_iota(jnp.int32, s.shape, 0)
    queries = lax.broadcasted_iota(jnp.int32, s.shape, 1) + low
    return jnp.where(keys <= queries, s, -1e30)


def flip(t):
    return jnp.transpose(t.astype(F32)).astype(BF16)


def embed_piece(x_row, vec, x0_ref, a_ref, r):
    xb = column(x_row, TILE)
    cuts, square = [], None
    for c in range(D // LANES):
        cols = slice(c * LANES, (c + 1) * LANES)
        u = xb * vec[3:4, cols]
        v = u * sigmoid(u) * (xb * vec[4:5, cols])
        x0_ref[r, cols] = v
        square = v * v if square is None else square + v * v
        cuts.append(v)
    scale = lax.rsqrt(jnp.sum(square, axis=1, keepdims=True) / D + norm_eps)
    for c in range(D // LANES):
        cols = slice(c * LANES, (c + 1) * LANES)
        a_ref[r, cols] = (cuts[c] * scale * vec[0:1, cols]).astype(BF16)


def project_piece(wt, a, cos, sin, qkv, width):
    for part in range(3):
        t = dot(wt[part * width:(part + 1) * width, :], a, 1, 1)
        for h in range(width // HEAD):
            u = t[h * HEAD:(h + 1) * HEAD]
            if part < 2:
                u = rotated(u, cos, sin)
            qkv[part * width + h * HEAD:part * width + (h + 1) * HEAD, :] = u.astype(BF16)


def forward_head(h, width, qkv, lse, o):
    length = qkv.shape[1]
    scale = HEAD ** (-0.5)
    q_rows = block(h, HEAD)
    k_rows = pl.ds(pl.multiple_of(width + h * HEAD, HEAD), HEAD)
    v_rows = pl.ds(pl.multiple_of(2 * width + h * HEAD, HEAD), HEAD)
    k = flip(qkv[k_rows, :])
    for j in range(length // TILE):
        n = TILE * (j + 1)
        cols = slice(j * TILE, (j + 1) * TILE)
        s = score_block(k[:n], qkv[q_rows, cols], j * TILE)
        peak = jnp.max(s, axis=0, keepdims=True)
        e = jnp.exp((s - peak) * scale)
        mass = jnp.sum(e, axis=0, keepdims=True)
        weights = (e * (1.0 / mass)).astype(BF16)
        o[q_rows, cols] = dot(qkv[v_rows, :n], weights).astype(BF16)
        lse[pl.ds(h, 1), cols] = peak * scale + jnp.log(mass)


def backward_head(h, width, qkv, do_t, lse, cos, sin, dqkv, dk_ref, dv_ref):
    length = qkv.shape[1]
    scale = HEAD ** (-0.5)
    q_rows = block(h, HEAD)
    k_rows = pl.ds(pl.multiple_of(width + h * HEAD, HEAD), HEAD)
    v_rows = pl.ds(pl.multiple_of(2 * width + h * HEAD, HEAD), HEAD)
    q, k, v, do = flip(qkv[q_rows, :]), flip(qkv[k_rows, :]), flip(qkv[v_rows, :]), flip(do_t[q_rows, :])
    dk_ref[...] = jnp.zeros_like(dk_ref)
    dv_ref[...] = jnp.zeros_like(dv_ref)
    for j in range(length // TILE):
        n = TILE * (j + 1)
        cols = slice(j * TILE, (j + 1) * TILE)
        s = score_block(k[:n], qkv[q_rows, cols], j * TILE)
        w = jnp.exp(s * scale - lse[pl.ds(h, 1), cols])
        dv_ref[:n] += dot(w.astype(BF16), do[cols])
        dw = dot(v[:n], do_t[q_rows, cols])
        mean = jnp.sum(w * dw, axis=0, keepdims=True)
        ds = (w * (dw - mean) * scale).astype(BF16)
        dk_ref[:n] += dot(ds, q[cols])
        dq = dot(qkv[k_rows, :n], ds)
        dqkv[q_rows, cols] = unrotated(dq, cos[:, cols], sin[:, cols]).astype(BF16)
    dqkv[k_rows, :] = unrotated(jnp.transpose(dk_ref[...]), cos, sin).astype(BF16)
    dqkv[v_rows, :] = jnp.transpose(dv_ref[...]).astype(BF16)


def mid_forward_piece(x, gain, table):
    scale = lax.rsqrt(jnp.mean(x * x, axis=1, keepdims=True) + norm_eps)
    low = (x * scale * gain).astype(BF16)
    logits = dot(low, table)
    lanes = lax.broadcasted_iota(jnp.int32, logits.shape, 1)
    routed = (lanes >= ROUTER) & (lanes < SHARED)
    peak = jnp.max(jnp.where(routed, logits, -jnp.inf), axis=1, keepdims=True)
    e = jnp.where(routed, jnp.exp(jnp.where(routed, logits - peak, 0.0)), 0.0)
    probability = e / jnp.sum(e, axis=1, keepdims=True)
    gates = jnp.where(lanes == SHARED, sigmoid(jnp.where(lanes == SHARED, logits, 0.0)), probability)
    return low, gates, jnp.sum(probability, axis=0, keepdims=True)


def embed_backward_piece(x_row, da, dx1, vec):
    xb = column(x_row, TILE)
    xb = jnp.concatenate([xb] * (D // LANES), axis=1)
    u = xb * vec[3:4, :]
    up = xb * vec[4:5, :]
    s = sigmoid(u)
    silu = u * s
    x = silu * up
    scale = lax.rsqrt(jnp.mean(x * x, axis=1, keepdims=True) + norm_eps)
    unit = x * scale
    dn = da * vec[0:1, :]
    dx = dx1 + scale * (dn - unit * jnp.mean(dn * unit, axis=1, keepdims=True))
    du = dx * up * (s * (1.0 + u * (1.0 - s)))
    total = lambda v: jnp.sum(v, axis=0, keepdims=True)
    return total(da * unit), total(du * xb), total(dx * silu * xb)


def forward_kernel(
    small_own, big_own, tally, x_ref, cos_ref, sin_ref,
    big, wt, wo, table_t, vec, table, a, qkv, lse, o, x1, b, pc, total, tallies,
    stage, small, x0, part, other,
    in_sem, own_sem, send_xy, send_up, send_dn, z_sem, p2_sem, p3_sem,
    small_send, small_z, small_y, small_x, tally_send, tally_recv, pair_send, pair_recv,
):
    dp, mp, x, y, z = place()
    xp, yp = dp + 1 - 2 * x, dp + 2 - 4 * y
    count = big_own.shape[0]
    series, _, length = x_ref.shape
    width = o.shape[1]
    per = length // TILE
    load = pltpu.make_async_copy(big_own, stage, in_sem)
    load.start()
    meet_everyone(dp, mp)

    def home(zs):
        return zs * 4 + 2 * y + x

    def small_put(src, slot, recv, peer):
        remote(src, small.at[slot], small_send, recv, peer, mp).start()

    for dist in (1, 2, 3):
        @pl.when(z >= dist)
        def _():
            small_put(small_own, dp, small_z.at[z], dp - 4 * dist)

        @pl.when(z + dist <= 3)
        def _():
            small_put(small_own, dp, small_z.at[z], dp + 4 * dist)
    small_put(small_own, dp, small_y.at[z], yp)
    small_put(small_own, dp, small_x, xp)
    small[dp] = small_own[...]
    me = dp * 2 + mp

    def tell(k, carry):
        peer = lax.rem(me + k, 32)
        remote(tally, tallies.at[me], tally_send, tally_recv, peer // 2, lax.rem(peer, 2)).start()
        return carry

    lax.fori_loop(1, 32, tell, 0)
    tallies[me] = tally[...]

    load.wait()

    def rows(c, slot):
        return big.at[c, block(slot, SHARD), :]

    def put(src, c, slot, send, recv, peer):
        remote(src, rows(c, slot), send, recv, peer, mp).start()

    def climb(c, zs, src):
        put(src, c, home(zs), send_up, z_sem.at[c, zs], dp + 4)

    def drop(c, zs, src):
        put(src, c, home(zs), send_dn, z_sem.at[c, zs], dp - 4)

    def turn_of(c, zs):
        return jnp.where(c == count - 1, jnp.where(zs == 0, 0, 1), lax.rem(c, 2))

    def ends(c, zs):
        k = turn_of(c, zs)
        return jnp.where(k == 0, yp, xp), jnp.where(k == 0, xp, yp)

    def spread(c, zs, src):
        first, second = ends(c, zs)
        put(src, c, home(zs), send_xy, p2_sem.at[c, zs], first)
        put(src, c, home(zs), send_xy, p3_sem, second)

    def own_z(c, carry):
        @pl.when(z < 3)
        def _():
            climb(c, z, stage.at[c])

        @pl.when(z > 0)
        def _():
            drop(c, z, stage.at[c])
        pltpu.make_async_copy(stage.at[c], rows(c, dp), own_sem).start()
        return carry

    lax.fori_loop(0, count, own_z, 0)

    def own_xy(c, carry):
        spread(c, z, stage.at[c])
        return carry

    early = 4
    lax.fori_loop(0, early, own_xy, 0)

    for dist in (1, 2, 3):
        for sign in (-1, 1):
            zs = z + sign * dist

            @pl.when((zs >= 0) & (zs <= 3))
            def _():
                done(small.at[home(zs)], small_z.at[zs])
                small_put(small.at[home(zs)], home(zs), small_y.at[zs], yp)
                small_put(small.at[home(zs)], home(zs), small_x, xp)
    for turn in range(4):
        zs = lax.rem(z + turn, 4)
        slot = zs * 4 + 2 * (1 - y) + x
        done(small.at[slot], small_y.at[zs])
        small_put(small.at[slot], slot, small_x, xp)
    done(small.at[pl.ds(0, 8)], small_x)

    lax.fori_loop(early, count, own_xy, 0)

    whole = small[...].astype(F32).reshape(D, -1)
    table[...] = whole[:, 4 * width:].astype(BF16)
    turned = jnp.transpose(whole)
    wt[...] = turned[:3 * width].astype(BF16)
    wo[...] = turned[3 * width:4 * width].astype(BF16)
    table_t[...] = turned[4 * width:].astype(BF16)
    vec[...] = jnp.concatenate(
        [turned[4 * width + VECTOR:4 * width + VECTOR + 5], jnp.zeros((3, D), F32)], axis=0)
    total[...] = jnp.zeros_like(total)

    def relay(c, dist):
        def second(zs):
            k = turn_of(c, zs)
            slot = zs * 4 + jnp.where(k == 0, 2 * (1 - y) + x, 2 * y + 1 - x)
            done(rows(c, slot), p2_sem.at[c, zs])
            put(rows(c, slot), c, slot, send_xy, p3_sem, ends(c, zs)[1])

        @pl.when(z >= dist)
        def _():
            zs = z - dist
            done(rows(c, home(zs)), z_sem.at[c, zs])

            @pl.when(z < 3)
            def _():
                climb(c, zs, rows(c, home(zs)))
            spread(c, zs, rows(c, home(zs)))

        @pl.when(z + dist <= 3)
        def _():
            zs = z + dist
            done(rows(c, home(zs)), z_sem.at[c, zs])

            @pl.when(z > 0)
            def _():
                drop(c, zs, rows(c, home(zs)))
            spread(c, zs, rows(c, home(zs)))

        @pl.when(z - (dist - 1) >= 0)
        def _():
            second(z - (dist - 1))

        @pl.when((dist > 1) & (z + dist - 1 <= 3))
        def _():
            second(z + dist - 1)

    def pair(n):
        r = block(n, length)
        return remote(part.at[r], other.at[r], pair_send.at[n], pair_recv.at[n], dp, 1 - mp)

    heads = width // HEAD
    pieces = heads + 2

    def attention(i):
        n, j = i // pieces, lax.rem(i, pieces)
        r = block(n, length)

        @pl.when(j == 0)
        def _():
            def tile(m, carry):
                t = pl.ds(pl.multiple_of(n * length + m * TILE, TILE), TILE)
                embed_piece(x_ref[n, :, block(m, TILE, TILE)], vec, x0, a, t)
                return carry
            lax.fori_loop(0, per, tile, 0)

        @pl.when(j == 1)
        def _():
            project_piece(wt, a[r, :], cos_ref[...], sin_ref[...], qkv.at[n], width)

        @pl.when(j >= 2)
        def _():
            forward_head(j - 2, width, qkv.at[n], lse.at[n], o.at[n])

        @pl.when(j == pieces - 1)
        def _():
            part[r, :] = dot(o[n], wo[...], 0, 0)
            pair(n).start()

    def middle(m):
        r = block(m, TILE)

        @pl.when(lax.rem(m, per) == 0)
        def _():
            pair(m // per).wait()
        v = x0[r, :] + (part[r, :] + other[r, :])
        x1[r, :] = v
        low, gates, sums = mid_forward_piece(v, vec[1:2, :], table[...])
        b[r, :] = low
        pc[r, :] = gates
        total[...] += sums

    def step(i, carry):
        relay(lax.rem(i, count), i // count + 1)

        @pl.when(i < series * pieces)
        def _():
            attention(i)

        for n in range(series):
            begin = (n + 1) * pieces + 4

            @pl.when((i >= begin) & (i < begin + per))
            def _():
                middle(n * per + i - begin)
        return carry

    lax.fori_loop(0, 4 * count, step, 0)

    def whole_wait(n, sem):
        done(big.at[:, pl.ds(0, n * SHARD), :], sem)
    whole_wait(8, p3_sem)
    whole_wait(12, send_xy)
    whole_wait(1, own_sem)
    done(small.at[pl.ds(0, 15)], small_send)
    done(tallies.at[pl.ds(0, 31)], tally_recv)
    done(tallies.at[pl.ds(0, 31)], tally_send)
    for k in range(4):
        @pl.when(z == k)
        def _():
            if k < 3:
                whole_wait(k + 1, send_up)
            if k > 0:
                whole_wait(4 - k, send_dn)


def forward_near(small_own, big_own, tally, x, cos, sin, width, ident):
    series, _, length = x.shape
    tokens = series * length
    count, shard, columns = big_own.shape
    shape = jax.ShapeDtypeStruct
    return pl.pallas_call(
        forward_kernel,
        in_specs=[VMEM, ANY, VMEM, VMEM, VMEM, VMEM],
        out_specs=[ANY] + [VMEM] * 14,
        out_shape=[
            shape((count, D, columns), BF16),
            shape((3 * width, D), BF16), shape((width, D), BF16), shape((LANES, D), BF16),
            shape((8, D), F32), shape((D, LANES), BF16),
            shape((tokens, D), BF16), shape((series, 3 * width, length), BF16), shape((series, 8, length), F32),
            shape((series, width, length), BF16),
            shape((tokens, D), F32), shape((tokens, D), BF16), shape((tokens, LANES), F32), shape((1, LANES), F32),
            shape((32,) + tally.shape, F32),
        ],
        scratch_shapes=[
            pltpu.VMEM(big_own.shape, BF16), pltpu.VMEM((16,) + small_own.shape, BF16),
            pltpu.VMEM((tokens, D), F32), pltpu.VMEM((tokens, D), F32), pltpu.VMEM((tokens, D), F32),
            DMA, DMA, DMA, DMA, DMA, DMA((count, 4)), DMA((count, 4)), DMA,
            DMA, DMA((4,)), DMA((4,)), DMA, DMA, DMA, DMA((series,)), DMA((series,)),
        ],
        compiler_params=params(collective_id=ident, has_side_effects=True),
        name="forward_near",
    )(small_own, big_own, tally, x, cos, sin)


GROUP = 16


def spread_rows(dest, value, start, count):
    for c in range(value.shape[1] // LANES):
        dest[pl.ds(start * 8 + c, count, stride=8), :] = value[:, c * LANES:(c + 1) * LANES]


def rows_at(ref, index):
    return ref[pl.ds(pl.multiple_of(index, 8), 8), :]


def pick_rows(source, tile, index_ref, base):
    for i in range(0, TILE, GROUP):
        values = [rows_at(source, index_ref[base + k]) for k in range(i, i + GROUP)]
        for k in range(i, i + GROUP):
            tile[k * 8:k * 8 + 8, :] = values[k - i]


def sum_rows(results, tile, index_ref, base, tokens):
    for i in range(0, TILE, GROUP):
        values = [
            rows_at(results, index_ref[base + k]) + rows_at(results, index_ref[tokens + base + k])
            for k in range(i, i + GROUP)]
        for k in range(i, i + GROUP):
            tile[k * 8:k * 8 + 8, :] = values[k - i]


def gathered_columns(tile, columns):
    return [tile[pl.ds(c, TILE, stride=8), :] for c in range(columns)]


def lane_of(value, lane):
    lanes = lax.broadcasted_iota(jnp.int32, value.shape, 1)
    return jnp.sum(jnp.where(lanes == lane, value, 0.0), axis=1, keepdims=True)


def lay_rows(values, pc_ref, rows8):
    tokens = values.shape[0]

    def lay(i, carry):
        r = block(i, TILE)
        spread_rows(rows8, values[r, :].astype(F32), i * TILE, TILE)
        rows8[pl.ds(i * TILE * 8 + 3, TILE, stride=8), :] = pc_ref[r, :]
        return carry

    lax.fori_loop(0, tokens // TILE, lay, 0)
    rows8[pl.ds(tokens * 8, 8), :] = jnp.zeros((8, LANES), F32)


def expert_tiles(e, used, capacity, tile, blank, shared):
    tiles = capacity // TILE

    @pl.when(e < ROUTED_EXPERTS)
    def _():
        def one(i, carry):
            tile(e * tiles + i, block(i, TILE))
            return carry

        def none(i, carry):
            blank(block(i, TILE))
            return carry

        lax.fori_loop(0, used[e], one, 0)
        lax.fori_loop(used[e], tiles, none, 0)

    @pl.when(e >= ROUTED_EXPERTS)
    def _():
        def one(i, carry):
            shared((e - ROUTED_EXPERTS) * tiles + i, block(i, TILE))
            return carry

        lax.fori_loop(0, tiles, one, 0)


def expert_forward_kernel(
    used, order, after, source, slots, b_ref, pc_ref, w_ref, x_ref, y_ref, mix_ref, rows8, done8, tile8, sum8
):
    e = pl.program_id(0)
    tokens = b_ref.shape[0]
    hidden = w_ref.shape[2] // 3

    @pl.when(e == 0)
    def _():
        lay_rows(b_ref, pc_ref, rows8)
        pick_rows(rows8, tile8, source, after[after.shape[0] - 1])

    def run(x):
        g = dot(x, w_ref[0, :, : 2 * hidden])
        gate, up = g[:, :hidden], g[:, hidden:]
        h = (gate * sigmoid(gate) * up).astype(BF16)
        return dot(h, w_ref[0, :, 2 * hidden:], 1, 1)

    def tile(s, here):
        c0, c1, c2, pc = gathered_columns(tile8, 4)
        x = jnp.concatenate([c0, c1, c2], axis=1).astype(BF16)
        x_ref[0, here, :] = x
        gate_column = lane_of(pc, ROUTER + e)
        pick_rows(rows8, tile8, source, after[s])
        y = run(x)
        y_ref[0, here, :] = y
        spread_rows(done8, y * gate_column, order[s], TILE)

    def blank(here):
        x_ref[0, here, :] = jnp.zeros((TILE, D), BF16)

    def shared(j, here):
        r = block(j, TILE)
        x = b_ref[r, :]
        x_ref[0, here, :] = x
        sum_rows(done8, sum8, slots, j * TILE, tokens)
        y = run(x)
        y_ref[0, here, :] = y
        scaled = y * lane_of(pc_ref[r, :], SHARED)
        for c, part in enumerate(gathered_columns(sum8, D // LANES)):
            cols = slice(c * LANES, (c + 1) * LANES)
            mix_ref[r, cols] = part + scaled[:, cols]

    expert_tiles(e, used, y_ref.shape[1], tile, blank, shared)


def expert_specs(tokens, weights):
    full = lambda shape: pl.BlockSpec(shape, lambda e, *_: (0,) * len(shape), pipeline_mode=pl.Buffered(1))
    tile = lambda w: pl.BlockSpec((1, tokens // 2, w), lambda e, *_: (e, 0, 0))
    weight = pl.BlockSpec((1,) + weights.shape[1:], lambda e, *_: (jnp.minimum(e, ROUTED_EXPERTS), 0, 0))
    scratch = [
        pltpu.VMEM(((tokens + 1) * 8, LANES), F32), pltpu.VMEM(((2 * tokens + TILE) * 8, LANES), F32),
        pltpu.VMEM((TILE * 8, LANES), F32), pltpu.VMEM((TILE * 8, LANES), F32)]
    return full, tile, weight, scratch


def expert_forward(plan, b, pc, weights):
    tokens = b.shape[0]
    full, tile, weight, scratch = expert_specs(tokens, weights)
    return pl.pallas_call(
        expert_forward_kernel,
        grid_spec=pltpu.PrefetchScalarGridSpec(
            num_scalar_prefetch=5,
            grid=(ROUTED_EXPERTS + 2,),
            in_specs=[full(b.shape), full(pc.shape), weight],
            out_specs=[tile(D), tile(D), full((tokens, D))],
            scratch_shapes=scratch,
        ),
        out_shape=[
            jax.ShapeDtypeStruct((ROUTED_EXPERTS + 2, tokens // 2, D), BF16),
            jax.ShapeDtypeStruct((ROUTED_EXPERTS + 2, tokens // 2, D), F32),
            jax.ShapeDtypeStruct((tokens, D), F32),
        ],
        compiler_params=params(),
        name="expert_forward",
    )(*plan, b, pc, weights)


def expert_backward_kernel(
    used, order, after, source, slots, pc_ref, dx_ref, w_ref, x_ref, y_ref, dy_ref, dg_ref, h_ref, acc_ref,
    rows8, done8, tile8, sum8,
):
    e = pl.program_id(0)
    tokens = dx_ref.shape[0]
    hidden = w_ref.shape[2] // 3
    lanes = lax.broadcasted_iota(jnp.int32, (TILE, LANES), 1)

    @pl.when(e == 0)
    def _():
        lay_rows(dx_ref, pc_ref, rows8)
        pick_rows(rows8, tile8, source, after[after.shape[0] - 1])

    def run(here, dy):
        dy_ref[0, here, :] = dy
        u = w_ref[0, :, : 2 * hidden]
        g = dot(x_ref[0, here, :], u)
        gate, up = g[:, :hidden], g[:, hidden:]
        sig = sigmoid(gate)
        silu = gate * sig
        h_ref[0, here, :] = (silu * up).astype(BF16)
        dh = dot(dy, w_ref[0, :, 2 * hidden:])
        d_up = (dh * silu).astype(BF16)
        d_gate = (dh * up * (sig * (1.0 + gate * (1.0 - sig)))).astype(BF16)
        dg_ref[0, here, :hidden] = d_gate
        dg_ref[0, here, hidden:] = d_up
        return dot(d_gate, u[:, :hidden], 1, 1) + dot(d_up, u[:, hidden:], 1, 1)

    def tile(s, here):
        c0, c1, c2, pc = gathered_columns(tile8, 4)
        dx = jnp.concatenate([c0, c1, c2], axis=1)
        d_value = jnp.sum(y_ref[0, here, :] * dx, axis=1, keepdims=True)
        dy = (dx * lane_of(pc, ROUTER + e)).astype(BF16)
        pick_rows(rows8, tile8, source, after[s])
        back = run(here, dy)
        spread_rows(done8, back, order[s], TILE)
        done8[pl.ds(order[s] * 8 + 3, TILE, stride=8), :] = jnp.where(lanes == ROUTER + e, d_value, 0.0)

    def blank(here):
        dy_ref[0, here, :] = jnp.zeros((TILE, D), BF16)
        dg_ref[0, here, :] = jnp.zeros((TILE, 2 * hidden), BF16)
        h_ref[0, here, :] = jnp.zeros((TILE, hidden), BF16)

    def shared(j, here):
        r = block(j, TILE)
        dx = dx_ref[r, :]
        d_value = jnp.sum(y_ref[0, here, :] * dx, axis=1, keepdims=True)
        sum_rows(done8, sum8, slots, j * TILE, tokens)
        back = run(here, (dx * lane_of(pc_ref[r, :], SHARED)).astype(BF16))
        sums = gathered_columns(sum8, D // LANES + 1)
        for c in range(D // LANES):
            cols = slice(c * LANES, (c + 1) * LANES)
            acc_ref[r, cols] = sums[c] + back[:, cols]
        acc_ref[r, D:] = jnp.where(lanes == SHARED, d_value, sums[-1])

    expert_tiles(e, used, y_ref.shape[1], tile, blank, shared)


def expert_backward(plan, pc, dx, weights, x, y):
    tokens = dx.shape[0]
    hidden = weights.shape[2] // 3
    full, tile, weight, scratch = expert_specs(tokens, weights)
    return pl.pallas_call(
        expert_backward_kernel,
        grid_spec=pltpu.PrefetchScalarGridSpec(
            num_scalar_prefetch=5,
            grid=(ROUTED_EXPERTS + 2,),
            in_specs=[full(pc.shape), full(dx.shape), weight, tile(D), tile(D)],
            out_specs=[tile(D), tile(2 * hidden), tile(hidden), full((tokens, D + LANES))],
            scratch_shapes=scratch,
        ),
        out_shape=[
            jax.ShapeDtypeStruct((ROUTED_EXPERTS + 2, tokens // 2, D), BF16),
            jax.ShapeDtypeStruct((ROUTED_EXPERTS + 2, tokens // 2, 2 * hidden), BF16),
            jax.ShapeDtypeStruct((ROUTED_EXPERTS + 2, tokens // 2, hidden), BF16),
            jax.ShapeDtypeStruct((tokens, D + LANES), F32),
        ],
        compiler_params=params(),
        name="expert_backward",
    )(*plan, pc, dx, weights, x, y)


def exchange(part, other, send_sem, recv_sem):
    dp, mp = lax.axis_index("dp"), lax.axis_index("mp")
    barrier = pltpu.get_barrier_semaphore()
    pl.semaphore_signal(barrier, inc=1, device_id=(dp, 1 - mp), device_id_type=MESH)
    pl.semaphore_wait(barrier, 1)

    def copy(i):
        r = block(i, TILE)
        return remote(part.at[r], other.at[r], send_sem.at[i], recv_sem.at[i], dp, 1 - mp)

    def begin(i, carry):
        copy(i).start()
        return carry

    lax.fori_loop(0, part.shape[0] // TILE, begin, 0)
    return lambda i: copy(i).wait()


def exchange_scratch(part):
    tiles = part.shape[0] // TILE
    return [pltpu.VMEM(part.shape, F32), DMA((tiles,)), DMA((tiles,))]


def hankel(base):
    block_rows = jnp.broadcast_to(base, (LANES, 2 * LANES))
    m = pltpu.roll(block_rows, 0, 1, stride=1, stride_axis=0)[:, :LANES]
    lanes = lax.broadcasted_iota(jnp.int32, (LANES, LANES), 1)
    out = pltpu.roll(m, 41, 1)
    out = jnp.where(lanes < 104, pltpu.roll(m, 40, 1), out)
    out = jnp.where(lanes < 96, pltpu.roll(m, 32, 1), out)
    return jnp.where(lanes < 64, m, out)


def loss_piece(x, gain, table, table_t, value_rows, mark_rows, weight):
    scale = lax.rsqrt(jnp.mean(x * x, axis=1, keepdims=True) + norm_eps)
    unit = x * scale
    low = (unit * gain).astype(BF16)
    z = dot(low, table)
    target = jnp.concatenate([hankel(row) for row in value_rows], axis=0)
    valid = jnp.concatenate([hankel(row) for row in mark_rows], axis=0)
    factor = valid * weight
    miss = z - target
    size = jnp.abs(miss)
    huber = jnp.where(
        size <= quadratic_cutoff, 0.5 * miss * miss, quadratic_cutoff * (size - 0.5 * quadratic_cutoff))
    dz = (jnp.clip(miss, -quadratic_cutoff, quadratic_cutoff) * factor).astype(BF16)
    df = dot(dz, table_t)
    dn = df * gain
    dx = scale * (dn - unit * jnp.mean(dn * unit, axis=1, keepdims=True))
    total = lambda v: jnp.sum(v, axis=0, keepdims=True)
    return dx, dot(dz, low, 0, 0), total(df * unit), total(huber * factor)


def loss_kernel(part, x1, vec, table, table_t, values, marks, weight, dx2, d_table, d_gain, loss,
                other, send_sem, recv_sem):
    wait = exchange(part, other, send_sem, recv_sem)
    d_table[...] = jnp.zeros_like(d_table)
    d_gain[...] = jnp.zeros_like(d_gain)
    loss[...] = jnp.zeros_like(loss)
    per = TILE // LANES

    def step(i, carry):
        r = block(i, TILE)
        wait(i)
        dx, dt, dg, fit = loss_piece(
            x1[r, :] + (part[r, :] + other[r, :]), vec[2:3, :], table[...], table_t[...],
            [values[pl.ds(per * i + k, 1), :] for k in range(per)],
            [marks[pl.ds(per * i + k, 1), :] for k in range(per)], weight[...])
        dx2[r, :] = dx
        d_table[...] += dt
        d_gain[...] += dg
        loss[...] += fit
        return carry

    lax.fori_loop(0, part.shape[0] // TILE, step, 0)


def loss_stage(part, x1, vec, table, table_t, values, marks, weight, ident):
    tokens = part.shape[0]
    return pl.pallas_call(
        loss_kernel,
        in_specs=[VMEM] * 8,
        out_specs=[VMEM] * 4,
        out_shape=[
            jax.ShapeDtypeStruct((tokens, D), F32), jax.ShapeDtypeStruct((LANES, D), F32),
            jax.ShapeDtypeStruct((1, D), F32), jax.ShapeDtypeStruct((1, LANES), F32),
        ],
        scratch_shapes=exchange_scratch(part),
        compiler_params=params(collective_id=ident, has_side_effects=True),
        name="loss_stage",
    )(part, x1, vec, table, table_t, values, marks, weight)


def mid_backward_kernel(part, dx2, x1, b, pc, vec, table_t, balance, wo, o, d_table, d_gain3, dx1, do, rest,
                        other, send_sem, recv_sem):
    wait = exchange(part, other, send_sem, recv_sem)
    width = wo.shape[0]
    rest[:width, :] = jnp.zeros((width, D), F32)
    rest[width:, :] = d_table[...]
    rest[width + VECTOR + 2:width + VECTOR + 3, :] = d_gain3[...]
    per = o.shape[2] // TILE

    def step(i, carry):
        r = block(i, TILE)
        wait(i)
        dp = part[r, D:] + other[r, D:] + balance[...]
        p = pc[r, :]
        lanes = lax.broadcasted_iota(jnp.int32, p.shape, 1)
        routed = (lanes >= ROUTER) & (lanes < SHARED)
        weighted = jnp.sum(jnp.where(routed, p * dp, 0.0), axis=1, keepdims=True)
        dl = jnp.where(routed, p * (dp - weighted), jnp.where(lanes == SHARED, dp * p * (1.0 - p), 0.0))
        dl = dl.astype(BF16)
        low = b[r, :]
        rest[width:, :] += dot(dl, low, 0, 0)
        db = part[r, :D] + other[r, :D] + dot(dl, table_t[...])
        x = x1[r, :]
        scale = lax.rsqrt(jnp.mean(x * x, axis=1, keepdims=True) + norm_eps)
        unit = x * scale
        g2 = width + VECTOR + 1
        rest[g2:g2 + 1, :] += jnp.sum(db * unit, axis=0, keepdims=True)
        dn = db * vec[1:2, :]
        dx = dx2[r, :] + scale * (dn - unit * jnp.mean(dn * unit, axis=1, keepdims=True))
        dx1[r, :] = dx
        d_low = dx.astype(BF16)
        n, cols = i // per, block(lax.rem(i, per), TILE, TILE)
        do[n, :, cols] = dot(wo[...], d_low, 1, 1).astype(BF16)
        rest[:width, :] += dot(o[n, :, cols], d_low)
        return carry

    lax.fori_loop(0, part.shape[0] // TILE, step, 0)


def mid_backward(part, dx2, x1, b, pc, vec, table_t, balance, wo, o, d_table, d_gain3, ident):
    tokens = part.shape[0]
    return pl.pallas_call(
        mid_backward_kernel,
        in_specs=[VMEM] * 12,
        out_specs=[VMEM] * 3,
        out_shape=[
            jax.ShapeDtypeStruct((tokens, D), F32), jax.ShapeDtypeStruct(o.shape, BF16),
            jax.ShapeDtypeStruct((wo.shape[0] + LANES, D), F32),
        ],
        scratch_shapes=exchange_scratch(part),
        compiler_params=params(collective_id=ident, has_side_effects=True),
        name="mid_backward",
    )(part, dx2, x1, b, pc, vec, table_t, balance, wo, o, d_table, d_gain3)


SLOTS = 3
HOPS = 2
ACCS = 5


def encode(dest, v):
    width = v.shape[1]
    top = jnp.max(jnp.abs(v), axis=1, keepdims=True)
    power = jnp.ceil(jnp.log2(jnp.maximum(top, 1e-30) * (1.001 / 32767.0)))
    power = jnp.broadcast_to(power, (v.shape[0], LANES))
    inverse = jnp.exp2(-power)
    dest[:, width:] = power.astype(jnp.int32).astype(I16)
    for c in range(width // LANES):
        cols = slice(c * LANES, (c + 1) * LANES)
        dest[:, cols] = jnp.round(v[:, cols] * inverse).astype(jnp.int32).astype(I16)


def decode(source):
    width = source.shape[1] - LANES
    unit = jnp.exp2(source[:, width:].astype(jnp.int32).astype(F32))
    return jnp.concatenate(
        [source[:, c * LANES:(c + 1) * LANES].astype(jnp.int32).astype(F32) * unit for c in range(width // LANES)],
        axis=1)


def squared(v):
    v = jnp.sum(v * v, axis=0, keepdims=True)
    total = v[:, :LANES]
    for c in range(1, v.shape[1] // LANES):
        total = total + v[:, c * LANES:(c + 1) * LANES]
    return total


def backward_kernel(
    xs, dys, dgs, hs, qkvs, dos, lses, a_all, dx1_all, rest, x_ref, wt, vec, cos_ref, sin_ref, losses,
    out_up, out_down, out_small, sums,
    x_in, dy_in, dg_in, h_in, xt, dyt, temp, dw, acc, send1, recv1, send2, recv2, zs_up, zs_dn, up, dn,
    qkv, do_t, lse, a, dx1, dqkv, dk, dv, stack, part, other,
    sm, small_a1, small_b1, small_a2, small_b2, small_up, small_dn,
    load_sem, sem_s1, sem_r1, sem_s2, sem_r2, sem_su, sem_sd, sem_ru, sem_rd,
    attn_sem, dx1_sem, rest_sem, pair_send, pair_recv,
    small_send, small_sa, small_sb, small_r, small_su, small_sd, small_ru, small_rd,
    mine, everyone, sum_send, sum_recv,
):
    dp, mp, x, y, z = place()
    xp, yp = dp + 1 - 2 * x, dp + 2 - 4 * y
    count = out_up.shape[0]
    blocks = xs.shape[0]
    hidden = hs.shape[2]
    series, _, length = x_ref.shape
    width = do_t.shape[0]
    heads = width // HEAD
    per = length // TILE

    def loads(n):
        return [
            pltpu.make_async_copy(src.at[n], dst, load_sem.at[i])
            for i, (src, dst) in enumerate(((xs, x_in), (dys, dy_in), (dgs, dg_in), (hs, h_in)))]

    def attn_loads(n):
        pairs = ((qkvs.at[n], qkv), (dos.at[n], do_t), (lses.at[n], lse), (a_all.at[block(n, length)], a))
        return [pltpu.make_async_copy(src, dst, attn_sem.at[i]) for i, (src, dst) in enumerate(pairs)]

    def dx1_load(n):
        return pltpu.make_async_copy(dx1_all.at[block(n, length)], dx1, dx1_sem)

    rest_load = pltpu.make_async_copy(rest, stack.at[pl.ds(3 * width, width + LANES)], rest_sem)
    for copy in loads(0) + attn_loads(0) + [dx1_load(0), rest_load]:
        copy.start()

    meet_everyone(dp, mp)
    mine[...] = losses[...]
    stack[0:3 * width, :] = jnp.zeros((3 * width, D), F32)

    def shard(slot, i):
        return dw.at[slot, i]


    def weights(n, more):
        for copy in loads(n):
            copy.wait()
        xt[...] = jnp.transpose(x_in[...])
        dyt[...] = jnp.transpose(dy_in[...])

        def wide(j, carry):
            cols = block(j, TILE, TILE)
            v = dot(xt[...], dg_in[:, cols])
            temp[:, cols] = temp[:, cols] + v if more else v
            return carry

        def tall(j, carry):
            there = pl.ds(pl.multiple_of(2 * hidden + j * TILE, TILE), TILE)
            v = dot(dyt[...], h_in[:, block(j, TILE, TILE)])
            temp[:, there] = temp[:, there] + v if more else v
            return carry

        lax.fori_loop(0, 2 * hidden // TILE, wide, 0)
        lax.fori_loop(0, hidden // TILE, tall, 0)

        @pl.when(n + 1 < blocks)
        def _():
            for copy in loads(n + 1):
                copy.start()

    def begin(c):
        slot = lax.rem(c, SLOTS)
        weights(c, False)

        @pl.when(c == count - 1)
        def _():
            weights(c + 1, True)

        @pl.when(c >= SLOTS)
        def _():
            done(send1.at[slot], sem_s1.at[slot])

        def pack(i, carry):
            m, n = i // 2, lax.rem(i, 2)
            k = m // 2
            gone = m * 4 + jnp.where(k == 0, n * 2 + 1 - x, (1 - y) * 2 + n)
            kept = m * 4 + jnp.where(k == 0, n * 2 + x, y * 2 + n)
            encode(send1.at[slot, i], temp[block(gone, SHARD), :])
            dw[slot, i] = temp[block(kept, SHARD), :]
            return carry

        lax.fori_loop(0, 8, pack, 0)
        for k, peer in enumerate((xp, yp)):
            part = pl.ds(4 * k, 4)
            remote(send1.at[slot, part], recv1.at[c, part], sem_s1.at[slot], sem_r1.at[c], peer, mp).start()

    def fold(c):
        slot, hop = lax.rem(c, SLOTS), lax.rem(c, HOPS)
        done(recv1.at[c], sem_r1.at[c])

        @pl.when(c >= HOPS)
        def _():
            done(send2.at[hop], sem_s2.at[hop])

        def add(m, carry):
            o = jnp.where(m // 2 == 0, y, x)
            gone, kept = m * 2 + 1 - o, m * 2 + o
            encode(send2.at[hop, m], dw[slot, gone] + decode(recv1.at[c, gone]))
            acc[lax.rem(c, ACCS), m] = dw[slot, kept] + decode(recv1.at[c, kept])
            return carry

        lax.fori_loop(0, 4, add, 0)
        for k, peer in enumerate((yp, xp)):
            part = pl.ds(2 * k, 2)
            remote(send2.at[hop, part], recv2.at[c, part], sem_s2.at[hop], sem_r2.at[c], peer, mp).start()

    def climb(c, t, relay):
        slot = lax.rem(c, HOPS)
        v = acc[lax.rem(c, ACCS), t]
        if relay:
            done(up.at[c, t - 1], sem_ru.at[c, t - 1])
            v = v + decode(up.at[c, t - 1])

        @pl.when(c >= HOPS)
        def _():
            done(zs_up.at[slot, t - 1], sem_su.at[slot, t - 1])
        encode(zs_up.at[slot, t - 1], v)
        remote(zs_up.at[slot, t - 1], up.at[c, t - 1], sem_su.at[slot, t - 1], sem_ru.at[c, t - 1], dp + 4, mp).start()

    def drop(c, t, relay):
        slot = lax.rem(c, HOPS)
        v = acc[lax.rem(c, ACCS), t]
        if relay:
            done(dn.at[c, t], sem_rd.at[c, t])
            v = v + decode(dn.at[c, t])

        @pl.when(c >= HOPS)
        def _():
            done(zs_dn.at[slot, t], sem_sd.at[slot, t])
        encode(zs_dn.at[slot, t], v)
        remote(zs_dn.at[slot, t], dn.at[c, t], sem_sd.at[slot, t], sem_rd.at[c, t], dp - 4, mp).start()

    def line_a(c):
        done(recv2.at[c], sem_r2.at[c])
        there = lax.rem(c, ACCS)

        def add(m, carry):
            acc[there, m] = acc[there, m] + decode(recv2.at[c, m])
            return carry

        lax.fori_loop(0, 4, add, 0)

        @pl.when(z == 0)
        def _():
            for t in (3, 2, 1):
                climb(c, t, False)

        @pl.when(z == 3)
        def _():
            for t in (0, 1, 2):
                drop(c, t, False)

    def line_b(c):
        @pl.when(z == 1)
        def _():
            for t in (3, 2):
                climb(c, t, True)

        @pl.when(z == 2)
        def _():
            for t in (0, 1):
                drop(c, t, True)

    def line_c(c):
        @pl.when(z == 2)
        def _():
            climb(c, 3, True)

        @pl.when(z == 1)
        def _():
            drop(c, 0, True)

    def finish(c):
        there = lax.rem(c, ACCS)

        @pl.when(z > 0)
        def _():
            done(up.at[c, z - 1], sem_ru.at[c, z - 1])
            acc[there, z] = acc[there, z] + decode(up.at[c, z - 1])

        @pl.when(z < 3)
        def _():
            done(dn.at[c, z], sem_rd.at[c, z])
            acc[there, z] = acc[there, z] + decode(dn.at[c, z])
        v = acc[there, z]
        mine[0:1, :] = mine[0:1, :] + squared(v)
        for r in range(SHARD):
            for part in range(2):
                out_up[c, r, part:part + 1, :] = v[r:r + 1, part * hidden:(part + 1) * hidden]
        out_down[c] = v[:, 2 * hidden:]


    def pair(n):
        r = block(n, length)
        return remote(part, other.at[r], pair_send.at[n], pair_recv.at[n], dp, 1 - mp)

    def head(p):
        n, h = p // heads, lax.rem(p, heads)

        @pl.when(h == 0)
        def _():
            for copy in attn_loads(n):
                copy.wait()
        backward_head(h, width, qkv, do_t, lse, cos_ref[...], sin_ref[...], dqkv, dk, dv)

        @pl.when(h == heads - 1)
        def _():
            stack[0:3 * width, :] = stack[0:3 * width, :] + dot(dqkv[...], a[...])
            part[...] = dot(dqkv[...], wt[0:3 * width, :], 0, 0)
            pair(n).start()

            @pl.when(n + 1 < series)
            def _():
                for copy in attn_loads(n + 1):
                    copy.start()

    def embed(m):
        n, i = m // per, lax.rem(m, per)
        t = block(i, TILE, TILE)

        @pl.when(m == 0)
        def _():
            rest_load.wait()

        @pl.when(i == 0)
        def _():
            pair(n).wait()
            dx1_load(n).wait()
        da = part[t, :] + other[block(m, TILE), :]
        sums = embed_backward_piece(x_ref[n, :, t], da, dx1[t, :], vec)
        for row, value in zip((0, 3, 4), sums):
            there = slice(4 * width + VECTOR + row, 4 * width + VECTOR + row + 1)
            stack[there, :] = stack[there, :] + value

        @pl.when((i == per - 1) & (n + 1 < series))
        def _():
            dx1_load(n + 1).start()


    half = 512
    total_width = sm.shape[-1]
    ca, cb = pl.ds(0, half), pl.ds(half, total_width - half)

    def small_begin():
        sm[...] = jnp.transpose(stack[...]).reshape(sm.shape)
        remote(sm.at[:, :, 1 - x, :, ca], small_a1, small_sa, small_r.at[0], xp, mp).start()
        remote(sm.at[:, 1 - y, :, :, cb], small_b1, small_sb, small_r.at[1], yp, mp).start()

    def small_fold():
        done(small_a1, small_r.at[0])
        done(small_b1, small_r.at[1])
        for m in range(4):
            for n in range(2):
                sm[m, n, x, :, ca] = sm[m, n, x, :, ca] + small_a1[m, n]
                sm[m, y, n, :, cb] = sm[m, y, n, :, cb] + small_b1[m, n]
        remote(sm.at[:, 1 - y, x, :, ca], small_a2, small_send.at[0], small_r.at[2], yp, mp).start()
        remote(sm.at[:, y, 1 - x, :, cb], small_b2, small_send.at[1], small_r.at[3], xp, mp).start()

    def small_climb(t, relay):
        if relay:
            done(small_up.at[t - 1], small_ru.at[t - 1])
            sm[t, y, x] = sm[t, y, x] + small_up[t - 1]
        remote(sm.at[t, y, x], small_up.at[t - 1], small_su.at[t - 1], small_ru.at[t - 1], dp + 4, mp).start()

    def small_drop(t, relay):
        if relay:
            done(small_dn.at[t], small_rd.at[t])
            sm[t, y, x] = sm[t, y, x] + small_dn[t]
        remote(sm.at[t, y, x], small_dn.at[t], small_sd.at[t], small_rd.at[t], dp - 4, mp).start()

    def small_a():
        done(small_a2, small_r.at[2])
        done(small_b2, small_r.at[3])
        for m in range(4):
            sm[m, y, x, :, ca] = sm[m, y, x, :, ca] + small_a2[m]
            sm[m, y, x, :, cb] = sm[m, y, x, :, cb] + small_b2[m]
        out_small[...] = sm[z, y, x]

        @pl.when(z == 0)
        def _():
            for t in (3, 2, 1):
                small_climb(t, False)

        @pl.when(z == 3)
        def _():
            for t in (0, 1, 2):
                small_drop(t, False)

    def small_b():
        @pl.when(z == 1)
        def _():
            for t in (3, 2):
                small_climb(t, True)

        @pl.when(z == 2)
        def _():
            for t in (0, 1):
                small_drop(t, True)

    def small_c():
        @pl.when(z == 2)
        def _():
            small_climb(3, True)

        @pl.when(z == 1)
        def _():
            small_drop(0, True)

    def small_finish():
        @pl.when(z > 0)
        def _():
            done(small_up.at[z - 1], small_ru.at[z - 1])
            out_small[...] = out_small[...] + small_up[z - 1]

        @pl.when(z < 3)
        def _():
            done(small_dn.at[z], small_rd.at[z])
            out_small[...] = out_small[...] + small_dn[z]
        mine[0:1, :] = mine[0:1, :] + squared(out_small[:, :4 * width]) + 0.5 * squared(out_small[:, 4 * width:])


    def at(i, first, number, run):
        @pl.when((i >= first) & (i < first + number))
        def _():
            run(i - first)

    small_first = count + 1

    def step(i, carry):
        at(i, 0, count, begin)

        def run(p, carry):
            head(p)
            return carry

        @pl.when(i <= count)
        def _():
            lax.fori_loop(i, jnp.where(i == count, series * heads, i + 1), run, 0)

        def piece(m, carry):
            embed(m)
            return carry

        at(i, heads + 1, 1, lambda _: lax.fori_loop(0, per, piece, 0))
        at(i, count + 1, 1, lambda _: lax.fori_loop(per, series * per, piece, 0))
        at(i, small_first, 1, lambda _: small_begin())
        at(i, 7, count, finish)
        at(i, 2, count, fold)
        at(i, small_first + 1, 1, lambda _: small_fold())
        at(i, 4, count, line_a)
        at(i, small_first + 2, 1, lambda _: small_a())
        at(i, 5, count, line_b)
        at(i, small_first + 3, 1, lambda _: small_b())
        at(i, 6, count, line_c)
        at(i, small_first + 4, 1, lambda _: small_c())
        at(i, small_first + 5, 1, lambda _: small_finish())
        return carry

    lax.fori_loop(0, count + 7, step, 0)

    me = dp * 2 + mp

    def tell(k, carry):
        peer = lax.rem(me + k, 32)
        remote(mine, everyone.at[me], sum_send, sum_recv, peer // 2, lax.rem(peer, 2)).start()
        return carry

    lax.fori_loop(1, 32, tell, 0)
    everyone[me] = mine[...]

    for slot in range(SLOTS):
        done(send1.at[slot], sem_s1.at[slot])
    for slot in range(HOPS):
        done(send2.at[slot], sem_s2.at[slot])
        for t in (1, 2, 3):
            @pl.when(z < t)
            def _():
                done(zs_up.at[slot, t - 1], sem_su.at[slot, t - 1])
        for t in (0, 1, 2):
            @pl.when(z > t)
            def _():
                done(zs_dn.at[slot, t], sem_sd.at[slot, t])
    done(small_a1, small_sa)
    done(small_b1, small_sb)
    done(small_a2, small_send.at[0])
    done(small_b2, small_send.at[1])
    for t in (1, 2, 3):
        @pl.when(z < t)
        def _():
            done(small_up.at[t - 1], small_su.at[t - 1])
    for t in (0, 1, 2):
        @pl.when(z > t)
        def _():
            done(small_dn.at[t], small_sd.at[t])
    done(everyone.at[pl.ds(0, 31)], sum_recv)
    done(everyone.at[pl.ds(0, 31)], sum_send)
    sums[...] = jnp.sum(everyone[...], axis=0)


def backward_near(xs, dys, dgs, hs, qkv, do, lse, a, dx1, rest, x, wt, vec, cos, sin, losses, ident):
    capacity, hidden = hs.shape[1], hs.shape[2]
    series, rows, length = qkv.shape
    heads_width = rows // 3
    count = ROUTED_EXPERTS + 1
    width = 3 * hidden
    coded = width + LANES
    small = 4 * heads_width + LANES
    tokens = series * length
    v = pltpu.VMEM
    return pl.pallas_call(
        backward_kernel,
        in_specs=[ANY] * 10 + [VMEM] * 6,
        out_specs=[VMEM] * 4,
        out_shape=[
            jax.ShapeDtypeStruct((count, SHARD, 2, hidden), F32),
            jax.ShapeDtypeStruct((count, SHARD, hidden), F32), jax.ShapeDtypeStruct((SHARD, small), F32),
            jax.ShapeDtypeStruct((8, LANES), F32)],
        scratch_shapes=[
            v((capacity, D), BF16), v((capacity, D), BF16), v((capacity, 2 * hidden), BF16), v((capacity, hidden), BF16),
            v((D, capacity), BF16), v((D, capacity), BF16),
            v((D, width), F32), v((SLOTS, 8, SHARD, width), F32), v((ACCS, 4, SHARD, width), F32),
            v((SLOTS, 8, SHARD, coded), I16), v((count, 8, SHARD, coded), I16),
            v((HOPS, 4, SHARD, coded), I16), v((count, 4, SHARD, coded), I16),
            v((HOPS, 3, SHARD, coded), I16), v((HOPS, 3, SHARD, coded), I16),
            v((count, 3, SHARD, coded), I16), v((count, 3, SHARD, coded), I16),
            v((rows, length), BF16), v((heads_width, length), BF16), v((8, length), F32), v((length, D), BF16),
            v((length, D), F32), v((rows, length), BF16), v((length, HEAD), F32), v((length, HEAD), F32),
            v((small, D), F32), v((length, D), F32), v((tokens, D), F32),
            v((4, 2, 2, SHARD, small), F32),
            v((4, 2, SHARD, 512), F32), v((4, 2, SHARD, small - 512), F32),
            v((4, SHARD, 512), F32), v((4, SHARD, small - 512), F32),
            v((3, SHARD, small), F32), v((3, SHARD, small), F32),
            DMA((4,)), DMA((SLOTS,)), DMA((count,)), DMA((HOPS,)), DMA((count,)),
            DMA((HOPS, 3)), DMA((HOPS, 3)), DMA((count, 3)), DMA((count, 3)),
            DMA((4,)), DMA, DMA, DMA((series,)), DMA((series,)),
            DMA((2,)), DMA, DMA, DMA((4,)), DMA((3,)), DMA((3,)), DMA((3,)), DMA((3,)),
            v((8, LANES), F32), v((32, 8, LANES), F32), DMA, DMA,
        ],
        compiler_params=pltpu.CompilerParams(
            vmem_limit_bytes=67_000_000, collective_id=ident, has_side_effects=True),
        name="backward_near",
    )(xs, dys, dgs, hs, qkv, do, lse, a, dx1, rest, x, wt, vec, cos, sin, losses)


def rope_rows(length):
    halfway = HEAD // 2
    frequency = rope_base ** (-2.0 * jnp.arange(halfway, dtype=F32) / HEAD)
    angles = frequency[:, None] * jnp.arange(length, dtype=F32)[None, :]
    return jnp.cos(angles), jnp.sin(angles)


def hankel_rows(track):
    length = track.shape[1]
    padded = jnp.pad(track, ((0, 0), (63, 2 * LANES)))
    first = padded[:, :length].reshape(-1, LANES)[:, ::-1]
    second = padded[:, LANES:LANES + length].reshape(-1, LANES)[:, ::-1]
    return jnp.concatenate([first, second], axis=1)


def table_columns(read, vec):
    parts, end = [], read.shape[1]
    for horizon in horizons[::-1]:
        parts.append(read[:, end - horizon:end][:, ::-1])
        end -= horizon
    gap = jnp.zeros((read.shape[0], ROUTER - sum(horizons)), read.dtype)
    tail = jnp.zeros((read.shape[0], LANES - VECTOR - vec.shape[1]), read.dtype)
    return jnp.concatenate(parts + [gap, read[:, :ROUTED_EXPERTS + 1], vec, tail], axis=1)


def table_columns_back(table):
    parts, begin = [], 0
    for horizon in horizons[::-1]:
        parts.append(table[:, begin:begin + horizon][:, ::-1])
        begin += horizon
    return jnp.concatenate([table[:, ROUTER:VECTOR]] + parts[::-1], axis=1)


def dispatch(route_rows, capacity):
    tokens = route_rows.shape[0]
    experts = jnp.arange(ROUTED_EXPERTS, dtype=jnp.int32)
    member = jnp.any(route_rows[:, :, None] == experts[None, None, :], axis=1)
    count = jnp.cumsum(member.astype(jnp.int32), axis=0)
    total = count[-1]
    place = jnp.where(member, count - 1, -1)
    high = (place[:, :, None] // LANES == jnp.arange(capacity // LANES)[None, None, :]) & member[:, :, None]
    low = (place[:, :, None] % LANES == jnp.arange(LANES)[None, None, :]).astype(BF16)
    token = jnp.arange(tokens, dtype=jnp.int32)
    left = jnp.concatenate(
        [jnp.where(high, part[:, None, None], 0).astype(BF16) for part in (token // 16, token % 16)], axis=2)
    found = jnp.einsum("teh,tel->ehl", left, low, preferred_element_type=F32)
    half = capacity // LANES
    source = (found[:, :half] * 16.0 + found[:, half:]).reshape(ROUTED_EXPERTS, capacity).astype(jnp.int32)
    source = jnp.where(jnp.arange(capacity, dtype=jnp.int32)[None, :] < total[:, None], source, tokens)
    source = jnp.concatenate([source.reshape(-1), jnp.full((TILE,), tokens, jnp.int32)]) * 8
    per = capacity // TILE
    routed = ROUTED_EXPERTS * per
    tile = jnp.arange(routed + tokens // TILE, dtype=jnp.int32)
    need = (total + TILE - 1) // TILE
    begin = jnp.sum(jnp.where(experts[None, :] < experts[:, None], total[None, :], 0), axis=1)
    mine = jnp.minimum(tile // per, ROUTED_EXPERTS - 1)[:, None] == experts[None, :]
    used = (tile < routed) & (tile % per < jnp.sum(jnp.where(mine, need[None, :], 0), axis=1))
    order = jnp.where(used, jnp.sum(jnp.where(mine, begin[None, :], 0), axis=1) + tile % per * TILE, -1)
    next_tile = jnp.concatenate([tile, jnp.full((1,), -1, jnp.int32)])
    later = used[None, :] & (tile[None, :] > next_tile[:, None])
    after = jnp.min(jnp.where(later, tile[None, :], routed), axis=1) * TILE
    slot = (begin[None, :] + count - 1) * 8
    slots = jnp.sum(jnp.where(route_rows[:, :, None] == experts[None, None, :], slot[:, None, :], 0), axis=2)
    return total, (need, order, after, source, slots.T.reshape(-1))


def adam_update(master, moment, square, gradient, factor, bias_one, bias_two, step_rate):
    clipped = gradient * factor
    new_moment = beta_one * moment + (1.0 - beta_one) * clipped
    new_square = beta_two * square + (1.0 - beta_two) * clipped * clipped
    updated = master - step_rate * (
        new_moment / bias_one / (jnp.sqrt(new_square / bias_two) + adam_eps) + decay_rate * master
    )
    return (updated, new_moment, new_square)


def on_device(
    series, observed, routes, step_count,
    joint_proj, joint_moment, joint_square,
    mixer_proj, mixer_moment, mixer_square,
    upward_proj, upward_moment, upward_square,
    downward_proj, downward_moment, downward_square,
    readout, readout_moment, readout_square,
    vectors, vectors_moment, vectors_square,
):
    dp_count = lax.axis_size("dp")
    mp_count = lax.axis_size("mp")
    shard = joint_proj.shape[1]
    width = joint_proj.shape[2]
    hidden = upward_proj.shape[3]
    experts = upward_proj.shape[0]
    series_count, length = series.shape
    tokens = series_count * length
    capacity = tokens // 2

    small_own = jnp.concatenate(
        [joint_proj[k].astype(BF16) for k in range(3)]
        + [mixer_proj.T.astype(BF16), table_columns(readout.astype(BF16), vectors.T.astype(BF16))], axis=1)
    big_own = jnp.concatenate(
        [upward_proj.astype(BF16).reshape(experts, shard, 2 * hidden), downward_proj.transpose(0, 2, 1).astype(BF16)],
        axis=2)
    marks = observed.astype(F32)
    expert_here, plan = dispatch(routes.reshape(tokens, 2), capacity)
    point = jnp.arange(length, dtype=F32)
    reach = jnp.minimum(point[None], jnp.array(horizons, F32)[:, None])
    head_here = jnp.sum(jnp.sum(marks, axis=0)[None] * reach, axis=1)
    tally = jnp.pad(jnp.concatenate([expert_here.astype(F32), head_here]), (0, LANES - 12))
    tally = jnp.broadcast_to(tally[None], (8, LANES))
    cos, sin = rope_rows(length)
    x = (series * marks).reshape(series_count, 1, length)

    big, wt, wo, table_t, vec, table, a, qkv, lse, o, x1, b, pc, pr_total, tallies = forward_near(
        small_own, big_own, tally, x, cos, sin, width, 0)
    tally = jnp.sum(tallies[:, 0], axis=0) / mp_count
    expert_count, head_count = tally[:ROUTED_EXPERTS], tally[ROUTED_EXPERTS:ROUTED_EXPERTS + 4]
    total_tokens = tokens * dp_count

    xs, ys, mixed = expert_forward(plan, b, pc, big)
    head_weight = jnp.concatenate(
        [jnp.zeros((horizon,), F32) + 0.25 / head_count[3 - index] for index, horizon in enumerate(horizons[::-1])])
    head_weight = jnp.pad(head_weight, (0, LANES - head_weight.shape[0]))[None]
    dx2, d_table, d_gain3, fit = loss_stage(
        mixed, x1, vec, table, table_t, hankel_rows(series), hankel_rows(marks), head_weight, 1)
    dys, dgs, hs, back = expert_backward(plan, pc, dx2, big, xs, ys)
    balance = aux_factor * ROUTED_EXPERTS * expert_count / total_tokens / total_tokens
    balance = jnp.pad(balance, (ROUTER, LANES - SHARED))[None]
    dx1, do, rest = mid_backward(back, dx2, x1, b, pc, vec, table_t, balance, wo, o, d_table, d_gain3, 2)
    losses = jnp.pad((fit + pr_total * balance) / mp_count, ((1, 6), (0, 0)))
    upward_red, down_red, small_red, sums = backward_near(
        xs, dys, dgs, hs, qkv, do, lse, a, dx1, rest, x, wt, vec, cos, sin, losses, 3)

    attn_red, table_red = small_red[:, :4 * width], small_red[:, 4 * width:]
    grad_norm, loss_total = jnp.sqrt(jnp.sum(sums[0])), jnp.sum(sums[1])

    factor = clip_limit / (grad_norm + 1e-06)
    steps_taken = step_count[0].astype(F32)
    bias_one = 1.0 - beta_one**steps_taken
    bias_two = 1.0 - beta_two**steps_taken

    def update(master, moment, square, gradient, rate=matrix_rate):
        return adam_update(master, moment, square, gradient, factor, bias_one, bias_two, rate)

    joint_red = jnp.stack([attn_red[:, k * width:(k + 1) * width] for k in range(3)], axis=0)
    mixer_red = attn_red[:, 3 * width:].T
    downward_red = down_red.transpose(0, 2, 1)
    return (
        loss_total,
        grad_norm,
        *update(joint_proj, joint_moment, joint_square, joint_red),
        *update(mixer_proj, mixer_moment, mixer_square, mixer_red),
        *update(upward_proj, upward_moment, upward_square, upward_red),
        *update(downward_proj, downward_moment, downward_square, downward_red),
        *update(readout, readout_moment, readout_square, table_columns_back(table_red)),
        *update(vectors, vectors_moment, vectors_square, table_red[:, VECTOR:VECTOR + 5].T, vector_rate),
    )


def rms_scale(tensor, gain_row):
    return (
        tensor * lax.rsqrt(jnp.mean(tensor * tensor, axis=-1, keepdims=True) + norm_eps) * gain_row
    )


def rope_tables(length, columns):
    halfway = columns // 2
    frequency = rope_base ** (-2.0 * jnp.arange(halfway, dtype=jnp.float32) / columns)
    angles = jnp.arange(length, dtype=jnp.float32)[:, None] * frequency[None, :]
    return (jnp.cos(angles), jnp.sin(angles))


def rotate(tensor, cosine_table, sine_table):
    halfway = tensor.shape[-1] // 2
    front_part = tensor[..., :halfway]
    back_part = tensor[..., halfway:]
    return jnp.concatenate(
        [
            front_part * cosine_table - back_part * sine_table,
            back_part * cosine_table + front_part * sine_table,
        ],
        axis=-1,
    )


def swiglu(tensor):
    halfway = tensor.shape[-1] // 2
    return jax.nn.silu(tensor[..., :halfway]) * tensor[..., halfway:]


def targets_of(series, observed):
    row_count, length = series.shape
    longest = max(horizons)
    padded_values = jnp.concatenate([series, jnp.zeros((row_count, longest), jnp.float32)], axis=1)
    padded_marks = jnp.concatenate(
        [observed.astype(jnp.float32), jnp.zeros((row_count, longest), jnp.float32)], axis=1
    )
    value_window = jnp.stack(
        [padded_values[:, 1 + offset : 1 + offset + length] for offset in range(longest)], axis=-1
    )
    mark_window = jnp.stack(
        [padded_marks[:, 1 + offset : 1 + offset + length] for offset in range(longest)], axis=-1
    )
    observed_future_series = jnp.concatenate(
        [value_window[..., :horizon] for horizon in horizons], axis=-1
    )
    valid_mask = jnp.concatenate([mark_window[..., :horizon] for horizon in horizons], axis=-1)
    return (
        observed_future_series.reshape(row_count * length, -1),
        valid_mask.reshape(row_count * length, -1),
    )


def head_counts(valid_mask):
    beginnings = [sum(horizons[:index]) for index in range(len(horizons))]
    return jnp.stack(
        [
            jnp.sum(valid_mask[:, beginning : beginning + horizon])
            for beginning, horizon in zip(beginnings, horizons)
        ]
    )


def head_weights(head_count):
    return jnp.concatenate(
        [
            jnp.zeros((horizon,), jnp.float32) + 0.25 / head_count[index]
            for index, horizon in enumerate(horizons)
        ]
    )


def dispatch_plan(route_rows, experts, capacity):
    flat_routes = route_rows.reshape(-1)
    entries = flat_routes.shape[0]
    onehot = (flat_routes[:, None] == jnp.arange(experts, dtype=jnp.int32)[None, :]).astype(
        jnp.int32
    )
    position = jnp.sum(jnp.cumsum(onehot, axis=0) * onehot, axis=1) - 1
    slot_index = flat_routes * capacity + position
    source = (
        jnp.full((experts * capacity,), entries, jnp.int32)
        .at[slot_index]
        .set(jnp.arange(entries, dtype=jnp.int32))
    )
    return (slot_index, source)


def split_heads(matrix, series_count, length):
    return matrix.reshape(series_count, length, matrix.shape[1] // HEAD, HEAD).transpose(0, 2, 1, 3)


def merge_heads(tensor):
    series_count, heads_here, length, head_size = tensor.shape
    return tensor.transpose(0, 2, 1, 3).reshape(series_count * length, heads_here * head_size)


def block_scores(query_block, key_heads, offset, length):
    block_rows = query_block.shape[1]
    scores = jnp.einsum(
        "hqe,hke->hqk", query_block, key_heads, preferred_element_type=jnp.float32
    ) * HEAD ** (-0.5)
    allowed = (offset + jnp.arange(block_rows))[:, None] >= jnp.arange(length)[None, :]
    return jnp.where(allowed[None], scores, -1e30)


def attend_forward(pieces):
    query_heads, key_heads, value_heads = pieces
    length = query_heads.shape[1]
    block_rows = min(length, 512)
    outputs = []
    totals = []
    for offset in range(0, length, block_rows):
        scores = block_scores(
            query_heads[:, offset : offset + block_rows], key_heads, offset, length
        )
        row_peak = jnp.max(scores, axis=-1, keepdims=True)
        exponent = jnp.exp(scores - row_peak)
        row_mass = jnp.sum(exponent, axis=-1, keepdims=True)
        outputs.append(
            jnp.einsum(
                "hqk,hke->hqe",
                (exponent / row_mass).astype(jnp.bfloat16),
                value_heads,
                preferred_element_type=jnp.float32,
            )
        )
        totals.append(row_peak + jnp.log(row_mass))
    return (jnp.concatenate(outputs, axis=1), jnp.concatenate(totals, axis=1))


def attend_backward(pieces):
    query_heads, key_heads, value_heads, grads_out, totals = pieces
    length = query_heads.shape[1]
    block_rows = min(length, 512)
    key_grad = jnp.zeros(key_heads.shape, jnp.float32)
    value_grad = jnp.zeros(value_heads.shape, jnp.float32)
    query_grads = []
    for offset in range(0, length, block_rows):
        query_block = query_heads[:, offset : offset + block_rows]
        grad_block = grads_out[:, offset : offset + block_rows]
        weights = jnp.exp(
            block_scores(query_block, key_heads, offset, length)
            - totals[:, offset : offset + block_rows]
        )
        grad_weights = jnp.einsum(
            "hqe,hke->hqk", grad_block, value_heads, preferred_element_type=jnp.float32
        )
        score_grad = (
            weights
            * (grad_weights - jnp.sum(weights * grad_weights, axis=-1, keepdims=True))
            * HEAD ** (-0.5)
        ).astype(jnp.bfloat16)
        query_grads.append(
            jnp.einsum("hqk,hke->hqe", score_grad, key_heads, preferred_element_type=jnp.float32)
        )
        key_grad = key_grad + jnp.einsum(
            "hqk,hqe->hke", score_grad, query_block, preferred_element_type=jnp.float32
        )
        value_grad = value_grad + jnp.einsum(
            "hqk,hqe->hke",
            weights.astype(jnp.bfloat16),
            grad_block,
            preferred_element_type=jnp.float32,
        )
    return (jnp.concatenate(query_grads, axis=1), key_grad, value_grad)


def branch_total(partial_sum):
    return lax.psum(partial_sum, "mp")


def input_total(partial_sum):
    return lax.psum(partial_sum, "mp")


def on_device_wide(
    series,
    observed,
    routes,
    step_count,
    joint_proj,
    joint_moment,
    joint_square,
    mixer_proj,
    mixer_moment,
    mixer_square,
    upward_proj,
    upward_moment,
    upward_square,
    downward_proj,
    downward_moment,
    downward_square,
    readout,
    readout_moment,
    readout_square,
    vectors,
    vectors_moment,
    vectors_square,
):
    dp_count = lax.axis_size("dp")
    hidden_local = upward_proj.shape[3]
    joint_full, mixer_full, upward_full, downward_full, readout_complete, vector_full = (
        lax.all_gather(joint_proj.astype(jnp.bfloat16), "dp", axis=1, tiled=True),
        lax.all_gather(mixer_proj.astype(jnp.bfloat16), "dp", axis=1, tiled=True),
        lax.all_gather(upward_proj.astype(jnp.bfloat16), "dp", axis=1, tiled=True),
        lax.all_gather(downward_proj.astype(jnp.bfloat16), "dp", axis=2, tiled=True),
        lax.all_gather(readout.astype(jnp.bfloat16), "dp", axis=0, tiled=True),
        lax.all_gather(vectors.astype(jnp.bfloat16), "dp", axis=1, tiled=True),
    )
    up_local = upward_full.reshape(upward_full.shape[0], D, -1)
    shared_up_weight = up_local[-1]
    shared_down_weight = downward_full[-1]
    expert_up = up_local[:ROUTED_EXPERTS]
    expert_down = downward_full[:ROUTED_EXPERTS]
    gain_rows = vector_full.astype(jnp.float32)
    series_count, length = series.shape
    entries = series_count * length
    route_rows = routes.reshape(entries, 2)
    onehot = route_rows[:, :, None] == jnp.arange(ROUTED_EXPERTS, dtype=jnp.int32)[None, None, :]
    observed_future_series, valid_mask = targets_of(series, observed)
    expert_count, head_count = lax.psum(
        (jnp.sum(onehot.astype(jnp.float32), axis=(0, 1)), head_counts(valid_mask)), "dp"
    )
    total_tokens = entries * dp_count
    inputs = (series * observed.astype(jnp.float32)).reshape(entries, 1)

    def embed(gate_vector, up_vector):
        return jax.nn.silu(inputs * gate_vector) * (inputs * up_vector)

    embedded, embed_back = jax.vjp(embed, gain_rows[3], gain_rows[4])
    normed_one, norm_one_back = jax.vjp(rms_scale, embedded, gain_rows[0])
    first_input = normed_one.astype(jnp.bfloat16)
    projected = jnp.einsum(
        "td,cde->cte", first_input, joint_full, preferred_element_type=jnp.float32
    )
    cosine_table, sine_table = rope_tables(length, HEAD)
    query_heads = rotate(
        split_heads(projected[0], series_count, length), cosine_table, sine_table
    ).astype(jnp.bfloat16)
    key_heads = rotate(
        split_heads(projected[1], series_count, length), cosine_table, sine_table
    ).astype(jnp.bfloat16)
    value_heads = split_heads(projected[2], series_count, length).astype(jnp.bfloat16)
    attended, totals = lax.map(attend_forward, (query_heads, key_heads, value_heads))
    attended_low = merge_heads(attended).astype(jnp.bfloat16)
    after_attn = embedded + branch_total(
        jnp.dot(attended_low, mixer_full, preferred_element_type=jnp.float32)
    )
    normed_two, norm_two_back = jax.vjp(rms_scale, after_attn, gain_rows[1])
    second_input = normed_two.astype(jnp.bfloat16)
    logits = jnp.dot(
        second_input, readout_complete[:, : ROUTED_EXPERTS + 1], preferred_element_type=jnp.float32
    )

    def gating(logit_rows):
        probabilities = jax.nn.softmax(logit_rows[:, :ROUTED_EXPERTS], axis=-1)
        chosen = jnp.sum(jnp.where(onehot, probabilities[:, None, :], 0.0), axis=-1)
        balance = (
            aux_factor
            * ROUTED_EXPERTS
            * jnp.sum(expert_count / total_tokens * jnp.sum(probabilities, axis=0) / total_tokens)
        )
        return (chosen, jax.nn.sigmoid(logit_rows[:, ROUTED_EXPERTS]), balance)

    (gate_values, shared_gate, balance), gating_back = jax.vjp(gating, logits)
    capacity = entries // 2
    slot_index, source = dispatch_plan(route_rows, ROUTED_EXPERTS, capacity)
    token_of = source // 2
    padded_input = jnp.concatenate([second_input, jnp.zeros((1, D), jnp.bfloat16)], axis=0)
    gathered = padded_input[token_of].reshape(ROUTED_EXPERTS, capacity, D)
    gate_up = jnp.einsum("ecd,edf->ecf", gathered, expert_up, preferred_element_type=jnp.float32)
    hidden_f, swiglu_back = jax.vjp(swiglu, gate_up)
    hidden = hidden_f.astype(jnp.bfloat16)
    expert_out = jnp.einsum(
        "ecf,efd->ecd", hidden, expert_down, preferred_element_type=jnp.float32
    ).reshape(ROUTED_EXPERTS * capacity, D)
    picked = expert_out[slot_index].reshape(entries, 2, D)
    shared_up = jnp.dot(second_input, shared_up_weight, preferred_element_type=jnp.float32)
    shared_f, shared_back = jax.vjp(swiglu, shared_up)
    shared_hidden = shared_f.astype(jnp.bfloat16)
    shared_out = jnp.dot(shared_hidden, shared_down_weight, preferred_element_type=jnp.float32)
    mixed_part = (
        jnp.sum(gate_values[:, :, None] * picked, axis=1) + shared_gate[:, None] * shared_out
    )
    after_mixer = after_attn + branch_total(mixed_part)
    normalized_output, norm_out_back = jax.vjp(rms_scale, after_mixer, gain_rows[2])
    output_input = normalized_output.astype(jnp.bfloat16)
    model_estimates = jnp.dot(
        output_input, readout_complete[:, ROUTED_EXPERTS + 1 :], preferred_element_type=jnp.float32
    )
    prediction_misses = model_estimates - observed_future_series
    absolute_miss = jnp.abs(prediction_misses)
    horizon_importance_factors = head_weights(head_count)[None, :] * valid_mask
    robust_penalty_entries = jnp.where(
        absolute_miss <= quadratic_cutoff,
        0.5 * prediction_misses * prediction_misses,
        quadratic_cutoff * (absolute_miss - 0.5 * quadratic_cutoff),
    )
    local_loss = jnp.sum(robust_penalty_entries * horizon_importance_factors) + balance
    mp_count = lax.axis_size("mp")
    loss_total = lax.psum(local_loss, "dp")
    predicted_gradient = (
        jnp.clip(prediction_misses, -quadratic_cutoff, quadratic_cutoff)
        * horizon_importance_factors
    ).astype(jnp.bfloat16)
    head_grad = jnp.einsum(
        "ka,ky->ay", output_input, predicted_gradient, preferred_element_type=jnp.float32
    )
    out_input_grad = jnp.einsum(
        "aw,iw->ai",
        predicted_gradient,
        readout_complete[:, ROUTED_EXPERTS + 1 :],
        preferred_element_type=jnp.float32,
    )
    mixer_grad_in, gain_three_grad = norm_out_back(out_input_grad)
    picked_dots = jnp.sum(picked * mixer_grad_in[:, None, :], axis=-1)
    shared_dots = jnp.sum(shared_out * mixer_grad_in, axis=-1)
    gate_grads, shared_gate_grad = lax.psum((picked_dots, shared_dots), "mp")
    (logit_grad,) = gating_back((gate_grads, shared_gate_grad, jnp.ones((), jnp.float32)))
    logit_low = logit_grad.astype(jnp.bfloat16)
    router_grad = jnp.einsum(
        "ka,ky->ay", second_input, logit_low, preferred_element_type=jnp.float32
    )
    router_input_grad = jnp.einsum(
        "aw,iw->ai",
        logit_low,
        readout_complete[:, : ROUTED_EXPERTS + 1],
        preferred_element_type=jnp.float32,
    )
    gates_padded = jnp.concatenate([gate_values.reshape(-1), jnp.zeros((1,), jnp.float32)], axis=0)
    residual_padded = jnp.concatenate([mixer_grad_in, jnp.zeros((1, D), jnp.float32)], axis=0)
    expert_out_grad = (
        (gates_padded[source][:, None] * residual_padded[token_of])
        .astype(jnp.bfloat16)
        .reshape(ROUTED_EXPERTS, capacity, D)
    )
    hidden_grad = jnp.einsum(
        "ecd,efd->ecf", expert_out_grad, expert_down, preferred_element_type=jnp.float32
    )
    down_grad_experts = jnp.einsum(
        "ecf,ecd->efd", hidden, expert_out_grad, preferred_element_type=jnp.float32
    )
    gate_up_grad = swiglu_back(hidden_grad)[0].astype(jnp.bfloat16)
    up_grad_experts = jnp.einsum(
        "ecd,ecf->edf", gathered, gate_up_grad, preferred_element_type=jnp.float32
    )
    rows_grad = jnp.einsum(
        "ecf,edf->ecd", gate_up_grad, expert_up, preferred_element_type=jnp.float32
    ).reshape(ROUTED_EXPERTS * capacity, D)
    routed_grad = jnp.sum(rows_grad[slot_index].reshape(entries, 2, D), axis=1)
    shared_out_grad = (shared_gate[:, None] * mixer_grad_in).astype(jnp.bfloat16)
    shared_hidden_grad = jnp.einsum(
        "td,fd->tf", shared_out_grad, shared_down_weight, preferred_element_type=jnp.float32
    )
    down_grad_shared = jnp.einsum(
        "tf,td->fd", shared_hidden, shared_out_grad, preferred_element_type=jnp.float32
    )
    shared_up_grad = shared_back(shared_hidden_grad)[0].astype(jnp.bfloat16)
    up_grad_shared = jnp.einsum(
        "td,tf->df", second_input, shared_up_grad, preferred_element_type=jnp.float32
    )
    input_part = routed_grad + jnp.einsum(
        "tf,df->td", shared_up_grad, shared_up_weight, preferred_element_type=jnp.float32
    )
    second_input_grad = input_total(input_part) + router_input_grad
    upward_grad = jnp.concatenate([up_grad_experts, up_grad_shared[None]], axis=0).reshape(
        ROUTED_EXPERTS + 1, D, 2, hidden_local
    )
    downward_grad = jnp.concatenate([down_grad_experts, down_grad_shared[None]], axis=0)
    attn_grad_in, gain_two_grad = norm_two_back(second_input_grad)
    attn_total_grad = mixer_grad_in + attn_grad_in
    attn_low = attn_total_grad.astype(jnp.bfloat16)
    mixer_grad = jnp.einsum("tf,td->fd", attended_low, attn_low, preferred_element_type=jnp.float32)
    attended_grad = jnp.einsum(
        "td,fd->tf", attn_low, mixer_full, preferred_element_type=jnp.float32
    ).astype(jnp.bfloat16)
    query_grad, key_grad, value_grad = lax.map(
        attend_backward,
        (
            query_heads,
            key_heads,
            value_heads,
            split_heads(attended_grad, series_count, length),
            totals,
        ),
    )
    projected_grad = jnp.stack(
        [
            merge_heads(rotate(query_grad, cosine_table, -sine_table)),
            merge_heads(rotate(key_grad, cosine_table, -sine_table)),
            merge_heads(value_grad),
        ],
        axis=0,
    ).astype(jnp.bfloat16)
    joint_grad = jnp.einsum(
        "td,cte->cde", first_input, projected_grad, preferred_element_type=jnp.float32
    )
    first_input_grad = input_total(
        jnp.einsum("cte,cde->td", projected_grad, joint_full, preferred_element_type=jnp.float32)
    )
    embed_grad_in, gain_one_grad = norm_one_back(first_input_grad)
    gate_vector_grad, up_vector_grad = embed_back(attn_total_grad + embed_grad_in)
    vector_grad = jnp.stack(
        [gain_one_grad, gain_two_grad, gain_three_grad, gate_vector_grad, up_vector_grad], axis=0
    )
    readout_grad = jnp.concatenate([router_grad, head_grad], axis=1)
    joint_red, mixer_red, upward_red, downward_red, readout_red, vector_red = (
        lax.psum_scatter(joint_grad, "dp", scatter_dimension=1, tiled=True),
        lax.psum_scatter(mixer_grad, "dp", scatter_dimension=1, tiled=True),
        lax.psum_scatter(upward_grad, "dp", scatter_dimension=1, tiled=True),
        lax.psum_scatter(downward_grad, "dp", scatter_dimension=2, tiled=True),
        lax.psum_scatter(readout_grad, "dp", scatter_dimension=0, tiled=True),
        lax.psum_scatter(vector_grad, "dp", scatter_dimension=1, tiled=True),
    )
    split_squares = (
        jnp.sum(joint_red * joint_red)
        + jnp.sum(mixer_red * mixer_red)
        + jnp.sum(upward_red * upward_red)
        + jnp.sum(downward_red * downward_red)
    )
    shared_squares = jnp.sum(readout_red * readout_red) + jnp.sum(vector_red * vector_red)
    partial_squares = split_squares + shared_squares / mp_count
    norm_squared = lax.psum(partial_squares, ("dp", "mp"))
    grad_norm = jnp.sqrt(norm_squared)
    factor = clip_limit / (grad_norm + 1e-06)
    steps_taken = step_count[0].astype(jnp.float32)
    bias_one = 1.0 - beta_one**steps_taken
    bias_two = 1.0 - beta_two**steps_taken
    joint_new = adam_update(
        joint_proj, joint_moment, joint_square, joint_red, factor, bias_one, bias_two, matrix_rate
    )
    mixer_new = adam_update(
        mixer_proj, mixer_moment, mixer_square, mixer_red, factor, bias_one, bias_two, matrix_rate
    )
    upward_new = adam_update(
        upward_proj,
        upward_moment,
        upward_square,
        upward_red,
        factor,
        bias_one,
        bias_two,
        matrix_rate,
    )
    downward_new = adam_update(
        downward_proj,
        downward_moment,
        downward_square,
        downward_red,
        factor,
        bias_one,
        bias_two,
        matrix_rate,
    )
    readout_new = adam_update(
        readout,
        readout_moment,
        readout_square,
        readout_red,
        factor,
        bias_one,
        bias_two,
        matrix_rate,
    )
    vector_new = adam_update(
        vectors, vectors_moment, vectors_square, vector_red, factor, bias_one, bias_two, vector_rate
    )
    return (
        loss_total,
        grad_norm,
        joint_new[0],
        joint_new[1],
        joint_new[2],
        mixer_new[0],
        mixer_new[1],
        mixer_new[2],
        upward_new[0],
        upward_new[1],
        upward_new[2],
        downward_new[0],
        downward_new[1],
        downward_new[2],
        readout_new[0],
        readout_new[1],
        readout_new[2],
        vector_new[0],
        vector_new[1],
        vector_new[2],
    )


def solution(mesh):
    token = [P("dp", None), P("dp", None), P("dp", None, None), P()]
    weights = [
        P(None, "dp", "mp"), P("mp", "dp"), P(None, "dp", None, "mp"), P(None, "mp", "dp"), P("dp", None), P(None, "dp"),
    ]
    triple = tuple(spec for spec in weights for _ in range(3))
    near = mesh.shape["dp"] == 16 and mesh.shape["mp"] == 2
    return jax.shard_map(
        on_device if near else on_device_wide,
        mesh=mesh,
        in_specs=tuple(token) + triple,
        out_specs=(P(), P()) + triple,
        check_vma=False,
    )
```
